32 devices in a mesh: ctx: 8 (over z, x), fsdp: 4 (over y, core).
Axes of the slice: x: 2, y: 2, z: 4, core: 2. Of those that a mesh axis runs over, the one named last changes fastest.
Arguments:
- clean_in: bfloat16 [16, 2, 512, 768], P('fsdp', None, 'ctx'), may hold values from -6 to 6
- segments: int32 [16, 2, 512], P('fsdp', None, 'ctx'), may hold values from 0 to 6, as said below
- noise: int32 [16, 2, 512], P('fsdp', None, 'ctx'), may hold values 0 or 1
- mask_embed: bfloat16 [768], P('fsdp'), may hold values from -6 to 6
- norm1_gain: bfloat16 [768], P('fsdp'), may hold values from 0.25 to 1.75
- qkv_weight: bfloat16 [768, 2304], P('fsdp'), may hold values from -0.21875 to 0.21875
- out_weight: bfloat16 [768, 768], P('fsdp'), may hold values from -0.875 to 0.875
- norm2_gain: bfloat16 [768], P('fsdp'), may hold values from 0.25 to 1.75
- up_weight: bfloat16 [768, 3072], P('fsdp'), may hold values from -0.21875 to 0.21875
- up_bias: bfloat16 [3072], P('fsdp'), may hold values from -3 to 3
- down_weight: bfloat16 [3072, 768], P('fsdp'), may hold values from -0.109375 to 0.109375
- down_bias: bfloat16 [768], P('fsdp'), may hold values from -3 to 3
- out_grad: bfloat16 [16, 2, 2, 512, 768], P('fsdp', None, None, 'ctx'), may hold values from -6 to 6
Outputs:
- block_out: bfloat16 [16, 2, 2, 512, 768], P('fsdp', None, None, 'ctx')
- input_grad: float32 [16, 2, 512, 768], P('fsdp', None, 'ctx')
- mask_embed_grad: float32 [768], P('fsdp')
- norm1_gain_grad: float32 [768], P('fsdp')
- qkv_weight_grad: float32 [768, 2304], P('fsdp')
- out_weight_grad: float32 [768, 768], P('fsdp')
- norm2_gain_grad: float32 [768], P('fsdp')
- up_weight_grad: float32 [768, 3072], P('fsdp')
- up_bias_grad: float32 [3072], P('fsdp')
- down_weight_grad: float32 [3072, 768], P('fsdp')
- down_bias_grad: float32 [768], P('fsdp')
The draws below stay inside these ranges and needn't reach their ends.
Inputs may be any that keep to these rules, and one draw needn't show every extreme that they name: `segments`: document numbers never fall as the position grows within a sequence, and distinct documents have distinct numbers; the first document is numbered 0 and the last of a sequence has the largest number; each document has 2000 tokens at most, only the last of a sequence has fewer than 200, and the first has min(2000, max(200, 576)).
All inputs are finite; a program needn't handle non-finite values. No bound on the sum of `noise` on one device may be relied on, other than what follows from the above.
Results may differ from the reference program's by a relative error of at most 0.012.
Values may be sent and summed in bfloat16 or wider, within the bound.
A program may use at most 384 MiB of HBM per device.

```python
import math
from functools import partial
import jax
import jax.numpy as jnp
from jax import lax

D = 768
HEADS = 12
HEAD = 64
FF = 3072
BLK = 16
DOC_MIN = 200
DOC_MAX = 2000
SEQ = 1024
HALF = 512
PIECE = 64
SEQS = 16


def draw_segments(key, part):
    count = SEQ // DOC_MIN + 2
    drawn = jax.random.randint(key, (SEQS, count - 1), DOC_MIN, DOC_MAX + 1, dtype=jnp.int32)
    opening = jnp.full((SEQS, 1), min(DOC_MAX, max(DOC_MIN, HALF + PIECE)), dtype=jnp.int32)
    lengths = jnp.concatenate([opening, drawn], axis=1)
    ends = jnp.cumsum(lengths, axis=1)
    index = jnp.arange(HALF, dtype=jnp.int32)
    later = (2 * (HALF // PIECE) - 1 - index // PIECE) * PIECE + index % PIECE
    positions = jnp.stack([index, later])
    passed = (ends[:, :, None, None] <= positions[None, None, :, :]).astype(jnp.int32)
    counted = jnp.sum(passed, axis=1).astype(jnp.int32)
    highest = jnp.max(counted, axis=(1, 2), keepdims=True)
    shifted = counted + (count - 1) - highest
    return jnp.where(counted == 0, 0, shifted).astype(jnp.int32)


def with_ends(values, own_key, low, largest):
    spot = [jax.random.randint(jax.random.fold_in(own_key, axis), (), 0, length) for axis, length in enumerate(values.shape)]
    main_axis = values.shape.index(max(values.shape))
    next_to = spot[:main_axis] + [(spot[main_axis] + 1) % values.shape[main_axis]] + spot[main_axis + 1:]
    return values.at[tuple(spot)].set(low).at[tuple(next_to)].set(largest)


def levels(rng, extent, pieces, low, top_value):
    gain = 1.0
    for dim, blocks in pieces:
        steps = jax.random.uniform(jax.random.fold_in(jax.random.fold_in(rng, 6), dim), (blocks,), jnp.float32, low / len(pieces), top_value / len(pieces))
        gain = gain * jnp.repeat(jnp.exp(steps), extent[dim] // blocks).reshape((-1,) + (1,) * (len(extent) - 1 - dim))
    return gain


def centred(key, shape, deviation, limit, cuts=(), kind=jnp.bfloat16):
    values = deviation * jax.random.normal(key, shape, jnp.float32)
    if cuts:
        values = values * levels(key, shape, cuts, -0.22, 0.18)
    return jnp.clip(values, -limit, limit).astype(kind)


def setup_inputs(seed: int = 0) -> dict:
    arg_keys = jax.random.split(jax.random.key(seed), 14)
    return {
        "clean_in": centred(arg_keys[0], (SEQS, 2, HALF, D), 1.0, 6.0, ((0, 4), (2, 8))),
        "segments": draw_segments(jax.random.fold_in(arg_keys[13], 71), 0),
        "noise": with_ends((jax.random.randint(arg_keys[2], (SEQS, 2, HALF), 0, 2) < 1).astype(jnp.int32), jax.random.fold_in(arg_keys[2], 1), 0, 1),
        "mask_embed": centred(arg_keys[3], (D,), 1.0, 6.0, ((0, 4),)),
        "norm1_gain": jnp.clip(1.0 + 0.15 * jax.random.normal(arg_keys[4], (D,), jnp.float32), 0.25, 1.75).astype(jnp.bfloat16),
        "qkv_weight": centred(arg_keys[5], (D, 3 * D), D ** -0.5, 0.21875, ((0, 4),)),
        "out_weight": centred(arg_keys[6], (D, D), (D // 16) ** -0.5, 0.875, ((0, 4),)),
        "norm2_gain": jnp.clip(1.0 + 0.15 * jax.random.normal(arg_keys[7], (D,), jnp.float32), 0.25, 1.75).astype(jnp.bfloat16),
        "up_weight": centred(arg_keys[8], (D, FF), D ** -0.5, 0.21875, ((0, 4),)),
        "up_bias": centred(arg_keys[9], (FF,), 0.5, 3.0, ((0, 4),)),
        "down_weight": centred(arg_keys[10], (FF, D), FF ** -0.5, 0.109375, ((0, 4),)),
        "down_bias": centred(arg_keys[11], (D,), 0.5, 3.0, ((0, 4),)),
        "out_grad": centred(arg_keys[12], (SEQS, 2, 2, HALF, D), 1.0, 6.0, ((0, 4), (3, 8))),
    }


@jax.custom_vjp
def low(v):
    return lax.optimization_barrier(v.astype(jnp.bfloat16)).astype(jnp.float32)

@jax.custom_vjp
def low_back(v):
    return v

def low_keep(v):
    return (low(v), None)

def low_pass(kept, grad):
    return (grad,)

def back_keep(v):
    return (v, None)

def back_low(kept, grad):
    return (low(grad),)
low.defvjp(low_keep, low_pass)
low_back.defvjp(back_keep, back_low)
EPS = 1e-05
HIGH = lax.Precision.HIGHEST

def normalize(values):
    centre = values - lax.optimization_barrier(jnp.mean(values, axis=-1, keepdims=True))
    return centre * lax.rsqrt(lax.optimization_barrier(jnp.mean(centre * centre, axis=-1, keepdims=True)) + EPS)

def layout_positions():
    index = jnp.arange(HALF, dtype=jnp.int32)
    later = (2 * (HALF // PIECE) - 1 - index // PIECE) * PIECE + index % PIECE
    return jnp.concatenate([index, later])

def rope_tables(positions):
    half_head = HEAD // 2
    frequency = 10000.0 ** (-(jnp.arange(half_head, dtype=jnp.float32) * 2.0) / HEAD)
    angles = positions.astype(jnp.float32)[:, None] * frequency[None, :]
    return (jnp.cos(angles), jnp.sin(angles))

def rotate(values, cos_part, sin_part):
    count = values.shape[0]
    heads = values.reshape(count, HEADS, HEAD)
    half_head = HEAD // 2
    leading = heads[..., :half_head]
    trailing = heads[..., half_head:]
    cosine = cos_part[:, None, :]
    sine_part = sin_part[:, None, :]
    turned = jnp.concatenate([leading * cosine - trailing * sine_part, trailing * cosine + leading * sine_part], axis=-1)
    return turned.reshape(count, D)

def allowed_pairs(query_meta, key_meta):
    query_copy, query_block, query_doc = query_meta
    key_copy, key_block, key_doc = key_meta
    same_doc = query_doc[:, None] == key_doc[None, :]
    query_noisy = (query_copy == 0)[:, None]
    key_noisy = (key_copy == 0)[None, :]
    query_column = query_block[:, None]
    key_row = key_block[None, :]
    inner = query_noisy & key_noisy & (key_row == query_column)
    earlier = query_noisy & ~key_noisy & (key_row < query_column)
    causal = ~query_noisy & ~key_noisy & (key_row <= query_column)
    return same_doc & (inner | earlier | causal)

def attend_block(query_block, meta_block, keys, values, key_meta):
    scores = low_back(jnp.einsum('qhd,khd->hqk', query_block, keys, precision=HIGH) * HEAD ** (-0.5))
    allowed = allowed_pairs(meta_block, key_meta)[None]
    scores = jnp.where(allowed, scores, -1e+30)
    top = lax.optimization_barrier(jnp.max(scores, axis=-1, keepdims=True))
    weights = jnp.exp(scores - top)
    probs = weights / lax.optimization_barrier(jnp.sum(weights, axis=-1, keepdims=True))
    return jnp.einsum('hqk,khd->qhd', low(probs), values, precision=HIGH)

def layer(clean, embed, gain_one, qkv_matrix, out_matrix, gain_two, up_matrix, up_shift, down_matrix, down_shift, noise_row, doc_row, cos_part, sin_part, positions):
    noisy = jnp.where(noise_row[:, None] == 1, embed[None, :], clean)
    stacked = jnp.concatenate([noisy, clean], axis=0)
    row_count = stacked.shape[0]
    normed = low(normalize(stacked) * gain_one)
    projected = low_back(jnp.dot(normed, qkv_matrix, precision=HIGH))
    queries = low(rotate(projected[:, :D], cos_part, sin_part))
    keys = low(rotate(projected[:, D:2 * D], cos_part, sin_part))
    values = low(projected[:, 2 * D:])
    copy_ids = jnp.concatenate([jnp.zeros((SEQ,), jnp.int32), jnp.ones((SEQ,), jnp.int32)])
    blocks = jnp.concatenate([positions, positions]) // BLK
    docs = jnp.concatenate([doc_row, doc_row])
    block_rows = math.gcd(512, row_count)
    block_count = row_count // block_rows
    query_heads = queries.reshape(block_count, block_rows, HEADS, HEAD)
    meta = (copy_ids.reshape(block_count, block_rows), blocks.reshape(block_count, block_rows), docs.reshape(block_count, block_rows))
    key_heads = keys.reshape(row_count, HEADS, HEAD)
    value_heads = values.reshape(row_count, HEADS, HEAD)
    step_fn = jax.checkpoint(partial(attend_block, keys=key_heads, values=value_heads, key_meta=(copy_ids, blocks, docs)))
    mixed = lax.map(lambda items: step_fn(items[0], items[1]), (query_heads, meta))
    mixed = low(low_back(mixed.reshape(row_count, D)))
    attn = low_back(jnp.dot(mixed, out_matrix, precision=HIGH))
    resid = stacked + attn
    normed_two = low(normalize(resid) * gain_two)
    hidden = low_back(jnp.dot(normed_two, up_matrix, precision=HIGH) + up_shift)
    active = low(jax.nn.gelu(hidden, approximate=True))
    branch = low_back(jnp.dot(active, down_matrix, precision=HIGH) + down_shift)
    return resid + branch

def reference(clean_in, segments, noise, mask_embed, norm1_gain, qkv_weight, out_weight, norm2_gain, up_weight, up_bias, down_weight, down_bias, out_grad):
    positions = layout_positions()
    cos_part, sin_part = rope_tables(jnp.concatenate([positions, positions]))
    params = tuple((item.astype(jnp.float32) for item in (mask_embed, norm1_gain, qkv_weight, out_weight, norm2_gain, up_weight, up_bias, down_weight, down_bias)))
    cleans = clean_in.astype(jnp.float32).reshape(SEQS, SEQ, D)
    docs = segments.reshape(SEQS, SEQ)
    noises = noise.reshape(SEQS, SEQ)
    cotangents = out_grad.astype(jnp.float32).reshape(SEQS, 2 * SEQ, D)

    def per_sequence(totals, inputs):
        clean, doc_row, noise_row, cotangent = inputs
        forward = partial(layer, noise_row=noise_row, doc_row=doc_row, cos_part=cos_part, sin_part=sin_part, positions=positions)
        output, pullback = jax.vjp(forward, clean, *params)
        grads = pullback(cotangent)
        totals = tuple((total + grad_item for total, grad_item in zip(totals, grads[1:])))
        return (totals, (output.astype(jnp.bfloat16), grads[0]))
    zeros = tuple((jnp.zeros_like(item) for item in params))
    totals, scanned = lax.scan(per_sequence, zeros, (cleans, docs, noises, cotangents))
    block_out = scanned[0].reshape(SEQS, 2, 2, HALF, D)
    input_grad = scanned[1].reshape(SEQS, 2, HALF, D)
    return (block_out, input_grad, totals[0], totals[1], totals[2], totals[3], totals[4], totals[5], totals[6], totals[7], totals[8])
```

```python
from functools import partial

import jax
import jax.numpy as jnp
from jax import lax
from jax.experimental import pallas as pl
from jax.experimental.pallas import tpu as pltpu
from jax.sharding import PartitionSpec as P

D = 768
HEADS = 12
HEAD = 64
FF = 3072
BLK = 16


EPS = 1e-05
together = 4


def normalize(values):
    centre = values - jnp.mean(values, axis=-1, keepdims=True)
    scale = lax.rsqrt(jnp.mean(centre * centre, axis=-1, keepdims=True) + EPS)
    return (centre * scale, scale)


def norm_back(grad_in, normed, scale):
    centred = grad_in - jnp.mean(grad_in, axis=-1, keepdims=True)
    return scale * (centred - normed * jnp.mean(grad_in * normed, axis=-1, keepdims=True))


def rope_tables(positions):
    half_head = HEAD // 2
    frequency = 10000.0 ** (-(jnp.arange(half_head, dtype=jnp.float32) * 2.0) / HEAD)
    angles = positions.astype(jnp.float32)[:, None] * frequency[None, :]
    return (jnp.cos(angles), jnp.sin(angles))


def rotate(values, cos_part, sin_part, reverse):
    count = values.shape[0]
    heads = values.reshape(count, HEADS, HEAD)
    half_head = HEAD // 2
    leading = heads[..., :half_head]
    trailing = heads[..., half_head:]
    cosine = cos_part[:, None, :]
    sine_part = sin_part[:, None, :]
    if reverse:
        parts = [leading * cosine + trailing * sine_part, trailing * cosine - leading * sine_part]
    else:
        parts = [leading * cosine - trailing * sine_part, trailing * cosine + leading * sine_part]
    return jnp.concatenate(parts, axis=-1).reshape(count, D)


def split_heads(values):
    count = values.shape[0]
    return values.reshape(count, HEADS // together, together * HEAD).transpose(1, 0, 2)


def join_heads(values):
    groups, count, width = values.shape
    return values.transpose(1, 0, 2).reshape(count, groups * width)


def allowed_pairs(query_copy, query_block, query_doc, key_copy, key_block, key_doc):
    same_doc = query_doc[:, None] == key_doc[None, :]
    query_noisy = (query_copy == 0)[:, None]
    key_noisy = (key_copy == 0)[None, :]
    query_column = query_block[:, None]
    key_row = key_block[None, :]
    inner = query_noisy & key_noisy & (key_row == query_column)
    earlier = query_noisy & ~key_noisy & (key_row < query_column)
    causal = ~query_noisy & ~key_noisy & (key_row <= query_column)
    return same_doc & (inner | earlier | causal)


def masked_scores(query_group, key_group, allowed):
    query_heads = query_group.reshape(query_group.shape[0], together, HEAD)
    key_heads = key_group.reshape(key_group.shape[0], together, HEAD)
    raw = jnp.einsum(
        "qhd,khd->hqk", query_heads, key_heads, preferred_element_type=jnp.float32
    ) * HEAD ** (-0.5)
    return (jnp.where(allowed[None], raw, -1e30), query_heads, key_heads)


def group_forward(items, allowed):
    query_group, key_group, value_group = items
    count = query_group.shape[0]
    scores, query_heads, key_heads = masked_scores(query_group, key_group, allowed)
    value_heads = value_group.reshape(value_group.shape[0], together, HEAD)
    top = jnp.max(scores, axis=-1, keepdims=True)
    weights = jnp.exp(scores - top)
    total = jnp.sum(weights, axis=-1, keepdims=True)
    probs = (weights / total).astype(jnp.bfloat16)
    mixed = jnp.einsum("hqk,khd->qhd", probs, value_heads, preferred_element_type=jnp.float32)
    return (mixed.reshape(count, together * HEAD), (top + jnp.log(total))[..., 0])


def group_backward(items, allowed, tail):
    query_group, key_group, value_group, grad_group, log_total = items
    count = query_group.shape[0]
    key_count = key_group.shape[0]
    scores, query_heads, key_heads = masked_scores(query_group, key_group, allowed)
    value_heads = value_group.reshape(key_count, together, HEAD)
    grad_heads = grad_group.reshape(count, together, HEAD)
    probs = jnp.exp(scores - log_total[..., None])
    prob_grad = jnp.einsum(
        "qhd,khd->hqk", grad_heads, value_heads, preferred_element_type=jnp.float32
    )
    centre = jnp.sum(probs * prob_grad, axis=-1, keepdims=True)
    score_grad = (probs * (prob_grad - centre)).astype(jnp.bfloat16)
    query_grad = jnp.einsum(
        "hqk,khd->qhd", score_grad, key_heads, preferred_element_type=jnp.float32
    ) * HEAD ** (-0.5)
    tail_probs = probs.astype(jnp.bfloat16)
    value_grad = jnp.einsum(
        "hqk,qhd->khd", tail_probs, grad_heads, preferred_element_type=jnp.float32
    )
    key_grad = jnp.einsum(
        "hqk,qhd->khd", score_grad, query_heads, preferred_element_type=jnp.float32
    ) * HEAD ** (-0.5)
    return (
        query_grad.reshape(count, together * HEAD),
        key_grad.reshape(tail, together * HEAD),
        value_grad.reshape(tail, together * HEAD),
        centre[..., 0],
    )


def reduce_grads(grads):
    shards = (
        lax.psum_scatter(grads[0], "fsdp", scatter_dimension=0, tiled=True),
        lax.psum_scatter(grads[1], "fsdp", scatter_dimension=0, tiled=True),
        lax.psum_scatter(grads[2], "fsdp", scatter_dimension=0, tiled=True),
        lax.psum_scatter(grads[3], "fsdp", scatter_dimension=0, tiled=True),
        lax.psum_scatter(grads[4], "fsdp", scatter_dimension=0, tiled=True),
        lax.psum_scatter(grads[5], "fsdp", scatter_dimension=0, tiled=True),
        lax.psum_scatter(grads[6], "fsdp", scatter_dimension=0, tiled=True),
        lax.psum_scatter(grads[7], "fsdp", scatter_dimension=0, tiled=True),
        lax.psum_scatter(grads[8], "fsdp", scatter_dimension=0, tiled=True),
    )
    return lax.psum(
        (
            shards[0],
            shards[1],
            shards[2],
            shards[3],
            shards[4],
            shards[5],
            shards[6],
            shards[7],
            shards[8],
        ),
        "ctx",
    )


def add_tuples(left_items, right_items):
    return tuple((left_item + right_item for left_item, right_item in zip(left_items, right_items)))


def general_body(
    clean_in,
    segments,
    noise,
    mask_embed,
    norm1_gain,
    qkv_weight,
    out_weight,
    norm2_gain,
    up_weight,
    up_bias,
    down_weight,
    down_bias,
    out_grad,
):
    qkv_full, out_full, gain_low, embed_low = (
        lax.all_gather(qkv_weight, "fsdp", axis=0, tiled=True),
        lax.all_gather(out_weight, "fsdp", axis=0, tiled=True),
        lax.all_gather(norm1_gain, "fsdp", axis=0, tiled=True),
        lax.all_gather(mask_embed, "fsdp", axis=0, tiled=True),
    )
    up_full, up_low, down_full, down_low, gain_two_low = (
        lax.all_gather(up_weight, "fsdp", axis=0, tiled=True),
        lax.all_gather(up_bias, "fsdp", axis=0, tiled=True),
        lax.all_gather(down_weight, "fsdp", axis=0, tiled=True),
        lax.all_gather(down_bias, "fsdp", axis=0, tiled=True),
        lax.all_gather(norm2_gain, "fsdp", axis=0, tiled=True),
    )
    gain_one = gain_low.astype(jnp.float32)
    gain_two = gain_two_low.astype(jnp.float32)
    embed_row = embed_low.astype(jnp.float32)
    up_shift = up_low.astype(jnp.float32)
    down_shift = down_low.astype(jnp.float32)
    micro_count = clean_in.shape[0]
    piece = clean_in.shape[2]
    local_rows = 2 * piece
    ctx_count = lax.axis_size("ctx")
    ctx_rank = lax.axis_index("ctx")
    span = jnp.arange(piece, dtype=jnp.int32)
    local_pos = jnp.concatenate(
        [ctx_rank * piece + span, (2 * ctx_count - 1 - ctx_rank) * piece + span]
    )
    ranks = jnp.arange(ctx_count, dtype=jnp.int32)[:, None]
    far_pos = jnp.concatenate(
        [ranks * piece + span[None, :], (2 * ctx_count - 1 - ranks) * piece + span[None, :]], axis=1
    ).reshape(-1)
    seq_len = ctx_count * local_rows
    cos_part, sin_part = rope_tables(jnp.concatenate([local_pos, local_pos]))
    query_copy = jnp.concatenate(
        [jnp.zeros((local_rows,), jnp.int32), jnp.ones((local_rows,), jnp.int32)]
    )
    key_copy = jnp.concatenate(
        [jnp.ones((seq_len,), jnp.int32), jnp.zeros((local_rows,), jnp.int32)]
    )
    query_block = jnp.concatenate([local_pos, local_pos]) // BLK
    key_block = jnp.concatenate([far_pos, local_pos]) // BLK
    full_shapes = ((D,), (D,), (D, 3 * D), (D, D), (D,), (D, FF), (FF,), (FF, D), (D,))
    totals = tuple((jnp.zeros(shape_item, jnp.float32) for shape_item in full_shapes))
    tail = seq_len + local_rows
    outputs = []
    input_grads = []
    for micro_step in range(micro_count):
        clean_rows = clean_in[micro_step].reshape(local_rows, D).astype(jnp.float32)
        noise_rows = noise[micro_step].reshape(-1)
        masked_rows = noise_rows[:, None] == 1
        doc_local = segments[micro_step].reshape(-1).astype(jnp.float32)
        noisy_rows = jnp.where(masked_rows, embed_row[None, :], clean_rows)
        stacked = jnp.concatenate([noisy_rows, clean_rows], axis=0)
        normed_one, scale_one = normalize(stacked)
        h_one = (normed_one * gain_one).astype(jnp.bfloat16)
        projected = jnp.dot(h_one, qkv_full, preferred_element_type=jnp.float32)
        queries = rotate(projected[:, :D], cos_part, sin_part, False).astype(jnp.bfloat16)
        keys = rotate(projected[:, D : 2 * D], cos_part, sin_part, False).astype(jnp.bfloat16)
        values = projected[:, 2 * D :].astype(jnp.bfloat16)
        far_keys, far_values, far_docs = (
            lax.all_gather(keys[local_rows:], "ctx", axis=0, tiled=True),
            lax.all_gather(values[local_rows:], "ctx", axis=0, tiled=True),
            lax.all_gather(doc_local.astype(jnp.bfloat16), "ctx", axis=0, tiled=True),
        )
        key_all = jnp.concatenate([far_keys, keys[:local_rows]], axis=0)
        value_all = jnp.concatenate([far_values, values[:local_rows]], axis=0)
        query_doc = jnp.concatenate([doc_local, doc_local])
        key_doc = jnp.concatenate([far_docs.astype(jnp.float32), doc_local])
        allowed = allowed_pairs(query_copy, query_block, query_doc, key_copy, key_block, key_doc)
        query_groups = split_heads(queries)
        key_groups = split_heads(key_all)
        value_groups = split_heads(value_all)
        mixed_groups, log_totals = lax.map(
            partial(group_forward, allowed=allowed), (query_groups, key_groups, value_groups)
        )
        mixed = join_heads(mixed_groups).astype(jnp.bfloat16)
        resid = stacked + jnp.dot(mixed, out_full, preferred_element_type=jnp.float32)
        normed_two, scale_two = normalize(resid)
        h_two = (normed_two * gain_two).astype(jnp.bfloat16)
        hidden = jnp.dot(h_two, up_full, preferred_element_type=jnp.float32) + up_shift
        active = jax.nn.gelu(hidden, approximate=True).astype(jnp.bfloat16)
        result = resid + jnp.dot(active, down_full, preferred_element_type=jnp.float32) + down_shift
        outputs.append(result.astype(jnp.bfloat16).reshape(2, 2, piece, D))
        cotangent = out_grad[micro_step].reshape(2 * local_rows, D).astype(jnp.float32)
        grad_out = cotangent.astype(jnp.bfloat16)
        down_grad = jnp.einsum("rf,rd->fd", active, grad_out, preferred_element_type=jnp.float32)
        down_shift_grad = jnp.sum(grad_out.astype(jnp.float32), axis=0)
        grad_active = jnp.einsum(
            "rd,fd->rf", grad_out, down_full, preferred_element_type=jnp.float32
        )
        unused, gelu_back = jax.vjp(partial(jax.nn.gelu, approximate=True), hidden)
        grad_hidden = gelu_back(grad_active)[0].astype(jnp.bfloat16)
        up_grad = jnp.einsum("rd,rf->df", h_two, grad_hidden, preferred_element_type=jnp.float32)
        up_shift_grad = jnp.sum(grad_hidden.astype(jnp.float32), axis=0)
        grad_h_two = jnp.einsum(
            "rf,df->rd", grad_hidden, up_full, preferred_element_type=jnp.float32
        )
        gain_two_grad = jnp.sum(grad_h_two * normed_two, axis=0)
        grad_resid = cotangent + norm_back(grad_h_two * gain_two, normed_two, scale_two)
        grad_attn = grad_resid.astype(jnp.bfloat16)
        out_grad_full = jnp.einsum(
            "rd,re->de", mixed, grad_attn, preferred_element_type=jnp.float32
        )
        grad_mixed = jnp.einsum(
            "re,de->rd", grad_attn, out_full, preferred_element_type=jnp.float32
        ).astype(jnp.bfloat16)
        query_grads, key_grads, value_grads, centres = lax.map(
            partial(group_backward, allowed=allowed, tail=tail),
            (query_groups, key_groups, value_groups, split_heads(grad_mixed), log_totals),
        )
        query_grad = join_heads(query_grads)
        key_grad_all = join_heads(key_grads)
        value_grad_all = join_heads(value_grads)
        key_mine, value_mine = (
            lax.psum_scatter(key_grad_all[:seq_len], "ctx", scatter_dimension=0, tiled=True),
            lax.psum_scatter(value_grad_all[:seq_len], "ctx", scatter_dimension=0, tiled=True),
        )
        key_grad = jnp.concatenate([key_grad_all[seq_len:], key_mine], axis=0)
        value_grad = jnp.concatenate([value_grad_all[seq_len:], value_mine], axis=0)
        grad_proj = jnp.concatenate(
            [
                rotate(query_grad, cos_part, sin_part, True),
                rotate(key_grad, cos_part, sin_part, True),
                value_grad,
            ],
            axis=1,
        ).astype(jnp.bfloat16)
        qkv_grad = jnp.einsum("rd,re->de", h_one, grad_proj, preferred_element_type=jnp.float32)
        grad_h_one = jnp.einsum(
            "re,de->rd", grad_proj, qkv_full, preferred_element_type=jnp.float32
        )
        gain_one_grad = jnp.sum(grad_h_one * normed_one, axis=0)
        grad_rows = grad_resid + norm_back(grad_h_one * gain_one, normed_one, scale_one)
        grad_noisy = grad_rows[:local_rows]
        input_grads.append(
            (grad_rows[local_rows:] + jnp.where(masked_rows, 0.0, grad_noisy)).reshape(2, piece, D)
        )
        embed_grad = jnp.sum(jnp.where(masked_rows, grad_noisy, 0.0), axis=0)
        step_grads = (
            embed_grad,
            gain_one_grad,
            qkv_grad,
            out_grad_full,
            gain_two_grad,
            up_grad,
            up_shift_grad,
            down_grad,
            down_shift_grad,
        )
        totals = add_tuples(totals, step_grads)
    reduced = reduce_grads(totals)
    block_out = jnp.stack(outputs)
    input_grad = jnp.stack(input_grads)
    return (
        block_out,
        input_grad,
        reduced[0],
        reduced[1],
        reduced[2],
        reduced[3],
        reduced[4],
        reduced[5],
        reduced[6],
        reduced[7],
        reduced[8],
    )


PAIR=2*HEAD; PAIRS=D//PAIR
NEG=-1e30
VMEM_LIMIT=60<<20
F32=jnp.float32; BF=jnp.bfloat16

def dot_nn(a,b): return lax.dot_general(a,b,(((1,),(0,)),((),())),preferred_element_type=F32)
def dot_nt(a,b): return lax.dot_general(a,b,(((1,),(1,)),((),())),preferred_element_type=F32)
def dot_tn(a,b): return lax.dot_general(a,b,(((0,),(0,)),((),())),preferred_element_type=F32)

def tiles_of(half):
    return [(s,min(128,half-s)) for s in range(0,half,128)]

def norm_rows(rows):
    centre=rows-jnp.mean(rows,axis=-1,keepdims=True)
    scale=lax.rsqrt(jnp.mean(centre*centre,axis=-1,keepdims=True)+EPS)
    return centre*scale, scale

def swap_halves(z):
    lane=lax.broadcasted_iota(jnp.int32,z.shape,1)
    low=(lane & (HEAD-1)) < HEAD//2
    return jnp.where(low,pltpu.roll(z,PAIR-HEAD//2,1),pltpu.roll(z,HEAD//2,1))

def head_stack(z):
    lane=lax.broadcasted_iota(jnp.int32,z.shape,1)
    first=lane<HEAD
    zero=jnp.zeros_like(z)
    return jnp.concatenate([jnp.where(first,z,zero),jnp.where(first,zero,z)],axis=0)

def head_merge(z):
    n=z.shape[0]//2
    lane=lax.broadcasted_iota(jnp.int32,(n,z.shape[1]),1)
    return jnp.where(lane<HEAD,z[:n],z[n:])

def layer_rows(xc_ref,noise_ref,emb_ref):
    clean=xc_ref[...].astype(F32)
    noisy=jnp.where(noise_ref[...]==1,emb_ref[...].astype(F32),clean)
    return noisy,clean

def fwd_attn_kernel(half,xc,noise,segc,segr,emb,gain,wq,wk,wv,wout,cos,sin,
                    q_o,k_o,v_o,mix_o,lse_o,x1_o,h_s,bias_s,self_s,mix_s):
    p=pl.program_id(0)
    tiles=tiles_of(half)
    @pl.when(p==0)
    def _():
        g=gain[...].astype(F32)
        for c,rows in enumerate(layer_rows(xc,noise,emb)):
            x1_o[c*half:(c+1)*half]=rows
            n,_=norm_rows(rows)
            h_s[c*half:(c+1)*half]=(n*g).astype(BF)
        for s,m in tiles:
            n=s+m
            qb=(lax.broadcasted_iota(jnp.int32,(m,n),0)+s)//BLK
            kb=lax.broadcasted_iota(jnp.int32,(m,n),1)//BLK
            same=segc[s:n]==segr[:,:n]
            bias_s[0,s:n,:n]=jnp.where(same&(kb<qb),0.0,NEG)
            bias_s[1,s:n,:n]=jnp.where(same&(kb<=qb),0.0,NEG)
            qb=lax.broadcasted_iota(jnp.int32,(m,m),0)//BLK
            kb=lax.broadcasted_iota(jnp.int32,(m,m),1)//BLK
            same=segc[s:n]==segr[:,s:n]
            self_s[s:n,:m]=jnp.where(same&(kb==qb),0.0,NEG)
    h=h_s[...]
    cs=jnp.concatenate([cos[...],cos[...]],axis=0)
    sn=jnp.concatenate([sin[...],sin[...]],axis=0)
    z=dot_nn(h,wq[...]); q_o[...]=((z*cs+swap_halves(z)*sn).astype(BF)*BF(HEAD**-0.5)).astype(BF)
    z=dot_nn(h,wk[...]); k_o[...]=(z*cs+swap_halves(z)*sn).astype(BF)
    v_o[...]=dot_nn(h,wv[...]).astype(BF)
    idx=0
    for s,m in tiles:
        n=s+m
        for c in (0,1):
            qs=head_stack(q_o[c*half+s:c*half+n])
            kc=k_o[half:half+n]; vc=v_o[half:half+n]
            sc=dot_nt(qs,kc).reshape(2,m,n)+bias_s[c,s:n,:n][None]
            top=jnp.max(sc,axis=-1,keepdims=True)
            if c==0:
                ss=dot_nt(qs,k_o[s:n]).reshape(2,m,m)+self_s[s:n,:m][None]
                top=jnp.maximum(top,jnp.max(ss,axis=-1,keepdims=True))
            w=jnp.exp(sc-top); tot=jnp.sum(w,axis=-1,keepdims=True)
            o=dot_nn(w.astype(BF).reshape(2*m,n),vc)
            if c==0:
                w2=jnp.exp(ss-top); tot=tot+jnp.sum(w2,axis=-1,keepdims=True)
                o=o+dot_nn(w2.astype(BF).reshape(2*m,m),v_o[s:n])
            tot=tot.reshape(2*m,1)
            o=o*(1.0/tot)
            mx=head_merge(o).astype(BF)
            mix_o[c*half+s:c*half+n]=mx
            mix_s[p,c*half+s:c*half+n]=mx
            lse=top.reshape(2*m,1)+jnp.log(tot)
            lse_o[0,idx:idx+1,:2*m]=jnp.broadcast_to(lse,(2*m,128)).T[0:1]
            idx+=1
    @pl.when(p==pl.num_programs(0)-1)
    def _():
        full=jnp.concatenate([mix_s[i] for i in range(PAIRS)],axis=1)
        x1_o[...]=x1_o[...]+dot_nn(full,wout[...])

def whole(shape): return pl.BlockSpec(shape,lambda *i:(0,)*len(shape))

def fwd_attn(xc,noise,segc,segr,emb,gain,wqkv,wout,cos,sin):
    half=xc.shape[0]; R=2*half
    nt=len(tiles_of(half))*2; ntp=-(-nt//8)*8
    ws=[pl.BlockSpec((D,PAIR),(lambda off:(lambda p:(0,off+p)))(o*PAIRS)) for o in range(3)]
    rows=pl.BlockSpec((R,PAIR),lambda p:(0,p))
    return pl.pallas_call(partial(fwd_attn_kernel,half),grid=(PAIRS,),
        in_specs=[whole((half,D)),whole((half,1)),whole((half,1)),whole((1,half)),whole((1,D)),whole((1,D)),*ws,whole((D,D)),whole((half,PAIR)),whole((half,PAIR))],
        out_specs=[rows,rows,rows,rows,pl.BlockSpec((1,ntp,256),lambda p:(p,0,0)),whole((R,D))],
        out_shape=[jax.ShapeDtypeStruct((R,D),BF)]*4+[jax.ShapeDtypeStruct((PAIRS,ntp,256),F32),jax.ShapeDtypeStruct((R,D),F32)],
        scratch_shapes=[pltpu.VMEM((R,D),BF),pltpu.VMEM((2,half,half),F32),pltpu.VMEM((half,128),F32),pltpu.VMEM((PAIRS,R,PAIR),BF)],
        compiler_params=pltpu.CompilerParams(vmem_limit_bytes=VMEM_LIMIT,dimension_semantics=("arbitrary",)),
        cost_estimate=pl.CostEstimate(flops=2*R*D*(3*D+D)+24*R*half*D//2*2,bytes_accessed=16<<20,transcendentals=R*half*HEADS),
        name="fwd_attn")(xc,noise,segc,segr,emb,gain,wqkv,wqkv,wqkv,wout,cos,sin)

GC=(2.0/3.141592653589793)**0.5
def ffn_fwd_kernel(x1,gain,wup,bup,wdn,bdn,out_o,act_o,dg_o,h_s,acc):
    j=pl.program_id(0)
    @pl.when(j==0)
    def _():
        n,_=norm_rows(x1[...])
        h_s[...]=(n*gain[...].astype(F32)).astype(BF)
        acc[...]=x1[...]+bdn[...].astype(F32)
    R=h_s.shape[0]; ch=R//3
    for i in range(3):
        r=slice(i*ch,(i+1)*ch)
        u=dot_nn(h_s[r],wup[...])+bup[...].astype(F32)
        u2=u*u
        t=jnp.tanh(GC*(u+0.044715*u*u2))
        a=0.5*(1.0+t)
        act=(u*a).astype(BF)
        act_o[r]=act
        dg_o[r]=(a+0.5*u*(1.0-t*t)*(GC*(1.0+3*0.044715*u2))).astype(BF)
        acc[r]+=dot_nn(act,wdn[...])
    @pl.when(j==pl.num_programs(0)-1)
    def _(): out_o[...]=acc[...].astype(BF)

def ffn_fwd(x1,gain,wup,bup,wdn,bdn,tile=512):
    R=x1.shape[0]
    return pl.pallas_call(ffn_fwd_kernel,grid=(FF//tile,),
        in_specs=[whole((R,D)),whole((1,D)),pl.BlockSpec((D,tile),lambda j:(0,j)),pl.BlockSpec((1,tile),lambda j:(0,j)),pl.BlockSpec((tile,D),lambda j:(j,0)),whole((1,D))],
        out_specs=[whole((R,D)),pl.BlockSpec((R,tile),lambda j:(0,j)),pl.BlockSpec((R,tile),lambda j:(0,j))],
        out_shape=[jax.ShapeDtypeStruct((R,D),BF),jax.ShapeDtypeStruct((R,FF),BF),jax.ShapeDtypeStruct((R,FF),BF)],
        scratch_shapes=[pltpu.VMEM((R,D),BF),pltpu.VMEM((R,D),F32)],
        compiler_params=pltpu.CompilerParams(vmem_limit_bytes=VMEM_LIMIT,dimension_semantics=("arbitrary",)),
        cost_estimate=pl.CostEstimate(flops=4*R*D*FF,bytes_accessed=30<<20,transcendentals=R*FF),
        name="ffn_fwd")(x1,gain,wup,bup,wdn,bdn)

def ffn_bwd_kernel(x1,gain,gy,act,dg,wup,wdn,dwup_o,dwdn_o,dbup_o,dbdn_o,dgain_o,gx1_o,ga_o,hT_s,gh):
    j=pl.program_id(0)
    @pl.when(j==0)
    def _():
        n,_=norm_rows(x1[...])
        hT_s[...]=(n*gain[...].astype(F32)).astype(BF).T
        gh[...]=jnp.zeros_like(gh)
        dbdn_o[...]=jnp.sum(gy[...].astype(F32),axis=0,keepdims=True)
    ga=dot_nt(gy[...],wdn[...])
    gu=(dg[...].astype(F32)*ga).astype(BF)
    dwdn_o[...]=dot_tn(act[...],gy[...]).astype(BF)
    dwup_o[...]=dot_nn(hT_s[...],gu).astype(BF)
    dbup_o[...]=jnp.sum(gu.astype(F32),axis=0,keepdims=True)
    gh[...]+=dot_nt(gu,wup[...])
    @pl.when(j==pl.num_programs(0)-1)
    def _():
        n,scale=norm_rows(x1[...])
        g2=gh[...]
        dgain_o[...]=jnp.sum(g2*n,axis=0,keepdims=True)
        e=g2*gain[...].astype(F32)
        gx=gy[...].astype(F32)+scale*(e-jnp.mean(e,axis=-1,keepdims=True)-n*jnp.mean(e*n,axis=-1,keepdims=True))
        gx1_o[...]=gx
        ga_o[...]=gx.astype(BF)

def ffn_bwd(x1,gain,gy,act,dg,wup,wdn,tile=512):
    R=x1.shape[0]
    col=pl.BlockSpec((R,tile),lambda j:(0,j))
    return pl.pallas_call(ffn_bwd_kernel,grid=(FF//tile,),
        in_specs=[whole((R,D)),whole((1,D)),whole((R,D)),col,col,pl.BlockSpec((D,tile),lambda j:(0,j)),pl.BlockSpec((tile,D),lambda j:(j,0))],
        out_specs=[pl.BlockSpec((D,tile),lambda j:(0,j)),pl.BlockSpec((tile,D),lambda j:(j,0)),pl.BlockSpec((1,tile),lambda j:(0,j)),whole((1,D)),whole((1,D)),whole((R,D)),whole((R,D))],
        out_shape=[jax.ShapeDtypeStruct((D,FF),BF),jax.ShapeDtypeStruct((FF,D),BF),jax.ShapeDtypeStruct((1,FF),F32),jax.ShapeDtypeStruct((1,D),F32),jax.ShapeDtypeStruct((1,D),F32),jax.ShapeDtypeStruct((R,D),F32),jax.ShapeDtypeStruct((R,D),BF)],
        scratch_shapes=[pltpu.VMEM((D,R),BF),pltpu.VMEM((R,D),F32)],
        compiler_params=pltpu.CompilerParams(vmem_limit_bytes=VMEM_LIMIT,dimension_semantics=("arbitrary",)),
        cost_estimate=pl.CostEstimate(flops=8*R*D*FF,bytes_accessed=40<<20,transcendentals=0),
        name="ffn_bwd")(x1,gain,gy,act,dg,wup,wdn)

def bwd_attn_kernel(half,xc,noise,segc,segr,emb,gain,gx1,ga,q,k,v,mix,lse,wq,wk,wv,wout,cos,sin,
                    dw_o,dwout_o,gin_o,demb_o,dgain_o,hT_s,gh,biasT_s,selfT_s,dq_s,dk_s,dv_s):
    p=pl.program_id(0)
    R=2*half
    tiles=tiles_of(half)
    @pl.when(p==0)
    def _():
        g=gain[...].astype(F32)
        for c,rows in enumerate(layer_rows(xc,noise,emb)):
            n,_=norm_rows(rows)
            hT_s[:,c*half:(c+1)*half]=(n*g).astype(BF).T
        gh[...]=jnp.zeros_like(gh)
        for s,m in tiles:
            n=s+m
            qb=(lax.broadcasted_iota(jnp.int32,(n,m),1)+s)//BLK
            kb=lax.broadcasted_iota(jnp.int32,(n,m),0)//BLK
            same=segc[:n]==segr[:,s:n]
            biasT_s[0,:n,s:n]=jnp.where(same&(kb<qb),0.0,NEG)
            biasT_s[1,:n,s:n]=jnp.where(same&(kb<=qb),0.0,NEG)
            qb=lax.broadcasted_iota(jnp.int32,(m,m),1)//BLK
            kb=lax.broadcasted_iota(jnp.int32,(m,m),0)//BLK
            same=segc[s:n]==segr[:,s:n]
            selfT_s[s:n,:m]=jnp.where(same&(kb==qb),0.0,NEG)
    gm=dot_nt(ga[...],wout[...]).astype(BF)
    dwout_o[...]=dot_tn(mix[...],ga[...]).astype(BF)
    gd=gm.astype(F32)*mix[...].astype(F32)
    dk_s[...]=jnp.zeros_like(dk_s); dv_s[...]=jnp.zeros_like(dv_s)
    idx=0
    for s,m in tiles:
        n=s+m
        for c in (0,1):
            rs=slice(c*half+s,c*half+n)
            qs=head_stack(q[rs]); gs=head_stack(gm[rs])
            delta=jnp.sum(head_stack(gd[rs]).T,axis=0,keepdims=True)
            row=lse[0,idx:idx+1,:2*m]
            def part(krows,bias):
                kc=k[krows]; vc=v[krows]
                st=dot_nt(kc,qs)+jnp.concatenate([bias,bias],axis=1)
                pt=jnp.exp(st-row)
                dp=dot_nt(vc,gs)
                ds=(pt*(dp-delta)).astype(BF)
                dv_s[krows]+=dot_nn(pt.astype(BF),gs)
                dk_s[krows]+=dot_nn(ds,qs)
                return dot_tn(ds,kc)
            dq=part(slice(half,half+n),biasT_s[c,:n,s:n])
            if c==0: dq=dq+part(slice(s,n),selfT_s[s:n,:m])
            dq_s[rs]=head_merge(dq)*HEAD**-0.5
            idx+=1
    cs=jnp.concatenate([cos[...],cos[...]],axis=0)
    sn=jnp.concatenate([sin[...],sin[...]],axis=0)
    total=None
    for i,(g,w) in enumerate(((dq_s,wq),(dk_s,wk),(dv_s,wv))):
        z=g[...]
        if i<2: z=z*cs-swap_halves(z)*sn
        z=z.astype(BF)
        dw_o[i]=dot_nn(hT_s[...],z).astype(BF)
        gh[...]+=dot_nt(z,w[...])
    @pl.when(p==pl.num_programs(0)-1)
    def _():
        g=gain[...].astype(F32)
        outs=[]; dg=0.0
        for c,rows in enumerate(layer_rows(xc,noise,emb)):
            n,scale=norm_rows(rows)
            g1=gh[c*half:(c+1)*half]
            dg=dg+jnp.sum(g1*n,axis=0,keepdims=True)
            e=g1*g
            outs.append(gx1[c*half:(c+1)*half]+scale*(e-jnp.mean(e,axis=-1,keepdims=True)-n*jnp.mean(e*n,axis=-1,keepdims=True)))
        masked=noise[...]==1
        gin_o[...]=(outs[1]+jnp.where(masked,0.0,outs[0])).astype(gin_o.dtype)
        demb_o[...]=jnp.sum(jnp.where(masked,outs[0],0.0),axis=0,keepdims=True)
        dgain_o[...]=dg

def bwd_attn(xc,noise,segc,segr,emb,gain,gx1,ga,q,k,v,mix,lse,wqkv,wout,cos,sin):
    half=xc.shape[0]; R=2*half
    ntp=lse.shape[1]
    ws=[pl.BlockSpec((D,PAIR),(lambda off:(lambda p:(0,off+p)))(o*PAIRS)) for o in range(3)]
    rows=pl.BlockSpec((R,PAIR),lambda p:(0,p))
    return pl.pallas_call(partial(bwd_attn_kernel,half),grid=(PAIRS,),
        in_specs=[whole((half,D)),whole((half,1)),whole((half,1)),whole((1,half)),whole((1,D)),whole((1,D)),whole((R,D)),whole((R,D)),rows,rows,rows,rows,
                  pl.BlockSpec((1,ntp,256),lambda p:(p,0,0)),*ws,pl.BlockSpec((PAIR,D),lambda p:(p,0)),whole((half,PAIR)),whole((half,PAIR))],
        out_specs=[pl.BlockSpec((3,D,PAIR),lambda p:(0,0,p)),pl.BlockSpec((PAIR,D),lambda p:(p,0)),whole((half,D)),whole((1,D)),whole((1,D))],
        out_shape=[jax.ShapeDtypeStruct((3,D,D),BF),jax.ShapeDtypeStruct((D,D),BF),jax.ShapeDtypeStruct((half,D),BF),jax.ShapeDtypeStruct((1,D),F32),jax.ShapeDtypeStruct((1,D),F32)],
        scratch_shapes=[pltpu.VMEM((D,R),BF),pltpu.VMEM((R,D),F32),pltpu.VMEM((2,half,-(-half//128)*128),F32),pltpu.VMEM((half,128),F32)]+[pltpu.VMEM((R,PAIR),F32)]*3,
        compiler_params=pltpu.CompilerParams(vmem_limit_bytes=VMEM_LIMIT,dimension_semantics=("arbitrary",)),
        cost_estimate=pl.CostEstimate(flops=4*R*D*(3*D+D)+60*R*half*D//2*2,bytes_accessed=30<<20,transcendentals=R*half*HEADS),
        name="bwd_attn")(xc,noise,segc,segr,emb,gain,gx1,ga,q,k,v,mix,lse,wqkv,wqkv,wqkv,wout,cos,sin)


def flip(values, axis, count, bit):
    return lax.ppermute(values, axis, [(i, i ^ bit) for i in range(count)])


def pick(values, index, axis):
    return lax.dynamic_index_in_dim(values, index, axis, keepdims=False)


def order_two(mine, other, index, axis):
    return jnp.where(index == 0, jnp.stack([mine, other], axis), jnp.stack([other, mine], axis))


def gather_rows(shard, core, chip):
    near = order_two(shard, flip(shard, "fsdp", 4, 2), chip, 0)
    full = order_two(near, flip(near, "fsdp", 4, 1), core, 1)
    return full.reshape((4 * shard.shape[0],) + shard.shape[1:])


def halve(values, index, axis, mesh_axis, count, bit):
    received = flip(pick(values, 1 - index, axis), mesh_axis, count, bit)
    kept = pick(values, index, axis)
    return (kept.astype(F32) + received.astype(F32)).astype(BF)


def reduce_shard(grad, lead, core, chip, ranks):
    rows, cols = grad.shape[-2] // 4, grad.shape[-1]
    axis = len(lead)
    part = grad.reshape(lead + (2, 2, rows, cols))
    part = halve(part, core, axis + 1, "fsdp", 4, 1)
    part = halve(part, chip, axis, "fsdp", 4, 2)
    shape = part.shape
    for level in range(3):
        size = part.shape[-2] // 2
        part = halve(part.reshape(lead + (2, size, cols)), ranks[level], axis, "ctx", 8, 1 << level)
    for level in (2, 1, 0):
        size = part.shape[-2]
        other = flip(part, "ctx", 8, 1 << level)
        part = order_two(part, other, ranks[level], axis).reshape(lead + (2 * size, cols))
    return part.reshape(shape).astype(F32)


def to_unit(blocks, part, fill):
    extra = flip(blocks[7], "ctx", 8, 1)[None]
    pads = jnp.full((2,) + blocks.shape[1:], fill, blocks.dtype)
    first = jnp.concatenate([blocks, extra], axis=0)
    second = jnp.concatenate([blocks[6::-1], pads], axis=0)
    return jnp.where(part == 0, first, second)


def from_unit(pieces, part):
    extra = flip(pieces[8], "ctx", 8, 1)[None]
    second = jnp.concatenate([pieces[6::-1], extra], axis=0)
    return jnp.where(part == 0, pieces[:8], second)


def exchange(blocks):
    return lax.all_to_all(blocks, "ctx", 0, 0)


def even_body(clean_in, segments, noise, mask_embed, norm1_gain, qkv_weight, out_weight, norm2_gain, up_weight, up_bias,
              down_weight, down_bias, out_grad):
    rank = lax.axis_index("ctx")
    place = lax.axis_index("fsdp")
    core, chip = place & 1, place >> 1
    part = rank & 1
    ranks = (rank & 1, (rank >> 1) & 1, rank >> 2)
    piece = clean_in.shape[2]
    half = 9 * piece
    meta = jnp.concatenate([segments.reshape(8, piece), noise.reshape(8, piece)], axis=1)
    clean = to_unit(exchange(clean_in.reshape(8, piece, D)), part, 0).reshape(half, D)
    meta = exchange(meta)
    seg = to_unit(meta[:, :piece], part, -1).reshape(half)
    mask = to_unit(meta[:, piece:], part, 0).reshape(half, 1)
    qkv_full = gather_rows(qkv_weight, core, chip)
    out_full = gather_rows(out_weight, core, chip)
    small = jnp.concatenate([mask_embed, norm1_gain, norm2_gain, down_bias, up_bias])
    small = lax.all_gather(small, "fsdp", axis=0).reshape(4, -1)
    width = mask_embed.shape[0]
    embed, gain_one, gain_two, down_shift = (small[:, i * width:(i + 1) * width].reshape(1, D) for i in range(4))
    up_shift = small[:, 4 * width:].reshape(1, FF)
    up_full = gather_rows(up_weight, core, chip)
    down_full = gather_rows(down_weight, core, chip)
    cotangent = exchange(out_grad.transpose(0, 2, 1, 3, 4).reshape(8, 2, piece, D))
    cotangent = to_unit(cotangent, part, 0).transpose(1, 0, 2, 3).reshape(2 * half, D)

    cos_part, sin_part = rope_tables(part * half + jnp.arange(half, dtype=jnp.int32))
    cosine = jnp.tile(cos_part, (1, 4))
    sine = jnp.tile(jnp.concatenate([-sin_part, sin_part], axis=1), (1, 2))
    seg_col, seg_row = seg[:, None], seg[None, :]

    q, k, v, mixed, lse, resid = fwd_attn(clean, mask, seg_col, seg_row, embed, gain_one, qkv_full, out_full, cosine, sine)
    result, active, slope = ffn_fwd(resid, gain_two, up_full, up_shift, down_full, down_shift)
    up_grad, down_grad, up_shift_grad, down_shift_grad, gain_two_grad, grad_resid, grad_attn = ffn_bwd(
        resid, gain_two, cotangent, active, slope, up_full, down_full)
    block_out = from_unit(result.reshape(2, 9, piece, D).transpose(1, 0, 2, 3), part)
    block_out = exchange(block_out).reshape(4, 2, 2, piece, D).transpose(0, 2, 1, 3, 4)
    qkv_grad, out_weight_grad, grad_in, embed_grad, gain_one_grad = bwd_attn(
        clean, mask, seg_col, seg_row, embed, gain_one, grad_resid, grad_attn, q, k, v, mixed, lse, qkv_full, out_full,
        cosine, sine)
    input_grad = exchange(from_unit(grad_in.reshape(9, piece, D), part)).reshape(4, 2, piece, D).astype(F32)

    down_sum = reduce_shard(down_grad, (), core, chip, ranks)
    up_sum = reduce_shard(up_grad, (), core, chip, ranks)
    out_sum = reduce_shard(out_weight_grad, (), core, chip, ranks)
    qkv_sum = reduce_shard(qkv_grad, (3,), core, chip, ranks)
    qkv_sum = jnp.concatenate([qkv_sum[0], qkv_sum[1], qkv_sum[2]], axis=1)
    sums = jnp.concatenate([x.reshape(-1) for x in (embed_grad, gain_one_grad, gain_two_grad, down_shift_grad, up_shift_grad)])
    sums = lax.psum(sums, ("ctx", "fsdp"))
    own = [lax.dynamic_slice_in_dim(sums, i * D + place * width, width) for i in range(4)]
    own_up = lax.dynamic_slice_in_dim(sums, 4 * D + place * (FF // 4), FF // 4)
    return (block_out, input_grad, own[0], own[1], qkv_sum, out_sum, own[2], up_sum, own_up, down_sum, own[3])


def choose_body(axes, *arrays):
    even = axes["ctx"] == 8 and axes["fsdp"] == 4 and arrays[0].shape[0] == 4
    return (even_body if even else general_body)(*arrays)


def solution(mesh):
    placed = (
        P("fsdp", None, "ctx", None),
        P("fsdp", None, "ctx"),
        P("fsdp", None, "ctx"),
        P("fsdp"),
        P("fsdp"),
        P("fsdp", None),
        P("fsdp", None),
        P("fsdp"),
        P("fsdp", None),
        P("fsdp"),
        P("fsdp", None),
        P("fsdp"),
        P("fsdp", None, None, "ctx", None),
    )
    return jax.shard_map(
        partial(choose_body, dict(mesh.shape)),
        mesh=mesh,
        in_specs=placed,
        out_specs=(
            P("fsdp", None, None, "ctx", None),
            P("fsdp", None, "ctx", None),
            P("fsdp"),
            P("fsdp"),
            P("fsdp", None),
            P("fsdp", None),
            P("fsdp"),
            P("fsdp", None),
            P("fsdp"),
            P("fsdp", None),
            P("fsdp"),
        ),
        check_vma=False,
    )
```

```python
from functools import partial

import jax
import jax.numpy as jnp
from jax import lax
from jax.experimental import pallas as pl
from jax.experimental.pallas import tpu as pltpu
from jax.sharding import PartitionSpec as P

D = 768
HEADS = 12
HEAD = 64
FF = 3072
BLK = 16


EPS = 1e-05
together = 4


def normalize(values):
    centre = values - jnp.mean(values, axis=-1, keepdims=True)
    scale = lax.rsqrt(jnp.mean(centre * centre, axis=-1, keepdims=True) + EPS)
    return (centre * scale, scale)


def norm_back(grad_in, normed, scale):
    centred = grad_in - jnp.mean(grad_in, axis=-1, keepdims=True)
    return scale * (centred - normed * jnp.mean(grad_in * normed, axis=-1, keepdims=True))


def rope_tables(positions):
    half_head = HEAD // 2
    frequency = 10000.0 ** (-(jnp.arange(half_head, dtype=jnp.float32) * 2.0) / HEAD)
    angles = positions.astype(jnp.float32)[:, None] * frequency[None, :]
    return (jnp.cos(angles), jnp.sin(angles))


def rotate(values, cos_part, sin_part, reverse):
    count = values.shape[0]
    heads = values.reshape(count, HEADS, HEAD)
    half_head = HEAD // 2
    leading = heads[..., :half_head]
    trailing = heads[..., half_head:]
    cosine = cos_part[:, None, :]
    sine_part = sin_part[:, None, :]
    if reverse:
        parts = [leading * cosine + trailing * sine_part, trailing * cosine - leading * sine_part]
    else:
        parts = [leading * cosine - trailing * sine_part, trailing * cosine + leading * sine_part]
    return jnp.concatenate(parts, axis=-1).reshape(count, D)


def split_heads(values):
    count = values.shape[0]
    return values.reshape(count, HEADS // together, together * HEAD).transpose(1, 0, 2)


def join_heads(values):
    groups, count, width = values.shape
    return values.transpose(1, 0, 2).reshape(count, groups * width)


def allowed_pairs(query_copy, query_block, query_doc, key_copy, key_block, key_doc):
    same_doc = query_doc[:, None] == key_doc[None, :]
    query_noisy = (query_copy == 0)[:, None]
    key_noisy = (key_copy == 0)[None, :]
    query_column = query_block[:, None]
    key_row = key_block[None, :]
    inner = query_noisy & key_noisy & (key_row == query_column)
    earlier = query_noisy & ~key_noisy & (key_row < query_column)
    causal = ~query_noisy & ~key_noisy & (key_row <= query_column)
    return same_doc & (inner | earlier | causal)


def masked_scores(query_group, key_group, allowed):
    query_heads = query_group.reshape(query_group.shape[0], together, HEAD)
    key_heads = key_group.reshape(key_group.shape[0], together, HEAD)
    raw = jnp.einsum(
        "qhd,khd->hqk", query_heads, key_heads, preferred_element_type=jnp.float32
    ) * HEAD ** (-0.5)
    return (jnp.where(allowed[None], raw, -1e30), query_heads, key_heads)


def group_forward(items, allowed):
    query_group, key_group, value_group = items
    count = query_group.shape[0]
    scores, query_heads, key_heads = masked_scores(query_group, key_group, allowed)
    value_heads = value_group.reshape(value_group.shape[0], together, HEAD)
    top = jnp.max(scores, axis=-1, keepdims=True)
    weights = jnp.exp(scores - top)
    total = jnp.sum(weights, axis=-1, keepdims=True)
    probs = (weights / total).astype(jnp.bfloat16)
    mixed = jnp.einsum("hqk,khd->qhd", probs, value_heads, preferred_element_type=jnp.float32)
    return (mixed.reshape(count, together * HEAD), (top + jnp.log(total))[..., 0])


def group_backward(items, allowed, tail):
    query_group, key_group, value_group, grad_group, log_total = items
    count = query_group.shape[0]
    key_count = key_group.shape[0]
    scores, query_heads, key_heads = masked_scores(query_group, key_group, allowed)
    value_heads = value_group.reshape(key_count, together, HEAD)
    grad_heads = grad_group.reshape(count, together, HEAD)
    probs = jnp.exp(scores - log_total[..., None])
    prob_grad = jnp.einsum(
        "qhd,khd->hqk", grad_heads, value_heads, preferred_element_type=jnp.float32
    )
    centre = jnp.sum(probs * prob_grad, axis=-1, keepdims=True)
    score_grad = (probs * (prob_grad - centre)).astype(jnp.bfloat16)
    query_grad = jnp.einsum(
        "hqk,khd->qhd", score_grad, key_heads, preferred_element_type=jnp.float32
    ) * HEAD ** (-0.5)
    tail_probs = probs.astype(jnp.bfloat16)
    value_grad = jnp.einsum(
        "hqk,qhd->khd", tail_probs, grad_heads, preferred_element_type=jnp.float32
    )
    key_grad = jnp.einsum(
        "hqk,qhd->khd", score_grad, query_heads, preferred_element_type=jnp.float32
    ) * HEAD ** (-0.5)
    return (
        query_grad.reshape(count, together * HEAD),
        key_grad.reshape(tail, together * HEAD),
        value_grad.reshape(tail, together * HEAD),
        centre[..., 0],
    )


def reduce_grads(grads):
    shards = (
        lax.psum_scatter(grads[0], "fsdp", scatter_dimension=0, tiled=True),
        lax.psum_scatter(grads[1], "fsdp", scatter_dimension=0, tiled=True),
        lax.psum_scatter(grads[2], "fsdp", scatter_dimension=0, tiled=True),
        lax.psum_scatter(grads[3], "fsdp", scatter_dimension=0, tiled=True),
        lax.psum_scatter(grads[4], "fsdp", scatter_dimension=0, tiled=True),
        lax.psum_scatter(grads[5], "fsdp", scatter_dimension=0, tiled=True),
        lax.psum_scatter(grads[6], "fsdp", scatter_dimension=0, tiled=True),
        lax.psum_scatter(grads[7], "fsdp", scatter_dimension=0, tiled=True),
        lax.psum_scatter(grads[8], "fsdp", scatter_dimension=0, tiled=True),
    )
    return lax.psum(
        (
            shards[0],
            shards[1],
            shards[2],
            shards[3],
            shards[4],
            shards[5],
            shards[6],
            shards[7],
            shards[8],
        ),
        "ctx",
    )


def add_tuples(left_items, right_items):
    return tuple((left_item + right_item for left_item, right_item in zip(left_items, right_items)))


def general_body(
    clean_in,
    segments,
    noise,
    mask_embed,
    norm1_gain,
    qkv_weight,
    out_weight,
    norm2_gain,
    up_weight,
    up_bias,
    down_weight,
    down_bias,
    out_grad,
):
    qkv_full, out_full, gain_low, embed_low = (
        lax.all_gather(qkv_weight, "fsdp", axis=0, tiled=True),
        lax.all_gather(out_weight, "fsdp", axis=0, tiled=True),
        lax.all_gather(norm1_gain, "fsdp", axis=0, tiled=True),
        lax.all_gather(mask_embed, "fsdp", axis=0, tiled=True),
    )
    up_full, up_low, down_full, down_low, gain_two_low = (
        lax.all_gather(up_weight, "fsdp", axis=0, tiled=True),
        lax.all_gather(up_bias, "fsdp", axis=0, tiled=True),
        lax.all_gather(down_weight, "fsdp", axis=0, tiled=True),
        lax.all_gather(down_bias, "fsdp", axis=0, tiled=True),
        lax.all_gather(norm2_gain, "fsdp", axis=0, tiled=True),
    )
    gain_one = gain_low.astype(jnp.float32)
    gain_two = gain_two_low.astype(jnp.float32)
    embed_row = embed_low.astype(jnp.float32)
    up_shift = up_low.astype(jnp.float32)
    down_shift = down_low.astype(jnp.float32)
    micro_count = clean_in.shape[0]
    piece = clean_in.shape[2]
    local_rows = 2 * piece
    ctx_count = lax.axis_size("ctx")
    ctx_rank = lax.axis_index("ctx")
    span = jnp.arange(piece, dtype=jnp.int32)
    local_pos = jnp.concatenate(
        [ctx_rank * piece + span, (2 * ctx_count - 1 - ctx_rank) * piece + span]
    )
    ranks = jnp.arange(ctx_count, dtype=jnp.int32)[:, None]
    far_pos = jnp.concatenate(
        [ranks * piece + span[None, :], (2 * ctx_count - 1 - ranks) * piece + span[None, :]], axis=1
    ).reshape(-1)
    seq_len = ctx_count * local_rows
    cos_part, sin_part = rope_tables(jnp.concatenate([local_pos, local_pos]))
    query_copy = jnp.concatenate(
        [jnp.zeros((local_rows,), jnp.int32), jnp.ones((local_rows,), jnp.int32)]
    )
    key_copy = jnp.concatenate(
        [jnp.ones((seq_len,), jnp.int32), jnp.zeros((local_rows,), jnp.int32)]
    )
    query_block = jnp.concatenate([local_pos, local_pos]) // BLK
    key_block = jnp.concatenate([far_pos, local_pos]) // BLK
    full_shapes = ((D,), (D,), (D, 3 * D), (D, D), (D,), (D, FF), (FF,), (FF, D), (D,))
    totals = tuple((jnp.zeros(shape_item, jnp.float32) for shape_item in full_shapes))
    tail = seq_len + local_rows
    outputs = []
    input_grads = []
    for micro_step in range(micro_count):
        clean_rows = clean_in[micro_step].reshape(local_rows, D).astype(jnp.float32)
        noise_rows = noise[micro_step].reshape(-1)
        masked_rows = noise_rows[:, None] == 1
        doc_local = segments[micro_step].reshape(-1).astype(jnp.float32)
        noisy_rows = jnp.where(masked_rows, embed_row[None, :], clean_rows)
        stacked = jnp.concatenate([noisy_rows, clean_rows], axis=0)
        normed_one, scale_one = normalize(stacked)
        h_one = (normed_one * gain_one).astype(jnp.bfloat16)
        projected = jnp.dot(h_one, qkv_full, preferred_element_type=jnp.float32)
        queries = rotate(projected[:, :D], cos_part, sin_part, False).astype(jnp.bfloat16)
        keys = rotate(projected[:, D : 2 * D], cos_part, sin_part, False).astype(jnp.bfloat16)
        values = projected[:, 2 * D :].astype(jnp.bfloat16)
        far_keys, far_values, far_docs = (
            lax.all_gather(keys[local_rows:], "ctx", axis=0, tiled=True),
            lax.all_gather(values[local_rows:], "ctx", axis=0, tiled=True),
            lax.all_gather(doc_local.astype(jnp.bfloat16), "ctx", axis=0, tiled=True),
        )
        key_all = jnp.concatenate([far_keys, keys[:local_rows]], axis=0)
        value_all = jnp.concatenate([far_values, values[:local_rows]], axis=0)
        query_doc = jnp.concatenate([doc_local, doc_local])
        key_doc = jnp.concatenate([far_docs.astype(jnp.float32), doc_local])
        allowed = allowed_pairs(query_copy, query_block, query_doc, key_copy, key_block, key_doc)
        query_groups = split_heads(queries)
        key_groups = split_heads(key_all)
        value_groups = split_heads(value_all)
        mixed_groups, log_totals = lax.map(
            partial(group_forward, allowed=allowed), (query_groups, key_groups, value_groups)
        )
        mixed = join_heads(mixed_groups).astype(jnp.bfloat16)
        resid = stacked + jnp.dot(mixed, out_full, preferred_element_type=jnp.float32)
        normed_two, scale_two = normalize(resid)
        h_two = (normed_two * gain_two).astype(jnp.bfloat16)
        hidden = jnp.dot(h_two, up_full, preferred_element_type=jnp.float32) + up_shift
        active = jax.nn.gelu(hidden, approximate=True).astype(jnp.bfloat16)
        result = resid + jnp.dot(active, down_full, preferred_element_type=jnp.float32) + down_shift
        outputs.append(result.astype(jnp.bfloat16).reshape(2, 2, piece, D))
        cotangent = out_grad[micro_step].reshape(2 * local_rows, D).astype(jnp.float32)
        grad_out = cotangent.astype(jnp.bfloat16)
        down_grad = jnp.einsum("rf,rd->fd", active, grad_out, preferred_element_type=jnp.float32)
        down_shift_grad = jnp.sum(grad_out.astype(jnp.float32), axis=0)
        grad_active = jnp.einsum(
            "rd,fd->rf", grad_out, down_full, preferred_element_type=jnp.float32
        )
        unused, gelu_back = jax.vjp(partial(jax.nn.gelu, approximate=True), hidden)
        grad_hidden = gelu_back(grad_active)[0].astype(jnp.bfloat16)
        up_grad = jnp.einsum("rd,rf->df", h_two, grad_hidden, preferred_element_type=jnp.float32)
        up_shift_grad = jnp.sum(grad_hidden.astype(jnp.float32), axis=0)
        grad_h_two = jnp.einsum(
            "rf,df->rd", grad_hidden, up_full, preferred_element_type=jnp.float32
        )
        gain_two_grad = jnp.sum(grad_h_two * normed_two, axis=0)
        grad_resid = cotangent + norm_back(grad_h_two * gain_two, normed_two, scale_two)
        grad_attn = grad_resid.astype(jnp.bfloat16)
        out_grad_full = jnp.einsum(
            "rd,re->de", mixed, grad_attn, preferred_element_type=jnp.float32
        )
        grad_mixed = jnp.einsum(
            "re,de->rd", grad_attn, out_full, preferred_element_type=jnp.float32
        ).astype(jnp.bfloat16)
        query_grads, key_grads, value_grads, centres = lax.map(
            partial(group_backward, allowed=allowed, tail=tail),
            (query_groups, key_groups, value_groups, split_heads(grad_mixed), log_totals),
        )
        query_grad = join_heads(query_grads)
        key_grad_all = join_heads(key_grads)
        value_grad_all = join_heads(value_grads)
        key_mine, value_mine = (
            lax.psum_scatter(key_grad_all[:seq_len], "ctx", scatter_dimension=0, tiled=True),
            lax.psum_scatter(value_grad_all[:seq_len], "ctx", scatter_dimension=0, tiled=True),
        )
        key_grad = jnp.concatenate([key_grad_all[seq_len:], key_mine], axis=0)
        value_grad = jnp.concatenate([value_grad_all[seq_len:], value_mine], axis=0)
        grad_proj = jnp.concatenate(
            [
                rotate(query_grad, cos_part, sin_part, True),
                rotate(key_grad, cos_part, sin_part, True),
                value_grad,
            ],
            axis=1,
        ).astype(jnp.bfloat16)
        qkv_grad = jnp.einsum("rd,re->de", h_one, grad_proj, preferred_element_type=jnp.float32)
        grad_h_one = jnp.einsum(
            "re,de->rd", grad_proj, qkv_full, preferred_element_type=jnp.float32
        )
        gain_one_grad = jnp.sum(grad_h_one * normed_one, axis=0)
        grad_rows = grad_resid + norm_back(grad_h_one * gain_one, normed_one, scale_one)
        grad_noisy = grad_rows[:local_rows]
        input_grads.append(
            (grad_rows[local_rows:] + jnp.where(masked_rows, 0.0, grad_noisy)).reshape(2, piece, D)
        )
        embed_grad = jnp.sum(jnp.where(masked_rows, grad_noisy, 0.0), axis=0)
        step_grads = (
            embed_grad,
            gain_one_grad,
            qkv_grad,
            out_grad_full,
            gain_two_grad,
            up_grad,
            up_shift_grad,
            down_grad,
            down_shift_grad,
        )
        totals = add_tuples(totals, step_grads)
    reduced = reduce_grads(totals)
    block_out = jnp.stack(outputs)
    input_grad = jnp.stack(input_grads)
    return (
        block_out,
        input_grad,
        reduced[0],
        reduced[1],
        reduced[2],
        reduced[3],
        reduced[4],
        reduced[5],
        reduced[6],
        reduced[7],
        reduced[8],
    )


PAIR=2*HEAD; PAIRS=D//PAIR
NEG=-1e30
VMEM_LIMIT=60<<20
F32=jnp.float32; BF=jnp.bfloat16

def dot_nn(a,b): return lax.dot_general(a,b,(((1,),(0,)),((),())),preferred_element_type=F32)
def dot_nt(a,b): return lax.dot_general(a,b,(((1,),(1,)),((),())),preferred_element_type=F32)
def dot_tn(a,b): return lax.dot_general(a,b,(((0,),(0,)),((),())),preferred_element_type=F32)

def tiles_of(half):
    return [(s,min(128,half-s)) for s in range(0,half,128)]

def norm_rows(rows):
    centre=rows-jnp.mean(rows,axis=-1,keepdims=True)
    scale=lax.rsqrt(jnp.mean(centre*centre,axis=-1,keepdims=True)+EPS)
    return centre*scale, scale

def swap_halves(z):
    lane=lax.broadcasted_iota(jnp.int32,z.shape,1)
    low=(lane & (HEAD-1)) < HEAD//2
    return jnp.where(low,pltpu.roll(z,PAIR-HEAD//2,1),pltpu.roll(z,HEAD//2,1))

def head_stack(z):
    lane=lax.broadcasted_iota(jnp.int32,z.shape,1)
    first=lane<HEAD
    zero=jnp.zeros_like(z)
    return jnp.concatenate([jnp.where(first,z,zero),jnp.where(first,zero,z)],axis=0)

def head_merge(z):
    n=z.shape[0]//2
    lane=lax.broadcasted_iota(jnp.int32,(n,z.shape[1]),1)
    return jnp.where(lane<HEAD,z[:n],z[n:])

def layer_rows(xc_ref,noise_ref,emb_ref):
    clean=xc_ref[...].astype(F32)
    noisy=jnp.where(noise_ref[...]==1,emb_ref[...].astype(F32),clean)
    return noisy,clean

def fwd_attn_kernel(half,xc,noise,segc,segr,emb,gain,wq,wk,wv,wout,cos,sin,
                    q_o,k_o,v_o,mix_o,lse_o,x1_o,h_s,bias_s,self_s,mix_s):
    p=pl.program_id(0)
    tiles=tiles_of(half)
    @pl.when(p==0)
    def _():
        g=gain[...].astype(F32)
        for c,rows in enumerate(layer_rows(xc,noise,emb)):
            x1_o[c*half:(c+1)*half]=rows
            n,_=norm_rows(rows)
            h_s[c*half:(c+1)*half]=(n*g).astype(BF)
        for s,m in tiles:
            n=s+m
            qb=(lax.broadcasted_iota(jnp.int32,(m,n),0)+s)//BLK
            kb=lax.broadcasted_iota(jnp.int32,(m,n),1)//BLK
            same=segc[s:n]==segr[:,:n]
            bias_s[0,s:n,:n]=jnp.where(same&(kb<qb),0.0,NEG)
            bias_s[1,s:n,:n]=jnp.where(same&(kb<=qb),0.0,NEG)
            qb=lax.broadcasted_iota(jnp.int32,(m,m),0)//BLK
            kb=lax.broadcasted_iota(jnp.int32,(m,m),1)//BLK
            same=segc[s:n]==segr[:,s:n]
            self_s[s:n,:m]=jnp.where(same&(kb==qb),0.0,NEG)
    h=h_s[...]
    cs=jnp.concatenate([cos[...],cos[...]],axis=0)
    sn=jnp.concatenate([sin[...],sin[...]],axis=0)
    z=dot_nn(h,wq[...]); q_o[...]=((z*cs+swap_halves(z)*sn).astype(BF)*BF(HEAD**-0.5)).astype(BF)
    z=dot_nn(h,wk[...]); k_o[...]=(z*cs+swap_halves(z)*sn).astype(BF)
    v_o[...]=dot_nn(h,wv[...]).astype(BF)
    idx=0
    for s,m in tiles:
        n=s+m
        for c in (0,1):
            qs=head_stack(q_o[c*half+s:c*half+n])
            kc=k_o[half:half+n]; vc=v_o[half:half+n]
            sc=dot_nt(qs,kc).reshape(2,m,n)+bias_s[c,s:n,:n][None]
            top=jnp.max(sc,axis=-1,keepdims=True)
            if c==0:
                ss=dot_nt(qs,k_o[s:n]).reshape(2,m,m)+self_s[s:n,:m][None]
                top=jnp.maximum(top,jnp.max(ss,axis=-1,keepdims=True))
            w=jnp.exp(sc-top); tot=jnp.sum(w,axis=-1,keepdims=True)
            o=dot_nn(w.astype(BF).reshape(2*m,n),vc)
            if c==0:
                w2=jnp.exp(ss-top); tot=tot+jnp.sum(w2,axis=-1,keepdims=True)
                o=o+dot_nn(w2.astype(BF).reshape(2*m,m),v_o[s:n])
            tot=tot.reshape(2*m,1)
            o=o*(1.0/tot)
            mx=head_merge(o).astype(BF)
            mix_o[c*half+s:c*half+n]=mx
            mix_s[p,c*half+s:c*half+n]=mx
            lse=top.reshape(2*m,1)+jnp.log(tot)
            lse_o[0,idx:idx+1,:2*m]=jnp.broadcast_to(lse,(2*m,128)).T[0:1]
            idx+=1
    @pl.when(p==pl.num_programs(0)-1)
    def _():
        full=jnp.concatenate([mix_s[i] for i in range(PAIRS)],axis=1)
        x1_o[...]=x1_o[...]+dot_nn(full,wout[...])

def whole(shape): return pl.BlockSpec(shape,lambda *i:(0,)*len(shape))

def fwd_attn_comm_kernel(half,*refs):
    ins,(up,down,gout,zeros),rest=refs[:12],refs[12:16],refs[16:]
    outs,(up_o,down_o,cot_o),scratch=rest[:6],rest[6:9],rest[9:13]
    a_send,a_recv,w_send,w_recv,local=rest[13:]
    p=pl.program_id(0)
    c,_=place_ids()
    weights=[GatherRows(up,up_o,w_send.at[0],w_recv.at[0],local.at[0]),GatherRows(down,down_o,w_send.at[1],w_recv.at[1],local.at[1])]
    rows=[ToUnit(lambda q,h,i=i:gout.at[q,i,h],lambda t,i=i:cot_o.at[i,t],a_send.at[i],a_recv.at[i],local.at[2+i]) for i in range(2)]
    pads=[pltpu.make_async_copy(zeros,cot_o.at[i,pl.ds(7,2)],local.at[4+i]) for i in range(2)]
    @pl.when(p==0)
    def _():
        meet(True,(1,2))
        for w in weights: w.begin()
        for r in rows: r.begin()
        @pl.when(c%2==1)
        def _():
            for d in pads: d.start()
            for d in pads: d.wait()
    fwd_attn_kernel(half,*ins,*outs,*scratch)
    @pl.when(p==2)
    def _():
        for w in weights: w.relay_far()
    @pl.when(p==3)
    def _():
        for w in weights: w.relay_x()
    @pl.when(p==pl.num_programs(0)-1)
    def _():
        for w in weights: w.finish()
        for r in rows: r.finish()

def fwd_attn(xc,noise,segc,segr,emb,gain,wqkv,wout,cos,sin,up,down,gout):
    half=xc.shape[0]; R=2*half
    piece=gout.shape[3]
    zeros=jnp.zeros((2,piece,D),BF)
    nt=len(tiles_of(half))*2; ntp=-(-nt//8)*8
    ws=[pl.BlockSpec((D,PAIR),(lambda off:(lambda p:(0,off+p)))(o*PAIRS)) for o in range(3)]
    rows=pl.BlockSpec((R,PAIR),lambda p:(0,p))
    return pl.pallas_call(partial(fwd_attn_comm_kernel,half),grid=(PAIRS,),
        in_specs=[whole((half,D)),whole((half,1)),whole((half,1)),whole((1,half)),whole((1,D)),whole((1,D)),*ws,whole((D,D)),whole((half,PAIR)),whole((half,PAIR)),whole(up.shape),whole(down.shape),ANYSPACE,whole(zeros.shape)],
        out_specs=[rows,rows,rows,rows,pl.BlockSpec((1,ntp,256),lambda p:(p,0,0)),whole((R,D))]+[ANYSPACE]*3,
        out_shape=[jax.ShapeDtypeStruct((R,D),BF)]*4+[jax.ShapeDtypeStruct((PAIRS,ntp,256),F32),jax.ShapeDtypeStruct((R,D),F32)]
            +[jax.ShapeDtypeStruct((D,FF),BF),jax.ShapeDtypeStruct((FF,D),BF),jax.ShapeDtypeStruct((2,9,piece,D),BF)],
        scratch_shapes=[pltpu.VMEM((R,D),BF),pltpu.VMEM((2,half,half),F32),pltpu.VMEM((half,128),F32),pltpu.VMEM((PAIRS,R,PAIR),BF),
            DMA((2,8)),DMA((2,9)),DMA((2,5)),DMA((2,5)),DMA((6,))],
        compiler_params=pltpu.CompilerParams(vmem_limit_bytes=VMEM_LIMIT,dimension_semantics=("arbitrary",),collective_id=1,has_side_effects=True),
        cost_estimate=pl.CostEstimate(flops=2*R*D*(3*D+D)+24*R*half*D//2*2,bytes_accessed=16<<20,transcendentals=R*half*HEADS),
        name="fwd_attn")(xc,noise,segc,segr,emb,gain,wqkv,wqkv,wqkv,wout,cos,sin,up,down,gout,zeros)

GC=(2.0/3.141592653589793)**0.5
def ffn_fwd_kernel(x1,gain,wup,bup,wdn,bdn,out_o,act_o,dg_o,h_s,acc):
    j=pl.program_id(0)
    @pl.when(j==0)
    def _():
        n,_=norm_rows(x1[...])
        h_s[...]=(n*gain[...].astype(F32)).astype(BF)
        acc[...]=x1[...]+bdn[...].astype(F32)
    R=h_s.shape[0]; ch=R//3
    for i in range(3):
        r=slice(i*ch,(i+1)*ch)
        u=dot_nn(h_s[r],wup[...])+bup[...].astype(F32)
        u2=u*u
        t=jnp.tanh(GC*(u+0.044715*u*u2))
        a=0.5*(1.0+t)
        act=(u*a).astype(BF)
        act_o[r]=act
        dg_o[r]=(a+0.5*u*(1.0-t*t)*(GC*(1.0+3*0.044715*u2))).astype(BF)
        acc[r]+=dot_nn(act,wdn[...])
    @pl.when(j==pl.num_programs(0)-1)
    def _(): out_o[...]=acc[...].astype(BF)

def ffn_fwd(x1,gain,wup,bup,wdn,bdn,tile=512):
    R=x1.shape[0]
    return pl.pallas_call(ffn_fwd_kernel,grid=(FF//tile,),
        in_specs=[whole((R,D)),whole((1,D)),pl.BlockSpec((D,tile),lambda j:(0,j)),pl.BlockSpec((1,tile),lambda j:(0,j)),pl.BlockSpec((tile,D),lambda j:(j,0)),whole((1,D))],
        out_specs=[whole((R,D)),pl.BlockSpec((R,tile),lambda j:(0,j)),pl.BlockSpec((R,tile),lambda j:(0,j))],
        out_shape=[jax.ShapeDtypeStruct((R,D),BF),jax.ShapeDtypeStruct((R,FF),BF),jax.ShapeDtypeStruct((R,FF),BF)],
        scratch_shapes=[pltpu.VMEM((R,D),BF),pltpu.VMEM((R,D),F32)],
        compiler_params=pltpu.CompilerParams(vmem_limit_bytes=VMEM_LIMIT,dimension_semantics=("arbitrary",)),
        cost_estimate=pl.CostEstimate(flops=4*R*D*FF,bytes_accessed=30<<20,transcendentals=R*FF),
        name="ffn_fwd")(x1,gain,wup,bup,wdn,bdn)

def ffn_bwd_kernel(x1,gain,gy,act,dg,wup,wdn,dwup_o,dwdn_o,dbup_o,dbdn_o,dgain_o,gx1_o,ga_o,hT_s,gh):
    j=pl.program_id(0)
    @pl.when(j==0)
    def _():
        n,_=norm_rows(x1[...])
        hT_s[...]=(n*gain[...].astype(F32)).astype(BF).T
        gh[...]=jnp.zeros_like(gh)
        dbdn_o[...]=jnp.sum(gy[...].astype(F32),axis=0,keepdims=True)
    ga=dot_nt(gy[...],wdn[...])
    gu=(dg[...].astype(F32)*ga).astype(BF)
    dwdn_o[...]=dot_tn(act[...],gy[...]).astype(BF)
    dwup_o[...]=dot_nn(hT_s[...],gu).astype(BF)
    dbup_o[...]=jnp.sum(gu.astype(F32),axis=0,keepdims=True)
    gh[...]+=dot_nt(gu,wup[...])
    @pl.when(j==pl.num_programs(0)-1)
    def _():
        n,scale=norm_rows(x1[...])
        g2=gh[...]
        dgain_o[...]=jnp.sum(g2*n,axis=0,keepdims=True)
        e=g2*gain[...].astype(F32)
        gx=gy[...].astype(F32)+scale*(e-jnp.mean(e,axis=-1,keepdims=True)-n*jnp.mean(e*n,axis=-1,keepdims=True))
        gx1_o[...]=gx
        ga_o[...]=gx.astype(BF)

def ffn_bwd_comm_kernel(*refs):
    ins,(res,),outs,(out_o,),scratch,(send,recv,local)=refs[:7],refs[7:8],refs[8:15],refs[15:16],refs[16:18],refs[18:]
    j=pl.program_id(0)
    rows=[FromUnit(lambda t,i=i:res.at[i,t],lambda q,h,i=i:out_o.at[q,i,h],send.at[i],recv.at[i],local.at[i]) for i in range(2)]
    @pl.when(j==0)
    def _():
        meet(True,())
        for r in rows: r.begin()
    ffn_bwd_kernel(*ins,*outs,*scratch)
    @pl.when(j==pl.num_programs(0)-1)
    def _():
        for r in rows: r.finish()

def ffn_bwd(x1,gain,gy,act,dg,wup,wdn,res,tile=512):
    R=x1.shape[0]
    piece=R//18
    col=pl.BlockSpec((R,tile),lambda j:(0,j))
    return pl.pallas_call(ffn_bwd_comm_kernel,grid=(FF//tile,),
        in_specs=[whole((R,D)),whole((1,D)),whole((R,D)),col,col,pl.BlockSpec((D,tile),lambda j:(0,j)),pl.BlockSpec((tile,D),lambda j:(j,0)),ANYSPACE],
        out_specs=[pl.BlockSpec((D,tile),lambda j:(0,j)),pl.BlockSpec((tile,D),lambda j:(j,0)),pl.BlockSpec((1,tile),lambda j:(0,j)),whole((1,D)),whole((1,D)),whole((R,D)),whole((R,D)),ANYSPACE],
        out_shape=[jax.ShapeDtypeStruct((D,FF),BF),jax.ShapeDtypeStruct((FF,D),BF),jax.ShapeDtypeStruct((1,FF),F32),jax.ShapeDtypeStruct((1,D),F32),jax.ShapeDtypeStruct((1,D),F32),jax.ShapeDtypeStruct((R,D),F32),jax.ShapeDtypeStruct((R,D),BF),jax.ShapeDtypeStruct((4,2,2,piece,D),BF)],
        scratch_shapes=[pltpu.VMEM((D,R),BF),pltpu.VMEM((R,D),F32),DMA((2,8)),DMA((2,8)),DMA((2,))],
        compiler_params=pltpu.CompilerParams(vmem_limit_bytes=VMEM_LIMIT,dimension_semantics=("arbitrary",),collective_id=2,has_side_effects=True),
        cost_estimate=pl.CostEstimate(flops=8*R*D*FF,bytes_accessed=40<<20,transcendentals=0),
        name="ffn_bwd")(x1,gain,gy,act,dg,wup,wdn,res)

def bwd_attn_kernel(half,xc,noise,segc,segr,emb,gain,gx1,ga,q,k,v,mix,lse,wq,wk,wv,wout,cos,sin,
                    dw_o,dwout_o,gin_o,demb_o,dgain_o,hT_s,gh,biasT_s,selfT_s,dq_s,dk_s,dv_s):
    p=pl.program_id(0)
    R=2*half
    tiles=tiles_of(half)
    @pl.when(p==0)
    def _():
        g=gain[...].astype(F32)
        for c,rows in enumerate(layer_rows(xc,noise,emb)):
            n,_=norm_rows(rows)
            hT_s[:,c*half:(c+1)*half]=(n*g).astype(BF).T
        gh[...]=jnp.zeros_like(gh)
        for s,m in tiles:
            n=s+m
            qb=(lax.broadcasted_iota(jnp.int32,(n,m),1)+s)//BLK
            kb=lax.broadcasted_iota(jnp.int32,(n,m),0)//BLK
            same=segc[:n]==segr[:,s:n]
            biasT_s[0,:n,s:n]=jnp.where(same&(kb<qb),0.0,NEG)
            biasT_s[1,:n,s:n]=jnp.where(same&(kb<=qb),0.0,NEG)
            qb=lax.broadcasted_iota(jnp.int32,(m,m),1)//BLK
            kb=lax.broadcasted_iota(jnp.int32,(m,m),0)//BLK
            same=segc[s:n]==segr[:,s:n]
            selfT_s[s:n,:m]=jnp.where(same&(kb==qb),0.0,NEG)
    gm=dot_nt(ga[...],wout[...]).astype(BF)
    dwout_o[...]=dot_tn(mix[...],ga[...]).astype(BF)
    gd=gm.astype(F32)*mix[...].astype(F32)
    dk_s[...]=jnp.zeros_like(dk_s); dv_s[...]=jnp.zeros_like(dv_s)
    idx=0
    for s,m in tiles:
        n=s+m
        for c in (0,1):
            rs=slice(c*half+s,c*half+n)
            qs=head_stack(q[rs]); gs=head_stack(gm[rs])
            delta=jnp.sum(head_stack(gd[rs]).T,axis=0,keepdims=True)
            row=lse[0,idx:idx+1,:2*m]
            def part(krows,bias):
                kc=k[krows]; vc=v[krows]
                st=dot_nt(kc,qs)+jnp.concatenate([bias,bias],axis=1)
                pt=jnp.exp(st-row)
                dp=dot_nt(vc,gs)
                ds=(pt*(dp-delta)).astype(BF)
                dv_s[krows]+=dot_nn(pt.astype(BF),gs)
                dk_s[krows]+=dot_nn(ds,qs)
                return dot_tn(ds,kc)
            dq=part(slice(half,half+n),biasT_s[c,:n,s:n])
            if c==0: dq=dq+part(slice(s,n),selfT_s[s:n,:m])
            dq_s[rs]=head_merge(dq)*HEAD**-0.5
            idx+=1
    cs=jnp.concatenate([cos[...],cos[...]],axis=0)
    sn=jnp.concatenate([sin[...],sin[...]],axis=0)
    total=None
    for i,(g,w) in enumerate(((dq_s,wq),(dk_s,wk),(dv_s,wv))):
        z=g[...]
        if i<2: z=z*cs-swap_halves(z)*sn
        z=z.astype(BF)
        dw_o[i]=dot_nn(hT_s[...],z).astype(BF)
        gh[...]+=dot_nt(z,w[...])
    @pl.when(p==pl.num_programs(0)-1)
    def _():
        g=gain[...].astype(F32)
        outs=[]; dg=0.0
        for c,rows in enumerate(layer_rows(xc,noise,emb)):
            n,scale=norm_rows(rows)
            g1=gh[c*half:(c+1)*half]
            dg=dg+jnp.sum(g1*n,axis=0,keepdims=True)
            e=g1*g
            outs.append(gx1[c*half:(c+1)*half]+scale*(e-jnp.mean(e,axis=-1,keepdims=True)-n*jnp.mean(e*n,axis=-1,keepdims=True)))
        masked=noise[...]==1
        gin_o[...]=(outs[1]+jnp.where(masked,0.0,outs[0])).astype(gin_o.dtype)
        demb_o[...]=jnp.sum(jnp.where(masked,outs[0],0.0),axis=0,keepdims=True)
        dgain_o[...]=dg

def bwd_attn(xc,noise,segc,segr,emb,gain,gx1,ga,q,k,v,mix,lse,wqkv,wout,cos,sin):
    half=xc.shape[0]; R=2*half
    ntp=lse.shape[1]
    ws=[pl.BlockSpec((D,PAIR),(lambda off:(lambda p:(0,off+p)))(o*PAIRS)) for o in range(3)]
    rows=pl.BlockSpec((R,PAIR),lambda p:(0,p))
    return pl.pallas_call(partial(bwd_attn_kernel,half),grid=(PAIRS,),
        in_specs=[whole((half,D)),whole((half,1)),whole((half,1)),whole((1,half)),whole((1,D)),whole((1,D)),whole((R,D)),whole((R,D)),rows,rows,rows,rows,
                  pl.BlockSpec((1,ntp,256),lambda p:(p,0,0)),*ws,pl.BlockSpec((PAIR,D),lambda p:(p,0)),whole((half,PAIR)),whole((half,PAIR))],
        out_specs=[pl.BlockSpec((3,D,PAIR),lambda p:(0,0,p)),pl.BlockSpec((PAIR,D),lambda p:(p,0)),whole((half,D)),whole((1,D)),whole((1,D))],
        out_shape=[jax.ShapeDtypeStruct((3,D,D),BF),jax.ShapeDtypeStruct((D,D),BF),jax.ShapeDtypeStruct((half,D),BF),jax.ShapeDtypeStruct((1,D),F32),jax.ShapeDtypeStruct((1,D),F32)],
        scratch_shapes=[pltpu.VMEM((D,R),BF),pltpu.VMEM((R,D),F32),pltpu.VMEM((2,half,-(-half//128)*128),F32),pltpu.VMEM((half,128),F32)]+[pltpu.VMEM((R,PAIR),F32)]*3,
        compiler_params=pltpu.CompilerParams(vmem_limit_bytes=VMEM_LIMIT,dimension_semantics=("arbitrary",)),
        cost_estimate=pl.CostEstimate(flops=4*R*D*(3*D+D)+60*R*half*D//2*2,bytes_accessed=30<<20,transcendentals=R*half*HEADS),
        name="bwd_attn")(xc,noise,segc,segr,emb,gain,gx1,ga,q,k,v,mix,lse,wqkv,wqkv,wqkv,wout,cos,sin)


MESH = pl.DeviceIdType.MESH
INVMEM = pl.BlockSpec(memory_space=pltpu.VMEM)
ANYSPACE = pl.BlockSpec(memory_space=pl.ANY)


def place_ids():
    return lax.axis_index("ctx"), lax.axis_index("fsdp")


def meet(all_ranks, fsdp_partners):
    c, f = place_ids()
    sem = pltpu.get_barrier_semaphore()
    count = 0
    ranks = [(c + s) % 8 for s in range(1, 8)] if all_ranks else [c + 1 - 2 * (c % 2)]
    for rank in ranks:
        pl.semaphore_signal(sem, inc=1, device_id={"ctx": rank}, device_id_type=MESH)
        count += 1
    for s in fsdp_partners:
        other = (f + 2) % 4 if s == 2 else f + 1 - 2 * (f % 2) if s == 1 else 3 - f
        pl.semaphore_signal(sem, inc=1, device_id={"fsdp": other}, device_id_type=MESH)
        count += 1
    pl.semaphore_wait(sem, count)


def remote(src, dst, send, recv, where):
    return pltpu.make_async_remote_copy(src_ref=src, dst_ref=dst, send_sem=send, recv_sem=recv, device_id=where,
                                        device_id_type=MESH)


class ToUnit:
    def __init__(self, source, target, send, recv, local):
        self.source, self.target, self.send, self.recv, self.local = source, target, send, recv, local
        self.c, _ = place_ids()

    def message(self, s):
        c = self.c
        t = (c + s) % 8
        odd, last = t % 2, c // 7
        slot = (1 - odd) * c + odd * ((1 - last) * (6 - c) + last * 8)
        return remote(self.source(t // 2, odd), self.target(slot), self.send.at[s], self.recv.at[slot],
                      {"ctx": t - odd * last})

    def begin(self):
        for s in range(1, 8):
            self.message(s).start()

        @pl.when(self.c == 7)
        def _():
            self.message(0).start()

        @pl.when(self.c != 7)
        def _():
            self.own_safe().start()

    def own_safe(self):
        c = self.c
        part = c % 2
        slot = (1 - part) * c + part * (6 - c + c // 7)
        return pltpu.make_async_copy(self.source(c // 2, part), self.target(slot), self.local)

    def finish(self):
        c = self.c
        part = c % 2

        @pl.when(c == 7)
        def _():
            self.message(0).wait_send()

        @pl.when(c != 7)
        def _():
            self.own_safe().wait()

        for s in range(1, 8):
            self.message(s).wait_send()
        own = (1 - part) * c + part * (6 - c)
        for slot in range(9):
            take = slot != own
            if slot > 6:
                take = take & (part == 0)

            @pl.when(take)
            def _():
                remote(self.target(slot), self.target(slot), self.send.at[0], self.recv.at[slot], {"ctx": c}).wait_recv()


class FromUnit:
    def __init__(self, source, target, send, recv, local):
        self.source, self.target, self.send, self.recv, self.local = source, target, send, recv, local
        self.c, _ = place_ids()

    def message(self, s):
        c = self.c
        part = c % 2
        rank = (c + s) % 8
        slot = (1 - part) * rank + part * (6 - rank + rank // 7)
        return remote(self.source(slot), self.target(c // 2, part), self.send.at[s], self.recv.at[c], {"ctx": rank})

    def extra(self):
        c = self.c
        seq = c // 2
        return remote(self.source(8), self.target(seq, 1), self.send.at[0], self.recv.at[2 * seq + 1], {"ctx": 7})

    def own(self):
        c = self.c
        part = c % 2
        slot = (1 - part) * c + part * (6 - c + c // 7)
        return pltpu.make_async_copy(self.source(slot), self.target(c // 2, part), self.local)

    def each(self, remote_op, own_op):
        c = self.c
        part = c % 2
        for s in range(1, 8):
            rank = (c + s) % 8

            @pl.when((part == 0) | (rank != 7))
            def _():
                remote_op(self.message(s))

        @pl.when(part == 0)
        def _():
            remote_op(self.extra())

        @pl.when(c != 7)
        def _():
            own_op(self.own())

    def begin(self):
        self.each(lambda m: m.start(), lambda m: m.start())

    def finish(self):
        self.each(lambda m: m.wait_send(), lambda m: m.wait())
        c = self.c
        for block in range(8):
            @pl.when((c == 7) | (c != block))
            def _():
                ref = self.target(block // 2, block % 2)
                remote(ref, ref, self.send.at[0], self.recv.at[block], {"ctx": c}).wait_recv()


class GatherRows:
    def __init__(self, shard, full, send, recv, local, parts=1):
        c, f = place_ids()
        n = shard.shape[0]
        n2 = n // 2
        m = n2 // parts
        h = c % 2
        sib, far, xn = f + 1 - 2 * (f % 2), (f + 2) % 4, c + 1 - 2 * (c % 2)
        diag = (sib + 2) % 4
        rows = lambda start, size: full.at[pl.ds(pl.multiple_of(start, 16), size)]
        same = lambda ref, i, where: remote(ref, ref, send.at[i], recv.at[i], where)
        mine = rows(f * n, n)
        self.copy = pltpu.make_async_copy(shard, mine, local)
        self.to_core = remote(shard, mine, send.at[0], recv.at[0], {"fsdp": sib})
        self.from_core = same(rows(sib * n, n), 0, {"fsdp": sib})
        self.to_far, self.from_far, self.to_x, self.from_x = [], [], [], []
        self.near_core, self.away_core, self.from_near, self.from_away = [], [], [], []
        for i in range(parts):
            a, b = h * n2 + i * m, (1 - h) * n2 + i * m
            near, away = rows(far * n + a, m), rows(far * n + b, m)
            k = 1 + 4 * i
            self.to_far.append(remote(shard.at[pl.ds(pl.multiple_of(a, 16), m)], rows(f * n + a, m), send.at[k], recv.at[k],
                                      {"fsdp": far}))
            self.from_far.append(same(near, k, {"fsdp": far}))
            self.to_x.append(same(near, k + 1, {"ctx": xn}))
            self.from_x.append(same(away, k + 1, {"ctx": xn}))
            self.near_core.append(same(near, k + 2, {"fsdp": sib}))
            self.away_core.append(same(away, k + 3, {"fsdp": sib}))
            self.from_near.append(same(rows(diag * n + a, m), k + 2, {"fsdp": sib}))
            self.from_away.append(same(rows(diag * n + b, m), k + 3, {"fsdp": sib}))

    def begin(self):
        for copy in self.to_far:
            copy.start()
        self.to_core.start()
        self.copy.start()

    def relay_far(self, i=0):
        self.from_far[i].wait_recv()
        self.to_x[i].start()
        self.near_core[i].start()

    def relay_x(self, i=0):
        self.from_x[i].wait_recv()
        self.away_core[i].start()

    def finish(self):
        self.copy.wait()
        for copy in [self.to_core] + self.to_far + self.to_x + self.near_core + self.away_core:
            copy.wait_send()
        for copy in [self.from_core] + self.from_near + self.from_away:
            copy.wait_recv()


def prologue_kernel(clean, meta, qkv, out, small, zeros, blank, clean_o, meta_o, qkv_o, out_o, small_o,
                    a_send, a_recv, m_send, m_recv, w_send, w_recv, s_send, s_recv, local):
    c, f = place_ids()
    meet(True, (1, 2, 3))
    rows = ToUnit(lambda q, h: clean.at[q, h], lambda i: clean_o.at[i], a_send, a_recv, local.at[0])
    notes = ToUnit(lambda q, h: meta.at[2 * q + h], lambda i: meta_o.at[i], m_send, m_recv, local.at[1])
    weights = [GatherRows(qkv, qkv_o, w_send.at[0], w_recv.at[0], local.at[2], 3),
               GatherRows(out, out_o, w_send.at[1], w_recv.at[1], local.at[3], 3)]
    weights[0].begin()
    notes.begin()
    rows.begin()
    weights[1].begin()
    others = [f + 1 - 2 * (f % 2), (f + 2) % 4, 3 - f]
    sends = [remote(small, small_o.at[f], s_send.at[i], s_recv.at[i], {"fsdp": other}) for i, other in enumerate(others)]
    for copy in sends:
        copy.start()
    own = pltpu.make_async_copy(small, small_o.at[f], local.at[4])
    own.start()
    pads = [pltpu.make_async_copy(zeros, clean_o.at[pl.ds(7, 2)], local.at[5]),
            pltpu.make_async_copy(blank, meta_o.at[pl.ds(7, 2)], local.at[6])]

    @pl.when(c % 2 == 1)
    def _():
        for copy in pads:
            copy.start()
        for copy in pads:
            copy.wait()

    for i in range(3):
        weights[0].relay_far(i)
    for i in range(3):
        weights[0].relay_x(i)
        weights[1].relay_far(i)
    for i in range(3):
        weights[1].relay_x(i)
    own.wait()
    for i, other in enumerate(others):
        sends[i].wait_send()
        remote(small_o.at[other], small_o.at[other], s_send.at[i], s_recv.at[i], {"fsdp": other}).wait_recv()
    notes.finish()
    rows.finish()
    for weight in weights:
        weight.finish()


DMA = pltpu.SemaphoreType.DMA


def prologue(clean, meta, qkv, out, small):
    piece = clean.shape[2]
    zeros = jnp.zeros((2, piece, D), BF)
    blank = jnp.concatenate([jnp.full((2, 8, piece), -1, jnp.int32), jnp.zeros((2, 8, 128 - piece), jnp.int32)], axis=2)
    return pl.pallas_call(
        prologue_kernel,
        in_specs=[ANYSPACE] * 2 + [INVMEM] * 5,
        out_specs=[ANYSPACE] * 5,
        out_shape=[jax.ShapeDtypeStruct((9, piece, D), BF), jax.ShapeDtypeStruct((9, 8, 128), jnp.int32),
                   jax.ShapeDtypeStruct((D, 3 * D), BF), jax.ShapeDtypeStruct((D, D), BF),
                   jax.ShapeDtypeStruct((4,) + small.shape, BF)],
        scratch_shapes=[DMA((8,)), DMA((9,)), DMA((8,)), DMA((9,)), DMA((2, 13)), DMA((2, 13)), DMA((3,)), DMA((3,)), DMA((7,))],
        compiler_params=pltpu.CompilerParams(collective_id=0, has_side_effects=True),
        name="prologue")(clean, meta, qkv, out, small, zeros, blank)


def flip(values, axis, count, bit):
    return lax.ppermute(values, axis, [(i, i ^ bit) for i in range(count)])


def pick(values, index, axis):
    return lax.dynamic_index_in_dim(values, index, axis, keepdims=False)


def order_two(mine, other, index, axis):
    return jnp.where(index == 0, jnp.stack([mine, other], axis), jnp.stack([other, mine], axis))


def gather_rows(shard, core, chip):
    near = order_two(shard, flip(shard, "fsdp", 4, 2), chip, 0)
    full = order_two(near, flip(near, "fsdp", 4, 1), core, 1)
    return full.reshape((4 * shard.shape[0],) + shard.shape[1:])


def halve(values, index, axis, mesh_axis, count, bit):
    received = flip(pick(values, 1 - index, axis), mesh_axis, count, bit)
    kept = pick(values, index, axis)
    return (kept.astype(F32) + received.astype(F32)).astype(BF)


def reduce_shard(grad, lead, core, chip, ranks):
    rows, cols = grad.shape[-2] // 4, grad.shape[-1]
    axis = len(lead)
    part = grad.reshape(lead + (2, 2, rows, cols))
    part = halve(part, core, axis + 1, "fsdp", 4, 1)
    part = halve(part, chip, axis, "fsdp", 4, 2)
    shape = part.shape
    for level in range(3):
        size = part.shape[-2] // 2
        part = halve(part.reshape(lead + (2, size, cols)), ranks[level], axis, "ctx", 8, 1 << level)
    for level in (2, 1, 0):
        size = part.shape[-2]
        other = flip(part, "ctx", 8, 1 << level)
        part = order_two(part, other, ranks[level], axis).reshape(lead + (2 * size, cols))
    return part.reshape(shape).astype(F32)


def to_unit(blocks, part, fill):
    extra = flip(blocks[7], "ctx", 8, 1)[None]
    pads = jnp.full((2,) + blocks.shape[1:], fill, blocks.dtype)
    first = jnp.concatenate([blocks, extra], axis=0)
    second = jnp.concatenate([blocks[6::-1], pads], axis=0)
    return jnp.where(part == 0, first, second)


def from_unit(pieces, part):
    extra = flip(pieces[8], "ctx", 8, 1)[None]
    second = jnp.concatenate([pieces[6::-1], extra], axis=0)
    return jnp.where(part == 0, pieces[:8], second)


def exchange(blocks):
    return lax.all_to_all(blocks, "ctx", 0, 0)


def even_body(clean_in, segments, noise, mask_embed, norm1_gain, qkv_weight, out_weight, norm2_gain, up_weight, up_bias,
              down_weight, down_bias, out_grad):
    rank = lax.axis_index("ctx")
    place = lax.axis_index("fsdp")
    core, chip = place & 1, place >> 1
    part = rank & 1
    ranks = (rank & 1, (rank >> 1) & 1, rank >> 2)
    piece = clean_in.shape[2]
    half = 9 * piece
    meta = jnp.concatenate([segments.reshape(8, 1, piece), noise.reshape(8, 1, piece)], axis=2)
    meta = jnp.broadcast_to(meta, (8, 8, 2 * piece))
    small = jnp.concatenate([mask_embed, norm1_gain, norm2_gain, down_bias, up_bias]).reshape(-1, 128)
    small = jnp.pad(small, ((0, 16 - small.shape[0]), (0, 0)))
    clean, meta, qkv_full, out_full, small = prologue(clean_in, meta, qkv_weight, out_weight, small)
    clean = clean.reshape(half, D)
    seg = meta[:, 0, :piece].reshape(half)
    mask = meta[:, 0, piece:].reshape(half, 1)
    small = small.reshape(4, -1)
    width = mask_embed.shape[0]
    embed, gain_one, gain_two, down_shift = (small[:, i * width:(i + 1) * width].reshape(1, D) for i in range(4))
    up_shift = small[:, 4 * width:4 * width + up_bias.shape[0]].reshape(1, FF)

    cos_part, sin_part = rope_tables(part * half + jnp.arange(half, dtype=jnp.int32))
    cosine = jnp.tile(cos_part, (1, 4))
    sine = jnp.tile(jnp.concatenate([-sin_part, sin_part], axis=1), (1, 2))
    seg_col, seg_row = seg[:, None], seg[None, :]

    q, k, v, mixed, lse, resid, up_full, down_full, cotangent = fwd_attn(
        clean, mask, seg_col, seg_row, embed, gain_one, qkv_full, out_full, cosine, sine, up_weight, down_weight, out_grad)
    cotangent = cotangent.reshape(2 * half, D)
    result, active, slope = ffn_fwd(resid, gain_two, up_full, up_shift, down_full, down_shift)
    up_grad, down_grad, up_shift_grad, down_shift_grad, gain_two_grad, grad_resid, grad_attn, block_out = ffn_bwd(
        resid, gain_two, cotangent, active, slope, up_full, down_full, result.reshape(2, 9, piece, D))
    qkv_grad, out_weight_grad, grad_in, embed_grad, gain_one_grad = bwd_attn(
        clean, mask, seg_col, seg_row, embed, gain_one, grad_resid, grad_attn, q, k, v, mixed, lse, qkv_full, out_full,
        cosine, sine)
    input_grad = exchange(from_unit(grad_in.reshape(9, piece, D), part)).reshape(4, 2, piece, D).astype(F32)

    down_sum = reduce_shard(down_grad, (), core, chip, ranks)
    up_sum = reduce_shard(up_grad, (), core, chip, ranks)
    out_sum = reduce_shard(out_weight_grad, (), core, chip, ranks)
    qkv_sum = reduce_shard(qkv_grad, (3,), core, chip, ranks)
    qkv_sum = jnp.concatenate([qkv_sum[0], qkv_sum[1], qkv_sum[2]], axis=1)
    sums = jnp.concatenate([x.reshape(-1) for x in (embed_grad, gain_one_grad, gain_two_grad, down_shift_grad, up_shift_grad)])
    sums = lax.psum(sums, ("ctx", "fsdp"))
    own = [lax.dynamic_slice_in_dim(sums, i * D + place * width, width) for i in range(4)]
    own_up = lax.dynamic_slice_in_dim(sums, 4 * D + place * (FF // 4), FF // 4)
    return (block_out, input_grad, own[0], own[1], qkv_sum, out_sum, own[2], up_sum, own_up, down_sum, own[3])


def choose_body(axes, *arrays):
    even = axes["ctx"] == 8 and axes["fsdp"] == 4 and arrays[0].shape[0] == 4
    return (even_body if even else general_body)(*arrays)


def solution(mesh):
    placed = (
        P("fsdp", None, "ctx", None),
        P("fsdp", None, "ctx"),
        P("fsdp", None, "ctx"),
        P("fsdp"),
        P("fsdp"),
        P("fsdp", None),
        P("fsdp", None),
        P("fsdp"),
        P("fsdp", None),
        P("fsdp"),
        P("fsdp", None),
        P("fsdp"),
        P("fsdp", None, None, "ctx", None),
    )
    return jax.shard_map(
        partial(choose_body, dict(mesh.shape)),
        mesh=mesh,
        in_specs=placed,
        out_specs=(
            P("fsdp", None, None, "ctx", None),
            P("fsdp", None, "ctx", None),
            P("fsdp"),
            P("fsdp"),
            P("fsdp", None),
            P("fsdp", None),
            P("fsdp"),
            P("fsdp", None),
            P("fsdp"),
            P("fsdp", None),
            P("fsdp"),
        ),
        check_vma=False,
    )
```

```python
from functools import partial

import jax
import jax.numpy as jnp
import numpy as np
from jax import lax
from jax.experimental import pallas as pl
from jax.experimental.pallas import tpu as pltpu
from jax.sharding import PartitionSpec as P

D = 768
HEADS = 12
HEAD = 64
FF = 3072
BLK = 16


EPS = 1e-05
together = 4


def normalize(values):
    centre = values - jnp.mean(values, axis=-1, keepdims=True)
    scale = lax.rsqrt(jnp.mean(centre * centre, axis=-1, keepdims=True) + EPS)
    return (centre * scale, scale)


def norm_back(grad_in, normed, scale):
    centred = grad_in - jnp.mean(grad_in, axis=-1, keepdims=True)
    return scale * (centred - normed * jnp.mean(grad_in * normed, axis=-1, keepdims=True))


def rope_tables(positions):
    half_head = HEAD // 2
    frequency = 10000.0 ** (-(jnp.arange(half_head, dtype=jnp.float32) * 2.0) / HEAD)
    angles = positions.astype(jnp.float32)[:, None] * frequency[None, :]
    return (jnp.cos(angles), jnp.sin(angles))


def rotate(values, cos_part, sin_part, reverse):
    count = values.shape[0]
    heads = values.reshape(count, HEADS, HEAD)
    half_head = HEAD // 2
    leading = heads[..., :half_head]
    trailing = heads[..., half_head:]
    cosine = cos_part[:, None, :]
    sine_part = sin_part[:, None, :]
    if reverse:
        parts = [leading * cosine + trailing * sine_part, trailing * cosine - leading * sine_part]
    else:
        parts = [leading * cosine - trailing * sine_part, trailing * cosine + leading * sine_part]
    return jnp.concatenate(parts, axis=-1).reshape(count, D)


def split_heads(values):
    count = values.shape[0]
    return values.reshape(count, HEADS // together, together * HEAD).transpose(1, 0, 2)


def join_heads(values):
    groups, count, width = values.shape
    return values.transpose(1, 0, 2).reshape(count, groups * width)


def allowed_pairs(query_copy, query_block, query_doc, key_copy, key_block, key_doc):
    same_doc = query_doc[:, None] == key_doc[None, :]
    query_noisy = (query_copy == 0)[:, None]
    key_noisy = (key_copy == 0)[None, :]
    query_column = query_block[:, None]
    key_row = key_block[None, :]
    inner = query_noisy & key_noisy & (key_row == query_column)
    earlier = query_noisy & ~key_noisy & (key_row < query_column)
    causal = ~query_noisy & ~key_noisy & (key_row <= query_column)
    return same_doc & (inner | earlier | causal)


def masked_scores(query_group, key_group, allowed):
    query_heads = query_group.reshape(query_group.shape[0], together, HEAD)
    key_heads = key_group.reshape(key_group.shape[0], together, HEAD)
    raw = jnp.einsum(
        "qhd,khd->hqk", query_heads, key_heads, preferred_element_type=jnp.float32
    ) * HEAD ** (-0.5)
    return (jnp.where(allowed[None], raw, -1e30), query_heads, key_heads)


def group_forward(items, allowed):
    query_group, key_group, value_group = items
    count = query_group.shape[0]
    scores, query_heads, key_heads = masked_scores(query_group, key_group, allowed)
    value_heads = value_group.reshape(value_group.shape[0], together, HEAD)
    top = jnp.max(scores, axis=-1, keepdims=True)
    weights = jnp.exp(scores - top)
    total = jnp.sum(weights, axis=-1, keepdims=True)
    probs = (weights / total).astype(jnp.bfloat16)
    mixed = jnp.einsum("hqk,khd->qhd", probs, value_heads, preferred_element_type=jnp.float32)
    return (mixed.reshape(count, together * HEAD), (top + jnp.log(total))[..., 0])


def group_backward(items, allowed, tail):
    query_group, key_group, value_group, grad_group, log_total = items
    count = query_group.shape[0]
    key_count = key_group.shape[0]
    scores, query_heads, key_heads = masked_scores(query_group, key_group, allowed)
    value_heads = value_group.reshape(key_count, together, HEAD)
    grad_heads = grad_group.reshape(count, together, HEAD)
    probs = jnp.exp(scores - log_total[..., None])
    prob_grad = jnp.einsum(
        "qhd,khd->hqk", grad_heads, value_heads, preferred_element_type=jnp.float32
    )
    centre = jnp.sum(probs * prob_grad, axis=-1, keepdims=True)
    score_grad = (probs * (prob_grad - centre)).astype(jnp.bfloat16)
    query_grad = jnp.einsum(
        "hqk,khd->qhd", score_grad, key_heads, preferred_element_type=jnp.float32
    ) * HEAD ** (-0.5)
    tail_probs = probs.astype(jnp.bfloat16)
    value_grad = jnp.einsum(
        "hqk,qhd->khd", tail_probs, grad_heads, preferred_element_type=jnp.float32
    )
    key_grad = jnp.einsum(
        "hqk,qhd->khd", score_grad, query_heads, preferred_element_type=jnp.float32
    ) * HEAD ** (-0.5)
    return (
        query_grad.reshape(count, together * HEAD),
        key_grad.reshape(tail, together * HEAD),
        value_grad.reshape(tail, together * HEAD),
        centre[..., 0],
    )


def reduce_grads(grads):
    shards = (
        lax.psum_scatter(grads[0], "fsdp", scatter_dimension=0, tiled=True),
        lax.psum_scatter(grads[1], "fsdp", scatter_dimension=0, tiled=True),
        lax.psum_scatter(grads[2], "fsdp", scatter_dimension=0, tiled=True),
        lax.psum_scatter(grads[3], "fsdp", scatter_dimension=0, tiled=True),
        lax.psum_scatter(grads[4], "fsdp", scatter_dimension=0, tiled=True),
        lax.psum_scatter(grads[5], "fsdp", scatter_dimension=0, tiled=True),
        lax.psum_scatter(grads[6], "fsdp", scatter_dimension=0, tiled=True),
        lax.psum_scatter(grads[7], "fsdp", scatter_dimension=0, tiled=True),
        lax.psum_scatter(grads[8], "fsdp", scatter_dimension=0, tiled=True),
    )
    return lax.psum(
        (
            shards[0],
            shards[1],
            shards[2],
            shards[3],
            shards[4],
            shards[5],
            shards[6],
            shards[7],
            shards[8],
        ),
        "ctx",
    )


def add_tuples(left_items, right_items):
    return tuple((left_item + right_item for left_item, right_item in zip(left_items, right_items)))


def general_body(
    clean_in,
    segments,
    noise,
    mask_embed,
    norm1_gain,
    qkv_weight,
    out_weight,
    norm2_gain,
    up_weight,
    up_bias,
    down_weight,
    down_bias,
    out_grad,
):
    qkv_full, out_full, gain_low, embed_low = (
        lax.all_gather(qkv_weight, "fsdp", axis=0, tiled=True),
        lax.all_gather(out_weight, "fsdp", axis=0, tiled=True),
        lax.all_gather(norm1_gain, "fsdp", axis=0, tiled=True),
        lax.all_gather(mask_embed, "fsdp", axis=0, tiled=True),
    )
    up_full, up_low, down_full, down_low, gain_two_low = (
        lax.all_gather(up_weight, "fsdp", axis=0, tiled=True),
        lax.all_gather(up_bias, "fsdp", axis=0, tiled=True),
        lax.all_gather(down_weight, "fsdp", axis=0, tiled=True),
        lax.all_gather(down_bias, "fsdp", axis=0, tiled=True),
        lax.all_gather(norm2_gain, "fsdp", axis=0, tiled=True),
    )
    gain_one = gain_low.astype(jnp.float32)
    gain_two = gain_two_low.astype(jnp.float32)
    embed_row = embed_low.astype(jnp.float32)
    up_shift = up_low.astype(jnp.float32)
    down_shift = down_low.astype(jnp.float32)
    micro_count = clean_in.shape[0]
    piece = clean_in.shape[2]
    local_rows = 2 * piece
    ctx_count = lax.axis_size("ctx")
    ctx_rank = lax.axis_index("ctx")
    span = jnp.arange(piece, dtype=jnp.int32)
    local_pos = jnp.concatenate(
        [ctx_rank * piece + span, (2 * ctx_count - 1 - ctx_rank) * piece + span]
    )
    ranks = jnp.arange(ctx_count, dtype=jnp.int32)[:, None]
    far_pos = jnp.concatenate(
        [ranks * piece + span[None, :], (2 * ctx_count - 1 - ranks) * piece + span[None, :]], axis=1
    ).reshape(-1)
    seq_len = ctx_count * local_rows
    cos_part, sin_part = rope_tables(jnp.concatenate([local_pos, local_pos]))
    query_copy = jnp.concatenate(
        [jnp.zeros((local_rows,), jnp.int32), jnp.ones((local_rows,), jnp.int32)]
    )
    key_copy = jnp.concatenate(
        [jnp.ones((seq_len,), jnp.int32), jnp.zeros((local_rows,), jnp.int32)]
    )
    query_block = jnp.concatenate([local_pos, local_pos]) // BLK
    key_block = jnp.concatenate([far_pos, local_pos]) // BLK
    full_shapes = ((D,), (D,), (D, 3 * D), (D, D), (D,), (D, FF), (FF,), (FF, D), (D,))
    totals = tuple((jnp.zeros(shape_item, jnp.float32) for shape_item in full_shapes))
    tail = seq_len + local_rows
    outputs = []
    input_grads = []
    for micro_step in range(micro_count):
        clean_rows = clean_in[micro_step].reshape(local_rows, D).astype(jnp.float32)
        noise_rows = noise[micro_step].reshape(-1)
        masked_rows = noise_rows[:, None] == 1
        doc_local = segments[micro_step].reshape(-1).astype(jnp.float32)
        noisy_rows = jnp.where(masked_rows, embed_row[None, :], clean_rows)
        stacked = jnp.concatenate([noisy_rows, clean_rows], axis=0)
        normed_one, scale_one = normalize(stacked)
        h_one = (normed_one * gain_one).astype(jnp.bfloat16)
        projected = jnp.dot(h_one, qkv_full, preferred_element_type=jnp.float32)
        queries = rotate(projected[:, :D], cos_part, sin_part, False).astype(jnp.bfloat16)
        keys = rotate(projected[:, D : 2 * D], cos_part, sin_part, False).astype(jnp.bfloat16)
        values = projected[:, 2 * D :].astype(jnp.bfloat16)
        far_keys, far_values, far_docs = (
            lax.all_gather(keys[local_rows:], "ctx", axis=0, tiled=True),
            lax.all_gather(values[local_rows:], "ctx", axis=0, tiled=True),
            lax.all_gather(doc_local.astype(jnp.bfloat16), "ctx", axis=0, tiled=True),
        )
        key_all = jnp.concatenate([far_keys, keys[:local_rows]], axis=0)
        value_all = jnp.concatenate([far_values, values[:local_rows]], axis=0)
        query_doc = jnp.concatenate([doc_local, doc_local])
        key_doc = jnp.concatenate([far_docs.astype(jnp.float32), doc_local])
        allowed = allowed_pairs(query_copy, query_block, query_doc, key_copy, key_block, key_doc)
        query_groups = split_heads(queries)
        key_groups = split_heads(key_all)
        value_groups = split_heads(value_all)
        mixed_groups, log_totals = lax.map(
            partial(group_forward, allowed=allowed), (query_groups, key_groups, value_groups)
        )
        mixed = join_heads(mixed_groups).astype(jnp.bfloat16)
        resid = stacked + jnp.dot(mixed, out_full, preferred_element_type=jnp.float32)
        normed_two, scale_two = normalize(resid)
        h_two = (normed_two * gain_two).astype(jnp.bfloat16)
        hidden = jnp.dot(h_two, up_full, preferred_element_type=jnp.float32) + up_shift
        active = jax.nn.gelu(hidden, approximate=True).astype(jnp.bfloat16)
        result = resid + jnp.dot(active, down_full, preferred_element_type=jnp.float32) + down_shift
        outputs.append(result.astype(jnp.bfloat16).reshape(2, 2, piece, D))
        cotangent = out_grad[micro_step].reshape(2 * local_rows, D).astype(jnp.float32)
        grad_out = cotangent.astype(jnp.bfloat16)
        down_grad = jnp.einsum("rf,rd->fd", active, grad_out, preferred_element_type=jnp.float32)
        down_shift_grad = jnp.sum(grad_out.astype(jnp.float32), axis=0)
        grad_active = jnp.einsum(
            "rd,fd->rf", grad_out, down_full, preferred_element_type=jnp.float32
        )
        unused, gelu_back = jax.vjp(partial(jax.nn.gelu, approximate=True), hidden)
        grad_hidden = gelu_back(grad_active)[0].astype(jnp.bfloat16)
        up_grad = jnp.einsum("rd,rf->df", h_two, grad_hidden, preferred_element_type=jnp.float32)
        up_shift_grad = jnp.sum(grad_hidden.astype(jnp.float32), axis=0)
        grad_h_two = jnp.einsum(
            "rf,df->rd", grad_hidden, up_full, preferred_element_type=jnp.float32
        )
        gain_two_grad = jnp.sum(grad_h_two * normed_two, axis=0)
        grad_resid = cotangent + norm_back(grad_h_two * gain_two, normed_two, scale_two)
        grad_attn = grad_resid.astype(jnp.bfloat16)
        out_grad_full = jnp.einsum(
            "rd,re->de", mixed, grad_attn, preferred_element_type=jnp.float32
        )
        grad_mixed = jnp.einsum(
            "re,de->rd", grad_attn, out_full, preferred_element_type=jnp.float32
        ).astype(jnp.bfloat16)
        query_grads, key_grads, value_grads, centres = lax.map(
            partial(group_backward, allowed=allowed, tail=tail),
            (query_groups, key_groups, value_groups, split_heads(grad_mixed), log_totals),
        )
        query_grad = join_heads(query_grads)
        key_grad_all = join_heads(key_grads)
        value_grad_all = join_heads(value_grads)
        key_mine, value_mine = (
            lax.psum_scatter(key_grad_all[:seq_len], "ctx", scatter_dimension=0, tiled=True),
            lax.psum_scatter(value_grad_all[:seq_len], "ctx", scatter_dimension=0, tiled=True),
        )
        key_grad = jnp.concatenate([key_grad_all[seq_len:], key_mine], axis=0)
        value_grad = jnp.concatenate([value_grad_all[seq_len:], value_mine], axis=0)
        grad_proj = jnp.concatenate(
            [
                rotate(query_grad, cos_part, sin_part, True),
                rotate(key_grad, cos_part, sin_part, True),
                value_grad,
            ],
            axis=1,
        ).astype(jnp.bfloat16)
        qkv_grad = jnp.einsum("rd,re->de", h_one, grad_proj, preferred_element_type=jnp.float32)
        grad_h_one = jnp.einsum(
            "re,de->rd", grad_proj, qkv_full, preferred_element_type=jnp.float32
        )
        gain_one_grad = jnp.sum(grad_h_one * normed_one, axis=0)
        grad_rows = grad_resid + norm_back(grad_h_one * gain_one, normed_one, scale_one)
        grad_noisy = grad_rows[:local_rows]
        input_grads.append(
            (grad_rows[local_rows:] + jnp.where(masked_rows, 0.0, grad_noisy)).reshape(2, piece, D)
        )
        embed_grad = jnp.sum(jnp.where(masked_rows, grad_noisy, 0.0), axis=0)
        step_grads = (
            embed_grad,
            gain_one_grad,
            qkv_grad,
            out_grad_full,
            gain_two_grad,
            up_grad,
            up_shift_grad,
            down_grad,
            down_shift_grad,
        )
        totals = add_tuples(totals, step_grads)
    reduced = reduce_grads(totals)
    block_out = jnp.stack(outputs)
    input_grad = jnp.stack(input_grads)
    return (
        block_out,
        input_grad,
        reduced[0],
        reduced[1],
        reduced[2],
        reduced[3],
        reduced[4],
        reduced[5],
        reduced[6],
        reduced[7],
        reduced[8],
    )


PAIR=2*HEAD; PAIRS=D//PAIR
NEG=-1e30
VMEM_LIMIT=60<<20
F32=jnp.float32; BF=jnp.bfloat16

def dot_nn(a,b): return lax.dot_general(a,b,(((1,),(0,)),((),())),preferred_element_type=F32)
def dot_nt(a,b): return lax.dot_general(a,b,(((1,),(1,)),((),())),preferred_element_type=F32)
def dot_tn(a,b): return lax.dot_general(a,b,(((0,),(0,)),((),())),preferred_element_type=F32)

def tiles_of(half):
    return [(s,min(128,half-s)) for s in range(0,half,128)]

def norm_rows(rows):
    centre=rows-jnp.mean(rows,axis=-1,keepdims=True)
    scale=lax.rsqrt(jnp.mean(centre*centre,axis=-1,keepdims=True)+EPS)
    return centre*scale, scale

def swap_halves(z):
    lane=lax.broadcasted_iota(jnp.int32,z.shape,1)
    low=(lane & (HEAD-1)) < HEAD//2
    return jnp.where(low,pltpu.roll(z,PAIR-HEAD//2,1),pltpu.roll(z,HEAD//2,1))

def head_stack(z):
    lane=lax.broadcasted_iota(jnp.int32,z.shape,1)
    first=lane<HEAD
    zero=jnp.zeros_like(z)
    return jnp.concatenate([jnp.where(first,z,zero),jnp.where(first,zero,z)],axis=0)

def head_merge(z):
    n=z.shape[0]//2
    lane=lax.broadcasted_iota(jnp.int32,(n,z.shape[1]),1)
    return jnp.where(lane<HEAD,z[:n],z[n:])

def layer_rows(xc_ref,noise_ref,emb_ref):
    clean=xc_ref[...].astype(F32)
    noisy=jnp.where(noise_ref[...]==1,emb_ref[...].astype(F32),clean)
    return noisy,clean

def fwd_attn_kernel(half,xc,noise,segc,segr,small,wqkv,wout,trig,
                    q_o,k_o,v_o,mix_o,lse_o,x1_o,h_s,bias_s,self_s,mix_s):
    p=pl.program_id(0)
    tiles=tiles_of(half)
    @pl.when(p==0)
    def _():
        g=vector_row(small,1)
        clean=jnp.concatenate([xc[i] for i in range(9)],axis=0).astype(F32)
        noisy=jnp.where(noise[...]==1,vector_row(small,0),clean)
        for c,rows in enumerate((noisy,clean)):
            x1_o[c*half:(c+1)*half]=rows
            n,_=norm_rows(rows)
            h_s[c*half:(c+1)*half]=(n*g).astype(BF)
        for s,m in tiles:
            n=s+m
            qb=(lax.broadcasted_iota(jnp.int32,(m,n),0)+s)//BLK
            kb=lax.broadcasted_iota(jnp.int32,(m,n),1)//BLK
            same=segc[s:n]==segr[:,:n]
            bias_s[0,s:n,:n]=jnp.where(same&(kb<qb),0.0,NEG)
            bias_s[1,s:n,:n]=jnp.where(same&(kb<=qb),0.0,NEG)
            qb=lax.broadcasted_iota(jnp.int32,(m,m),0)//BLK
            kb=lax.broadcasted_iota(jnp.int32,(m,m),1)//BLK
            same=segc[s:n]==segr[:,s:n]
            self_s[s:n,:m]=jnp.where(same&(kb==qb),0.0,NEG)
    h=h_s[...]
    cs=jnp.concatenate([trig[:,:PAIR]]*2,axis=0)
    sn=jnp.concatenate([trig[:,PAIR:]]*2,axis=0)
    block=lambda i: wqkv[:,pl.ds(pl.multiple_of(i*D+p*PAIR,PAIR),PAIR)]
    zq=dot_nn(h,jnp.concatenate([block(0),block(1)],axis=1))
    z=zq[:,:PAIR]; q_o[...]=((z*cs+swap_halves(z)*sn).astype(BF)*BF(HEAD**-0.5)).astype(BF)
    z=zq[:,PAIR:]; k_o[...]=(z*cs+swap_halves(z)*sn).astype(BF)
    v_o[...]=dot_nn(h,block(2)).astype(BF)
    idx=0
    for s,m in tiles:
        n=s+m
        for c in (0,1):
            qs=head_stack(q_o[c*half+s:c*half+n])
            kc=k_o[half:half+n]; vc=v_o[half:half+n]
            sc=dot_nt(qs,kc).reshape(2,m,n)+bias_s[c,s:n,:n][None]
            top=jnp.max(sc,axis=-1,keepdims=True)
            if c==0:
                ss=dot_nt(qs,k_o[s:n]).reshape(2,m,m)+self_s[s:n,:m][None]
                top=jnp.maximum(top,jnp.max(ss,axis=-1,keepdims=True))
            w=jnp.exp(sc-top); tot=jnp.sum(w,axis=-1,keepdims=True)
            o=dot_nn(w.astype(BF).reshape(2*m,n),vc)
            if c==0:
                w2=jnp.exp(ss-top); tot=tot+jnp.sum(w2,axis=-1,keepdims=True)
                o=o+dot_nn(w2.astype(BF).reshape(2*m,m),v_o[s:n])
            tot=tot.reshape(2*m,1)
            o=o*(1.0/tot)
            mx=head_merge(o).astype(BF)
            mix_o[c*half+s:c*half+n]=mx
            mix_s[p,c*half+s:c*half+n]=mx
            lse=top.reshape(2*m,1)+jnp.log(tot)
            lse_o[0,idx:idx+1,:2*m]=jnp.broadcast_to(lse,(2*m,128)).T[0:1]
            idx+=1
    @pl.when(p==pl.num_programs(0)-1)
    def _():
        full=jnp.concatenate([mix_s[i] for i in range(PAIRS)],axis=1)
        x1_o[...]=x1_o[...]+dot_nn(full,wout[...])

def whole(shape): return pl.BlockSpec(shape,lambda *i:(0,)*len(shape))

def vector_row(small,i):
    return jnp.concatenate([small[f,i:i+1,:D//4] for f in range(4)],axis=1).astype(F32)

def fwd_attn_comm_kernel(half,*refs):
    clean,meta,gout,trig,qkv,out,up,down,small,zeros,blank=refs[:11]
    q_o,k_o,v_o,mix_o,lse_o,x1_o,noise_o,segc_o,segr_o,vec_o,bias_o,qkv_o,out_o,up_o,down_o,cot_o,clean_o=refs[11:28]
    h_s,bias_s,self_s,mix_s,clean_s,meta_s,small_s,qkv_s,out_s,trig_s=refs[28:38]
    a_send,a_recv,m_send,m_recv,c_send,c_recv,w_send,w_recv,s_send,s_recv,local=refs[38:]
    p=pl.program_id(0)
    c,f=place_ids()
    piece=half//9
    weight=lambda i,shard,full,parts: GatherRows(shard,full,w_send.at[i],w_recv.at[i],local.at[i],parts)
    w_qkv,w_out,w_up,w_down=weight(0,qkv,qkv_s,3),weight(1,out,out_s,1),weight(2,up,up_o,3),weight(3,down,down_o,3)
    rows=ToUnit(lambda q,h:clean.at[q,h],lambda t:clean_s.at[t],a_send,a_recv,local.at[4])
    notes=ToUnit(lambda q,h:meta.at[2*q+h],lambda t:meta_s.at[t],m_send,m_recv,local.at[5])
    grads=[ToUnit(lambda q,h:gout.at[q,0,h],lambda t:cot_o.at[t],c_send,c_recv,local.at[6])]
    copies=[pltpu.make_async_copy(qkv_s,qkv_o,local.at[8]),pltpu.make_async_copy(out_s,out_o,local.at[9]),pltpu.make_async_copy(clean_s,clean_o,local.at[10])]
    others=[f+1-2*(f%2),(f+2)%4,3-f]
    @pl.when(p==0)
    def _():
        meet(True,(1,2,3))
        w_qkv.begin()
        notes.begin()
        rows.begin()
        sends=[remote(small,small_s.at[f],s_send.at[i],s_recv.at[i],{"fsdp":other}) for i,other in enumerate(others)]
        for d in sends: d.start()
        own=pltpu.make_async_copy(small,small_s.at[f],local.at[11])
        own.start()
        table=pltpu.make_async_copy(trig.at[c%2],trig_s,local.at[12])
        table.start()
        w_out.begin()
        w_up.begin()
        w_down.begin()
        for i in range(3): w_qkv.relay_far(i)
        pads=[pltpu.make_async_copy(zeros,clean_s.at[pl.ds(7,2)],local.at[13]),pltpu.make_async_copy(blank,meta_s.at[pl.ds(7,2)],local.at[13])]
        pads.append(pltpu.make_async_copy(zeros,cot_o.at[pl.ds(7,2)],local.at[13]))
        @pl.when(c%2==1)
        def _():
            for d in pads:
                d.start()
                d.wait()
        for i in range(3): w_qkv.relay_x(i)
        for r in grads: r.begin()
        own.wait()
        table.wait()
        for i,other in enumerate(others):
            sends[i].wait_send()
            remote(small_s.at[other],small_s.at[other],s_send.at[i],s_recv.at[i],{"fsdp":other}).wait_recv()
        notes.finish()
        lane=lax.broadcasted_iota(jnp.int32,(1,128),1)
        for i in range(9):
            t=jnp.broadcast_to(meta_s[i,0:1].astype(F32),(128,128)).T
            segc_o[i*piece:(i+1)*piece]=t[:piece,0:1]
            noise_o[i*piece:(i+1)*piece]=t[piece:,0:1].astype(jnp.int32)
        for i in range(5):
            even=meta_s[2*i,0:1].astype(F32)
            odd=pltpu.roll(meta_s[min(2*i+1,8)].astype(F32),64,1)[0:1]
            segr_o[:,i*128:(i+1)*128]=jnp.where(lane<64,even,odd)
        for i in range(2): vec_o[i:i+1]=vector_row(small_s,2+i)
        for i in range(2): vec_o[2+i:3+i]=vector_row(small_s,i)
        for g in range(4):
            for i in range(3): bias_o[:,g*768+i*256:g*768+(i+1)*256]=small_s[g,4+i:5+i].astype(F32)
        rows.finish()
        w_qkv.finish()
        copies[0].start()
        copies[2].start()
    fwd_attn_kernel(half,clean_s,noise_o,segc_o,segr_o,small_s,qkv_s,out_s,trig_s,q_o,k_o,v_o,mix_o,lse_o,x1_o,h_s,bias_s,self_s,mix_s)
    def at(i,*ops):
        @pl.when(p==i)
        def _():
            for op in ops: op()
    at(0,w_out.relay_far,*[partial(w_up.relay_far,i) for i in range(3)])
    at(1,w_out.relay_x,partial(w_up.relay_x,0),partial(w_down.relay_far,0))
    at(2,partial(w_up.relay_x,1),partial(w_down.relay_far,1),partial(w_down.relay_far,2))
    at(3,partial(w_up.relay_x,2),w_out.finish,copies[1].start,partial(w_down.relay_x,0))
    at(4,partial(w_down.relay_x,1),partial(w_down.relay_x,2))
    @pl.when(p==pl.num_programs(0)-1)
    def _():
        for w in (w_up,w_down): w.finish()
        for r in grads: r.finish()
        for d in copies: d.wait()

def whole(shape): return pl.BlockSpec(shape,lambda *i:(0,)*len(shape))
def once(shape): return pl.BlockSpec(shape,lambda *i:(0,)*len(shape),pipeline_mode=pl.Buffered(1))

def fwd_attn(clean,meta,gout,trig,qkv,out,up,down,small):
    piece=clean.shape[2]; half=9*piece; R=2*half
    zeros=jnp.zeros((2,piece,D),BF)
    blank=jnp.concatenate([jnp.full((2,8,piece),-1,jnp.int32),jnp.zeros((2,8,128-piece),jnp.int32)],axis=2)
    nt=len(tiles_of(half))*2; ntp=-(-nt//8)*8
    rows=pl.BlockSpec((R,PAIR),lambda p:(0,p))
    sds=jax.ShapeDtypeStruct
    return pl.pallas_call(partial(fwd_attn_comm_kernel,half),grid=(PAIRS,),
        in_specs=[ANYSPACE]*4+[once(a.shape) for a in (qkv,out,up,down,small,zeros,blank)],
        out_specs=[rows,rows,rows,rows,pl.BlockSpec((1,ntp,256),lambda p:(p,0,0)),whole((R,D)),whole((half,1)),whole((half,1)),whole((1,640)),whole((4,D)),whole((1,FF))]+[ANYSPACE]*6,
        out_shape=[sds((R,D),BF)]*4+[sds((PAIRS,ntp,256),F32),sds((R,D),F32),sds((half,1),jnp.int32),sds((half,1),F32),sds((1,640),F32),sds((4,D),F32),sds((1,FF),F32),
            sds((D,3*D),BF),sds((D,D),BF),sds((D,FF),BF),sds((FF,D),BF),sds((9,piece,D),BF),sds((9,piece,D),BF)],
        scratch_shapes=[pltpu.VMEM((R,D),BF),pltpu.VMEM((2,half,half),F32),pltpu.VMEM((half,128),F32),pltpu.VMEM((PAIRS,R,PAIR),BF),
            pltpu.VMEM((9,piece,D),BF),pltpu.VMEM((9,8,128),jnp.int32),pltpu.VMEM((4,)+small.shape,BF),pltpu.VMEM((D,3*D),BF),pltpu.VMEM((D,D),BF),pltpu.VMEM((half,2*PAIR),F32),
            DMA((8,)),DMA((9,)),DMA((8,)),DMA((9,)),DMA((8,)),DMA((9,)),DMA((4,13)),DMA((4,13)),DMA((3,)),DMA((3,)),DMA((14,))],
        compiler_params=pltpu.CompilerParams(vmem_limit_bytes=VMEM_LIMIT,dimension_semantics=("arbitrary",),collective_id=1,has_side_effects=True),
        cost_estimate=pl.CostEstimate(flops=2*R*D*(3*D+D)+24*R*half*D//2*2,bytes_accessed=16<<20,transcendentals=R*half*HEADS),
        name="fwd_attn")(clean,meta,gout,trig,qkv,out,up,down,small,zeros,blank)

GC=(2.0/3.141592653589793)**0.5
def cols(refs): return jnp.concatenate([r[...] for r in refs],axis=1)
def rowcat(refs): return jnp.concatenate([r[...] for r in refs],axis=0)
STEPS=FF//512
def up_specs(): return [pl.BlockSpec((D,128),(lambda s:(lambda j:(0,s*STEPS+j)))(s)) for s in range(4)]
def down_specs(): return [pl.BlockSpec((128,D),(lambda s:(lambda j:(s*STEPS+j,0)))(s)) for s in range(4)]
def bias_specs(): return [pl.BlockSpec((1,128),(lambda s:(lambda j:(0,s*STEPS+j)))(s)) for s in range(4)]

FFN_TABLE={2: [(0, None, 0)], 3: [(0, 0, 1)], 4: [(1, None, 0)], 5: [(1, 0, 1)], 6: [(2, None, 0), (0, 1, None)], 7: [(2, 0, 1)], 8: [(3, None, 0), (1, 1, None)], 9: [(3, 0, 1)], 10: [(4, None, 0), (2, 1, None)], 11: [(4, 0, 1)], 12: [(5, None, 0)]}
FFN_END=[(3, 1), (5, 0), (4, 1)]
ATTN_TABLE={0: [(5, None, 1), (0, None, 2), (1, None, 2), (2, None, 2), (3, None, 2), (4, None, 2)], 1: [(6, None, 0)], 2: [(0, 2, 3), (6, 0, 1)], 3: [(0, 3, 4), (1, 2, 3), (5, 1, 2)], 4: [(7, None, 0), (2, 2, 3), (6, 1, 2)], 5: [(0, 4, 5), (1, 3, 4), (2, 3, 4), (3, 2, 3), (7, 0, 1)], 6: [(0, 5, 6), (4, 2, 3)], 7: [(1, 4, 5), (2, 4, 5), (3, 3, 4), (5, 2, 3), (7, 1, 2), (0, 6, 7)], 8: [(8, None, 0), (4, 3, 4), (6, 2, 3)], 9: [(1, 5, 6), (2, 5, 6), (5, 3, 4), (7, 2, 3), (8, 0, 1), (3, 4, 5)], 10: [(0, 7, None), (1, 6, 7), (4, 4, 5), (6, 3, 4)], 11: [(2, 6, 7), (5, 4, 5), (7, 3, 4), (8, 1, 2)], 12: [(9, None, 0)]}
ATTN_END=[(1, 7), (3, 5), (4, 5), (6, 4), (2, 7), (9, 0), (5, 5), (8, 2), (7, 4)]
TAIL_ORDER=[("sums", None, 0), (9, None, 1), (8, None, 3), (6, None, 5), (7, None, 5), (3, None, 6), (4, None, 6), (5, None, 6), ("rows", None, 1), ("rows", None, 2), ("sums", 0, 1), (8, 3, 4), (6, 5, 6), ("sums", 1, 2), (7, 5, 6), (3, 6, 7), (9, 1, 2), ("rows", None, 3), (4, 6, 7), ("sums", 2, 3), (5, 6, 7), (3, 7, None), ("sums", 3, 4), (9, 2, 3), ("rows", None, 4), (8, 4, 5), (6, 6, 7), ("sums", 4, None), (7, 6, 7), (4, 7, None), (9, 3, 4), ("rows", None, 5), (5, 7, None), (8, 5, 6), (9, 4, 5), ("rows", None, 6), (8, 6, 7), (6, 7, None), (9, 5, 6), ("rows", None, 7), (7, 7, None), (9, 6, 7), (8, 7, None), (9, 7, None)]

def after(state,table,end):
    state=dict(state)
    for ops in table.values():
        for chunk,take,start in ops:
            if take is not None: state[chunk]=take
    state.update(end)
    return state
FFN_STATE=after({},FFN_TABLE,FFN_END)
ATTN_STATE=after(FFN_STATE,ATTN_TABLE,ATTN_END)
def in_state(state,ids,low,high): return [i for i in ids if low<=state[i]<=high]
def started(chunk,table):
    return [start for ops in table.values() for i,take,start in ops if i==chunk and start is not None]

def run_table(table,chunks,position,pid,steps,per_step):
    for i in range(steps):
        ops=table.get(per_step*i+position+1,[])
        if ops:
            @pl.when(pid==i)
            def _(): do_ops(ops,chunks)

def do_ops(ops,chunks):
    for i,take,start in ops:
        if take is not None: chunks[i].take(take)
        if start is not None: chunks[i].start(start)

def ffn_kernel(x1,vec,*refs):
    wup,bup,wdn,rest=refs[:4],refs[4:8],refs[8:12],refs[12:]
    gain,bdn=vec.at[0:1],vec.at[1:2]
    gy0,gout,zeros,dbup_o,dbdn_o,dgain_o,gx1_o,block_o,pair_o,total_o,final_o=rest[:11]
    h_s,hT_s,acc,gy_s,out_s,act_s,gu_s,grad_s,pair_s,far_s,total_s,send,recv,g_send,g_recv,b_send,b_recv,local=rest[11:]
    g=pl.program_id(0)
    R=h_s.shape[0]; ch=R//3; piece=R//18
    chunks=[Reduce(TILE,send.at[i],recv.at[i],grad=grad_s.at[i%2],pair=pair_s.at[i],far=far_s.at[i],total=total_s.at[i]) for i in range(STEPS)]
    arrive=ToUnit(lambda q,h:gout.at[q,1,h],lambda t:gy_s.at[9+t],g_send,g_recv,local.at[0])
    leave=[FromUnit(lambda t,i=i:out_s.at[9*i+t],lambda q,h,i=i:block_o.at[q,i,h],b_send.at[i],b_recv.at[i],local.at[1+i]) for i in range(2)]
    first=pltpu.make_async_copy(gy0,gy_s.at[pl.ds(0,9)],local.at[3])
    rows=lambda ref,i: ref[6*i:6*i+6].reshape(ch,D)
    wu=lambda: cols(wup)
    wd=lambda: rowcat(wdn)
    bias=cols(bup).astype(F32)
    @pl.when(g==0)
    def _():
        meet(True,(1,2))
        arrive.begin()
        first.start()
        pad_unit(zeros,gy_s.at[pl.ds(9,9)],local.at[4])
        n,_=norm_rows(x1[...])
        h=(n*gain[...].astype(F32)).astype(BF)
        h_s[...]=h
        hT_s[...]=h.T
        acc[...]=x1[...]+bdn[...].astype(F32)
    @pl.when(g<STEPS)
    def _():
        for i in range(3):
            r=slice(i*ch,(i+1)*ch)
            u=dot_nn(h_s[r],wu())+bias
            act=(0.5*u*(1.0+jnp.tanh(GC*(u+0.044715*u*u*u)))).astype(BF)
            acc[r]+=dot_nn(act,wd())
    @pl.when(g==STEPS-1)
    def _():
        for i in range(3): out_s[6*i:6*i+6]=acc[i*ch:(i+1)*ch].astype(BF).reshape(6,piece,D)
        for r in leave: r.begin()
        arrive.finish()
        first.wait()
        acc[...]=jnp.zeros_like(acc)
        dbdn_o[...]=jnp.sum(gy_s[...].astype(F32).reshape(R,D),axis=0,keepdims=True)
    @pl.when(g>=STEPS)
    def _():
        j=g-STEPS
        for i in range(2,STEPS):
            @pl.when(j==i)
            def _(): chunks[i-2].sent(0)
        slot=lax.rem(j,2)
        for i in range(3):
            r=slice(i*ch,(i+1)*ch)
            u=dot_nn(h_s[r],wu())+bias
            ga=dot_nt(rows(gy_s,i),wd())
            u2=u*u
            t=jnp.tanh(GC*(u+0.044715*u*u2))
            a=0.5*(1.0+t)
            gu=((a+0.5*u*(1.0-t*t)*(GC*(1.0+3*0.044715*u2)))*ga).astype(BF)
            act_s[r]=(u*a).astype(BF)
            gu_s[r]=gu
            acc[r]+=dot_nt(gu,wu())
        run_table(FFN_TABLE,chunks,0,j,STEPS,2)
        def put(s,row,value):
            for k in range(0,value.shape[0],64):
                grad_s[slot,s%2,s//2,(row+k)//TILE,(row+k)%TILE:(row+k)%TILE+64]=value[k:k+64]
        r=dot_tn(act_s[...],gy_s[...].reshape(R,D)).astype(BF)
        for s in range(4):
            for t in range(6): put(s,768+t*128,r[s*128:(s+1)*128,t*128:(t+1)*128])
        r=dot_nn(hT_s[...],gu_s[...]).astype(BF)
        for s in range(4):
            for t in range(4): put(s,t*192,r[s*192:(s+1)*192,t*128:(t+1)*128])
        dbup_o[...]=jnp.sum(gu_s[...].astype(F32),axis=0,keepdims=True)
        run_table(FFN_TABLE,chunks,1,j,STEPS,2)
    @pl.when(g==pl.num_programs(0)-1)
    def _():
        n,scale=norm_rows(x1[...])
        g2=acc[...]
        dgain_o[...]=jnp.sum(g2*n,axis=0,keepdims=True)
        e=g2*gain[...].astype(F32)
        acc[...]=gy_s[...].astype(F32).reshape(R,D)+scale*(e-jnp.mean(e,axis=-1,keepdims=True)-n*jnp.mean(e*n,axis=-1,keepdims=True))
        outs=[pltpu.make_async_copy(acc,gx1_o,local.at[5])]
        outs[0].start()
        for i,stage in FFN_END: chunks[i].take(stage)
        for low,high,source,target in ((0,0,pair_s,pair_o),(1,3,total_s,total_o)):
            for place,i in enumerate(in_state(FFN_STATE,range(STEPS),low,high)):
                outs.append(pltpu.make_async_copy(source.at[i],target.at[place],local.at[5+len(outs)]))
                outs[-1].start()
        for i in range(STEPS):
            stages=started(i,FFN_TABLE)
            chunks[i].sent(*[x for x in stages if x>0 or i>=STEPS-2])
        for r in leave: r.finish()
        for d in outs: d.wait()

def ffn(x1,vec,wup,bup,wdn,gy0,gout):
    R=x1.shape[0]; half=R//2; piece=half//9
    zeros=jnp.zeros((2,piece,D),BF)
    count=lambda low,high: max(1,len(in_state(FFN_STATE,range(STEPS),low,high)))
    tile=lambda j: lax.rem(j,STEPS)
    ups=[pl.BlockSpec((D,128),(lambda s:(lambda j:(0,s*STEPS+tile(j))))(s)) for s in range(4)]
    downs=[pl.BlockSpec((128,D),(lambda s:(lambda j:(s*STEPS+tile(j),0)))(s)) for s in range(4)]
    biases=[pl.BlockSpec((1,128),(lambda s:(lambda j:(0,s*STEPS+tile(j))))(s)) for s in range(4)]
    return pl.pallas_call(ffn_kernel,grid=(2*STEPS,),
        in_specs=[once((R,D)),once((4,D))]+ups+biases+downs+[ANYSPACE]*2+[once(zeros.shape)],
        out_specs=[pl.BlockSpec((1,512),lambda j:(0,jnp.maximum(j-STEPS,0))),whole((1,D)),whole((1,D))]+[ANYSPACE]*5,
        out_shape=[jax.ShapeDtypeStruct((1,FF),F32),jax.ShapeDtypeStruct((1,D),F32),jax.ShapeDtypeStruct((1,D),F32),jax.ShapeDtypeStruct((R,D),F32),jax.ShapeDtypeStruct((4,2,2,piece,D),BF),
            jax.ShapeDtypeStruct((count(0,0),2,2,TILE,128),BF),jax.ShapeDtypeStruct((count(1,3),2,TILE,128),BF),jax.ShapeDtypeStruct((1,2,TILE,128),BF)],
        scratch_shapes=[pltpu.VMEM((R,D),BF),pltpu.VMEM((D,R),BF),pltpu.VMEM((R,D),F32),pltpu.VMEM((18,piece,D),BF),pltpu.VMEM((18,piece,D),BF),pltpu.VMEM((R,512),BF),pltpu.VMEM((R,512),BF),
            pltpu.VMEM((2,2,2,2,TILE,128),BF),pltpu.VMEM((STEPS,2,2,TILE,128),BF),pltpu.VMEM((STEPS,2,TILE,128),BF),pltpu.VMEM((STEPS,2,TILE,128),BF),
            DMA((STEPS,8)),DMA((STEPS,8)),DMA((8,)),DMA((9,)),DMA((2,8)),DMA((2,8)),DMA((STEPS+7,))],
        compiler_params=pltpu.CompilerParams(vmem_limit_bytes=VMEM_LIMIT,dimension_semantics=("arbitrary",),collective_id=2,has_side_effects=True),
        cost_estimate=pl.CostEstimate(flops=14*R*D*FF,bytes_accessed=40<<20,transcendentals=2*R*FF),
        name="ffn")(x1,vec,*[wup]*4,*[bup]*4,*[wdn]*4,gy0,gout,zeros)

def bwd_attn_kernel(half,xc,noise,segc,segr,vec,gx1,q,k,v,mix,lse,wq,wk,wv,wout,trig,mixed,tile_pair,tile_total,tile_final,
                    gin_o,demb_o,dgain_o,tiles_o,wpair_o,wtotal_o,wfinal_o,hT_s,gh,biasT_s,selfT_s,dq_s,dk_s,dv_s,ga,trig_s,
                    t_pair,t_far,t_total,t_over,t_final,w_grad,w_pair,w_far,w_total,w_over,w_final,t_send,t_recv,w_send,w_recv,local):
    p=pl.program_id(0)
    emb,gain=vec.at[2:3],vec.at[3:4]
    rank,_=place_ids()
    R=2*half
    tiles=tiles_of(half)
    pairs=in_state(FFN_STATE,range(STEPS),0,0)
    fars=in_state(FFN_STATE,range(STEPS),0,0)
    slot=lambda ids,i: ids.index(i) if i in ids else 0
    chunks=[Reduce(TILE,t_send.at[i],t_recv.at[i],pair=t_pair.at[slot(pairs,i)],far=t_far.at[slot(fars,i)],total=t_total.at[i],over=t_over.at[i],final=t_final.at[i]) for i in range(STEPS)]
    chunks+=[Reduce(WING,w_send.at[i],w_recv.at[i],grad=w_grad.at[i],pair=w_pair.at[i],far=w_far.at[i],total=w_total.at[i],over=w_over.at[i],final=w_final.at[i]) for i in range(4)]
    def tick(position):
        run_table(ATTN_TABLE,chunks,position,p,PAIRS,2)
    @pl.when(p==0)
    def _():
        loads=[pltpu.make_async_copy(trig.at[rank%2],trig_s,local.at[2])]
        loads[0].start()
        for low,high,source,target in ((0,0,tile_pair,t_pair),(1,3,tile_total,t_total),(4,7,tile_final,t_final)):
            for place,i in enumerate(in_state(FFN_STATE,range(STEPS),low,high)):
                loads.append(pltpu.make_async_copy(source.at[place],target.at[place if low==0 else i],local.at[2+len(loads)]))
                loads[-1].start()
        ga[...]=gx1[...].astype(BF)
        for d in loads: d.wait()
        meet(True,(1,2))
        do_ops(ATTN_TABLE.get(0,[]),chunks)
        g=gain[...].astype(F32)
        for c,rows in enumerate(layer_rows(xc,noise,emb)):
            n,_=norm_rows(rows)
            hT_s[:,c*half:(c+1)*half]=(n*g).astype(BF).T
        gh[...]=jnp.zeros_like(gh)
        for s,m in tiles:
            n=s+m
            qb=(lax.broadcasted_iota(jnp.int32,(n,m),1)+s)//BLK
            kb=lax.broadcasted_iota(jnp.int32,(n,m),0)//BLK
            same=segc[:n]==segr[:,s:n]
            biasT_s[0,:n,s:n]=jnp.where(same&(kb<qb),0.0,NEG)
            biasT_s[1,:n,s:n]=jnp.where(same&(kb<=qb),0.0,NEG)
            qb=lax.broadcasted_iota(jnp.int32,(m,m),1)//BLK
            kb=lax.broadcasted_iota(jnp.int32,(m,m),0)//BLK
            same=segc[s:n]==segr[:,s:n]
            selfT_s[s:n,:m]=jnp.where(same&(kb==qb),0.0,NEG)
    gm=dot_nt(ga[...],wout[...]).astype(BF)
    @pl.when(p==0)
    def _():
        r=dot_tn(mixed[...],ga[...]).astype(BF)
        for a in range(4):
            for t in range(6): w_grad[0,a%2,a//2,t//3,t%3*192:(t%3+1)*192]=r[a*192:(a+1)*192,t*128:(t+1)*128]
    gd=gm.astype(F32)*mix[...].astype(F32)
    dk_s[...]=jnp.zeros_like(dk_s); dv_s[...]=jnp.zeros_like(dv_s)
    idx=0
    for s,m in tiles:
        n=s+m
        for c in (0,1):
            rs=slice(c*half+s,c*half+n)
            qs=head_stack(q[rs]); gs=head_stack(gm[rs])
            delta=jnp.sum(head_stack(gd[rs]).T,axis=0,keepdims=True)
            row=lse[0,idx:idx+1,:2*m]
            def part(krows,bias):
                kc=k[krows]; vc=v[krows]
                st=dot_nt(kc,qs)+jnp.concatenate([bias,bias],axis=1)
                pt=jnp.exp(st-row)
                dp=dot_nt(vc,gs)
                ds=(pt*(dp-delta)).astype(BF)
                dv_s[krows]+=dot_nn(pt.astype(BF),gs)
                dk_s[krows]+=dot_nn(ds,qs)
                return dot_tn(ds,kc)
            dq=part(slice(half,half+n),biasT_s[c,:n,s:n])
            if c==0: dq=dq+part(slice(s,n),selfT_s[s:n,:m])
            dq_s[rs]=head_merge(dq)*HEAD**-0.5
            idx+=1
        if s==256: tick(0)
    cs=jnp.concatenate([trig_s[:,:PAIR]]*2,axis=0)
    sn=jnp.concatenate([trig_s[:,PAIR:]]*2,axis=0)
    z=jnp.concatenate([(g[...]*cs-swap_halves(g[...])*sn).astype(BF) for g in (dq_s,dk_s)]+[dv_s[...].astype(BF)],axis=1)
    r=dot_nn(hT_s[...],z).astype(BF)
    group=1+p//2
    for a in range(4):
        for t in range(3):
            w_grad[group,a%2,a//2,lax.rem(p,2),t*192:(t+1)*192]=r[a*192:(a+1)*192,t*128:(t+1)*128]
    gh[...]+=dot_nt(z,cols((wq,wk,wv)))
    tick(1)
    @pl.when(p==pl.num_programs(0)-1)
    def _():
        g=gain[...].astype(F32)
        outs=[]; dg=0.0
        for c,rows in enumerate(layer_rows(xc,noise,emb)):
            n,scale=norm_rows(rows)
            g1=gh[c*half:(c+1)*half]
            dg=dg+jnp.sum(g1*n,axis=0,keepdims=True)
            e=g1*g
            outs.append(gx1[c*half:(c+1)*half]+scale*(e-jnp.mean(e,axis=-1,keepdims=True)-n*jnp.mean(e*n,axis=-1,keepdims=True)))
        masked=noise[...]==1
        gin_o[...]=(outs[1]+jnp.where(masked,0.0,outs[0])).astype(gin_o.dtype)
        demb_o[...]=jnp.sum(jnp.where(masked,outs[0],0.0),axis=0,keepdims=True)
        dgain_o[...]=dg
        for i,stage in ATTN_END: chunks[i].take(stage)
        stores=[]
        for i in in_state(ATTN_STATE,range(STEPS),4,7): stores.append((t_final.at[i],tiles_o.at[i]))
        for low,high,source,target in ((0,0,w_pair,wpair_o),(1,3,w_total,wtotal_o),(4,7,w_final,wfinal_o)):
            for place,i in enumerate(in_state(ATTN_STATE,range(STEPS,STEPS+4),low,high)): stores.append((source.at[i-STEPS],target.at[place]))
        stores=[pltpu.make_async_copy(a,b,local.at[2+n]) for n,(a,b) in enumerate(stores)]
        for d in stores: d.start()
        for i,chunk in enumerate(chunks): chunk.sent(*started(i,ATTN_TABLE))
        for d in stores: d.wait()

def bwd_attn(xc,noise,segc,segr,vec,gx1,q,k,v,mix,lse,wqkv,wout,trig,tile_pair,tile_total,tile_final):
    half=xc.shape[0]; R=2*half; piece=half//9
    ntp=lse.shape[1]
    ws=[pl.BlockSpec((D,PAIR),(lambda off:(lambda p:(0,off+p)))(o*PAIRS)) for o in range(3)]
    rows=pl.BlockSpec((R,PAIR),lambda p:(0,p))
    pairs=max(1,len(in_state(FFN_STATE,range(STEPS),0,0)))
    count=lambda low,high: max(1,len(in_state(ATTN_STATE,range(STEPS,STEPS+4),low,high)))
    return pl.pallas_call(partial(bwd_attn_kernel,half),grid=(PAIRS,),
        in_specs=[once((half,D)),once((half,1)),once((half,1)),once((1,640)),once((4,D)),once((R,D)),rows,rows,rows,rows,
                  pl.BlockSpec((1,ntp,256),lambda p:(p,0,0)),*ws,pl.BlockSpec((PAIR,D),lambda p:(p,0)),ANYSPACE,once((R,D))]+[ANYSPACE]*3,
        out_specs=[whole((half,D)),whole((1,D)),whole((1,D))]+[ANYSPACE]*4,
        out_shape=[jax.ShapeDtypeStruct((half,D),BF),jax.ShapeDtypeStruct((1,D),F32),jax.ShapeDtypeStruct((1,D),F32),jax.ShapeDtypeStruct((STEPS,2,TILE,128),BF),jax.ShapeDtypeStruct((count(0,0),2,2,WING,128),BF),jax.ShapeDtypeStruct((count(1,3),2,WING,128),BF),jax.ShapeDtypeStruct((count(4,7),2,WING,128),BF)],
        scratch_shapes=[pltpu.VMEM((D,R),BF),pltpu.VMEM((R,D),F32),pltpu.VMEM((2,half,-(-half//128)*128),F32),pltpu.VMEM((half,128),F32)]+[pltpu.VMEM((R,PAIR),F32)]*3+[pltpu.VMEM((R,D),BF),pltpu.VMEM((half,2*PAIR),F32)]
            +[pltpu.VMEM((pairs,2,2,TILE,128),BF),pltpu.VMEM((pairs,2,TILE,128),BF),pltpu.VMEM((STEPS,2,TILE,128),BF),pltpu.VMEM((STEPS,2*TILE,128),BF),pltpu.VMEM((STEPS,2,TILE,128),BF),
              pltpu.VMEM((4,2,2,2,WING,128),BF),pltpu.VMEM((4,2,2,WING,128),BF),pltpu.VMEM((4,2,WING,128),BF),pltpu.VMEM((4,2,WING,128),BF),pltpu.VMEM((4,2*WING,128),BF),pltpu.VMEM((4,2,WING,128),BF),
              DMA((STEPS,8)),DMA((STEPS,8)),DMA((4,8)),DMA((4,8)),DMA((16,))],
        compiler_params=pltpu.CompilerParams(vmem_limit_bytes=VMEM_LIMIT,dimension_semantics=("arbitrary",),collective_id=3,has_side_effects=True),
        cost_estimate=pl.CostEstimate(flops=4*R*D*(3*D+D)+60*R*half*D//2*2,bytes_accessed=30<<20,transcendentals=R*half*HEADS),
        name="bwd_attn")(xc,noise,segc,segr,vec,gx1,q,k,v,mix,lse,wqkv,wqkv,wqkv,wout,trig,mix,tile_pair,tile_total,tile_final)

def assemble(ffn,wings,gin,block):
    piece=gin.shape[2]
    up,down,out,qkv,grad,rows=pl.pallas_call(assemble_kernel,grid=(STEPS,),
        in_specs=[pl.BlockSpec((1,2,TILE,128),lambda i:(i,0,0,0)),whole(wings.shape),
            pl.BlockSpec((2,piece,D),lambda i:(jnp.minimum(i,3),0,0)),pl.BlockSpec((4,piece,D),lambda i:(jnp.minimum(i,3),0,0))],
        out_specs=[whole((192,FF)),pl.BlockSpec((128,D),lambda i:(i,0)),whole((192,D)),whole((192,3*D)),
            pl.BlockSpec((2,piece,D),lambda i:(jnp.minimum(i,3),0,0)),pl.BlockSpec((4,piece,D),lambda i:(jnp.minimum(i,3),0,0))],
        out_shape=[jax.ShapeDtypeStruct((192,FF),F32),jax.ShapeDtypeStruct((768,D),F32),jax.ShapeDtypeStruct((192,D),F32),jax.ShapeDtypeStruct((192,3*D),F32),
            jax.ShapeDtypeStruct((8,piece,D),F32),jax.ShapeDtypeStruct((16,piece,D),BF)],
        compiler_params=pltpu.CompilerParams(vmem_limit_bytes=VMEM_LIMIT,dimension_semantics=("arbitrary",)),
        name="assemble")(ffn,wings,gin.reshape(8,piece,D),block.reshape(16,piece,D))
    return up,down,out,qkv,grad,rows


DMA = pltpu.SemaphoreType.DMA
MESH = pl.DeviceIdType.MESH
INVMEM = pl.BlockSpec(memory_space=pltpu.VMEM)
ANYSPACE = pl.BlockSpec(memory_space=pl.ANY)


def place_ids():
    return lax.axis_index("ctx"), lax.axis_index("fsdp")


def meet(all_ranks, fsdp_partners):
    c, f = place_ids()
    sem = pltpu.get_barrier_semaphore()
    count = 0
    ranks = [(c + s) % 8 for s in range(1, 8)] if all_ranks else [c + 1 - 2 * (c % 2)]
    for rank in ranks:
        pl.semaphore_signal(sem, inc=1, device_id={"ctx": rank}, device_id_type=MESH)
        count += 1
    for s in fsdp_partners:
        other = (f + 2) % 4 if s == 2 else f + 1 - 2 * (f % 2) if s == 1 else 3 - f
        pl.semaphore_signal(sem, inc=1, device_id={"fsdp": other}, device_id_type=MESH)
        count += 1
    pl.semaphore_wait(sem, count)


def remote(src, dst, send, recv, where):
    return pltpu.make_async_remote_copy(src_ref=src, dst_ref=dst, send_sem=send, recv_sem=recv, device_id=where,
                                        device_id_type=MESH)


class ToUnit:
    def __init__(self, source, target, send, recv, local):
        self.source, self.target, self.send, self.recv, self.local = source, target, send, recv, local
        self.c, _ = place_ids()

    def message(self, s):
        c = self.c
        t = (c + s) % 8
        odd, last = t % 2, c // 7
        slot = (1 - odd) * c + odd * ((1 - last) * (6 - c) + last * 8)
        return remote(self.source(t // 2, odd), self.target(slot), self.send.at[s], self.recv.at[slot],
                      {"ctx": t - odd * last})

    def begin(self):
        for s in range(1, 8):
            self.message(s).start()

        @pl.when(self.c == 7)
        def _():
            self.message(0).start()

        @pl.when(self.c != 7)
        def _():
            self.own_safe().start()

    def own_safe(self):
        c = self.c
        part = c % 2
        slot = (1 - part) * c + part * (6 - c + c // 7)
        return pltpu.make_async_copy(self.source(c // 2, part), self.target(slot), self.local)

    def finish(self):
        c = self.c
        part = c % 2

        @pl.when(c == 7)
        def _():
            self.message(0).wait_send()

        @pl.when(c != 7)
        def _():
            self.own_safe().wait()

        for s in range(1, 8):
            self.message(s).wait_send()
        own = (1 - part) * c + part * (6 - c)
        for slot in range(9):
            take = slot != own
            if slot > 6:
                take = take & (part == 0)

            @pl.when(take)
            def _():
                remote(self.target(slot), self.target(slot), self.send.at[0], self.recv.at[slot], {"ctx": c}).wait_recv()


def pad_unit(zeros, target, sem):
    c, _ = place_ids()
    copy = pltpu.make_async_copy(zeros, target.at[pl.ds(7, 2)], sem)

    @pl.when(c % 2 == 1)
    def _():
        copy.start()
        copy.wait()


class FromUnit:
    def __init__(self, source, target, send, recv, local):
        self.source, self.target, self.send, self.recv, self.local = source, target, send, recv, local
        self.c, _ = place_ids()

    def message(self, s):
        c = self.c
        part = c % 2
        rank = (c + s) % 8
        slot = (1 - part) * rank + part * (6 - rank + rank // 7)
        return remote(self.source(slot), self.target(c // 2, part), self.send.at[s], self.recv.at[c], {"ctx": rank})

    def extra(self):
        c = self.c
        seq = c // 2
        return remote(self.source(8), self.target(seq, 1), self.send.at[0], self.recv.at[2 * seq + 1], {"ctx": 7})

    def own(self):
        c = self.c
        part = c % 2
        slot = (1 - part) * c + part * (6 - c + c // 7)
        return pltpu.make_async_copy(self.source(slot), self.target(c // 2, part), self.local)

    def each(self, remote_op, own_op):
        c = self.c
        part = c % 2
        for s in range(1, 8):
            rank = (c + s) % 8

            @pl.when((part == 0) | (rank != 7))
            def _():
                remote_op(self.message(s))

        @pl.when(part == 0)
        def _():
            remote_op(self.extra())

        @pl.when(c != 7)
        def _():
            own_op(self.own())

    def begin_one(self, s):
        c = self.c

        @pl.when((c % 2 == 0) | ((c + s) % 8 != 7))
        def _():
            self.message(s).start()

    def begin_rest(self):
        c = self.c

        @pl.when(c % 2 == 0)
        def _():
            self.extra().start()

        @pl.when(c != 7)
        def _():
            self.own().start()

    def begin(self):
        self.each(lambda m: m.start(), lambda m: m.start())

    def finish(self):
        self.each(lambda m: m.wait_send(), lambda m: m.wait())
        c = self.c
        for block in range(8):
            @pl.when((c == 7) | (c != block))
            def _():
                ref = self.target(block // 2, block % 2)
                remote(ref, ref, self.send.at[0], self.recv.at[block], {"ctx": c}).wait_recv()


class GatherRows:
    def __init__(self, shard, full, send, recv, local, parts=1):
        c, f = place_ids()
        n = shard.shape[0]
        n2 = n // 2
        m = n2 // parts
        h = c % 2
        sib, far, xn = f + 1 - 2 * (f % 2), (f + 2) % 4, c + 1 - 2 * (c % 2)
        diag = (sib + 2) % 4
        rows = lambda start, size: full.at[pl.ds(pl.multiple_of(start, 16), size)]
        same = lambda ref, i, where: remote(ref, ref, send.at[i], recv.at[i], where)
        mine = rows(f * n, n)
        self.copy = pltpu.make_async_copy(shard, mine, local)
        self.to_core = remote(shard, mine, send.at[0], recv.at[0], {"fsdp": sib})
        self.from_core = same(rows(sib * n, n), 0, {"fsdp": sib})
        self.to_far, self.from_far, self.to_x, self.from_x = [], [], [], []
        self.near_core, self.away_core, self.from_near, self.from_away = [], [], [], []
        for i in range(parts):
            a, b = h * n2 + i * m, (1 - h) * n2 + i * m
            near, away = rows(far * n + a, m), rows(far * n + b, m)
            k = 1 + 4 * i
            self.to_far.append(remote(shard.at[pl.ds(pl.multiple_of(a, 16), m)], rows(f * n + a, m), send.at[k], recv.at[k],
                                      {"fsdp": far}))
            self.from_far.append(same(near, k, {"fsdp": far}))
            self.to_x.append(same(near, k + 1, {"ctx": xn}))
            self.from_x.append(same(away, k + 1, {"ctx": xn}))
            self.near_core.append(same(near, k + 2, {"fsdp": sib}))
            self.away_core.append(same(away, k + 3, {"fsdp": sib}))
            self.from_near.append(same(rows(diag * n + a, m), k + 2, {"fsdp": sib}))
            self.from_away.append(same(rows(diag * n + b, m), k + 3, {"fsdp": sib}))

    def begin(self):
        for copy in self.to_far:
            copy.start()
        self.to_core.start()
        self.copy.start()

    def relay_far(self, i=0):
        self.from_far[i].wait_recv()
        self.to_x[i].start()
        self.near_core[i].start()

    def relay_x(self, i=0):
        self.from_x[i].wait_recv()
        self.away_core[i].start()

    def finish(self):
        self.copy.wait()
        for copy in [self.to_core] + self.to_far + self.to_x + self.near_core + self.away_core:
            copy.wait_send()
        for copy in [self.from_core] + self.from_near + self.from_away:
            copy.wait_recv()


class Reduce:
    def __init__(self, rows, send, recv, across=False, grad=None, pair=None, far=None, total=None, over=None, final=None):
        c, f = place_ids()
        self.send, self.recv, self.across = send, recv, across
        self.grad, self.pair, self.far, self.total, self.over, self.final = grad, pair, far, total, over, final
        self.core, self.y, self.x = f % 2, f // 2, c % 2
        z1, z2 = (c // 2) % 2, c // 4
        self.sib, self.far_id = {"fsdp": f + 1 - 2 * self.core}, {"fsdp": (f + 2) % 4}
        self.xn, self.z1n, self.z2n = {"ctx": c + 1 - 2 * self.x}, {"ctx": c + 2 - 4 * z1}, {"ctx": c + 4 - 8 * z2}
        half, quarter = rows // 2, rows // 4
        self.rows = rows
        self.levels = [(z1 * half, (1 - z1) * half, half, rows, self.z1n)]
        base = z1 * half
        self.levels.append((base + z2 * quarter, base + (1 - z2) * quarter, quarter, rows + half, self.z2n))

    def at(self, ref, start, size):
        return ref.at[self.x, pl.ds(pl.multiple_of(start, 16), size)]

    def copy(self, stage):
        x, y = self.x, self.y
        if stage == 0:
            source, target, where = self.grad.at[1 - self.core], self.pair, self.sib
        elif stage == 1 and self.across:
            source, target, where = self.pair.at[:, 1 - x], self.far, self.xn
        elif stage == 1:
            source, target, where = self.pair.at[1 - y], self.far, self.far_id
        elif stage == 2 and self.across:
            source, target, where = self.pair.at[1 - y, x], self.over.at[pl.ds(0, self.rows)], self.far_id
        elif stage == 2:
            source, target, where = self.total.at[1 - x], self.over.at[pl.ds(0, self.rows)], self.xn
        elif stage < 5:
            keep, give, size, offset, where = self.levels[stage - 3]
            source, target = self.at(self.total, give, size), self.over.at[pl.ds(offset, size)]
        elif stage < 7:
            keep, give, size, offset, where = self.levels[6 - stage]
            source = target = self.at(self.final, keep, size)
        else:
            source, target, where = self.final.at[x], self.final.at[x], self.xn
        return remote(source, target, self.send.at[stage], self.recv.at[stage], where)

    def start(self, stage):
        self.copy(stage).start()

    def take(self, stage):
        x, y = self.x, self.y
        if stage < 5:
            self.copy(stage).wait_recv()
        if stage == 0:
            self.pair[...] = self.pair[...] + self.grad[self.core]
        elif stage == 1 and self.across:
            for i in range(2):
                self.pair[i, x] = self.pair[i, x] + self.far[i]
        elif stage == 1:
            self.total[...] = self.far[...] + self.pair[y]
        elif stage == 2 and self.across:
            self.total[x] = self.pair[y, x] + self.over[pl.ds(0, self.rows)]
        elif stage == 2:
            self.total[x] = self.total[x] + self.over[pl.ds(0, self.rows)]
        elif stage < 5:
            keep, give, size, offset, where = self.levels[stage - 3]
            into = self.at(self.final if stage == 4 else self.total, keep, size)
            into[...] = self.at(self.total, keep, size)[...] + self.over[pl.ds(offset, size)]
        elif stage < 7:
            keep, give, size, offset, where = self.levels[6 - stage]
            ref = self.at(self.final, give, size)
            remote(ref, ref, self.send.at[stage], self.recv.at[stage], where).wait_recv()
        else:
            ref = self.final.at[1 - x]
            remote(ref, ref, self.send.at[7], self.recv.at[7], self.xn).wait_recv()

    def sent(self, *stages):
        for stage in stages:
            self.copy(stage).wait_send()


TILE = 768
WING = 576


def tail_kernel(tiles, wpair, wtotal, wfinal, gin, embed, gain_one, gain_two, down_shift, up_shift, tiles_o, wings_o, gin_o, sums_o,
                t_over, t_total, t_final, w_pair, w_far, w_over, w_total, w_final, sum_s, in_s,
                t_send, t_recv, r_send, r_recv, v_send, v_recv, a_send, a_recv, local):
    rows = FromUnit(lambda i: gin.at[i], lambda q, h: gin_o.at[q, h], a_send, a_recv, local.at[0])
    open_tiles = in_state(ATTN_STATE, range(STEPS), 4, 6)
    chunks = {i: Reduce(TILE, t_send.at[k], t_recv.at[k], total=t_total, over=t_over, final=t_final.at[k])
              for k, i in enumerate(open_tiles)}
    loads = [(tiles.at[i], t_final.at[k]) for k, i in enumerate(open_tiles)]
    wings = range(STEPS, STEPS + 4)
    for w in wings:
        k = w - STEPS
        chunks[w] = Reduce(WING, r_send.at[k], r_recv.at[k], pair=w_pair, far=w_far, total=w_total.at[k], over=w_over.at[k],
                           final=w_final.at[k])
    for low, high, source, target in ((0, 0, wpair, None), (1, 3, wtotal, w_total), (4, 7, wfinal, w_final)):
        for place, w in enumerate(in_state(ATTN_STATE, wings, low, high)):
            loads.append((source.at[place], w_pair if target is None else target.at[w - STEPS]))
    loads = [pltpu.make_async_copy(a, b, local.at[1 + n]) for n, (a, b) in enumerate(loads)]
    for copy in loads:
        copy.start()
    row = 0
    for part in (embed, gain_one, gain_two, down_shift):
        for i in range(D // 128):
            sum_s[0, row:row + 1] = part[:, i * 128:(i + 1) * 128]
            row += 1
    for s in range(4):
        for j in range(STEPS):
            sum_s[0, row:row + 1] = up_shift[:, j * 512 + s * 128:j * 512 + (s + 1) * 128]
            row += 1
    some = chunks[STEPS]
    vectors = [remote(sum_s.at[i], in_s.at[i], v_send.at[i], v_recv.at[i], where)
               for i, where in enumerate((some.sib, some.far_id, some.xn, some.z1n, some.z2n))]
    for copy in loads:
        copy.wait()
    meet(True, (1, 2))
    for chunk, take, start in TAIL_ORDER:
        if chunk == "rows":
            if start == 1:
                rows.begin_rest()
            rows.begin_one(start)
        elif chunk == "sums":
            if take is not None:
                vectors[take].wait_recv()
                sum_s[take + 1] = sum_s[take] + in_s[take]
            if start is not None:
                vectors[start].start()
        else:
            if take is not None:
                chunks[chunk].take(take)
            if start is not None:
                chunks[chunk].start(start)
    stores = [(t_final.at[k], tiles_o.at[i]) for k, i in enumerate(open_tiles)] + [(w_final, wings_o)]
    stores = [pltpu.make_async_copy(a, b, local.at[1 + n]) for n, (a, b) in enumerate(stores)]
    for copy in stores:
        copy.start()
    sums_o[...] = sum_s[5]
    for i in range(5):
        vectors[i].wait_send()
    for i, chunk in chunks.items():
        chunk.sent(*range(ATTN_STATE[i] + 1, 8))
    rows.finish()
    for copy in stores:
        copy.wait()


def tail(tiles, wpair, wtotal, wfinal, gin, vectors):
    piece = gin.shape[1]
    n = max(1, len(in_state(ATTN_STATE, range(STEPS), 4, 6)))
    return pl.pallas_call(
        tail_kernel,
        in_specs=[ANYSPACE] * 5 + [INVMEM] * 5,
        out_specs=[ANYSPACE] * 3 + [INVMEM],
        out_shape=[jax.ShapeDtypeStruct(tiles.shape, BF), jax.ShapeDtypeStruct((4, 2, WING, 128), BF),
                   jax.ShapeDtypeStruct((4, 2, piece, D), BF), jax.ShapeDtypeStruct((48, 128), F32)],
        scratch_shapes=[pltpu.VMEM((16, 128), BF), pltpu.VMEM((2, 16, 128), BF), pltpu.VMEM((n, 2, TILE, 128), BF),
                        pltpu.VMEM((2, 2, WING, 128), BF), pltpu.VMEM((2, WING, 128), BF), pltpu.VMEM((4, 2 * WING, 128), BF),
                        pltpu.VMEM((4, 2, WING, 128), BF), pltpu.VMEM((4, 2, WING, 128), BF), pltpu.VMEM((6, 48, 128), F32),
                        pltpu.VMEM((5, 48, 128), F32),
                        DMA((n, 8)), DMA((n, 8)), DMA((4, 8)), DMA((4, 8)), DMA((5,)), DMA((5,)), DMA((8,)), DMA((8,)), DMA((n + 6,))],
        input_output_aliases={0: 0},
        compiler_params=pltpu.CompilerParams(collective_id=4, has_side_effects=True, vmem_limit_bytes=VMEM_LIMIT),
        name="tail")(tiles, wpair, wtotal, wfinal, gin, *vectors)


def assemble_kernel(ffn, wings, gin, block, up_o, down_o, out_o, qkv_o, gin_o, block_o):
    i = pl.program_id(0)
    tile = lambda r: ffn[0, r // TILE, r % TILE:r % TILE + 64].astype(F32)
    for s in range(4):
        for r in range(0, 192, 64):
            up_o[r:r + 64, pl.ds(pl.multiple_of((s * STEPS + i) * 128, 128), 128)] = tile(s * 192 + r)
    for t in range(6):
        for r in range(0, 128, 64):
            down_o[r:r + 64, t * 128:(t + 1) * 128] = tile(768 + t * 128 + r)
    gin_o[...] = gin[...].astype(F32)
    block_o[...] = block[...]

    @pl.when(i == 0)
    def _():
        def strip(ref, k, r):
            row = k * 192 + r
            return ref[row // WING, row % WING:row % WING + 64].astype(F32)

        for r in range(0, 192, 64):
            for t in range(6):
                out_o[r:r + 64, t * 128:(t + 1) * 128] = strip(wings.at[0], t, r)
                source = wings.at[1 + t // 2]
                for w in range(3):
                    qkv_o[r:r + 64, w * D + t * 128:w * D + (t + 1) * 128] = strip(source, t % 2 * 3 + w, r)


def rope_constant(half):
    position = np.arange(2 * half, dtype=np.float32)
    frequency = np.float32(10000.0) ** (-(np.arange(HEAD // 2, dtype=np.float32) * np.float32(2.0)) / np.float32(HEAD))
    angles = (position[:, None] * frequency[None, :]).astype(np.float64)
    cosine, sine = np.cos(angles), np.sin(angles)
    table = np.concatenate([np.tile(cosine, (1, 4)), np.tile(np.concatenate([-sine, sine], axis=1), (1, 2))], axis=1)
    return jnp.asarray(table.reshape(2, half, 4 * HEAD).astype(np.float32))


def even_body(clean_in, segments, noise, mask_embed, norm1_gain, qkv_weight, out_weight, norm2_gain, up_weight, up_bias,
              down_weight, down_bias, out_grad):
    place = lax.axis_index("fsdp")
    piece = clean_in.shape[2]
    half = 9 * piece
    width = mask_embed.shape[0]
    meta = jnp.concatenate([segments.reshape(8, 1, piece), noise.reshape(8, 1, piece)], axis=2)
    meta = jnp.broadcast_to(meta, (8, 8, 2 * piece))
    small = jnp.stack([mask_embed, norm1_gain, norm2_gain, down_bias])
    small = jnp.concatenate([jnp.pad(small, ((0, 0), (0, 256 - width))), up_bias.reshape(-1, 256)])
    small = jnp.pad(small, ((0, 16 - small.shape[0]), (0, 0)))
    q, k, v, mixed, lse, resid, mask, seg_col, seg_row, vectors, up_shift, qkv_full, out_full, up_full, down_full, cotangent, clean = fwd_attn(
        clean_in, meta, out_grad, rope_constant(half), qkv_weight, out_weight, up_weight, down_weight, small)
    clean = clean.reshape(half, D)
    up_shift_grad, down_shift_grad, gain_two_grad, grad_resid, block_out, tile_pair, tile_total, tile_final = ffn(
        resid, vectors, up_full, up_shift, down_full, cotangent, out_grad)
    grad_in, embed_grad, gain_one_grad, tiles, wpair, wtotal, wfinal = bwd_attn(
        clean, mask, seg_col, seg_row, vectors, grad_resid, q, k, v, mixed, lse, qkv_full, out_full, rope_constant(half),
        tile_pair, tile_total, tile_final)
    tiles, wings, input_grad, sums = tail(tiles, wpair, wtotal, wfinal, grad_in.reshape(9, piece, D),
                                          (embed_grad, gain_one_grad, gain_two_grad, down_shift_grad, up_shift_grad))
    up_sum, down_sum, out_sum, qkv_sum, input_grad, block_out = assemble(tiles, wings, input_grad, block_out)
    input_grad = input_grad.reshape(clean_in.shape)
    block_out = block_out.reshape(out_grad.shape)
    sums = sums.reshape(-1)
    own = [lax.dynamic_slice_in_dim(sums, i * D + place * width, width) for i in range(4)]
    own_up = lax.dynamic_slice_in_dim(sums, 4 * D + place * (FF // 4), FF // 4)
    return (block_out, input_grad, own[0], own[1], qkv_sum, out_sum, own[2], up_sum, own_up, down_sum, own[3])


def choose_body(axes, *arrays):
    even = axes["ctx"] == 8 and axes["fsdp"] == 4 and arrays[0].shape[0] == 4
    return (even_body if even else general_body)(*arrays)


def solution(mesh):
    placed = (
        P("fsdp", None, "ctx", None),
        P("fsdp", None, "ctx"),
        P("fsdp", None, "ctx"),
        P("fsdp"),
        P("fsdp"),
        P("fsdp", None),
        P("fsdp", None),
        P("fsdp"),
        P("fsdp", None),
        P("fsdp"),
        P("fsdp", None),
        P("fsdp"),
        P("fsdp", None, None, "ctx", None),
    )
    return jax.shard_map(
        partial(choose_body, dict(mesh.shape)),
        mesh=mesh,
        in_specs=placed,
        out_specs=(
            P("fsdp", None, None, "ctx", None),
            P("fsdp", None, "ctx", None),
            P("fsdp"),
            P("fsdp"),
            P("fsdp", None),
            P("fsdp", None),
            P("fsdp"),
            P("fsdp", None),
            P("fsdp"),
            P("fsdp", None),
            P("fsdp"),
        ),
        check_vma=False,
    )
```

```python
from functools import partial

import jax
import jax.numpy as jnp
import numpy as np
from jax import lax
from jax.experimental import pallas as pl
from jax.experimental.pallas import tpu as pltpu
from jax.sharding import PartitionSpec as P

D = 768
HEADS = 12
HEAD = 64
FF = 3072
BLK = 16


EPS = 1e-05
together = 4


def normalize(values):
    centre = values - jnp.mean(values, axis=-1, keepdims=True)
    scale = lax.rsqrt(jnp.mean(centre * centre, axis=-1, keepdims=True) + EPS)
    return (centre * scale, scale)


def norm_back(grad_in, normed, scale):
    centred = grad_in - jnp.mean(grad_in, axis=-1, keepdims=True)
    return scale * (centred - normed * jnp.mean(grad_in * normed, axis=-1, keepdims=True))


def rope_tables(positions):
    half_head = HEAD // 2
    frequency = 10000.0 ** (-(jnp.arange(half_head, dtype=jnp.float32) * 2.0) / HEAD)
    angles = positions.astype(jnp.float32)[:, None] * frequency[None, :]
    return (jnp.cos(angles), jnp.sin(angles))


def rotate(values, cos_part, sin_part, reverse):
    count = values.shape[0]
    heads = values.reshape(count, HEADS, HEAD)
    half_head = HEAD // 2
    leading = heads[..., :half_head]
    trailing = heads[..., half_head:]
    cosine = cos_part[:, None, :]
    sine_part = sin_part[:, None, :]
    if reverse:
        parts = [leading * cosine + trailing * sine_part, trailing * cosine - leading * sine_part]
    else:
        parts = [leading * cosine - trailing * sine_part, trailing * cosine + leading * sine_part]
    return jnp.concatenate(parts, axis=-1).reshape(count, D)


def split_heads(values):
    count = values.shape[0]
    return values.reshape(count, HEADS // together, together * HEAD).transpose(1, 0, 2)


def join_heads(values):
    groups, count, width = values.shape
    return values.transpose(1, 0, 2).reshape(count, groups * width)


def allowed_pairs(query_copy, query_block, query_doc, key_copy, key_block, key_doc):
    same_doc = query_doc[:, None] == key_doc[None, :]
    query_noisy = (query_copy == 0)[:, None]
    key_noisy = (key_copy == 0)[None, :]
    query_column = query_block[:, None]
    key_row = key_block[None, :]
    inner = query_noisy & key_noisy & (key_row == query_column)
    earlier = query_noisy & ~key_noisy & (key_row < query_column)
    causal = ~query_noisy & ~key_noisy & (key_row <= query_column)
    return same_doc & (inner | earlier | causal)


def masked_scores(query_group, key_group, allowed):
    query_heads = query_group.reshape(query_group.shape[0], together, HEAD)
    key_heads = key_group.reshape(key_group.shape[0], together, HEAD)
    raw = jnp.einsum(
        "qhd,khd->hqk", query_heads, key_heads, preferred_element_type=jnp.float32
    ) * HEAD ** (-0.5)
    return (jnp.where(allowed[None], raw, -1e30), query_heads, key_heads)


def group_forward(items, allowed):
    query_group, key_group, value_group = items
    count = query_group.shape[0]
    scores, query_heads, key_heads = masked_scores(query_group, key_group, allowed)
    value_heads = value_group.reshape(value_group.shape[0], together, HEAD)
    top = jnp.max(scores, axis=-1, keepdims=True)
    weights = jnp.exp(scores - top)
    total = jnp.sum(weights, axis=-1, keepdims=True)
    probs = (weights / total).astype(jnp.bfloat16)
    mixed = jnp.einsum("hqk,khd->qhd", probs, value_heads, preferred_element_type=jnp.float32)
    return (mixed.reshape(count, together * HEAD), (top + jnp.log(total))[..., 0])


def group_backward(items, allowed, tail):
    query_group, key_group, value_group, grad_group, log_total = items
    count = query_group.shape[0]
    key_count = key_group.shape[0]
    scores, query_heads, key_heads = masked_scores(query_group, key_group, allowed)
    value_heads = value_group.reshape(key_count, together, HEAD)
    grad_heads = grad_group.reshape(count, together, HEAD)
    probs = jnp.exp(scores - log_total[..., None])
    prob_grad = jnp.einsum(
        "qhd,khd->hqk", grad_heads, value_heads, preferred_element_type=jnp.float32
    )
    centre = jnp.sum(probs * prob_grad, axis=-1, keepdims=True)
    score_grad = (probs * (prob_grad - centre)).astype(jnp.bfloat16)
    query_grad = jnp.einsum(
        "hqk,khd->qhd", score_grad, key_heads, preferred_element_type=jnp.float32
    ) * HEAD ** (-0.5)
    tail_probs = probs.astype(jnp.bfloat16)
    value_grad = jnp.einsum(
        "hqk,qhd->khd", tail_probs, grad_heads, preferred_element_type=jnp.float32
    )
    key_grad = jnp.einsum(
        "hqk,qhd->khd", score_grad, query_heads, preferred_element_type=jnp.float32
    ) * HEAD ** (-0.5)
    return (
        query_grad.reshape(count, together * HEAD),
        key_grad.reshape(tail, together * HEAD),
        value_grad.reshape(tail, together * HEAD),
        centre[..., 0],
    )


def reduce_grads(grads):
    shards = (
        lax.psum_scatter(grads[0], "fsdp", scatter_dimension=0, tiled=True),
        lax.psum_scatter(grads[1], "fsdp", scatter_dimension=0, tiled=True),
        lax.psum_scatter(grads[2], "fsdp", scatter_dimension=0, tiled=True),
        lax.psum_scatter(grads[3], "fsdp", scatter_dimension=0, tiled=True),
        lax.psum_scatter(grads[4], "fsdp", scatter_dimension=0, tiled=True),
        lax.psum_scatter(grads[5], "fsdp", scatter_dimension=0, tiled=True),
        lax.psum_scatter(grads[6], "fsdp", scatter_dimension=0, tiled=True),
        lax.psum_scatter(grads[7], "fsdp", scatter_dimension=0, tiled=True),
        lax.psum_scatter(grads[8], "fsdp", scatter_dimension=0, tiled=True),
    )
    return lax.psum(
        (
            shards[0],
            shards[1],
            shards[2],
            shards[3],
            shards[4],
            shards[5],
            shards[6],
            shards[7],
            shards[8],
        ),
        "ctx",
    )


def add_tuples(left_items, right_items):
    return tuple((left_item + right_item for left_item, right_item in zip(left_items, right_items)))


def general_body(
    clean_in,
    segments,
    noise,
    mask_embed,
    norm1_gain,
    qkv_weight,
    out_weight,
    norm2_gain,
    up_weight,
    up_bias,
    down_weight,
    down_bias,
    out_grad,
):
    qkv_full, out_full, gain_low, embed_low = (
        lax.all_gather(qkv_weight, "fsdp", axis=0, tiled=True),
        lax.all_gather(out_weight, "fsdp", axis=0, tiled=True),
        lax.all_gather(norm1_gain, "fsdp", axis=0, tiled=True),
        lax.all_gather(mask_embed, "fsdp", axis=0, tiled=True),
    )
    up_full, up_low, down_full, down_low, gain_two_low = (
        lax.all_gather(up_weight, "fsdp", axis=0, tiled=True),
        lax.all_gather(up_bias, "fsdp", axis=0, tiled=True),
        lax.all_gather(down_weight, "fsdp", axis=0, tiled=True),
        lax.all_gather(down_bias, "fsdp", axis=0, tiled=True),
        lax.all_gather(norm2_gain, "fsdp", axis=0, tiled=True),
    )
    gain_one = gain_low.astype(jnp.float32)
    gain_two = gain_two_low.astype(jnp.float32)
    embed_row = embed_low.astype(jnp.float32)
    up_shift = up_low.astype(jnp.float32)
    down_shift = down_low.astype(jnp.float32)
    micro_count = clean_in.shape[0]
    piece = clean_in.shape[2]
    local_rows = 2 * piece
    ctx_count = lax.axis_size("ctx")
    ctx_rank = lax.axis_index("ctx")
    span = jnp.arange(piece, dtype=jnp.int32)
    local_pos = jnp.concatenate(
        [ctx_rank * piece + span, (2 * ctx_count - 1 - ctx_rank) * piece + span]
    )
    ranks = jnp.arange(ctx_count, dtype=jnp.int32)[:, None]
    far_pos = jnp.concatenate(
        [ranks * piece + span[None, :], (2 * ctx_count - 1 - ranks) * piece + span[None, :]], axis=1
    ).reshape(-1)
    seq_len = ctx_count * local_rows
    cos_part, sin_part = rope_tables(jnp.concatenate([local_pos, local_pos]))
    query_copy = jnp.concatenate(
        [jnp.zeros((local_rows,), jnp.int32), jnp.ones((local_rows,), jnp.int32)]
    )
    key_copy = jnp.concatenate(
        [jnp.ones((seq_len,), jnp.int32), jnp.zeros((local_rows,), jnp.int32)]
    )
    query_block = jnp.concatenate([local_pos, local_pos]) // BLK
    key_block = jnp.concatenate([far_pos, local_pos]) // BLK
    full_shapes = ((D,), (D,), (D, 3 * D), (D, D), (D,), (D, FF), (FF,), (FF, D), (D,))
    totals = tuple((jnp.zeros(shape_item, jnp.float32) for shape_item in full_shapes))
    tail = seq_len + local_rows
    outputs = []
    input_grads = []
    for micro_step in range(micro_count):
        clean_rows = clean_in[micro_step].reshape(local_rows, D).astype(jnp.float32)
        noise_rows = noise[micro_step].reshape(-1)
        masked_rows = noise_rows[:, None] == 1
        doc_local = segments[micro_step].reshape(-1).astype(jnp.float32)
        noisy_rows = jnp.where(masked_rows, embed_row[None, :], clean_rows)
        stacked = jnp.concatenate([noisy_rows, clean_rows], axis=0)
        normed_one, scale_one = normalize(stacked)
        h_one = (normed_one * gain_one).astype(jnp.bfloat16)
        projected = jnp.dot(h_one, qkv_full, preferred_element_type=jnp.float32)
        queries = rotate(projected[:, :D], cos_part, sin_part, False).astype(jnp.bfloat16)
        keys = rotate(projected[:, D : 2 * D], cos_part, sin_part, False).astype(jnp.bfloat16)
        values = projected[:, 2 * D :].astype(jnp.bfloat16)
        far_keys, far_values, far_docs = (
            lax.all_gather(keys[local_rows:], "ctx", axis=0, tiled=True),
            lax.all_gather(values[local_rows:], "ctx", axis=0, tiled=True),
            lax.all_gather(doc_local.astype(jnp.bfloat16), "ctx", axis=0, tiled=True),
        )
        key_all = jnp.concatenate([far_keys, keys[:local_rows]], axis=0)
        value_all = jnp.concatenate([far_values, values[:local_rows]], axis=0)
        query_doc = jnp.concatenate([doc_local, doc_local])
        key_doc = jnp.concatenate([far_docs.astype(jnp.float32), doc_local])
        allowed = allowed_pairs(query_copy, query_block, query_doc, key_copy, key_block, key_doc)
        query_groups = split_heads(queries)
        key_groups = split_heads(key_all)
        value_groups = split_heads(value_all)
        mixed_groups, log_totals = lax.map(
            partial(group_forward, allowed=allowed), (query_groups, key_groups, value_groups)
        )
        mixed = join_heads(mixed_groups).astype(jnp.bfloat16)
        resid = stacked + jnp.dot(mixed, out_full, preferred_element_type=jnp.float32)
        normed_two, scale_two = normalize(resid)
        h_two = (normed_two * gain_two).astype(jnp.bfloat16)
        hidden = jnp.dot(h_two, up_full, preferred_element_type=jnp.float32) + up_shift
        active = jax.nn.gelu(hidden, approximate=True).astype(jnp.bfloat16)
        result = resid + jnp.dot(active, down_full, preferred_element_type=jnp.float32) + down_shift
        outputs.append(result.astype(jnp.bfloat16).reshape(2, 2, piece, D))
        cotangent = out_grad[micro_step].reshape(2 * local_rows, D).astype(jnp.float32)
        grad_out = cotangent.astype(jnp.bfloat16)
        down_grad = jnp.einsum("rf,rd->fd", active, grad_out, preferred_element_type=jnp.float32)
        down_shift_grad = jnp.sum(grad_out.astype(jnp.float32), axis=0)
        grad_active = jnp.einsum(
            "rd,fd->rf", grad_out, down_full, preferred_element_type=jnp.float32
        )
        unused, gelu_back = jax.vjp(partial(jax.nn.gelu, approximate=True), hidden)
        grad_hidden = gelu_back(grad_active)[0].astype(jnp.bfloat16)
        up_grad = jnp.einsum("rd,rf->df", h_two, grad_hidden, preferred_element_type=jnp.float32)
        up_shift_grad = jnp.sum(grad_hidden.astype(jnp.float32), axis=0)
        grad_h_two = jnp.einsum(
            "rf,df->rd", grad_hidden, up_full, preferred_element_type=jnp.float32
        )
        gain_two_grad = jnp.sum(grad_h_two * normed_two, axis=0)
        grad_resid = cotangent + norm_back(grad_h_two * gain_two, normed_two, scale_two)
        grad_attn = grad_resid.astype(jnp.bfloat16)
        out_grad_full = jnp.einsum(
            "rd,re->de", mixed, grad_attn, preferred_element_type=jnp.float32
        )
        grad_mixed = jnp.einsum(
            "re,de->rd", grad_attn, out_full, preferred_element_type=jnp.float32
        ).astype(jnp.bfloat16)
        query_grads, key_grads, value_grads, centres = lax.map(
            partial(group_backward, allowed=allowed, tail=tail),
            (query_groups, key_groups, value_groups, split_heads(grad_mixed), log_totals),
        )
        query_grad = join_heads(query_grads)
        key_grad_all = join_heads(key_grads)
        value_grad_all = join_heads(value_grads)
        key_mine, value_mine = (
            lax.psum_scatter(key_grad_all[:seq_len], "ctx", scatter_dimension=0, tiled=True),
            lax.psum_scatter(value_grad_all[:seq_len], "ctx", scatter_dimension=0, tiled=True),
        )
        key_grad = jnp.concatenate([key_grad_all[seq_len:], key_mine], axis=0)
        value_grad = jnp.concatenate([value_grad_all[seq_len:], value_mine], axis=0)
        grad_proj = jnp.concatenate(
            [
                rotate(query_grad, cos_part, sin_part, True),
                rotate(key_grad, cos_part, sin_part, True),
                value_grad,
            ],
            axis=1,
        ).astype(jnp.bfloat16)
        qkv_grad = jnp.einsum("rd,re->de", h_one, grad_proj, preferred_element_type=jnp.float32)
        grad_h_one = jnp.einsum(
            "re,de->rd", grad_proj, qkv_full, preferred_element_type=jnp.float32
        )
        gain_one_grad = jnp.sum(grad_h_one * normed_one, axis=0)
        grad_rows = grad_resid + norm_back(grad_h_one * gain_one, normed_one, scale_one)
        grad_noisy = grad_rows[:local_rows]
        input_grads.append(
            (grad_rows[local_rows:] + jnp.where(masked_rows, 0.0, grad_noisy)).reshape(2, piece, D)
        )
        embed_grad = jnp.sum(jnp.where(masked_rows, grad_noisy, 0.0), axis=0)
        step_grads = (
            embed_grad,
            gain_one_grad,
            qkv_grad,
            out_grad_full,
            gain_two_grad,
            up_grad,
            up_shift_grad,
            down_grad,
            down_shift_grad,
        )
        totals = add_tuples(totals, step_grads)
    reduced = reduce_grads(totals)
    block_out = jnp.stack(outputs)
    input_grad = jnp.stack(input_grads)
    return (
        block_out,
        input_grad,
        reduced[0],
        reduced[1],
        reduced[2],
        reduced[3],
        reduced[4],
        reduced[5],
        reduced[6],
        reduced[7],
        reduced[8],
    )


PAIR=2*HEAD; PAIRS=D//PAIR
NEG=-1e30
VMEM_LIMIT=60<<20
F32=jnp.float32; BF=jnp.bfloat16

def dot_nn(a,b): return lax.dot_general(a,b,(((1,),(0,)),((),())),preferred_element_type=F32)
def dot_nt(a,b): return lax.dot_general(a,b,(((1,),(1,)),((),())),preferred_element_type=F32)
def dot_tn(a,b): return lax.dot_general(a,b,(((0,),(0,)),((),())),preferred_element_type=F32)

def tiles_of(half):
    return [(s,min(128,half-s)) for s in range(0,half,128)]

def norm_rows(rows):
    centre=rows-jnp.mean(rows,axis=-1,keepdims=True)
    scale=lax.rsqrt(jnp.mean(centre*centre,axis=-1,keepdims=True)+EPS)
    return centre*scale, scale

def swap_halves(z):
    lane=lax.broadcasted_iota(jnp.int32,z.shape,1)
    low=(lane & (HEAD-1)) < HEAD//2
    return jnp.where(low,pltpu.roll(z,PAIR-HEAD//2,1),pltpu.roll(z,HEAD//2,1))

def head_stack(z):
    lane=lax.broadcasted_iota(jnp.int32,z.shape,1)
    first=lane<HEAD
    zero=jnp.zeros_like(z)
    return jnp.concatenate([jnp.where(first,z,zero),jnp.where(first,zero,z)],axis=0)

def head_merge(z):
    n=z.shape[0]//2
    lane=lax.broadcasted_iota(jnp.int32,(n,z.shape[1]),1)
    return jnp.where(lane<HEAD,z[:n],z[n:])

def layer_rows(xc_ref,noise_ref,emb_ref):
    clean=xc_ref[...].astype(F32)
    noisy=jnp.where(noise_ref[...]==1,emb_ref[...].astype(F32),clean)
    return noisy,clean

def fwd_attn_kernel(half,xc,noise,segc,segr,small,wqkv,wout,trig,
                    q_o,k_o,v_o,mix_o,lse_o,x1_o,h_s,bias_s,self_s,mix_s):
    p=pl.program_id(0)
    tiles=tiles_of(half)
    @pl.when(p==0)
    def _():
        g=vector_row(small,1)
        clean=jnp.concatenate([xc[i] for i in range(9)],axis=0).astype(F32)
        noisy=jnp.where(noise[...]==1,vector_row(small,0),clean)
        for c,rows in enumerate((noisy,clean)):
            x1_o[c*half:(c+1)*half]=rows
            n,_=norm_rows(rows)
            h_s[c*half:(c+1)*half]=(n*g).astype(BF)
        for s,m in tiles:
            n=s+m
            qb=(lax.broadcasted_iota(jnp.int32,(m,n),0)+s)//BLK
            kb=lax.broadcasted_iota(jnp.int32,(m,n),1)//BLK
            same=segc[s:n]==segr[:,:n]
            bias_s[0,s:n,:n]=jnp.where(same&(kb<qb),0.0,NEG)
            bias_s[1,s:n,:n]=jnp.where(same&(kb<=qb),0.0,NEG)
            qb=lax.broadcasted_iota(jnp.int32,(m,m),0)//BLK
            kb=lax.broadcasted_iota(jnp.int32,(m,m),1)//BLK
            same=segc[s:n]==segr[:,s:n]
            self_s[s:n,:m]=jnp.where(same&(kb==qb),0.0,NEG)
    h=h_s[...]
    cs=jnp.concatenate([trig[:,:PAIR]]*2,axis=0)
    sn=jnp.concatenate([trig[:,PAIR:]]*2,axis=0)
    block=lambda i: wqkv[:,pl.ds(pl.multiple_of(i*D+p*PAIR,PAIR),PAIR)]
    zq=dot_nn(h,jnp.concatenate([block(0),block(1)],axis=1))
    z=zq[:,:PAIR]; q_o[...]=((z*cs+swap_halves(z)*sn).astype(BF)*BF(HEAD**-0.5)).astype(BF)
    z=zq[:,PAIR:]; k_o[...]=(z*cs+swap_halves(z)*sn).astype(BF)
    v_o[...]=dot_nn(h,block(2)).astype(BF)
    idx=0
    for s,m in tiles:
        n=s+m
        for c in (0,1):
            qs=head_stack(q_o[c*half+s:c*half+n])
            kc=k_o[half:half+n]; vc=v_o[half:half+n]
            sc=dot_nt(qs,kc).reshape(2,m,n)+bias_s[c,s:n,:n][None]
            top=jnp.max(sc,axis=-1,keepdims=True)
            if c==0:
                ss=dot_nt(qs,k_o[s:n]).reshape(2,m,m)+self_s[s:n,:m][None]
                top=jnp.maximum(top,jnp.max(ss,axis=-1,keepdims=True))
            w=jnp.exp(sc-top); tot=jnp.sum(w,axis=-1,keepdims=True)
            o=dot_nn(w.astype(BF).reshape(2*m,n),vc)
            if c==0:
                w2=jnp.exp(ss-top); tot=tot+jnp.sum(w2,axis=-1,keepdims=True)
                o=o+dot_nn(w2.astype(BF).reshape(2*m,m),v_o[s:n])
            tot=tot.reshape(2*m,1)
            o=o*(1.0/tot)
            mx=head_merge(o).astype(BF)
            mix_o[c*half+s:c*half+n]=mx
            mix_s[p,c*half+s:c*half+n]=mx
            lse=top.reshape(2*m,1)+jnp.log(tot)
            lse_o[0,idx:idx+1,:2*m]=jnp.broadcast_to(lse,(2*m,128)).T[0:1]
            idx+=1
    @pl.when(p==pl.num_programs(0)-1)
    def _():
        full=jnp.concatenate([mix_s[i] for i in range(PAIRS)],axis=1)
        x1_o[...]=x1_o[...]+dot_nn(full,wout[...])

def whole(shape): return pl.BlockSpec(shape,lambda *i:(0,)*len(shape))

def vector_row(small,i):
    return jnp.concatenate([small[f,i:i+1,:D//4] for f in range(4)],axis=1).astype(F32)

def fwd_attn_comm_kernel(half,*refs):
    clean,meta,gout,trig,qkv,out,up,down,small,zeros,blank=refs[:11]
    q_o,k_o,v_o,mix_o,lse_o,x1_o,noise_o,segc_o,segr_o,vec_o,bias_o,qkv_o,out_o,up_o,down_o,cot_o,clean_o=refs[11:28]
    h_s,bias_s,self_s,mix_s,clean_s,meta_s,small_s,qkv_s,out_s,trig_s=refs[28:38]
    a_send,a_recv,m_send,m_recv,c_send,c_recv,w_send,w_recv,s_send,s_recv,local=refs[38:]
    p=pl.program_id(0)
    c,f=place_ids()
    piece=half//9
    weight=lambda i,shard,full,parts: GatherRows(shard,full,w_send.at[i],w_recv.at[i],local.at[i],parts)
    w_qkv,w_out,w_up,w_down=weight(0,qkv,qkv_s,3),weight(1,out,out_s,1),weight(2,up,up_o,3),GatherRows(down,down_o,w_send.at[3],w_recv.at[3],local.at[3],3,False)
    rows=ToUnit(lambda q,h:clean.at[q,h],lambda t:clean_s.at[t],a_send,a_recv,local.at[4])
    notes=ToUnit(lambda q,h:meta.at[2*q+h],lambda t:meta_s.at[t],m_send,m_recv,local.at[5])
    grads=[ToUnit(lambda q,h:gout.at[q,0,h],lambda t:cot_o.at[t],c_send,c_recv,local.at[6])]
    copies=[pltpu.make_async_copy(qkv_s,qkv_o,local.at[8]),pltpu.make_async_copy(out_s,out_o,local.at[9]),pltpu.make_async_copy(clean_s,clean_o,local.at[10])]
    others=[f+1-2*(f%2),(f+2)%4,3-f]
    @pl.when(p==0)
    def _():
        meet(True,(1,2,3))
        w_qkv.begin()
        notes.begin()
        rows.begin()
        sends=[remote(small,small_s.at[f],s_send.at[i],s_recv.at[i],{"fsdp":other}) for i,other in enumerate(others)]
        for d in sends: d.start()
        own=pltpu.make_async_copy(small,small_s.at[f],local.at[11])
        own.start()
        table=pltpu.make_async_copy(trig.at[c%2],trig_s,local.at[12])
        table.start()
        w_out.begin()
        w_up.begin()
        w_down.begin()
        for i in range(3): w_qkv.relay_far(i)
        pads=[pltpu.make_async_copy(zeros,clean_s.at[pl.ds(7,2)],local.at[13]),pltpu.make_async_copy(blank,meta_s.at[pl.ds(7,2)],local.at[13])]
        pads.append(pltpu.make_async_copy(zeros,cot_o.at[pl.ds(7,2)],local.at[13]))
        @pl.when(c%2==1)
        def _():
            for d in pads:
                d.start()
                d.wait()
        for i in range(3): w_qkv.relay_x(i)
        for r in grads: r.begin_straight()
        own.wait()
        table.wait()
        for i,other in enumerate(others):
            sends[i].wait_send()
            remote(small_s.at[other],small_s.at[other],s_send.at[i],s_recv.at[i],{"fsdp":other}).wait_recv()
        notes.finish()
        lane=lax.broadcasted_iota(jnp.int32,(1,128),1)
        for i in range(9):
            t=jnp.broadcast_to(meta_s[i,0:1].astype(F32),(128,128)).T
            segc_o[i*piece:(i+1)*piece]=t[:piece,0:1]
            noise_o[i*piece:(i+1)*piece]=t[piece:,0:1].astype(jnp.int32)
        for i in range(5):
            even=meta_s[2*i,0:1].astype(F32)
            odd=pltpu.roll(meta_s[min(2*i+1,8)].astype(F32),64,1)[0:1]
            segr_o[:,i*128:(i+1)*128]=jnp.where(lane<64,even,odd)
        for i in range(2): vec_o[i:i+1]=vector_row(small_s,2+i)
        for i in range(2): vec_o[2+i:3+i]=vector_row(small_s,i)
        for g in range(4):
            for i in range(3): bias_o[:,g*768+i*256:g*768+(i+1)*256]=small_s[g,4+i:5+i].astype(F32)
        rows.finish()
        w_qkv.finish()
        copies[0].start()
        copies[2].start()
    fwd_attn_kernel(half,clean_s,noise_o,segc_o,segr_o,small_s,qkv_s,out_s,trig_s,q_o,k_o,v_o,mix_o,lse_o,x1_o,h_s,bias_s,self_s,mix_s)
    def at(i,*ops):
        @pl.when(p==i)
        def _():
            for op in ops: op()
    at(0,w_out.relay_far,*[partial(w_up.relay_far,i) for i in range(2)])
    at(1,w_out.relay_x,partial(w_up.relay_far,2),partial(w_up.relay_x,0),grads[0].begin_across)
    at(2,w_out.finish,copies[1].start,partial(w_up.relay_x,1),partial(w_down.relay_far,0))
    at(3,partial(w_up.relay_x,2),partial(w_down.relay_far,1))
    at(4,partial(w_down.relay_far,2))
    @pl.when(p==pl.num_programs(0)-1)
    def _():
        for w in (w_up,w_down): w.finish()
        for r in grads: r.finish()
        for d in copies: d.wait()

def whole(shape): return pl.BlockSpec(shape,lambda *i:(0,)*len(shape))
def once(shape): return pl.BlockSpec(shape,lambda *i:(0,)*len(shape),pipeline_mode=pl.Buffered(1))

def fwd_attn(clean,meta,gout,trig,qkv,out,up,down,small):
    piece=clean.shape[2]; half=9*piece; R=2*half
    zeros=np.zeros((2,piece,D),BF)
    blank=np.concatenate([np.full((2,8,piece),-1,np.int32),np.zeros((2,8,128-piece),np.int32)],axis=2)
    nt=len(tiles_of(half))*2; ntp=-(-nt//8)*8
    rows=pl.BlockSpec((R,PAIR),lambda p:(0,p))
    sds=jax.ShapeDtypeStruct
    return pl.pallas_call(partial(fwd_attn_comm_kernel,half),grid=(PAIRS,),
        in_specs=[ANYSPACE]*4+[once(a.shape) for a in (qkv,out,up,down,small,zeros,blank)],
        out_specs=[rows,rows,rows,rows,pl.BlockSpec((1,ntp,256),lambda p:(p,0,0)),whole((R,D)),whole((half,1)),whole((half,1)),whole((1,640)),whole((4,D)),whole((1,FF))]+[ANYSPACE]*6,
        out_shape=[sds((R,D),BF)]*4+[sds((PAIRS,ntp,256),F32),sds((R,D),F32),sds((half,1),jnp.int32),sds((half,1),F32),sds((1,640),F32),sds((4,D),F32),sds((1,FF),F32),
            sds((D,3*D),BF),sds((D,D),BF),sds((D,FF),BF),sds((FF,D),BF),sds((9,piece,D),BF),sds((9,piece,D),BF)],
        scratch_shapes=[pltpu.VMEM((R,D),BF),pltpu.VMEM((2,half,half),F32),pltpu.VMEM((half,128),F32),pltpu.VMEM((PAIRS,R,PAIR),BF),
            pltpu.VMEM((9,piece,D),BF),pltpu.VMEM((9,8,128),jnp.int32),pltpu.VMEM((4,)+small.shape,BF),pltpu.VMEM((D,3*D),BF),pltpu.VMEM((D,D),BF),pltpu.VMEM((half,2*PAIR),F32),
            DMA((8,)),DMA((9,)),DMA((8,)),DMA((9,)),DMA((8,)),DMA((9,)),DMA((4,13)),DMA((4,13)),DMA((3,)),DMA((3,)),DMA((14,))],
        compiler_params=pltpu.CompilerParams(vmem_limit_bytes=VMEM_LIMIT,dimension_semantics=("arbitrary",),collective_id=1,has_side_effects=True),
        cost_estimate=pl.CostEstimate(flops=2*R*D*(3*D+D)+24*R*half*D//2*2,bytes_accessed=16<<20,transcendentals=R*half*HEADS),
        name="fwd_attn")(clean,meta,gout,trig,qkv,out,up,down,small,zeros,blank)

GC=(2.0/3.141592653589793)**0.5
def cols(refs): return jnp.concatenate([r[...] for r in refs],axis=1)
def rowcat(refs): return jnp.concatenate([r[...] for r in refs],axis=0)
STEPS=FF//512
def up_specs(): return [pl.BlockSpec((D,128),(lambda s:(lambda j:(0,s*STEPS+j)))(s)) for s in range(4)]
def down_specs(): return [pl.BlockSpec((128,D),(lambda s:(lambda j:(s*STEPS+j,0)))(s)) for s in range(4)]
def bias_specs(): return [pl.BlockSpec((1,128),(lambda s:(lambda j:(0,s*STEPS+j)))(s)) for s in range(4)]

FFN_TABLE={2: [(0, None, 0)], 4: [(1, None, 0), (0, 0, 1)], 6: [(2, None, 0), (1, 0, 1)], 8: [(3, None, 0), (0, 1, None), (2, 0, 1)], 9: [(3, 0, None)], 10: [(4, None, 0), (1, 1, None)], 12: [(5, None, 0)]}
FFN_END=[(4, 0), (2, 1), (5, 0)]
ATTN_TABLE={0: [(3, None, 1), (4, None, 1), (5, None, 1), (0, None, 2), (1, None, 2), (2, None, 2)], 1: [(6, None, 0)], 2: [(0, 2, 3), (6, 0, 1)], 3: [(0, 3, 4), (1, 2, 3), (3, 1, 2)], 4: [(7, None, 0), (2, 2, 3)], 5: [(0, 4, 5), (1, 3, 4), (2, 3, 4), (3, 2, 3), (4, 1, 2), (7, 0, 1)], 6: [(0, 5, 6)], 7: [(1, 4, 5), (2, 4, 5), (3, 3, 4), (4, 2, 3), (5, 1, 2), (0, 6, 7)], 8: [(8, None, 0), (6, 1, 2), (1, 5, 6)], 9: [(2, 5, 6), (4, 3, 4), (3, 4, 5), (5, 2, 3), (8, 0, 1), (1, 6, 7)], 10: [(0, 7, None), (2, 6, 7), (7, 1, 2)], 11: [(3, 5, 6), (4, 4, 5), (5, 3, 4), (6, 2, 3), (8, 1, 2), (1, 7, None)], 12: [(9, None, 0)]}
ATTN_END=[(3, 6), (2, 7), (4, 5), (9, 0), (7, 2), (6, 3), (5, 4), (8, 2)]
TAIL_ORDER=[("sums", None, 0), (9, None, 1), (7, None, 3), (8, None, 3), (6, None, 4), (5, None, 5), (4, None, 6), (3, None, 7), ("rows", None, 1), ("rows", None, 2), ("sums", 0, 1), (7, 3, 4), (8, 3, 4), (3, 7, None), ("sums", 1, 2), (6, 4, 5), (9, 1, 2), ("rows", None, 3), (4, 6, 7), (5, 5, 6), ("sums", 2, 3), (9, 2, 3), ("rows", None, 4), ("sums", 3, 4), (7, 4, 5), (8, 4, 5), (4, 7, None), ("sums", 4, None), (6, 5, 6), (5, 6, 7), (9, 3, 4), ("rows", None, 5), (5, 7, None), (7, 5, 6), (6, 6, 7), (8, 5, 6), (9, 4, 5), ("rows", None, 6), (7, 6, 7), (6, 7, None), (8, 6, 7), (9, 5, 6), ("rows", None, 7), (7, 7, None), (9, 6, 7), (8, 7, None), (9, 7, None)]

def after(state,table,end):
    state=dict(state)
    for ops in table.values():
        for chunk,take,start in ops:
            if take is not None: state[chunk]=take
    state.update(end)
    return state
FFN_STATE=after({},FFN_TABLE,FFN_END)
ATTN_STATE=after(FFN_STATE,ATTN_TABLE,ATTN_END)
def in_state(state,ids,low,high): return [i for i in ids if low<=state[i]<=high]
def started(chunk,table):
    return [start for ops in table.values() for i,take,start in ops if i==chunk and start is not None]

def run_table(table,chunks,position,pid,steps,per_step):
    for i in range(steps):
        ops=table.get(per_step*i+position+1,[])
        if ops:
            @pl.when(pid==i)
            def _(): do_ops(ops,chunks)

def do_ops(ops,chunks):
    for i,take,start in ops:
        if take is not None: chunks[i].take(take)
        if start is not None: chunks[i].start(start)

PHASE=2*STEPS

def ffn_kernel(x1,vec,*refs):
    wup,bup,wdn,rest=refs[:4],refs[4:8],refs[8:12],refs[12:]
    gain,bdn=vec.at[0:1],vec.at[1:2]
    gy0,gout,zeros,dbup_o,dbdn_o,dgain_o,gx1_o,block_o,pair_o,total_o,final_o=rest[:11]
    h_s,hT_s,acc,gy_s,out_s,act_s,gu_s,grad_s,pair_s,far_s,total_s,send,recv,g_send,g_recv,b_send,b_recv,local=rest[11:]
    g=pl.program_id(0)
    R=h_s.shape[0]; ch=R//3; piece=R//18
    chunks=[Reduce(TILE,send.at[i],recv.at[i],grad=grad_s.at[i%2],pair=pair_s.at[i],far=far_s.at[i],total=total_s.at[i]) for i in range(STEPS)]
    arrive=ToUnit(lambda q,h:gout.at[q,1,h],lambda t:gy_s.at[9+t],g_send,g_recv,local.at[0])
    leave=[FromUnit(lambda t,i=i:out_s.at[9*i+t],lambda q,h,i=i:block_o.at[q,i,h],b_send.at[i],b_recv.at[i],local.at[1+i]) for i in range(2)]
    first=pltpu.make_async_copy(gy0,gy_s.at[pl.ds(0,9)],local.at[3])
    rows=lambda ref,i: ref[6*i:6*i+6].reshape(ch,D)
    wu=lambda: cols(wup)
    wd=lambda: rowcat(wdn)
    bias=cols(bup).astype(F32)
    @pl.when(g==0)
    def _():
        meet(True,(1,2))
        arrive.begin()
        first.start()
        pad_unit(zeros,gy_s.at[pl.ds(9,9)],local.at[4])
        n,_=norm_rows(x1[...])
        h=(n*gain[...].astype(F32)).astype(BF)
        h_s[...]=h
        hT_s[...]=h.T
        acc[...]=x1[...]+bdn[...].astype(F32)
    for copy in range(2):
        @pl.when((g>=copy*STEPS)&(g<(copy+1)*STEPS))
        def _():
            for i in range(2):
                r=slice((2*copy+i)*R//4,(2*copy+i+1)*R//4)
                u=dot_nn(h_s[r],wu())+bias
                act=(0.5*u*(1.0+jnp.tanh(GC*(u+0.044715*u*u*u)))).astype(BF)
                acc[r]+=dot_nn(act,wd())
        @pl.when(g==(copy+1)*STEPS-1)
        def _():
            out_s[9*copy:9*copy+9]=acc[copy*R//2:(copy+1)*R//2].astype(BF).reshape(9,piece,D)
            leave[copy].begin()
    @pl.when(g==PHASE-1)
    def _():
        arrive.finish()
        first.wait()
        acc[...]=jnp.zeros_like(acc)
        dbdn_o[...]=jnp.sum(gy_s[...].astype(F32).reshape(R,D),axis=0,keepdims=True)
    @pl.when(g>=PHASE)
    def _():
        j=g-PHASE
        for i in range(2,STEPS):
            @pl.when(j==i)
            def _(): chunks[i-2].sent(0)
        slot=lax.rem(j,2)
        for i in range(3):
            r=slice(i*ch,(i+1)*ch)
            u=dot_nn(h_s[r],wu())+bias
            ga=dot_nt(rows(gy_s,i),wd())
            u2=u*u
            t=jnp.tanh(GC*(u+0.044715*u*u2))
            a=0.5*(1.0+t)
            gu=((a+0.5*u*(1.0-t*t)*(GC*(1.0+3*0.044715*u2)))*ga).astype(BF)
            act_s[r]=(u*a).astype(BF)
            gu_s[r]=gu
            acc[r]+=dot_nt(gu,wu())
        run_table(FFN_TABLE,chunks,0,j,STEPS,2)
        def put(s,row,value):
            for k in range(0,value.shape[0],64):
                grad_s[slot,s%2,s//2,(row+k)//TILE,(row+k)%TILE:(row+k)%TILE+64]=value[k:k+64]
        r=dot_tn(act_s[...],gy_s[...].reshape(R,D)).astype(BF)
        for s in range(4):
            for t in range(6): put(s,768+t*128,r[s*128:(s+1)*128,t*128:(t+1)*128])
        r=dot_nn(hT_s[...],gu_s[...]).astype(BF)
        for s in range(4):
            for t in range(4): put(s,t*192,r[s*192:(s+1)*192,t*128:(t+1)*128])
        dbup_o[...]=jnp.sum(gu_s[...].astype(F32),axis=0,keepdims=True)
        run_table(FFN_TABLE,chunks,1,j,STEPS,2)
    @pl.when(g==pl.num_programs(0)-1)
    def _():
        n,scale=norm_rows(x1[...])
        g2=acc[...]
        dgain_o[...]=jnp.sum(g2*n,axis=0,keepdims=True)
        e=g2*gain[...].astype(F32)
        acc[...]=gy_s[...].astype(F32).reshape(R,D)+scale*(e-jnp.mean(e,axis=-1,keepdims=True)-n*jnp.mean(e*n,axis=-1,keepdims=True))
        outs=[pltpu.make_async_copy(acc,gx1_o,local.at[5])]
        outs[0].start()
        for i,stage in FFN_END: chunks[i].take(stage)
        for low,high,source,target in ((0,0,pair_s,pair_o),(1,3,total_s,total_o)):
            for place,i in enumerate(in_state(FFN_STATE,range(STEPS),low,high)):
                outs.append(pltpu.make_async_copy(source.at[i],target.at[place],local.at[5+len(outs)]))
                outs[-1].start()
        for i in range(STEPS):
            stages=started(i,FFN_TABLE)
            chunks[i].sent(*[x for x in stages if x>0 or i>=STEPS-2])
        for r in leave: r.finish()
        for d in outs: d.wait()

def ffn(x1,vec,wup,bup,wdn,gy0,gout):
    R=x1.shape[0]; half=R//2; piece=half//9
    zeros=np.zeros((2,piece,D),BF)
    count=lambda low,high: max(1,len(in_state(FFN_STATE,range(STEPS),low,high)))
    tile=lambda j: lax.rem(j,STEPS)
    ups=[pl.BlockSpec((D,128),(lambda s:(lambda j:(0,s*STEPS+tile(j))))(s)) for s in range(4)]
    downs=[pl.BlockSpec((128,D),(lambda s:(lambda j:(s*STEPS+tile(j),0)))(s)) for s in range(4)]
    biases=[pl.BlockSpec((1,128),(lambda s:(lambda j:(0,s*STEPS+tile(j))))(s)) for s in range(4)]
    return pl.pallas_call(ffn_kernel,grid=(PHASE+STEPS,),
        in_specs=[once((R,D)),once((4,D))]+ups+biases+downs+[ANYSPACE]*2+[once(zeros.shape)],
        out_specs=[pl.BlockSpec((1,512),lambda j:(0,jnp.maximum(j-PHASE,0))),whole((1,D)),whole((1,D))]+[ANYSPACE]*5,
        out_shape=[jax.ShapeDtypeStruct((1,FF),F32),jax.ShapeDtypeStruct((1,D),F32),jax.ShapeDtypeStruct((1,D),F32),jax.ShapeDtypeStruct((R,D),F32),jax.ShapeDtypeStruct((4,2,2,piece,D),BF),
            jax.ShapeDtypeStruct((count(0,0),2,2,TILE,128),BF),jax.ShapeDtypeStruct((count(1,3),2,TILE,128),BF),jax.ShapeDtypeStruct((1,2,TILE,128),BF)],
        scratch_shapes=[pltpu.VMEM((R,D),BF),pltpu.VMEM((D,R),BF),pltpu.VMEM((R,D),F32),pltpu.VMEM((18,piece,D),BF),pltpu.VMEM((18,piece,D),BF),pltpu.VMEM((R,512),BF),pltpu.VMEM((R,512),BF),
            pltpu.VMEM((2,2,2,2,TILE,128),BF),pltpu.VMEM((STEPS,2,2,TILE,128),BF),pltpu.VMEM((STEPS,2,TILE,128),BF),pltpu.VMEM((STEPS,2,TILE,128),BF),
            DMA((STEPS,8)),DMA((STEPS,8)),DMA((8,)),DMA((9,)),DMA((2,8)),DMA((2,8)),DMA((STEPS+7,))],
        compiler_params=pltpu.CompilerParams(vmem_limit_bytes=VMEM_LIMIT,dimension_semantics=("arbitrary",),collective_id=2,has_side_effects=True),
        cost_estimate=pl.CostEstimate(flops=14*R*D*FF,bytes_accessed=40<<20,transcendentals=2*R*FF),
        name="ffn")(x1,vec,*[wup]*4,*[bup]*4,*[wdn]*4,gy0,gout,zeros)

def bwd_attn_kernel(half,xc,noise,segc,segr,vec,gx1,q,k,v,mix,lse,wq,wk,wv,wout,trig,mixed,tile_pair,tile_total,tile_final,
                    gin_o,demb_o,dgain_o,tiles_o,wpair_o,wtotal_o,wfinal_o,hT_s,gh,biasT_s,selfT_s,dq_s,dk_s,dv_s,ga,trig_s,
                    t_pair,t_far,t_total,t_over,t_final,w_grad,w_pair,w_far,w_total,w_over,w_final,t_send,t_recv,w_send,w_recv,local):
    p=pl.program_id(0)
    emb,gain=vec.at[2:3],vec.at[3:4]
    rank,_=place_ids()
    R=2*half
    tiles=tiles_of(half)
    pairs=in_state(FFN_STATE,range(STEPS),0,0)
    fars=in_state(FFN_STATE,range(STEPS),0,0)
    slot=lambda ids,i: ids.index(i) if i in ids else 0
    chunks=[Reduce(TILE,t_send.at[i],t_recv.at[i],pair=t_pair.at[slot(pairs,i)],far=t_far.at[slot(fars,i)],total=t_total.at[i],over=t_over.at[i],final=t_final.at[i]) for i in range(STEPS)]
    chunks+=[Reduce(WING,w_send.at[i],w_recv.at[i],grad=w_grad.at[i],pair=w_pair.at[i],far=w_far.at[i],total=w_total.at[i],over=w_over.at[i],final=w_final.at[i]) for i in range(4)]
    def tick(position):
        run_table(ATTN_TABLE,chunks,position,p,PAIRS,2)
    @pl.when(p==0)
    def _():
        loads=[pltpu.make_async_copy(trig.at[rank%2],trig_s,local.at[2])]
        loads[0].start()
        for low,high,source,target in ((0,0,tile_pair,t_pair),(1,3,tile_total,t_total),(4,7,tile_final,t_final)):
            for place,i in enumerate(in_state(FFN_STATE,range(STEPS),low,high)):
                loads.append(pltpu.make_async_copy(source.at[place],target.at[place if low==0 else i],local.at[2+len(loads)]))
                loads[-1].start()
        ga[...]=gx1[...].astype(BF)
        for d in loads: d.wait()
        meet(True,(1,2))
        do_ops(ATTN_TABLE.get(0,[]),chunks)
        g=gain[...].astype(F32)
        for c,rows in enumerate(layer_rows(xc,noise,emb)):
            n,_=norm_rows(rows)
            hT_s[:,c*half:(c+1)*half]=(n*g).astype(BF).T
        gh[...]=jnp.zeros_like(gh)
        for s,m in tiles:
            n=s+m
            qb=(lax.broadcasted_iota(jnp.int32,(n,m),1)+s)//BLK
            kb=lax.broadcasted_iota(jnp.int32,(n,m),0)//BLK
            same=segc[:n]==segr[:,s:n]
            biasT_s[0,:n,s:n]=jnp.where(same&(kb<qb),0.0,NEG)
            biasT_s[1,:n,s:n]=jnp.where(same&(kb<=qb),0.0,NEG)
            qb=lax.broadcasted_iota(jnp.int32,(m,m),1)//BLK
            kb=lax.broadcasted_iota(jnp.int32,(m,m),0)//BLK
            same=segc[s:n]==segr[:,s:n]
            selfT_s[s:n,:m]=jnp.where(same&(kb==qb),0.0,NEG)
    gm=dot_nt(ga[...],wout[...]).astype(BF)
    @pl.when(p==0)
    def _():
        r=dot_tn(mixed[...],ga[...]).astype(BF)
        for a in range(4):
            for t in range(6): w_grad[0,a%2,a//2,t//3,t%3*192:(t%3+1)*192]=r[a*192:(a+1)*192,t*128:(t+1)*128]
    gd=gm.astype(F32)*mix[...].astype(F32)
    dk_s[...]=jnp.zeros_like(dk_s); dv_s[...]=jnp.zeros_like(dv_s)
    idx=0
    for s,m in tiles:
        n=s+m
        for c in (0,1):
            rs=slice(c*half+s,c*half+n)
            qs=head_stack(q[rs]); gs=head_stack(gm[rs])
            delta=jnp.sum(head_stack(gd[rs]).T,axis=0,keepdims=True)
            row=lse[0,idx:idx+1,:2*m]
            def part(krows,bias):
                kc=k[krows]; vc=v[krows]
                st=dot_nt(kc,qs)+jnp.concatenate([bias,bias],axis=1)
                pt=jnp.exp(st-row)
                dp=dot_nt(vc,gs)
                ds=(pt*(dp-delta)).astype(BF)
                dv_s[krows]+=dot_nn(pt.astype(BF),gs)
                dk_s[krows]+=dot_nn(ds,qs)
                return dot_tn(ds,kc)
            dq=part(slice(half,half+n),biasT_s[c,:n,s:n])
            if c==0: dq=dq+part(slice(s,n),selfT_s[s:n,:m])
            dq_s[rs]=head_merge(dq)*HEAD**-0.5
            idx+=1
        if s==256: tick(0)
    cs=jnp.concatenate([trig_s[:,:PAIR]]*2,axis=0)
    sn=jnp.concatenate([trig_s[:,PAIR:]]*2,axis=0)
    z=jnp.concatenate([(g[...]*cs-swap_halves(g[...])*sn).astype(BF) for g in (dq_s,dk_s)]+[dv_s[...].astype(BF)],axis=1)
    r=dot_nn(hT_s[...],z).astype(BF)
    group=1+p//2
    for a in range(4):
        for t in range(3):
            w_grad[group,a%2,a//2,lax.rem(p,2),t*192:(t+1)*192]=r[a*192:(a+1)*192,t*128:(t+1)*128]
    gh[...]+=dot_nt(z,cols((wq,wk,wv)))
    tick(1)
    @pl.when(p==pl.num_programs(0)-1)
    def _():
        g=gain[...].astype(F32)
        outs=[]; dg=0.0
        for c,rows in enumerate(layer_rows(xc,noise,emb)):
            n,scale=norm_rows(rows)
            g1=gh[c*half:(c+1)*half]
            dg=dg+jnp.sum(g1*n,axis=0,keepdims=True)
            e=g1*g
            outs.append(gx1[c*half:(c+1)*half]+scale*(e-jnp.mean(e,axis=-1,keepdims=True)-n*jnp.mean(e*n,axis=-1,keepdims=True)))
        masked=noise[...]==1
        gin_o[...]=(outs[1]+jnp.where(masked,0.0,outs[0])).astype(gin_o.dtype)
        demb_o[...]=jnp.sum(jnp.where(masked,outs[0],0.0),axis=0,keepdims=True)
        dgain_o[...]=dg
        for i,stage in ATTN_END: chunks[i].take(stage)
        stores=[]
        for i in in_state(ATTN_STATE,range(STEPS),4,7): stores.append((t_final.at[i],tiles_o.at[i]))
        for low,high,source,target in ((0,0,w_pair,wpair_o),(1,3,w_total,wtotal_o),(4,7,w_final,wfinal_o)):
            for place,i in enumerate(in_state(ATTN_STATE,range(STEPS,STEPS+4),low,high)): stores.append((source.at[i-STEPS],target.at[place]))
        stores=[pltpu.make_async_copy(a,b,local.at[2+n]) for n,(a,b) in enumerate(stores)]
        for d in stores: d.start()
        for i,chunk in enumerate(chunks): chunk.sent(*started(i,ATTN_TABLE))
        for d in stores: d.wait()

def bwd_attn(xc,noise,segc,segr,vec,gx1,q,k,v,mix,lse,wqkv,wout,trig,tile_pair,tile_total,tile_final):
    half=xc.shape[0]; R=2*half; piece=half//9
    ntp=lse.shape[1]
    ws=[pl.BlockSpec((D,PAIR),(lambda off:(lambda p:(0,off+p)))(o*PAIRS)) for o in range(3)]
    rows=pl.BlockSpec((R,PAIR),lambda p:(0,p))
    pairs=max(1,len(in_state(FFN_STATE,range(STEPS),0,0)))
    count=lambda low,high: max(1,len(in_state(ATTN_STATE,range(STEPS,STEPS+4),low,high)))
    return pl.pallas_call(partial(bwd_attn_kernel,half),grid=(PAIRS,),
        in_specs=[once((half,D)),once((half,1)),once((half,1)),once((1,640)),once((4,D)),once((R,D)),rows,rows,rows,rows,
                  pl.BlockSpec((1,ntp,256),lambda p:(p,0,0)),*ws,pl.BlockSpec((PAIR,D),lambda p:(p,0)),ANYSPACE,once((R,D))]+[ANYSPACE]*3,
        out_specs=[whole((half,D)),whole((1,D)),whole((1,D))]+[ANYSPACE]*4,
        out_shape=[jax.ShapeDtypeStruct((half,D),BF),jax.ShapeDtypeStruct((1,D),F32),jax.ShapeDtypeStruct((1,D),F32),jax.ShapeDtypeStruct((STEPS,2,TILE,128),BF),jax.ShapeDtypeStruct((count(0,0),2,2,WING,128),BF),jax.ShapeDtypeStruct((count(1,3),2,WING,128),BF),jax.ShapeDtypeStruct((count(4,7),2,WING,128),BF)],
        scratch_shapes=[pltpu.VMEM((D,R),BF),pltpu.VMEM((R,D),F32),pltpu.VMEM((2,half,-(-half//128)*128),F32),pltpu.VMEM((half,128),F32)]+[pltpu.VMEM((R,PAIR),F32)]*3+[pltpu.VMEM((R,D),BF),pltpu.VMEM((half,2*PAIR),F32)]
            +[pltpu.VMEM((pairs,2,2,TILE,128),BF),pltpu.VMEM((pairs,2,TILE,128),BF),pltpu.VMEM((STEPS,2,TILE,128),BF),pltpu.VMEM((STEPS,2*TILE,128),BF),pltpu.VMEM((STEPS,2,TILE,128),BF),
              pltpu.VMEM((4,2,2,2,WING,128),BF),pltpu.VMEM((4,2,2,WING,128),BF),pltpu.VMEM((4,2,WING,128),BF),pltpu.VMEM((4,2,WING,128),BF),pltpu.VMEM((4,2*WING,128),BF),pltpu.VMEM((4,2,WING,128),BF),
              DMA((STEPS,8)),DMA((STEPS,8)),DMA((4,8)),DMA((4,8)),DMA((16,))],
        compiler_params=pltpu.CompilerParams(vmem_limit_bytes=VMEM_LIMIT,dimension_semantics=("arbitrary",),collective_id=3,has_side_effects=True),
        cost_estimate=pl.CostEstimate(flops=4*R*D*(3*D+D)+60*R*half*D//2*2,bytes_accessed=30<<20,transcendentals=R*half*HEADS),
        name="bwd_attn")(xc,noise,segc,segr,vec,gx1,q,k,v,mix,lse,wqkv,wqkv,wqkv,wout,trig,mix,tile_pair,tile_total,tile_final)

def assemble(ffn,wings,gin,block):
    piece=gin.shape[2]
    up,down,out,qkv,grad,rows=pl.pallas_call(assemble_kernel,grid=(STEPS,),
        in_specs=[pl.BlockSpec((1,2,TILE,128),lambda i:(i,0,0,0)),whole(wings.shape),
            pl.BlockSpec((2,piece,D),lambda i:(jnp.minimum(i,3),0,0)),pl.BlockSpec((4,piece,D),lambda i:(jnp.minimum(i,3),0,0))],
        out_specs=[whole((192,FF)),pl.BlockSpec((128,D),lambda i:(i,0)),whole((192,D)),whole((192,3*D)),
            pl.BlockSpec((2,piece,D),lambda i:(jnp.minimum(i,3),0,0)),pl.BlockSpec((4,piece,D),lambda i:(jnp.minimum(i,3),0,0))],
        out_shape=[jax.ShapeDtypeStruct((192,FF),F32),jax.ShapeDtypeStruct((768,D),F32),jax.ShapeDtypeStruct((192,D),F32),jax.ShapeDtypeStruct((192,3*D),F32),
            jax.ShapeDtypeStruct((8,piece,D),F32),jax.ShapeDtypeStruct((16,piece,D),BF)],
        compiler_params=pltpu.CompilerParams(vmem_limit_bytes=VMEM_LIMIT,dimension_semantics=("arbitrary",)),
        name="assemble")(ffn,wings,gin.reshape(8,piece,D),block.reshape(16,piece,D))
    return up,down,out,qkv,grad,rows


DMA = pltpu.SemaphoreType.DMA
MESH = pl.DeviceIdType.MESH
INVMEM = pl.BlockSpec(memory_space=pltpu.VMEM)
ANYSPACE = pl.BlockSpec(memory_space=pl.ANY)


def place_ids():
    return lax.axis_index("ctx"), lax.axis_index("fsdp")


def meet(all_ranks, fsdp_partners):
    c, f = place_ids()
    sem = pltpu.get_barrier_semaphore()
    count = 0
    ranks = [(c + s) % 8 for s in range(1, 8)] if all_ranks else [c + 1 - 2 * (c % 2)]
    for rank in ranks:
        pl.semaphore_signal(sem, inc=1, device_id={"ctx": rank}, device_id_type=MESH)
        count += 1
    for s in fsdp_partners:
        other = (f + 2) % 4 if s == 2 else f + 1 - 2 * (f % 2) if s == 1 else 3 - f
        pl.semaphore_signal(sem, inc=1, device_id={"fsdp": other}, device_id_type=MESH)
        count += 1
    pl.semaphore_wait(sem, count)


def remote(src, dst, send, recv, where):
    return pltpu.make_async_remote_copy(src_ref=src, dst_ref=dst, send_sem=send, recv_sem=recv, device_id=where,
                                        device_id_type=MESH)


class ToUnit:
    def __init__(self, source, target, send, recv, local):
        self.source, self.target, self.send, self.recv, self.local = source, target, send, recv, local
        self.c, _ = place_ids()

    def message(self, s):
        c = self.c
        t = (c + s) % 8
        odd, last = t % 2, c // 7
        slot = (1 - odd) * c + odd * ((1 - last) * (6 - c) + last * 8)
        return remote(self.source(t // 2, odd), self.target(slot), self.send.at[s], self.recv.at[slot],
                      {"ctx": t - odd * last})

    def begin(self):
        for s in (1, 7, 3, 5, 2, 6, 4):
            self.message(s).start()

        @pl.when(self.c == 7)
        def _():
            self.message(0).start()

        @pl.when(self.c != 7)
        def _():
            self.own_safe().start()

    def begin_straight(self):
        for s in (2, 4, 6):
            self.message(s).start()

        @pl.when(self.c != 7)
        def _():
            self.own_safe().start()

    def begin_across(self):
        for s in (1, 3, 5, 7):
            self.message(s).start()

        @pl.when(self.c == 7)
        def _():
            self.message(0).start()

    def own_safe(self):
        c = self.c
        part = c % 2
        slot = (1 - part) * c + part * (6 - c + c // 7)
        return pltpu.make_async_copy(self.source(c // 2, part), self.target(slot), self.local)

    def finish(self):
        c = self.c
        part = c % 2

        @pl.when(c == 7)
        def _():
            self.message(0).wait_send()

        @pl.when(c != 7)
        def _():
            self.own_safe().wait()

        for s in range(1, 8):
            self.message(s).wait_send()
        own = (1 - part) * c + part * (6 - c)
        for slot in range(9):
            take = slot != own
            if slot > 6:
                take = take & (part == 0)

            @pl.when(take)
            def _():
                remote(self.target(slot), self.target(slot), self.send.at[0], self.recv.at[slot], {"ctx": c}).wait_recv()


def pad_unit(zeros, target, sem):
    c, _ = place_ids()
    copy = pltpu.make_async_copy(zeros, target.at[pl.ds(7, 2)], sem)

    @pl.when(c % 2 == 1)
    def _():
        copy.start()
        copy.wait()


class FromUnit:
    def __init__(self, source, target, send, recv, local):
        self.source, self.target, self.send, self.recv, self.local = source, target, send, recv, local
        self.c, _ = place_ids()

    def message(self, s):
        c = self.c
        part = c % 2
        rank = (c + s) % 8
        slot = (1 - part) * rank + part * (6 - rank + rank // 7)
        return remote(self.source(slot), self.target(c // 2, part), self.send.at[s], self.recv.at[c], {"ctx": rank})

    def extra(self):
        c = self.c
        seq = c // 2
        return remote(self.source(8), self.target(seq, 1), self.send.at[0], self.recv.at[2 * seq + 1], {"ctx": 7})

    def own(self):
        c = self.c
        part = c % 2
        slot = (1 - part) * c + part * (6 - c + c // 7)
        return pltpu.make_async_copy(self.source(slot), self.target(c // 2, part), self.local)

    def each(self, remote_op, own_op):
        c = self.c
        part = c % 2
        @pl.when(part == 0)
        def _():
            remote_op(self.extra())

        for s in (1, 7, 3, 5, 2, 6, 4):
            rank = (c + s) % 8

            @pl.when((part == 0) | (rank != 7))
            def _():
                remote_op(self.message(s))

        @pl.when(c != 7)
        def _():
            own_op(self.own())

    def begin_one(self, s):
        c = self.c

        @pl.when((c % 2 == 0) | ((c + s) % 8 != 7))
        def _():
            self.message(s).start()

    def begin_rest(self):
        c = self.c

        @pl.when(c % 2 == 0)
        def _():
            self.extra().start()

        @pl.when(c != 7)
        def _():
            self.own().start()

    def begin(self):
        self.each(lambda m: m.start(), lambda m: m.start())

    def finish(self):
        self.each(lambda m: m.wait_send(), lambda m: m.wait())
        c = self.c
        for block in range(8):
            @pl.when((c == 7) | (c != block))
            def _():
                ref = self.target(block // 2, block % 2)
                remote(ref, ref, self.send.at[0], self.recv.at[block], {"ctx": c}).wait_recv()


class GatherRows:
    def __init__(self, shard, full, send, recv, local, parts=1, share=True):
        c, f = place_ids()
        n = shard.shape[0]
        n2 = n // 2 if share else n
        m = n2 // parts
        h = c % 2 if share else 0
        sib, far, xn = f + 1 - 2 * (f % 2), (f + 2) % 4, c + 1 - 2 * (c % 2)
        diag = (sib + 2) % 4
        rows = lambda start, size: full.at[pl.ds(pl.multiple_of(start, 16), size)]
        same = lambda ref, i, where: remote(ref, ref, send.at[i], recv.at[i], where)
        mine = rows(f * n, n)
        self.copy = pltpu.make_async_copy(shard, mine, local)
        self.to_core = remote(shard, mine, send.at[0], recv.at[0], {"fsdp": sib})
        self.from_core = same(rows(sib * n, n), 0, {"fsdp": sib})
        self.to_far, self.from_far, self.to_x, self.from_x = [], [], [], []
        self.near_core, self.away_core, self.from_near, self.from_away = [], [], [], []
        for i in range(parts):
            a, b = h * n2 + i * m, (1 - h) * n2 + i * m
            near, away = rows(far * n + a, m), rows(far * n + b, m)
            k = 1 + 4 * i
            self.to_far.append(remote(shard.at[pl.ds(pl.multiple_of(a, 16), m)], rows(f * n + a, m), send.at[k], recv.at[k],
                                      {"fsdp": far}))
            self.from_far.append(same(near, k, {"fsdp": far}))
            self.near_core.append(same(near, k + 2, {"fsdp": sib}))
            self.from_near.append(same(rows(diag * n + a, m), k + 2, {"fsdp": sib}))
            if share:
                self.to_x.append(same(near, k + 1, {"ctx": xn}))
                self.from_x.append(same(away, k + 1, {"ctx": xn}))
                self.away_core.append(same(away, k + 3, {"fsdp": sib}))
                self.from_away.append(same(rows(diag * n + b, m), k + 3, {"fsdp": sib}))

    def begin(self):
        for copy in self.to_far:
            copy.start()
        self.to_core.start()
        self.copy.start()

    def relay_far(self, i=0):
        self.from_far[i].wait_recv()
        if self.to_x:
            self.to_x[i].start()
        self.near_core[i].start()

    def relay_x(self, i=0):
        self.from_x[i].wait_recv()
        self.away_core[i].start()

    def finish(self):
        self.copy.wait()
        for copy in [self.to_core] + self.to_far + self.to_x + self.near_core + self.away_core:
            copy.wait_send()
        for copy in [self.from_core] + self.from_near + self.from_away:
            copy.wait_recv()


class Reduce:
    def __init__(self, rows, send, recv, across=False, grad=None, pair=None, far=None, total=None, over=None, final=None):
        c, f = place_ids()
        self.send, self.recv, self.across = send, recv, across
        self.grad, self.pair, self.far, self.total, self.over, self.final = grad, pair, far, total, over, final
        self.core, self.y, self.x = f % 2, f // 2, c % 2
        z1, z2 = (c // 2) % 2, c // 4
        self.sib, self.far_id = {"fsdp": f + 1 - 2 * self.core}, {"fsdp": (f + 2) % 4}
        self.xn, self.z1n, self.z2n = {"ctx": c + 1 - 2 * self.x}, {"ctx": c + 2 - 4 * z1}, {"ctx": c + 4 - 8 * z2}
        half, quarter = rows // 2, rows // 4
        self.rows = rows
        self.levels = [(z1 * half, (1 - z1) * half, half, rows, self.z1n)]
        base = z1 * half
        self.levels.append((base + z2 * quarter, base + (1 - z2) * quarter, quarter, rows + half, self.z2n))

    def at(self, ref, start, size):
        return ref.at[self.x, pl.ds(pl.multiple_of(start, 16), size)]

    def copy(self, stage):
        x, y = self.x, self.y
        if stage == 0:
            source, target, where = self.grad.at[1 - self.core], self.pair, self.sib
        elif stage == 1 and self.across:
            source, target, where = self.pair.at[:, 1 - x], self.far, self.xn
        elif stage == 1:
            source, target, where = self.pair.at[1 - y], self.far, self.far_id
        elif stage == 2 and self.across:
            source, target, where = self.pair.at[1 - y, x], self.over.at[pl.ds(0, self.rows)], self.far_id
        elif stage == 2:
            source, target, where = self.total.at[1 - x], self.over.at[pl.ds(0, self.rows)], self.xn
        elif stage < 5:
            keep, give, size, offset, where = self.levels[stage - 3]
            source, target = self.at(self.total, give, size), self.over.at[pl.ds(offset, size)]
        elif stage < 7:
            keep, give, size, offset, where = self.levels[6 - stage]
            source = target = self.at(self.final, keep, size)
        else:
            source, target, where = self.final.at[x], self.final.at[x], self.xn
        return remote(source, target, self.send.at[stage], self.recv.at[stage], where)

    def start(self, stage):
        self.copy(stage).start()

    def take(self, stage):
        x, y = self.x, self.y
        if stage < 5:
            self.copy(stage).wait_recv()
        if stage == 0:
            self.pair[...] = self.pair[...] + self.grad[self.core]
        elif stage == 1 and self.across:
            for i in range(2):
                self.pair[i, x] = self.pair[i, x] + self.far[i]
        elif stage == 1:
            self.total[...] = self.far[...] + self.pair[y]
        elif stage == 2 and self.across:
            self.total[x] = self.pair[y, x] + self.over[pl.ds(0, self.rows)]
        elif stage == 2:
            self.total[x] = self.total[x] + self.over[pl.ds(0, self.rows)]
        elif stage < 5:
            keep, give, size, offset, where = self.levels[stage - 3]
            into = self.at(self.final if stage == 4 else self.total, keep, size)
            into[...] = self.at(self.total, keep, size)[...] + self.over[pl.ds(offset, size)]
        elif stage < 7:
            keep, give, size, offset, where = self.levels[6 - stage]
            ref = self.at(self.final, give, size)
            remote(ref, ref, self.send.at[stage], self.recv.at[stage], where).wait_recv()
        else:
            ref = self.final.at[1 - x]
            remote(ref, ref, self.send.at[7], self.recv.at[7], self.xn).wait_recv()

    def sent(self, *stages):
        for stage in stages:
            self.copy(stage).wait_send()


TILE = 768
WING = 576


def tail_kernel(tiles, wpair, wtotal, wfinal, gin, embed, gain_one, gain_two, down_shift, up_shift, tiles_o, wings_o, gin_o, sums_o,
                t_over, t_total, t_final, w_pair, w_far, w_over, w_total, w_final, sum_s, in_s,
                t_send, t_recv, r_send, r_recv, v_send, v_recv, a_send, a_recv, local):
    rows = FromUnit(lambda i: gin.at[i], lambda q, h: gin_o.at[q, h], a_send, a_recv, local.at[0])
    open_tiles = in_state(ATTN_STATE, range(STEPS), 4, 6)
    chunks = {i: Reduce(TILE, t_send.at[k], t_recv.at[k], total=t_total, over=t_over, final=t_final.at[k])
              for k, i in enumerate(open_tiles)}
    loads = [(tiles.at[i], t_final.at[k]) for k, i in enumerate(open_tiles)]
    wings = range(STEPS, STEPS + 4)
    for w in wings:
        k = w - STEPS
        chunks[w] = Reduce(WING, r_send.at[k], r_recv.at[k], pair=w_pair, far=w_far, total=w_total.at[k], over=w_over.at[k],
                           final=w_final.at[k])
    for low, high, source, target in ((0, 0, wpair, None), (1, 3, wtotal, w_total), (4, 7, wfinal, w_final)):
        for place, w in enumerate(in_state(ATTN_STATE, wings, low, high)):
            loads.append((source.at[place], w_pair if target is None else target.at[w - STEPS]))
    loads = [pltpu.make_async_copy(a, b, local.at[1 + n]) for n, (a, b) in enumerate(loads)]
    for copy in loads:
        copy.start()
    row = 0
    for part in (embed, gain_one, gain_two, down_shift):
        for i in range(D // 128):
            sum_s[0, row:row + 1] = part[:, i * 128:(i + 1) * 128]
            row += 1
    for s in range(4):
        for j in range(STEPS):
            sum_s[0, row:row + 1] = up_shift[:, j * 512 + s * 128:j * 512 + (s + 1) * 128]
            row += 1
    some = chunks[STEPS]
    vectors = [remote(sum_s.at[i], in_s.at[i], v_send.at[i], v_recv.at[i], where)
               for i, where in enumerate((some.sib, some.far_id, some.xn, some.z1n, some.z2n))]
    for copy in loads:
        copy.wait()
    meet(True, (1, 2))
    for chunk, take, start in TAIL_ORDER:
        if chunk == "rows":
            if start == 1:
                rows.begin_rest()
            rows.begin_one(start)
        elif chunk == "sums":
            if take is not None:
                vectors[take].wait_recv()
                sum_s[take + 1] = sum_s[take] + in_s[take]
            if start is not None:
                vectors[start].start()
        else:
            if take is not None:
                chunks[chunk].take(take)
            if start is not None:
                chunks[chunk].start(start)
    stores = [(t_final.at[k], tiles_o.at[i]) for k, i in enumerate(open_tiles)] + [(w_final, wings_o)]
    stores = [pltpu.make_async_copy(a, b, local.at[1 + n]) for n, (a, b) in enumerate(stores)]
    for copy in stores:
        copy.start()
    sums_o[...] = sum_s[5]
    for i in range(5):
        vectors[i].wait_send()
    for i, chunk in chunks.items():
        chunk.sent(*range(ATTN_STATE[i] + 1, 8))
    rows.finish()
    for copy in stores:
        copy.wait()


def tail(tiles, wpair, wtotal, wfinal, gin, vectors):
    piece = gin.shape[1]
    n = max(1, len(in_state(ATTN_STATE, range(STEPS), 4, 6)))
    return pl.pallas_call(
        tail_kernel,
        in_specs=[ANYSPACE] * 5 + [INVMEM] * 5,
        out_specs=[ANYSPACE] * 3 + [INVMEM],
        out_shape=[jax.ShapeDtypeStruct(tiles.shape, BF), jax.ShapeDtypeStruct((4, 2, WING, 128), BF),
                   jax.ShapeDtypeStruct((4, 2, piece, D), BF), jax.ShapeDtypeStruct((48, 128), F32)],
        scratch_shapes=[pltpu.VMEM((16, 128), BF), pltpu.VMEM((2, 16, 128), BF), pltpu.VMEM((n, 2, TILE, 128), BF),
                        pltpu.VMEM((2, 2, WING, 128), BF), pltpu.VMEM((2, WING, 128), BF), pltpu.VMEM((4, 2 * WING, 128), BF),
                        pltpu.VMEM((4, 2, WING, 128), BF), pltpu.VMEM((4, 2, WING, 128), BF), pltpu.VMEM((6, 48, 128), F32),
                        pltpu.VMEM((5, 48, 128), F32),
                        DMA((n, 8)), DMA((n, 8)), DMA((4, 8)), DMA((4, 8)), DMA((5,)), DMA((5,)), DMA((8,)), DMA((8,)), DMA((n + 6,))],
        input_output_aliases={0: 0},
        compiler_params=pltpu.CompilerParams(collective_id=4, has_side_effects=True, vmem_limit_bytes=VMEM_LIMIT),
        name="tail")(tiles, wpair, wtotal, wfinal, gin, *vectors)


def assemble_kernel(ffn, wings, gin, block, up_o, down_o, out_o, qkv_o, gin_o, block_o):
    i = pl.program_id(0)
    tile = lambda r: ffn[0, r // TILE, r % TILE:r % TILE + 64].astype(F32)
    for s in range(4):
        for r in range(0, 192, 64):
            up_o[r:r + 64, pl.ds(pl.multiple_of((s * STEPS + i) * 128, 128), 128)] = tile(s * 192 + r)
    for t in range(6):
        for r in range(0, 128, 64):
            down_o[r:r + 64, t * 128:(t + 1) * 128] = tile(768 + t * 128 + r)
    gin_o[...] = gin[...].astype(F32)
    block_o[...] = block[...]

    @pl.when(i == 0)
    def _():
        def strip(ref, k, r):
            row = k * 192 + r
            return ref[row // WING, row % WING:row % WING + 64].astype(F32)

        for r in range(0, 192, 64):
            for t in range(6):
                out_o[r:r + 64, t * 128:(t + 1) * 128] = strip(wings.at[0], t, r)
                source = wings.at[1 + t // 2]
                for w in range(3):
                    qkv_o[r:r + 64, w * D + t * 128:w * D + (t + 1) * 128] = strip(source, t % 2 * 3 + w, r)


def rope_constant(half):
    position = np.arange(2 * half, dtype=np.float32)
    frequency = np.float32(10000.0) ** (-(np.arange(HEAD // 2, dtype=np.float32) * np.float32(2.0)) / np.float32(HEAD))
    angles = (position[:, None] * frequency[None, :]).astype(np.float64)
    cosine, sine = np.cos(angles), np.sin(angles)
    table = np.concatenate([np.tile(cosine, (1, 4)), np.tile(np.concatenate([-sine, sine], axis=1), (1, 2))], axis=1)
    return jnp.asarray(table.reshape(2, half, 4 * HEAD).astype(np.float32))


def even_body(clean_in, segments, noise, mask_embed, norm1_gain, qkv_weight, out_weight, norm2_gain, up_weight, up_bias,
              down_weight, down_bias, out_grad):
    place = lax.axis_index("fsdp")
    piece = clean_in.shape[2]
    half = 9 * piece
    width = mask_embed.shape[0]
    meta = jnp.concatenate([segments.reshape(8, 1, piece), noise.reshape(8, 1, piece)], axis=2)
    meta = jnp.broadcast_to(meta, (8, 8, 2 * piece))
    row = lax.broadcasted_iota(jnp.int32, (16, 256), 0)
    small = jnp.zeros((16, 256), BF)
    for i, vector in enumerate((mask_embed, norm1_gain, norm2_gain, down_bias)):
        small = jnp.where(row == i, jnp.pad(vector, (0, 256 - width))[None], small)
    for i in range(up_bias.shape[0] // 256):
        small = jnp.where(row == 4 + i, up_bias[i * 256:(i + 1) * 256][None], small)
    q, k, v, mixed, lse, resid, mask, seg_col, seg_row, vectors, up_shift, qkv_full, out_full, up_full, down_full, cotangent, clean = fwd_attn(
        clean_in, meta, out_grad, rope_constant(half), qkv_weight, out_weight, up_weight, down_weight, small)
    clean = clean.reshape(half, D)
    up_shift_grad, down_shift_grad, gain_two_grad, grad_resid, block_out, tile_pair, tile_total, tile_final = ffn(
        resid, vectors, up_full, up_shift, down_full, cotangent, out_grad)
    grad_in, embed_grad, gain_one_grad, tiles, wpair, wtotal, wfinal = bwd_attn(
        clean, mask, seg_col, seg_row, vectors, grad_resid, q, k, v, mixed, lse, qkv_full, out_full, rope_constant(half),
        tile_pair, tile_total, tile_final)
    tiles, wings, input_grad, sums = tail(tiles, wpair, wtotal, wfinal, grad_in.reshape(9, piece, D),
                                          (embed_grad, gain_one_grad, gain_two_grad, down_shift_grad, up_shift_grad))
    up_sum, down_sum, out_sum, qkv_sum, input_grad, block_out = assemble(tiles, wings, input_grad, block_out)
    input_grad = input_grad.reshape(clean_in.shape)
    block_out = block_out.reshape(out_grad.shape)
    sums = sums.reshape(-1)
    own = [lax.dynamic_slice_in_dim(sums, i * D + place * width, width) for i in range(4)]
    own_up = lax.dynamic_slice_in_dim(sums, 4 * D + place * (FF // 4), FF // 4)
    return (block_out, input_grad, own[0], own[1], qkv_sum, out_sum, own[2], up_sum, own_up, down_sum, own[3])


def choose_body(axes, *arrays):
    even = axes["ctx"] == 8 and axes["fsdp"] == 4 and arrays[0].shape[0] == 4
    return (even_body if even else general_body)(*arrays)


def solution(mesh):
    placed = (
        P("fsdp", None, "ctx", None),
        P("fsdp", None, "ctx"),
        P("fsdp", None, "ctx"),
        P("fsdp"),
        P("fsdp"),
        P("fsdp", None),
        P("fsdp", None),
        P("fsdp"),
        P("fsdp", None),
        P("fsdp"),
        P("fsdp", None),
        P("fsdp"),
        P("fsdp", None, None, "ctx", None),
    )
    return jax.shard_map(
        partial(choose_body, dict(mesh.shape)),
        mesh=mesh,
        in_specs=placed,
        out_specs=(
            P("fsdp", None, None, "ctx", None),
            P("fsdp", None, "ctx", None),
            P("fsdp"),
            P("fsdp"),
            P("fsdp", None),
            P("fsdp", None),
            P("fsdp"),
            P("fsdp", None),
            P("fsdp"),
            P("fsdp", None),
            P("fsdp"),
        ),
        check_vma=False,
    )
```

```python
from functools import partial

import jax
import jax.numpy as jnp
import numpy as np
from jax import lax
from jax.experimental import pallas as pl
from jax.experimental.pallas import tpu as pltpu
from jax.sharding import PartitionSpec as P

D = 768
HEADS = 12
HEAD = 64
FF = 3072
BLK = 16


EPS = 1e-05
together = 4


def normalize(values):
    centre = values - jnp.mean(values, axis=-1, keepdims=True)
    scale = lax.rsqrt(jnp.mean(centre * centre, axis=-1, keepdims=True) + EPS)
    return (centre * scale, scale)


def norm_back(grad_in, normed, scale):
    centred = grad_in - jnp.mean(grad_in, axis=-1, keepdims=True)
    return scale * (centred - normed * jnp.mean(grad_in * normed, axis=-1, keepdims=True))


def rope_tables(positions):
    half_head = HEAD // 2
    frequency = 10000.0 ** (-(jnp.arange(half_head, dtype=jnp.float32) * 2.0) / HEAD)
    angles = positions.astype(jnp.float32)[:, None] * frequency[None, :]
    return (jnp.cos(angles), jnp.sin(angles))


def rotate(values, cos_part, sin_part, reverse):
    count = values.shape[0]
    heads = values.reshape(count, HEADS, HEAD)
    half_head = HEAD // 2
    leading = heads[..., :half_head]
    trailing = heads[..., half_head:]
    cosine = cos_part[:, None, :]
    sine_part = sin_part[:, None, :]
    if reverse:
        parts = [leading * cosine + trailing * sine_part, trailing * cosine - leading * sine_part]
    else:
        parts = [leading * cosine - trailing * sine_part, trailing * cosine + leading * sine_part]
    return jnp.concatenate(parts, axis=-1).reshape(count, D)


def split_heads(values):
    count = values.shape[0]
    return values.reshape(count, HEADS // together, together * HEAD).transpose(1, 0, 2)


def join_heads(values):
    groups, count, width = values.shape
    return values.transpose(1, 0, 2).reshape(count, groups * width)


def allowed_pairs(query_copy, query_block, query_doc, key_copy, key_block, key_doc):
    same_doc = query_doc[:, None] == key_doc[None, :]
    query_noisy = (query_copy == 0)[:, None]
    key_noisy = (key_copy == 0)[None, :]
    query_column = query_block[:, None]
    key_row = key_block[None, :]
    inner = query_noisy & key_noisy & (key_row == query_column)
    earlier = query_noisy & ~key_noisy & (key_row < query_column)
    causal = ~query_noisy & ~key_noisy & (key_row <= query_column)
    return same_doc & (inner | earlier | causal)


def masked_scores(query_group, key_group, allowed):
    query_heads = query_group.reshape(query_group.shape[0], together, HEAD)
    key_heads = key_group.reshape(key_group.shape[0], together, HEAD)
    raw = jnp.einsum(
        "qhd,khd->hqk", query_heads, key_heads, preferred_element_type=jnp.float32
    ) * HEAD ** (-0.5)
    return (jnp.where(allowed[None], raw, -1e30), query_heads, key_heads)


def group_forward(items, allowed):
    query_group, key_group, value_group = items
    count = query_group.shape[0]
    scores, query_heads, key_heads = masked_scores(query_group, key_group, allowed)
    value_heads = value_group.reshape(value_group.shape[0], together, HEAD)
    top = jnp.max(scores, axis=-1, keepdims=True)
    weights = jnp.exp(scores - top)
    total = jnp.sum(weights, axis=-1, keepdims=True)
    probs = (weights / total).astype(jnp.bfloat16)
    mixed = jnp.einsum("hqk,khd->qhd", probs, value_heads, preferred_element_type=jnp.float32)
    return (mixed.reshape(count, together * HEAD), (top + jnp.log(total))[..., 0])


def group_backward(items, allowed, tail):
    query_group, key_group, value_group, grad_group, log_total = items
    count = query_group.shape[0]
    key_count = key_group.shape[0]
    scores, query_heads, key_heads = masked_scores(query_group, key_group, allowed)
    value_heads = value_group.reshape(key_count, together, HEAD)
    grad_heads = grad_group.reshape(count, together, HEAD)
    probs = jnp.exp(scores - log_total[..., None])
    prob_grad = jnp.einsum(
        "qhd,khd->hqk", grad_heads, value_heads, preferred_element_type=jnp.float32
    )
    centre = jnp.sum(probs * prob_grad, axis=-1, keepdims=True)
    score_grad = (probs * (prob_grad - centre)).astype(jnp.bfloat16)
    query_grad = jnp.einsum(
        "hqk,khd->qhd", score_grad, key_heads, preferred_element_type=jnp.float32
    ) * HEAD ** (-0.5)
    tail_probs = probs.astype(jnp.bfloat16)
    value_grad = jnp.einsum(
        "hqk,qhd->khd", tail_probs, grad_heads, preferred_element_type=jnp.float32
    )
    key_grad = jnp.einsum(
        "hqk,qhd->khd", score_grad, query_heads, preferred_element_type=jnp.float32
    ) * HEAD ** (-0.5)
    return (
        query_grad.reshape(count, together * HEAD),
        key_grad.reshape(tail, together * HEAD),
        value_grad.reshape(tail, together * HEAD),
        centre[..., 0],
    )


def reduce_grads(grads):
    shards = (
        lax.psum_scatter(grads[0], "fsdp", scatter_dimension=0, tiled=True),
        lax.psum_scatter(grads[1], "fsdp", scatter_dimension=0, tiled=True),
        lax.psum_scatter(grads[2], "fsdp", scatter_dimension=0, tiled=True),
        lax.psum_scatter(grads[3], "fsdp", scatter_dimension=0, tiled=True),
        lax.psum_scatter(grads[4], "fsdp", scatter_dimension=0, tiled=True),
        lax.psum_scatter(grads[5], "fsdp", scatter_dimension=0, tiled=True),
        lax.psum_scatter(grads[6], "fsdp", scatter_dimension=0, tiled=True),
        lax.psum_scatter(grads[7], "fsdp", scatter_dimension=0, tiled=True),
        lax.psum_scatter(grads[8], "fsdp", scatter_dimension=0, tiled=True),
    )
    return lax.psum(
        (
            shards[0],
            shards[1],
            shards[2],
            shards[3],
            shards[4],
            shards[5],
            shards[6],
            shards[7],
            shards[8],
        ),
        "ctx",
    )


def add_tuples(left_items, right_items):
    return tuple((left_item + right_item for left_item, right_item in zip(left_items, right_items)))


def general_body(
    clean_in,
    segments,
    noise,
    mask_embed,
    norm1_gain,
    qkv_weight,
    out_weight,
    norm2_gain,
    up_weight,
    up_bias,
    down_weight,
    down_bias,
    out_grad,
):
    qkv_full, out_full, gain_low, embed_low = (
        lax.all_gather(qkv_weight, "fsdp", axis=0, tiled=True),
        lax.all_gather(out_weight, "fsdp", axis=0, tiled=True),
        lax.all_gather(norm1_gain, "fsdp", axis=0, tiled=True),
        lax.all_gather(mask_embed, "fsdp", axis=0, tiled=True),
    )
    up_full, up_low, down_full, down_low, gain_two_low = (
        lax.all_gather(up_weight, "fsdp", axis=0, tiled=True),
        lax.all_gather(up_bias, "fsdp", axis=0, tiled=True),
        lax.all_gather(down_weight, "fsdp", axis=0, tiled=True),
        lax.all_gather(down_bias, "fsdp", axis=0, tiled=True),
        lax.all_gather(norm2_gain, "fsdp", axis=0, tiled=True),
    )
    gain_one = gain_low.astype(jnp.float32)
    gain_two = gain_two_low.astype(jnp.float32)
    embed_row = embed_low.astype(jnp.float32)
    up_shift = up_low.astype(jnp.float32)
    down_shift = down_low.astype(jnp.float32)
    micro_count = clean_in.shape[0]
    piece = clean_in.shape[2]
    local_rows = 2 * piece
    ctx_count = lax.axis_size("ctx")
    ctx_rank = lax.axis_index("ctx")
    span = jnp.arange(piece, dtype=jnp.int32)
    local_pos = jnp.concatenate(
        [ctx_rank * piece + span, (2 * ctx_count - 1 - ctx_rank) * piece + span]
    )
    ranks = jnp.arange(ctx_count, dtype=jnp.int32)[:, None]
    far_pos = jnp.concatenate(
        [ranks * piece + span[None, :], (2 * ctx_count - 1 - ranks) * piece + span[None, :]], axis=1
    ).reshape(-1)
    seq_len = ctx_count * local_rows
    cos_part, sin_part = rope_tables(jnp.concatenate([local_pos, local_pos]))
    query_copy = jnp.concatenate(
        [jnp.zeros((local_rows,), jnp.int32), jnp.ones((local_rows,), jnp.int32)]
    )
    key_copy = jnp.concatenate(
        [jnp.ones((seq_len,), jnp.int32), jnp.zeros((local_rows,), jnp.int32)]
    )
    query_block = jnp.concatenate([local_pos, local_pos]) // BLK
    key_block = jnp.concatenate([far_pos, local_pos]) // BLK
    full_shapes = ((D,), (D,), (D, 3 * D), (D, D), (D,), (D, FF), (FF,), (FF, D), (D,))
    totals = tuple((jnp.zeros(shape_item, jnp.float32) for shape_item in full_shapes))
    tail = seq_len + local_rows
    outputs = []
    input_grads = []
    for micro_step in range(micro_count):
        clean_rows = clean_in[micro_step].reshape(local_rows, D).astype(jnp.float32)
        noise_rows = noise[micro_step].reshape(-1)
        masked_rows = noise_rows[:, None] == 1
        doc_local = segments[micro_step].reshape(-1).astype(jnp.float32)
        noisy_rows = jnp.where(masked_rows, embed_row[None, :], clean_rows)
        stacked = jnp.concatenate([noisy_rows, clean_rows], axis=0)
        normed_one, scale_one = normalize(stacked)
        h_one = (normed_one * gain_one).astype(jnp.bfloat16)
        projected = jnp.dot(h_one, qkv_full, preferred_element_type=jnp.float32)
        queries = rotate(projected[:, :D], cos_part, sin_part, False).astype(jnp.bfloat16)
        keys = rotate(projected[:, D : 2 * D], cos_part, sin_part, False).astype(jnp.bfloat16)
        values = projected[:, 2 * D :].astype(jnp.bfloat16)
        far_keys, far_values, far_docs = (
            lax.all_gather(keys[local_rows:], "ctx", axis=0, tiled=True),
            lax.all_gather(values[local_rows:], "ctx", axis=0, tiled=True),
            lax.all_gather(doc_local.astype(jnp.bfloat16), "ctx", axis=0, tiled=True),
        )
        key_all = jnp.concatenate([far_keys, keys[:local_rows]], axis=0)
        value_all = jnp.concatenate([far_values, values[:local_rows]], axis=0)
        query_doc = jnp.concatenate([doc_local, doc_local])
        key_doc = jnp.concatenate([far_docs.astype(jnp.float32), doc_local])
        allowed = allowed_pairs(query_copy, query_block, query_doc, key_copy, key_block, key_doc)
        query_groups = split_heads(queries)
        key_groups = split_heads(key_all)
        value_groups = split_heads(value_all)
        mixed_groups, log_totals = lax.map(
            partial(group_forward, allowed=allowed), (query_groups, key_groups, value_groups)
        )
        mixed = join_heads(mixed_groups).astype(jnp.bfloat16)
        resid = stacked + jnp.dot(mixed, out_full, preferred_element_type=jnp.float32)
        normed_two, scale_two = normalize(resid)
        h_two = (normed_two * gain_two).astype(jnp.bfloat16)
        hidden = jnp.dot(h_two, up_full, preferred_element_type=jnp.float32) + up_shift
        active = jax.nn.gelu(hidden, approximate=True).astype(jnp.bfloat16)
        result = resid + jnp.dot(active, down_full, preferred_element_type=jnp.float32) + down_shift
        outputs.append(result.astype(jnp.bfloat16).reshape(2, 2, piece, D))
        cotangent = out_grad[micro_step].reshape(2 * local_rows, D).astype(jnp.float32)
        grad_out = cotangent.astype(jnp.bfloat16)
        down_grad = jnp.einsum("rf,rd->fd", active, grad_out, preferred_element_type=jnp.float32)
        down_shift_grad = jnp.sum(grad_out.astype(jnp.float32), axis=0)
        grad_active = jnp.einsum(
            "rd,fd->rf", grad_out, down_full, preferred_element_type=jnp.float32
        )
        unused, gelu_back = jax.vjp(partial(jax.nn.gelu, approximate=True), hidden)
        grad_hidden = gelu_back(grad_active)[0].astype(jnp.bfloat16)
        up_grad = jnp.einsum("rd,rf->df", h_two, grad_hidden, preferred_element_type=jnp.float32)
        up_shift_grad = jnp.sum(grad_hidden.astype(jnp.float32), axis=0)
        grad_h_two = jnp.einsum(
            "rf,df->rd", grad_hidden, up_full, preferred_element_type=jnp.float32
        )
        gain_two_grad = jnp.sum(grad_h_two * normed_two, axis=0)
        grad_resid = cotangent + norm_back(grad_h_two * gain_two, normed_two, scale_two)
        grad_attn = grad_resid.astype(jnp.bfloat16)
        out_grad_full = jnp.einsum(
            "rd,re->de", mixed, grad_attn, preferred_element_type=jnp.float32
        )
        grad_mixed = jnp.einsum(
            "re,de->rd", grad_attn, out_full, preferred_element_type=jnp.float32
        ).astype(jnp.bfloat16)
        query_grads, key_grads, value_grads, centres = lax.map(
            partial(group_backward, allowed=allowed, tail=tail),
            (query_groups, key_groups, value_groups, split_heads(grad_mixed), log_totals),
        )
        query_grad = join_heads(query_grads)
        key_grad_all = join_heads(key_grads)
        value_grad_all = join_heads(value_grads)
        key_mine, value_mine = (
            lax.psum_scatter(key_grad_all[:seq_len], "ctx", scatter_dimension=0, tiled=True),
            lax.psum_scatter(value_grad_all[:seq_len], "ctx", scatter_dimension=0, tiled=True),
        )
        key_grad = jnp.concatenate([key_grad_all[seq_len:], key_mine], axis=0)
        value_grad = jnp.concatenate([value_grad_all[seq_len:], value_mine], axis=0)
        grad_proj = jnp.concatenate(
            [
                rotate(query_grad, cos_part, sin_part, True),
                rotate(key_grad, cos_part, sin_part, True),
                value_grad,
            ],
            axis=1,
        ).astype(jnp.bfloat16)
        qkv_grad = jnp.einsum("rd,re->de", h_one, grad_proj, preferred_element_type=jnp.float32)
        grad_h_one = jnp.einsum(
            "re,de->rd", grad_proj, qkv_full, preferred_element_type=jnp.float32
        )
        gain_one_grad = jnp.sum(grad_h_one * normed_one, axis=0)
        grad_rows = grad_resid + norm_back(grad_h_one * gain_one, normed_one, scale_one)
        grad_noisy = grad_rows[:local_rows]
        input_grads.append(
            (grad_rows[local_rows:] + jnp.where(masked_rows, 0.0, grad_noisy)).reshape(2, piece, D)
        )
        embed_grad = jnp.sum(jnp.where(masked_rows, grad_noisy, 0.0), axis=0)
        step_grads = (
            embed_grad,
            gain_one_grad,
            qkv_grad,
            out_grad_full,
            gain_two_grad,
            up_grad,
            up_shift_grad,
            down_grad,
            down_shift_grad,
        )
        totals = add_tuples(totals, step_grads)
    reduced = reduce_grads(totals)
    block_out = jnp.stack(outputs)
    input_grad = jnp.stack(input_grads)
    return (
        block_out,
        input_grad,
        reduced[0],
        reduced[1],
        reduced[2],
        reduced[3],
        reduced[4],
        reduced[5],
        reduced[6],
        reduced[7],
        reduced[8],
    )


PAIR=2*HEAD; PAIRS=D//PAIR
NEG=-1e30
VMEM_LIMIT=60<<20
F32=jnp.float32; BF=jnp.bfloat16

def dot_nn(a,b): return lax.dot_general(a,b,(((1,),(0,)),((),())),preferred_element_type=F32)
def dot_nt(a,b): return lax.dot_general(a,b,(((1,),(1,)),((),())),preferred_element_type=F32)
def dot_tn(a,b): return lax.dot_general(a,b,(((0,),(0,)),((),())),preferred_element_type=F32)

def tiles_of(half):
    return [(s,min(128,half-s)) for s in range(0,half,128)]

def norm_rows(rows):
    centre=rows-jnp.mean(rows,axis=-1,keepdims=True)
    scale=lax.rsqrt(jnp.mean(centre*centre,axis=-1,keepdims=True)+EPS)
    return centre*scale, scale

def swap_halves(z):
    lane=lax.broadcasted_iota(jnp.int32,z.shape,1)
    low=(lane & (HEAD-1)) < HEAD//2
    return jnp.where(low,pltpu.roll(z,PAIR-HEAD//2,1),pltpu.roll(z,HEAD//2,1))

def head_stack(z):
    lane=lax.broadcasted_iota(jnp.int32,z.shape,1)
    first=lane<HEAD
    zero=jnp.zeros_like(z)
    return jnp.concatenate([jnp.where(first,z,zero),jnp.where(first,zero,z)],axis=0)

def head_merge(z):
    n=z.shape[0]//2
    lane=lax.broadcasted_iota(jnp.int32,(n,z.shape[1]),1)
    return jnp.where(lane<HEAD,z[:n],z[n:])

def layer_rows(xc_ref,noise_ref,emb_ref):
    clean=xc_ref[...].astype(F32)
    noisy=jnp.where(noise_ref[...]==1,emb_ref[...].astype(F32),clean)
    return noisy,clean

def fwd_attn_kernel(half,xc,noise,segc,segr,small,wqkv,wout,trig,
                    q_o,k_o,v_o,mix_o,lse_o,x1_o,h_s,bias_s,self_s,mix_s):
    p=pl.program_id(0)
    tiles=tiles_of(half)
    @pl.when(p==0)
    def _():
        g=vector_row(small,1)
        clean=jnp.concatenate([xc[i] for i in range(9)],axis=0).astype(F32)
        noisy=jnp.where(noise[...]==1,vector_row(small,0),clean)
        for c,rows in enumerate((noisy,clean)):
            x1_o[c*half:(c+1)*half]=rows
            n,_=norm_rows(rows)
            h_s[c*half:(c+1)*half]=(n*g).astype(BF)
        for s,m in tiles:
            n=s+m
            qb=(lax.broadcasted_iota(jnp.int32,(m,n),0)+s)//BLK
            kb=lax.broadcasted_iota(jnp.int32,(m,n),1)//BLK
            same=segc[s:n]==segr[:,:n]
            bias_s[0,s:n,:n]=jnp.where(same&(kb<qb),0.0,NEG)
            bias_s[1,s:n,:n]=jnp.where(same&(kb<=qb),0.0,NEG)
            qb=lax.broadcasted_iota(jnp.int32,(m,m),0)//BLK
            kb=lax.broadcasted_iota(jnp.int32,(m,m),1)//BLK
            same=segc[s:n]==segr[:,s:n]
            self_s[s:n,:m]=jnp.where(same&(kb==qb),0.0,NEG)
    h=h_s[...]
    cs=jnp.concatenate([trig[:,:PAIR]]*2,axis=0)
    sn=jnp.concatenate([trig[:,PAIR:]]*2,axis=0)
    block=lambda i: wqkv[:,pl.ds(pl.multiple_of(i*D+p*PAIR,PAIR),PAIR)]
    zq=dot_nn(h,jnp.concatenate([block(0),block(1)],axis=1))
    z=zq[:,:PAIR]; q_o[...]=((z*cs+swap_halves(z)*sn).astype(BF)*BF(HEAD**-0.5)).astype(BF)
    z=zq[:,PAIR:]; k_o[...]=(z*cs+swap_halves(z)*sn).astype(BF)
    v_o[...]=dot_nn(h,block(2)).astype(BF)
    idx=0
    for s,m in tiles:
        n=s+m
        for c in (0,1):
            qs=head_stack(q_o[c*half+s:c*half+n])
            kc=k_o[half:half+n]; vc=v_o[half:half+n]
            sc=dot_nt(qs,kc).reshape(2,m,n)+bias_s[c,s:n,:n][None]
            top=jnp.max(sc,axis=-1,keepdims=True)
            if c==0:
                ss=dot_nt(qs,k_o[s:n]).reshape(2,m,m)+self_s[s:n,:m][None]
                top=jnp.maximum(top,jnp.max(ss,axis=-1,keepdims=True))
            w=jnp.exp(sc-top); tot=jnp.sum(w,axis=-1,keepdims=True)
            o=dot_nn(w.astype(BF).reshape(2*m,n),vc)
            if c==0:
                w2=jnp.exp(ss-top); tot=tot+jnp.sum(w2,axis=-1,keepdims=True)
                o=o+dot_nn(w2.astype(BF).reshape(2*m,m),v_o[s:n])
            tot=tot.reshape(2*m,1)
            o=o*(1.0/tot)
            mx=head_merge(o).astype(BF)
            mix_o[c*half+s:c*half+n]=mx
            mix_s[p,c*half+s:c*half+n]=mx
            lse=top.reshape(2*m,1)+jnp.log(tot)
            lse_o[0,idx:idx+1,:2*m]=jnp.broadcast_to(lse,(2*m,128)).T[0:1]
            idx+=1
    @pl.when(p==pl.num_programs(0)-1)
    def _():
        full=jnp.concatenate([mix_s[i] for i in range(PAIRS)],axis=1)
        x1_o[...]=x1_o[...]+dot_nn(full,wout[...])

def whole(shape): return pl.BlockSpec(shape,lambda *i:(0,)*len(shape))

def vector_row(small,i):
    return jnp.concatenate([small[f,i:i+1,:D//4] for f in range(4)],axis=1).astype(F32)

def fwd_attn_comm_kernel(half,*refs):
    clean,meta,gout,trig,qkv,out,up,down,small=refs[:9]
    q_o,k_o,v_o,mix_o,lse_o,x1_o,noise_o,segc_o,segr_o,vec_o,bias_o,qkv_o,out_o,up_o,down_o,cot_o,clean_o=refs[9:26]
    h_s,bias_s,self_s,mix_s,clean_s,meta_s,small_s,qkv_s,out_s,trig_s=refs[26:36]
    a_send,a_recv,m_send,m_recv,c_send,c_recv,w_send,w_recv,s_send,s_recv,local=refs[36:]
    p=pl.program_id(0)
    c,f=place_ids()
    piece=half//9
    weight=lambda i,shard,full,parts: GatherRows(shard,full,w_send.at[i],w_recv.at[i],local.at[i],parts)
    w_qkv,w_out,w_up,w_down=weight(0,qkv,qkv_s,3),weight(1,out,out_s,1),weight(2,up,up_o,3),GatherRows(down,down_o,w_send.at[3],w_recv.at[3],local.at[3],3,False)
    rows=ToUnit(lambda q,h:clean.at[q,h],lambda t:clean_s.at[t],a_send,a_recv,local.at[4])
    notes=ToUnit(lambda q,h:meta.at[2*q+h],lambda t:meta_s.at[t],m_send,m_recv,local.at[5])
    grads=[ToUnit(lambda q,h:gout.at[q,0,h],lambda t:cot_o.at[t],c_send,c_recv,local.at[6])]
    copies=[pltpu.make_async_copy(qkv_s,qkv_o,local.at[8]),pltpu.make_async_copy(out_s,out_o,local.at[9]),pltpu.make_async_copy(clean_s,clean_o,local.at[10])]
    others=[f+1-2*(f%2),(f+2)%4,3-f]
    @pl.when(p==0)
    def _():
        meet(True,(1,2,3))
        w_qkv.begin()
        notes.begin()
        rows.begin()
        sends=[remote(small,small_s.at[f],s_send.at[i],s_recv.at[i],{"fsdp":other}) for i,other in enumerate(others)]
        for d in sends: d.start()
        own=pltpu.make_async_copy(small,small_s.at[f],local.at[11])
        own.start()
        table=pltpu.make_async_copy(trig.at[c%2],trig_s,local.at[12])
        table.start()
        w_out.begin()
        w_up.begin()
        w_down.begin()
        for i in range(3): w_qkv.relay_far(i)
        @pl.when(c%2==1)
        def _():
            clean_s[7:9]=jnp.zeros((2,)+clean_s.shape[1:],BF)
            line=lax.broadcasted_iota(jnp.int32,(2,)+meta_s.shape[1:],1)
            meta_s[7:9]=jnp.where(line==0,-1,0)
            pad=pltpu.make_async_copy(clean_s.at[pl.ds(7,2)],cot_o.at[pl.ds(7,2)],local.at[13])
            pad.start()
            pad.wait()
        for i in range(3): w_qkv.relay_x(i)
        for r in grads: r.begin_straight()
        own.wait()
        table.wait()
        for i,other in enumerate(others):
            sends[i].wait_send()
            remote(small_s.at[other],small_s.at[other],s_send.at[i],s_recv.at[i],{"fsdp":other}).wait_recv()
        notes.finish()
        note=lambda i: jnp.concatenate([meta_s[i,0:1],meta_s[i,1:2]],axis=1).astype(F32)
        for i in range(9):
            t=jnp.broadcast_to(note(i),(128,128)).T
            segc_o[i*piece:(i+1)*piece]=t[:piece,0:1]
            noise_o[i*piece:(i+1)*piece]=t[piece:,0:1].astype(jnp.int32)
        for i in range(5):
            segr_o[:,i*128:(i+1)*128]=jnp.concatenate([meta_s[2*i,0:1],meta_s[min(2*i+1,8),0:1]],axis=1).astype(F32)
        for i in range(4): vec_o[i:i+1]=vector_row(small_s,(2,3,0,1)[i])
        for g in range(4): bias_o[:,g*768:(g+1)*768]=jnp.concatenate([small_s[g,4+i:5+i] for i in range(4)],axis=1).astype(F32)
        rows.finish()
        w_qkv.finish()
        copies[0].start()
        copies[2].start()
    fwd_attn_kernel(half,clean_s,noise_o,segc_o,segr_o,small_s,qkv_s,out_s,trig_s,q_o,k_o,v_o,mix_o,lse_o,x1_o,h_s,bias_s,self_s,mix_s)
    def at(i,*ops):
        @pl.when(p==i)
        def _():
            for op in ops: op()
    at(0,w_out.relay_far,*[partial(w_up.relay_far,i) for i in range(2)])
    at(1,w_out.relay_x,partial(w_up.relay_far,2),partial(w_up.relay_x,0),grads[0].begin_across)
    at(2,w_out.finish,copies[1].start,partial(w_up.relay_x,1),partial(w_down.relay_far,0))
    at(3,partial(w_up.relay_x,2),partial(w_down.relay_far,1))
    at(4,partial(w_down.relay_far,2))
    @pl.when(p==pl.num_programs(0)-1)
    def _():
        for w in (w_up,w_down): w.finish()
        for r in grads: r.finish()
        for d in copies: d.wait()

def whole(shape): return pl.BlockSpec(shape,lambda *i:(0,)*len(shape))
def once(shape): return pl.BlockSpec(shape,lambda *i:(0,)*len(shape),pipeline_mode=pl.Buffered(1))

def fwd_attn(clean,meta,gout,trig,qkv,out,up,down,small):
    piece=clean.shape[2]; half=9*piece; R=2*half
    nt=len(tiles_of(half))*2; ntp=-(-nt//8)*8
    rows=pl.BlockSpec((R,PAIR),lambda p:(0,p))
    sds=jax.ShapeDtypeStruct
    return pl.pallas_call(partial(fwd_attn_comm_kernel,half),grid=(PAIRS,),
        in_specs=[ANYSPACE]*4+[once(a.shape) for a in (qkv,out,up,down,small)],
        out_specs=[rows,rows,rows,rows,pl.BlockSpec((1,ntp,256),lambda p:(p,0,0)),whole((R,D)),whole((half,1)),whole((half,1)),whole((1,640)),whole((4,D)),whole((1,FF))]+[ANYSPACE]*6,
        out_shape=[sds((R,D),BF)]*4+[sds((PAIRS,ntp,256),F32),sds((R,D),F32),sds((half,1),jnp.int32),sds((half,1),F32),sds((1,640),F32),sds((4,D),F32),sds((1,FF),F32),
            sds((D,3*D),BF),sds((D,D),BF),sds((D,FF),BF),sds((FF,D),BF),sds((9,piece,D),BF),sds((9,piece,D),BF)],
        scratch_shapes=[pltpu.VMEM((R,D),BF),pltpu.VMEM((2,half,half),F32),pltpu.VMEM((half,128),F32),pltpu.VMEM((PAIRS,R,PAIR),BF),
            pltpu.VMEM((9,piece,D),BF),pltpu.VMEM((9,)+meta.shape[1:],jnp.int32),pltpu.VMEM((4,)+small.shape,BF),pltpu.VMEM((D,3*D),BF),pltpu.VMEM((D,D),BF),pltpu.VMEM((half,2*PAIR),F32),
            DMA((8,)),DMA((9,)),DMA((8,)),DMA((9,)),DMA((8,)),DMA((9,)),DMA((4,13)),DMA((4,13)),DMA((3,)),DMA((3,)),DMA((14,))],
        compiler_params=pltpu.CompilerParams(vmem_limit_bytes=VMEM_LIMIT,dimension_semantics=("arbitrary",),collective_id=1,has_side_effects=True),
        cost_estimate=pl.CostEstimate(flops=2*R*D*(3*D+D)+24*R*half*D//2*2,bytes_accessed=16<<20,transcendentals=R*half*HEADS),
        name="fwd_attn")(clean,meta,gout,trig,qkv,out,up,down,small)

GC=(2.0/3.141592653589793)**0.5
def cols(refs): return jnp.concatenate([r[...] for r in refs],axis=1)
def rowcat(refs): return jnp.concatenate([r[...] for r in refs],axis=0)
STEPS=FF//512
def up_specs(): return [pl.BlockSpec((D,128),(lambda s:(lambda j:(0,s*STEPS+j)))(s)) for s in range(4)]
def down_specs(): return [pl.BlockSpec((128,D),(lambda s:(lambda j:(s*STEPS+j,0)))(s)) for s in range(4)]
def bias_specs(): return [pl.BlockSpec((1,128),(lambda s:(lambda j:(0,s*STEPS+j)))(s)) for s in range(4)]

FFN_TABLE={2: [(0, None, 0)], 4: [(1, None, 0), (0, 0, 1)], 6: [(2, None, 0), (1, 0, 1)], 8: [(3, None, 0), (0, 1, None), (2, 0, 1)], 9: [(3, 0, None)], 10: [(4, None, 0), (1, 1, None)], 12: [(5, None, 0)]}
FFN_END=[(4, 0), (2, 1), (5, 0)]
ATTN_TABLE={0: [(3, None, 1), (4, None, 1), (5, None, 1), (0, None, 2), (1, None, 2), (2, None, 2)], 1: [(6, None, 0)], 2: [(0, 2, 3), (6, 0, 1)], 3: [(0, 3, 4), (1, 2, 3), (3, 1, 2)], 4: [(7, None, 0), (0, 4, 5), (2, 2, 3)], 5: [(1, 3, 4), (0, 5, 6), (3, 2, 3), (4, 1, 2), (7, 0, 1), (2, 3, 4)], 6: [(0, 6, 7), (1, 4, 5), (5, 1, 2)], 7: [(2, 4, 5), (3, 3, 4), (4, 2, 3)], 8: [(8, None, 0), (0, 7, None), (1, 5, 6), (2, 5, 6), (6, 1, 2)], 9: [(1, 6, 7), (3, 4, 5), (4, 3, 4), (5, 2, 3), (7, 1, 2), (8, 0, 1), (6, 2, 3)], 10: [(2, 6, 7), (3, 5, 6)], 11: [(1, 7, None), (3, 6, 7), (4, 4, 5), (5, 3, 4), (6, 3, 4), (7, 2, 3), (8, 1, 2)], 12: [(9, None, 0)]}
TAIL_ORDER=[("sums", None, 0), (3, 7, None), (2, 7, None), (4, 5, 6), (5, 4, 5), (6, 4, 5), (7, 3, 4), (9, 0, 1), ("rows", None, 1), ("rows", None, 2), (8, 2, 3), ("sums", 0, 1), (4, 6, 7), ("sums", 1, 2), (5, 5, 6), (6, 5, 6), (9, 1, 2), ("rows", None, 3), (4, 7, None), (7, 4, 5), ("sums", 2, 3), (8, 3, 4), (9, 2, 3), ("rows", None, 4), ("sums", 3, 4), (5, 6, 7), (6, 6, 7), ("sums", 4, None), (7, 5, 6), (5, 7, None), (9, 3, 4), ("rows", None, 5), (8, 4, 5), (6, 7, None), (7, 6, 7), (9, 4, 5), ("rows", None, 6), (7, 7, None), (8, 5, 6), (9, 5, 6), ("rows", None, 7), (8, 6, 7), (9, 6, 7), (8, 7, None), (9, 7, None)]

def after(state,table,end):
    state=dict(state)
    for ops in table.values():
        for chunk,take,start in ops:
            if take is not None: state[chunk]=take
    state.update(end)
    return state
FFN_STATE=after({},FFN_TABLE,FFN_END)
def in_state(state,ids,low,high): return [i for i in ids if low<=state[i]<=high]
def started(chunk,table):
    return [start for ops in table.values() for i,take,start in ops if i==chunk and start is not None]

def run_table(table,chunks,position,pid,steps,per_step):
    for i in range(steps):
        ops=table.get(per_step*i+position+1,[])
        if ops:
            @pl.when(pid==i)
            def _(): do_ops(ops,chunks)

def do_ops(ops,chunks):
    for i,take,start in ops:
        if take is not None: chunks[i].take(take)
        if start is not None: chunks[i].start(start)

PHASE=2*STEPS

def ffn_kernel(x1,vec,*refs):
    wup,bup,wdn,rest=refs[:4],refs[4:8],refs[8:12],refs[12:]
    gain,bdn=vec.at[0:1],vec.at[1:2]
    gy0,gout,dbup_o,dbdn_o,dgain_o,gx1_o,block_o,pair_o,total_o,final_o=rest[:10]
    h_s,hT_s,acc,gy_s,out_s,act_s,gu_s,grad_s,pair_s,far_s,total_s,send,recv,g_send,g_recv,b_send,b_recv,local=rest[10:]
    g=pl.program_id(0)
    R=h_s.shape[0]; ch=R//3; piece=R//18
    chunks=[Reduce(TILE,send.at[i],recv.at[i],grad=grad_s.at[i%2],pair=pair_s.at[i],far=far_s.at[i],total=total_s.at[i]) for i in range(STEPS)]
    arrive=ToUnit(lambda q,h:gout.at[q,1,h],lambda t:gy_s.at[9+t],g_send,g_recv,local.at[0])
    leave=[FromUnit(lambda t,i=i:out_s.at[9*i+t],lambda q,h,i=i:block_o.at[q,i,h],b_send.at[i],b_recv.at[i],local.at[1+i]) for i in range(2)]
    first=pltpu.make_async_copy(gy0,gy_s.at[pl.ds(0,9)],local.at[3])
    rows=lambda ref,i: ref[6*i:6*i+6].reshape(ch,D)
    wu=lambda: cols(wup)
    wd=lambda: rowcat(wdn)
    bias=cols(bup).astype(F32)
    @pl.when(g==0)
    def _():
        meet(True,(1,2))
        arrive.begin()
        first.start()
        @pl.when(lax.rem(place_ids()[0],2)==1)
        def _():
            gy_s[16:18]=jnp.zeros((2,)+gy_s.shape[1:],BF)
        n,_=norm_rows(x1[...])
        h=(n*gain[...].astype(F32)).astype(BF)
        h_s[...]=h
        hT_s[...]=h.T
        acc[...]=x1[...]+bdn[...].astype(F32)
    for copy in range(2):
        @pl.when((g>=copy*STEPS)&(g<(copy+1)*STEPS))
        def _():
            for i in range(2):
                r=slice((2*copy+i)*R//4,(2*copy+i+1)*R//4)
                u=dot_nn(h_s[r],wu())+bias
                act=(0.5*u*(1.0+jnp.tanh(GC*(u+0.044715*u*u*u)))).astype(BF)
                acc[r]+=dot_nn(act,wd())
        @pl.when(g==(copy+1)*STEPS-1)
        def _():
            out_s[9*copy:9*copy+9]=acc[copy*R//2:(copy+1)*R//2].astype(BF).reshape(9,piece,D)
            leave[copy].begin()
    @pl.when(g==PHASE-1)
    def _():
        arrive.finish()
        first.wait()
        acc[...]=jnp.zeros_like(acc)
        dbdn_o[...]=jnp.sum(gy_s[...].astype(F32).reshape(R,D),axis=0,keepdims=True)
    @pl.when(g>=PHASE)
    def _():
        j=g-PHASE
        for i in range(2,STEPS):
            @pl.when(j==i)
            def _(): chunks[i-2].sent(0)
        slot=lax.rem(j,2)
        for i in range(3):
            r=slice(i*ch,(i+1)*ch)
            u=dot_nn(h_s[r],wu())+bias
            ga=dot_nt(rows(gy_s,i),wd())
            u2=u*u
            t=jnp.tanh(GC*(u+0.044715*u*u2))
            a=0.5*(1.0+t)
            gu=((a+0.5*u*(1.0-t*t)*(GC*(1.0+3*0.044715*u2)))*ga).astype(BF)
            act_s[r]=(u*a).astype(BF)
            gu_s[r]=gu
            acc[r]+=dot_nt(gu,wu())
        run_table(FFN_TABLE,chunks,0,j,STEPS,2)
        def put(s,row,value):
            for k in range(0,value.shape[0],64):
                grad_s[slot,s%2,s//2,(row+k)//TILE,(row+k)%TILE:(row+k)%TILE+64]=value[k:k+64]
        r=dot_tn(act_s[...],gy_s[...].reshape(R,D)).astype(BF)
        for s in range(4):
            for t in range(6): put(s,768+t*128,r[s*128:(s+1)*128,t*128:(t+1)*128])
        r=dot_nn(hT_s[...],gu_s[...]).astype(BF)
        for s in range(4):
            for t in range(4): put(s,t*192,r[s*192:(s+1)*192,t*128:(t+1)*128])
        dbup_o[...]=jnp.sum(gu_s[...].astype(F32),axis=0,keepdims=True)
        run_table(FFN_TABLE,chunks,1,j,STEPS,2)
    @pl.when(g==pl.num_programs(0)-1)
    def _():
        n,scale=norm_rows(x1[...])
        g2=acc[...]
        dgain_o[...]=jnp.sum(g2*n,axis=0,keepdims=True)
        e=g2*gain[...].astype(F32)
        acc[...]=gy_s[...].astype(F32).reshape(R,D)+scale*(e-jnp.mean(e,axis=-1,keepdims=True)-n*jnp.mean(e*n,axis=-1,keepdims=True))
        outs=[pltpu.make_async_copy(acc,gx1_o,local.at[5])]
        outs[0].start()
        for i,stage in FFN_END: chunks[i].take(stage)
        for low,high,source,target in ((0,0,pair_s,pair_o),(1,3,total_s,total_o)):
            for place,i in enumerate(in_state(FFN_STATE,range(STEPS),low,high)):
                outs.append(pltpu.make_async_copy(source.at[i],target.at[place],local.at[5+len(outs)]))
                outs[-1].start()
        for i in range(STEPS):
            stages=started(i,FFN_TABLE)
            chunks[i].sent(*[x for x in stages if x>0 or i>=STEPS-2])
        for r in leave: r.finish()
        for d in outs: d.wait()

def ffn(x1,vec,wup,bup,wdn,gy0,gout):
    R=x1.shape[0]; half=R//2; piece=half//9
    count=lambda low,high: max(1,len(in_state(FFN_STATE,range(STEPS),low,high)))
    tile=lambda j: lax.rem(j,STEPS)
    ups=[pl.BlockSpec((D,128),(lambda s:(lambda j:(0,s*STEPS+tile(j))))(s)) for s in range(4)]
    downs=[pl.BlockSpec((128,D),(lambda s:(lambda j:(s*STEPS+tile(j),0)))(s)) for s in range(4)]
    biases=[pl.BlockSpec((1,128),(lambda s:(lambda j:(0,s*STEPS+tile(j))))(s)) for s in range(4)]
    return pl.pallas_call(ffn_kernel,grid=(PHASE+STEPS,),
        in_specs=[once((R,D)),once((4,D))]+ups+biases+downs+[ANYSPACE]*2,
        out_specs=[pl.BlockSpec((1,512),lambda j:(0,jnp.maximum(j-PHASE,0))),whole((1,D)),whole((1,D))]+[ANYSPACE]*5,
        out_shape=[jax.ShapeDtypeStruct((1,FF),F32),jax.ShapeDtypeStruct((1,D),F32),jax.ShapeDtypeStruct((1,D),F32),jax.ShapeDtypeStruct((R,D),F32),jax.ShapeDtypeStruct((4,2,2,piece,D),BF),
            jax.ShapeDtypeStruct((count(0,0),2,2,TILE,128),BF),jax.ShapeDtypeStruct((count(1,3),2,TILE,128),BF),jax.ShapeDtypeStruct((1,2,TILE,128),BF)],
        scratch_shapes=[pltpu.VMEM((R,D),BF),pltpu.VMEM((D,R),BF),pltpu.VMEM((R,D),F32),pltpu.VMEM((18,piece,D),BF),pltpu.VMEM((18,piece,D),BF),pltpu.VMEM((R,512),BF),pltpu.VMEM((R,512),BF),
            pltpu.VMEM((2,2,2,2,TILE,128),BF),pltpu.VMEM((STEPS,2,2,TILE,128),BF),pltpu.VMEM((STEPS,2,TILE,128),BF),pltpu.VMEM((STEPS,2,TILE,128),BF),
            DMA((STEPS,8)),DMA((STEPS,8)),DMA((8,)),DMA((9,)),DMA((2,8)),DMA((2,8)),DMA((STEPS+7,))],
        compiler_params=pltpu.CompilerParams(vmem_limit_bytes=VMEM_LIMIT,dimension_semantics=("arbitrary",),collective_id=2,has_side_effects=True),
        cost_estimate=pl.CostEstimate(flops=14*R*D*FF,bytes_accessed=40<<20,transcendentals=2*R*FF),
        name="ffn")(x1,vec,*[wup]*4,*[bup]*4,*[wdn]*4,gy0,gout)

def bwd_attn_kernel(half,xc,noise,segc,segr,vec,gx1,q,k,v,mix,lse,wq,wk,wv,wout,trig,mixed,gain_two,down_shift,up_shift,tile_pair,tile_total,tile_final,
                    tiles_o,wings_o,gin_o,sums_o,hT_s,gh,biasT_s,selfT_s,dq_s,dk_s,dv_s,ga,trig_s,
                    t_pair,t_far,t_total,t_over,t_final,w_grad,w_pair,w_far,w_total,w_over,w_final,gin_s,sum_s,in_s,t_send,t_recv,w_send,w_recv,v_send,v_recv,a_send,a_recv,local):
    p=pl.program_id(0)
    emb,gain=vec.at[2:3],vec.at[3:4]
    rank,_=place_ids()
    R=2*half
    tiles=tiles_of(half)
    pairs=in_state(FFN_STATE,range(STEPS),0,0)
    fars=in_state(FFN_STATE,range(STEPS),0,0)
    slot=lambda ids,i: ids.index(i) if i in ids else 0
    chunks=[Reduce(TILE,t_send.at[i],t_recv.at[i],pair=t_pair.at[slot(pairs,i)],far=t_far.at[slot(fars,i)],total=t_total.at[i],over=t_over.at[i],final=t_final.at[i]) for i in range(STEPS)]
    chunks+=[Reduce(WING,w_send.at[i],w_recv.at[i],grad=w_grad.at[i],pair=w_pair.at[i],far=w_far.at[i],total=w_total.at[i],over=w_over.at[i],final=w_final.at[i]) for i in range(4)]
    def tick(position):
        run_table(ATTN_TABLE,chunks,position,p,PAIRS,2)
    @pl.when(p==0)
    def _():
        loads=[pltpu.make_async_copy(trig.at[rank%2],trig_s,local.at[2])]
        loads[0].start()
        for low,high,source,target in ((0,0,tile_pair,t_pair),(1,3,tile_total,t_total),(4,7,tile_final,t_final)):
            for place,i in enumerate(in_state(FFN_STATE,range(STEPS),low,high)):
                loads.append(pltpu.make_async_copy(source.at[place],target.at[place if low==0 else i],local.at[2+len(loads)]))
                loads[-1].start()
        ga[...]=gx1[...].astype(BF)
        for d in loads: d.wait()
        meet(True,(1,2))
        do_ops(ATTN_TABLE.get(0,[]),chunks)
        g=gain[...].astype(F32)
        for c,rows in enumerate(layer_rows(xc,noise,emb)):
            n,_=norm_rows(rows)
            hT_s[:,c*half:(c+1)*half]=(n*g).astype(BF).T
        gh[...]=jnp.zeros_like(gh)
        for s,m in tiles:
            n=s+m
            qb=(lax.broadcasted_iota(jnp.int32,(n,m),1)+s)//BLK
            kb=lax.broadcasted_iota(jnp.int32,(n,m),0)//BLK
            same=segc[:n]==segr[:,s:n]
            biasT_s[0,:n,s:n]=jnp.where(same&(kb<qb),0.0,NEG)
            biasT_s[1,:n,s:n]=jnp.where(same&(kb<=qb),0.0,NEG)
            qb=lax.broadcasted_iota(jnp.int32,(m,m),1)//BLK
            kb=lax.broadcasted_iota(jnp.int32,(m,m),0)//BLK
            same=segc[s:n]==segr[:,s:n]
            selfT_s[s:n,:m]=jnp.where(same&(kb==qb),0.0,NEG)
    gm=dot_nt(ga[...],wout[...]).astype(BF)
    @pl.when(p==0)
    def _():
        r=dot_tn(mixed[...],ga[...]).astype(BF)
        for a in range(4):
            for t in range(6): w_grad[0,a%2,a//2,t//3,t%3*192:(t%3+1)*192]=r[a*192:(a+1)*192,t*128:(t+1)*128]
    gd=gm.astype(F32)*mix[...].astype(F32)
    dk_s[...]=jnp.zeros_like(dk_s); dv_s[...]=jnp.zeros_like(dv_s)
    idx=0
    for s,m in tiles:
        n=s+m
        for c in (0,1):
            rs=slice(c*half+s,c*half+n)
            qs=head_stack(q[rs]); gs=head_stack(gm[rs])
            delta=jnp.sum(head_stack(gd[rs]).T,axis=0,keepdims=True)
            row=lse[0,idx:idx+1,:2*m]
            def part(krows,bias):
                kc=k[krows]; vc=v[krows]
                st=dot_nt(kc,qs)+jnp.concatenate([bias,bias],axis=1)
                pt=jnp.exp(st-row)
                dp=dot_nt(vc,gs)
                ds=(pt*(dp-delta)).astype(BF)
                dv_s[krows]+=dot_nn(pt.astype(BF),gs)
                dk_s[krows]+=dot_nn(ds,qs)
                return dot_tn(ds,kc)
            dq=part(slice(half,half+n),biasT_s[c,:n,s:n])
            if c==0: dq=dq+part(slice(s,n),selfT_s[s:n,:m])
            dq_s[rs]=head_merge(dq)*HEAD**-0.5
            idx+=1
        if s==256: tick(0)
    cs=jnp.concatenate([trig_s[:,:PAIR]]*2,axis=0)
    sn=jnp.concatenate([trig_s[:,PAIR:]]*2,axis=0)
    z=jnp.concatenate([(g[...]*cs-swap_halves(g[...])*sn).astype(BF) for g in (dq_s,dk_s)]+[dv_s[...].astype(BF)],axis=1)
    r=dot_nn(hT_s[...],z).astype(BF)
    group=1+p//2
    for a in range(4):
        for t in range(3):
            w_grad[group,a%2,a//2,lax.rem(p,2),t*192:(t+1)*192]=r[a*192:(a+1)*192,t*128:(t+1)*128]
    gh[...]+=dot_nt(z,cols((wq,wk,wv)))
    tick(1)
    @pl.when(p==pl.num_programs(0)-1)
    def _():
        g=gain[...].astype(F32)
        outs=[]; dg=0.0
        for c,rows in enumerate(layer_rows(xc,noise,emb)):
            n,scale=norm_rows(rows)
            g1=gh[c*half:(c+1)*half]
            dg=dg+jnp.sum(g1*n,axis=0,keepdims=True)
            e=g1*g
            outs.append(gx1[c*half:(c+1)*half]+scale*(e-jnp.mean(e,axis=-1,keepdims=True)-n*jnp.mean(e*n,axis=-1,keepdims=True)))
        masked=noise[...]==1
        gin=(outs[1]+jnp.where(masked,0.0,outs[0])).astype(BF)
        gin_s[...]=gin.reshape(gin_s.shape)
        demb=jnp.sum(jnp.where(masked,outs[0],0.0),axis=0,keepdims=True)
        row=0
        for part in (demb,dg,gain_two,down_shift):
            for n in range(D//128):
                sum_s[0,row:row+1]=part[:,n*128:(n+1)*128]
                row+=1
        for a in range(4):
            for n in range(STEPS):
                sum_s[0,row:row+1]=up_shift[:,n*512+a*128:n*512+(a+1)*128]
                row+=1
        units=FromUnit(lambda t:gin_s.at[t],lambda q,h:gin_o.at[q,h],a_send,a_recv,local.at[0])
        some=chunks[STEPS]
        vectors=[remote(sum_s.at[n],in_s.at[n],v_send.at[n],v_recv.at[n],where) for n,where in enumerate((some.sib,some.far_id,some.xn,some.z1n,some.z2n))]
        for item,take,start in TAIL_ORDER:
            if item=="rows":
                if start==1: units.begin_rest()
                units.begin_one(start)
            elif item=="sums":
                if take is not None:
                    vectors[take].wait_recv()
                    sum_s[take+1]=sum_s[take]+in_s[take]
                if start is not None: vectors[start].start()
            else: do_ops([(item,take,start)],chunks)
        stores=[pltpu.make_async_copy(t_final,tiles_o,local.at[1]),pltpu.make_async_copy(w_final,wings_o,local.at[2])]
        for d in stores: d.start()
        sums_o[...]=sum_s[5]
        for d in vectors: d.wait_send()
        for n,chunk in enumerate(chunks):
            chunk.sent(*(started(n,ATTN_TABLE)+[start for item,take,start in TAIL_ORDER if item==n and start is not None]))
        units.finish()
        for d in stores: d.wait()

def bwd_attn(xc,noise,segc,segr,vec,gx1,q,k,v,mix,lse,wqkv,wout,trig,vectors,tile_pair,tile_total,tile_final):
    half=xc.shape[0]; R=2*half; piece=half//9
    ntp=lse.shape[1]
    ws=[pl.BlockSpec((D,PAIR),(lambda off:(lambda p:(0,off+p)))(o*PAIRS)) for o in range(3)]
    rows=pl.BlockSpec((R,PAIR),lambda p:(0,p))
    pairs=max(1,len(in_state(FFN_STATE,range(STEPS),0,0)))
    return pl.pallas_call(partial(bwd_attn_kernel,half),grid=(PAIRS,),
        in_specs=[once((half,D)),once((half,1)),once((half,1)),once((1,640)),once((4,D)),once((R,D)),rows,rows,rows,rows,
                  pl.BlockSpec((1,ntp,256),lambda p:(p,0,0)),*ws,pl.BlockSpec((PAIR,D),lambda p:(p,0)),ANYSPACE,once((R,D))]+[once(a.shape) for a in vectors]+[ANYSPACE]*3,
        out_specs=[ANYSPACE]*3+[whole((48,128))],
        out_shape=[jax.ShapeDtypeStruct((STEPS,2,TILE,128),BF),jax.ShapeDtypeStruct((4,2,WING,128),BF),jax.ShapeDtypeStruct((4,2,piece,D),BF),jax.ShapeDtypeStruct((48,128),F32)],
        scratch_shapes=[pltpu.VMEM((D,R),BF),pltpu.VMEM((R,D),F32),pltpu.VMEM((2,half,-(-half//128)*128),F32),pltpu.VMEM((half,128),F32)]+[pltpu.VMEM((R,PAIR),F32)]*3+[pltpu.VMEM((R,D),BF),pltpu.VMEM((half,2*PAIR),F32)]
            +[pltpu.VMEM((pairs,2,2,TILE,128),BF),pltpu.VMEM((pairs,2,TILE,128),BF),pltpu.VMEM((STEPS,2,TILE,128),BF),pltpu.VMEM((STEPS,2*TILE,128),BF),pltpu.VMEM((STEPS,2,TILE,128),BF),
              pltpu.VMEM((4,2,2,2,WING,128),BF),pltpu.VMEM((4,2,2,WING,128),BF),pltpu.VMEM((4,2,WING,128),BF),pltpu.VMEM((4,2,WING,128),BF),pltpu.VMEM((4,2*WING,128),BF),pltpu.VMEM((4,2,WING,128),BF),pltpu.VMEM((9,piece,D),BF),pltpu.VMEM((6,48,128),F32),pltpu.VMEM((5,48,128),F32),
              DMA((STEPS,8)),DMA((STEPS,8)),DMA((4,8)),DMA((4,8)),DMA((5,)),DMA((5,)),DMA((8,)),DMA((8,)),DMA((16,))],
        compiler_params=pltpu.CompilerParams(vmem_limit_bytes=VMEM_LIMIT,dimension_semantics=("arbitrary",),collective_id=3,has_side_effects=True),
        cost_estimate=pl.CostEstimate(flops=4*R*D*(3*D+D)+60*R*half*D//2*2,bytes_accessed=30<<20,transcendentals=R*half*HEADS),
        name="bwd_attn")(xc,noise,segc,segr,vec,gx1,q,k,v,mix,lse,wqkv,wqkv,wqkv,wout,trig,mix,*vectors,tile_pair,tile_total,tile_final)

def assemble(ffn,wings,gin,block):
    piece=gin.shape[2]
    up,down,out,qkv,grad,rows=pl.pallas_call(assemble_kernel,grid=(STEPS,),
        in_specs=[pl.BlockSpec((1,2,TILE,128),lambda i:(i,0,0,0)),whole(wings.shape),
            pl.BlockSpec((2,piece,D),lambda i:(jnp.minimum(i,3),0,0)),pl.BlockSpec((4,piece,D),lambda i:(jnp.minimum(i,3),0,0))],
        out_specs=[whole((192,FF)),pl.BlockSpec((128,D),lambda i:(i,0)),whole((192,D)),whole((192,3*D)),
            pl.BlockSpec((2,piece,D),lambda i:(jnp.minimum(i,3),0,0)),pl.BlockSpec((4,piece,D),lambda i:(jnp.minimum(i,3),0,0))],
        out_shape=[jax.ShapeDtypeStruct((192,FF),F32),jax.ShapeDtypeStruct((768,D),F32),jax.ShapeDtypeStruct((192,D),F32),jax.ShapeDtypeStruct((192,3*D),F32),
            jax.ShapeDtypeStruct((8,piece,D),F32),jax.ShapeDtypeStruct((16,piece,D),BF)],
        compiler_params=pltpu.CompilerParams(vmem_limit_bytes=VMEM_LIMIT,dimension_semantics=("arbitrary",)),
        name="assemble")(ffn,wings,gin.reshape(8,piece,D),block.reshape(16,piece,D))
    return up,down,out,qkv,grad,rows


DMA = pltpu.SemaphoreType.DMA
MESH = pl.DeviceIdType.MESH
INVMEM = pl.BlockSpec(memory_space=pltpu.VMEM)
ANYSPACE = pl.BlockSpec(memory_space=pl.ANY)


def place_ids():
    return lax.axis_index("ctx"), lax.axis_index("fsdp")


def meet(all_ranks, fsdp_partners):
    c, f = place_ids()
    sem = pltpu.get_barrier_semaphore()
    count = 0
    ranks = [(c + s) % 8 for s in range(1, 8)] if all_ranks else [c + 1 - 2 * (c % 2)]
    for rank in ranks:
        pl.semaphore_signal(sem, inc=1, device_id={"ctx": rank}, device_id_type=MESH)
        count += 1
    for s in fsdp_partners:
        other = (f + 2) % 4 if s == 2 else f + 1 - 2 * (f % 2) if s == 1 else 3 - f
        pl.semaphore_signal(sem, inc=1, device_id={"fsdp": other}, device_id_type=MESH)
        count += 1
    pl.semaphore_wait(sem, count)


def remote(src, dst, send, recv, where):
    return pltpu.make_async_remote_copy(src_ref=src, dst_ref=dst, send_sem=send, recv_sem=recv, device_id=where,
                                        device_id_type=MESH)


class ToUnit:
    def __init__(self, source, target, send, recv, local):
        self.source, self.target, self.send, self.recv, self.local = source, target, send, recv, local
        self.c, _ = place_ids()

    def message(self, s):
        c = self.c
        t = (c + s) % 8
        odd, last = t % 2, c // 7
        slot = (1 - odd) * c + odd * ((1 - last) * (6 - c) + last * 8)
        return remote(self.source(t // 2, odd), self.target(slot), self.send.at[s], self.recv.at[slot],
                      {"ctx": t - odd * last})

    def begin(self):
        for s in (1, 7, 3, 5, 2, 6, 4):
            self.message(s).start()

        @pl.when(self.c == 7)
        def _():
            self.message(0).start()

        @pl.when(self.c != 7)
        def _():
            self.own_safe().start()

    def begin_straight(self):
        for s in (2, 4, 6):
            self.message(s).start()

        @pl.when(self.c != 7)
        def _():
            self.own_safe().start()

    def begin_across(self):
        for s in (1, 3, 5, 7):
            self.message(s).start()

        @pl.when(self.c == 7)
        def _():
            self.message(0).start()

    def own_safe(self):
        c = self.c
        part = c % 2
        slot = (1 - part) * c + part * (6 - c + c // 7)
        return pltpu.make_async_copy(self.source(c // 2, part), self.target(slot), self.local)

    def finish(self):
        c = self.c
        part = c % 2

        @pl.when(c == 7)
        def _():
            self.message(0).wait_send()

        @pl.when(c != 7)
        def _():
            self.own_safe().wait()

        for s in range(1, 8):
            self.message(s).wait_send()
        own = (1 - part) * c + part * (6 - c)
        for slot in range(9):
            take = slot != own
            if slot > 6:
                take = take & (part == 0)

            @pl.when(take)
            def _():
                remote(self.target(slot), self.target(slot), self.send.at[0], self.recv.at[slot], {"ctx": c}).wait_recv()


class FromUnit:
    def __init__(self, source, target, send, recv, local):
        self.source, self.target, self.send, self.recv, self.local = source, target, send, recv, local
        self.c, _ = place_ids()

    def message(self, s):
        c = self.c
        part = c % 2
        rank = (c + s) % 8
        slot = (1 - part) * rank + part * (6 - rank + rank // 7)
        return remote(self.source(slot), self.target(c // 2, part), self.send.at[s], self.recv.at[c], {"ctx": rank})

    def extra(self):
        c = self.c
        seq = c // 2
        return remote(self.source(8), self.target(seq, 1), self.send.at[0], self.recv.at[2 * seq + 1], {"ctx": 7})

    def own(self):
        c = self.c
        part = c % 2
        slot = (1 - part) * c + part * (6 - c + c // 7)
        return pltpu.make_async_copy(self.source(slot), self.target(c // 2, part), self.local)

    def each(self, remote_op, own_op):
        c = self.c
        part = c % 2
        @pl.when(part == 0)
        def _():
            remote_op(self.extra())

        for s in (1, 7, 3, 5, 2, 6, 4):
            rank = (c + s) % 8

            @pl.when((part == 0) | (rank != 7))
            def _():
                remote_op(self.message(s))

        @pl.when(c != 7)
        def _():
            own_op(self.own())

    def begin_one(self, s):
        c = self.c

        @pl.when((c % 2 == 0) | ((c + s) % 8 != 7))
        def _():
            self.message(s).start()

    def begin_rest(self):
        c = self.c

        @pl.when(c % 2 == 0)
        def _():
            self.extra().start()

        @pl.when(c != 7)
        def _():
            self.own().start()

    def begin(self):
        self.each(lambda m: m.start(), lambda m: m.start())

    def finish(self):
        self.each(lambda m: m.wait_send(), lambda m: m.wait())
        c = self.c
        for block in range(8):
            @pl.when((c == 7) | (c != block))
            def _():
                ref = self.target(block // 2, block % 2)
                remote(ref, ref, self.send.at[0], self.recv.at[block], {"ctx": c}).wait_recv()


class GatherRows:
    def __init__(self, shard, full, send, recv, local, parts=1, share=True):
        c, f = place_ids()
        n = shard.shape[0]
        n2 = n // 2 if share else n
        m = n2 // parts
        h = c % 2 if share else 0
        sib, far, xn = f + 1 - 2 * (f % 2), (f + 2) % 4, c + 1 - 2 * (c % 2)
        diag = (sib + 2) % 4
        rows = lambda start, size: full.at[pl.ds(pl.multiple_of(start, 16), size)]
        same = lambda ref, i, where: remote(ref, ref, send.at[i], recv.at[i], where)
        mine = rows(f * n, n)
        self.copy = pltpu.make_async_copy(shard, mine, local)
        self.to_core = remote(shard, mine, send.at[0], recv.at[0], {"fsdp": sib})
        self.from_core = same(rows(sib * n, n), 0, {"fsdp": sib})
        self.to_far, self.from_far, self.to_x, self.from_x = [], [], [], []
        self.near_core, self.away_core, self.from_near, self.from_away = [], [], [], []
        for i in range(parts):
            a, b = h * n2 + i * m, (1 - h) * n2 + i * m
            near, away = rows(far * n + a, m), rows(far * n + b, m)
            k = 1 + 4 * i
            self.to_far.append(remote(shard.at[pl.ds(pl.multiple_of(a, 16), m)], rows(f * n + a, m), send.at[k], recv.at[k],
                                      {"fsdp": far}))
            self.from_far.append(same(near, k, {"fsdp": far}))
            self.near_core.append(same(near, k + 2, {"fsdp": sib}))
            self.from_near.append(same(rows(diag * n + a, m), k + 2, {"fsdp": sib}))
            if share:
                self.to_x.append(same(near, k + 1, {"ctx": xn}))
                self.from_x.append(same(away, k + 1, {"ctx": xn}))
                self.away_core.append(same(away, k + 3, {"fsdp": sib}))
                self.from_away.append(same(rows(diag * n + b, m), k + 3, {"fsdp": sib}))

    def begin(self):
        for copy in self.to_far:
            copy.start()
        self.to_core.start()
        self.copy.start()

    def relay_far(self, i=0):
        self.from_far[i].wait_recv()
        if self.to_x:
            self.to_x[i].start()
        self.near_core[i].start()

    def relay_x(self, i=0):
        self.from_x[i].wait_recv()
        self.away_core[i].start()

    def finish(self):
        self.copy.wait()
        for copy in [self.to_core] + self.to_far + self.to_x + self.near_core + self.away_core:
            copy.wait_send()
        for copy in [self.from_core] + self.from_near + self.from_away:
            copy.wait_recv()


class Reduce:
    def __init__(self, rows, send, recv, across=False, grad=None, pair=None, far=None, total=None, over=None, final=None):
        c, f = place_ids()
        self.send, self.recv, self.across = send, recv, across
        self.grad, self.pair, self.far, self.total, self.over, self.final = grad, pair, far, total, over, final
        self.core, self.y, self.x = f % 2, f // 2, c % 2
        z1, z2 = (c // 2) % 2, c // 4
        self.sib, self.far_id = {"fsdp": f + 1 - 2 * self.core}, {"fsdp": (f + 2) % 4}
        self.xn, self.z1n, self.z2n = {"ctx": c + 1 - 2 * self.x}, {"ctx": c + 2 - 4 * z1}, {"ctx": c + 4 - 8 * z2}
        half, quarter = rows // 2, rows // 4
        self.rows = rows
        self.levels = [(z1 * half, (1 - z1) * half, half, rows, self.z1n)]
        base = z1 * half
        self.levels.append((base + z2 * quarter, base + (1 - z2) * quarter, quarter, rows + half, self.z2n))

    def at(self, ref, start, size):
        return ref.at[self.x, pl.ds(pl.multiple_of(start, 16), size)]

    def copy(self, stage):
        x, y = self.x, self.y
        if stage == 0:
            source, target, where = self.grad.at[1 - self.core], self.pair, self.sib
        elif stage == 1 and self.across:
            source, target, where = self.pair.at[:, 1 - x], self.far, self.xn
        elif stage == 1:
            source, target, where = self.pair.at[1 - y], self.far, self.far_id
        elif stage == 2 and self.across:
            source, target, where = self.pair.at[1 - y, x], self.over.at[pl.ds(0, self.rows)], self.far_id
        elif stage == 2:
            source, target, where = self.total.at[1 - x], self.over.at[pl.ds(0, self.rows)], self.xn
        elif stage < 5:
            keep, give, size, offset, where = self.levels[stage - 3]
            source, target = self.at(self.total, give, size), self.over.at[pl.ds(offset, size)]
        elif stage < 7:
            keep, give, size, offset, where = self.levels[6 - stage]
            source = target = self.at(self.final, keep, size)
        else:
            source, target, where = self.final.at[x], self.final.at[x], self.xn
        return remote(source, target, self.send.at[stage], self.recv.at[stage], where)

    def start(self, stage):
        self.copy(stage).start()

    def take(self, stage):
        x, y = self.x, self.y
        if stage < 5:
            self.copy(stage).wait_recv()
        if stage == 0:
            self.pair[...] = self.pair[...] + self.grad[self.core]
        elif stage == 1 and self.across:
            for i in range(2):
                self.pair[i, x] = self.pair[i, x] + self.far[i]
        elif stage == 1:
            self.total[...] = self.far[...] + self.pair[y]
        elif stage == 2 and self.across:
            self.total[x] = self.pair[y, x] + self.over[pl.ds(0, self.rows)]
        elif stage == 2:
            self.total[x] = self.total[x] + self.over[pl.ds(0, self.rows)]
        elif stage < 5:
            keep, give, size, offset, where = self.levels[stage - 3]
            into = self.at(self.final if stage == 4 else self.total, keep, size)
            into[...] = self.at(self.total, keep, size)[...] + self.over[pl.ds(offset, size)]
        elif stage < 7:
            keep, give, size, offset, where = self.levels[6 - stage]
            ref = self.at(self.final, give, size)
            remote(ref, ref, self.send.at[stage], self.recv.at[stage], where).wait_recv()
        else:
            ref = self.final.at[1 - x]
            remote(ref, ref, self.send.at[7], self.recv.at[7], self.xn).wait_recv()

    def sent(self, *stages):
        for stage in stages:
            self.copy(stage).wait_send()


TILE = 768
WING = 576


def assemble_kernel(ffn, wings, gin, block, up_o, down_o, out_o, qkv_o, gin_o, block_o):
    i = pl.program_id(0)
    tile = lambda r: ffn[0, r // TILE, r % TILE:r % TILE + 64].astype(F32)
    for s in range(4):
        for r in range(0, 192, 64):
            up_o[r:r + 64, pl.ds(pl.multiple_of((s * STEPS + i) * 128, 128), 128)] = tile(s * 192 + r)
    for t in range(6):
        for r in range(0, 128, 64):
            down_o[r:r + 64, t * 128:(t + 1) * 128] = tile(768 + t * 128 + r)
    gin_o[...] = gin[...].astype(F32)
    block_o[...] = block[...]

    @pl.when(i == 0)
    def _():
        def strip(ref, k, r):
            row = k * 192 + r
            return ref[row // WING, row % WING:row % WING + 64].astype(F32)

        for r in range(0, 192, 64):
            for t in range(6):
                out_o[r:r + 64, t * 128:(t + 1) * 128] = strip(wings.at[0], t, r)
                source = wings.at[1 + t // 2]
                for w in range(3):
                    qkv_o[r:r + 64, w * D + t * 128:w * D + (t + 1) * 128] = strip(source, t % 2 * 3 + w, r)


def rope_constant(half):
    position = np.arange(2 * half, dtype=np.float32)
    frequency = np.float32(10000.0) ** (-(np.arange(HEAD // 2, dtype=np.float32) * np.float32(2.0)) / np.float32(HEAD))
    angles = (position[:, None] * frequency[None, :]).astype(np.float64)
    cosine, sine = np.cos(angles), np.sin(angles)
    table = np.concatenate([np.tile(cosine, (1, 4)), np.tile(np.concatenate([-sine, sine], axis=1), (1, 2))], axis=1)
    return jnp.asarray(table.reshape(2, half, 4 * HEAD).astype(np.float32))


def even_body(clean_in, segments, noise, mask_embed, norm1_gain, qkv_weight, out_weight, norm2_gain, up_weight, up_bias,
              down_weight, down_bias, out_grad):
    place = lax.axis_index("fsdp")
    piece = clean_in.shape[2]
    half = 9 * piece
    width = mask_embed.shape[0]
    line = lax.broadcasted_iota(jnp.int32, (8, 8, piece), 1)
    meta = jnp.where(line == 0, segments.reshape(8, 1, piece), noise.reshape(8, 1, piece))
    row = lax.broadcasted_iota(jnp.int32, (16, width), 0)
    small = jnp.zeros((16, width), BF)
    for i, vector in enumerate((mask_embed, norm1_gain, norm2_gain, down_bias)):
        small = jnp.where(row == i, vector[None], small)
    for i in range(4):
        small = jnp.where(row == 4 + i, up_bias[i * width:(i + 1) * width][None], small)
    q, k, v, mixed, lse, resid, mask, seg_col, seg_row, vectors, up_shift, qkv_full, out_full, up_full, down_full, cotangent, clean = fwd_attn(
        clean_in, meta, out_grad, rope_constant(half), qkv_weight, out_weight, up_weight, down_weight, small)
    clean = clean.reshape(half, D)
    up_shift_grad, down_shift_grad, gain_two_grad, grad_resid, block_out, tile_pair, tile_total, tile_final = ffn(
        resid, vectors, up_full, up_shift, down_full, cotangent, out_grad)
    tiles, wings, input_grad, sums = bwd_attn(
        clean, mask, seg_col, seg_row, vectors, grad_resid, q, k, v, mixed, lse, qkv_full, out_full, rope_constant(half),
        (gain_two_grad, down_shift_grad, up_shift_grad), tile_pair, tile_total, tile_final)
    up_sum, down_sum, out_sum, qkv_sum, input_grad, block_out = assemble(tiles, wings, input_grad, block_out)
    input_grad = input_grad.reshape(clean_in.shape)
    block_out = block_out.reshape(out_grad.shape)
    sums = sums.reshape(-1)
    own = [lax.dynamic_slice_in_dim(sums, i * D + place * width, width) for i in range(4)]
    own_up = lax.dynamic_slice_in_dim(sums, 4 * D + place * (FF // 4), FF // 4)
    return (block_out, input_grad, own[0], own[1], qkv_sum, out_sum, own[2], up_sum, own_up, down_sum, own[3])


def choose_body(axes, *arrays):
    even = axes["ctx"] == 8 and axes["fsdp"] == 4 and arrays[0].shape[0] == 4
    return (even_body if even else general_body)(*arrays)


def solution(mesh):
    placed = (
        P("fsdp", None, "ctx", None),
        P("fsdp", None, "ctx"),
        P("fsdp", None, "ctx"),
        P("fsdp"),
        P("fsdp"),
        P("fsdp", None),
        P("fsdp", None),
        P("fsdp"),
        P("fsdp", None),
        P("fsdp"),
        P("fsdp", None),
        P("fsdp"),
        P("fsdp", None, None, "ctx", None),
    )
    return jax.shard_map(
        partial(choose_body, dict(mesh.shape)),
        mesh=mesh,
        in_specs=placed,
        out_specs=(
            P("fsdp", None, None, "ctx", None),
            P("fsdp", None, "ctx", None),
            P("fsdp"),
            P("fsdp"),
            P("fsdp", None),
            P("fsdp", None),
            P("fsdp"),
            P("fsdp", None),
            P("fsdp"),
            P("fsdp", None),
            P("fsdp"),
        ),
        check_vma=False,
    )
```

```python
from functools import partial

import jax
import jax.numpy as jnp
import numpy as np
from jax import lax
from jax.experimental import pallas as pl
from jax.experimental.pallas import tpu as pltpu
from jax.sharding import PartitionSpec as P

D = 768
HEADS = 12
HEAD = 64
FF = 3072
BLK = 16


EPS = 1e-05
together = 4


def normalize(values):
    centre = values - jnp.mean(values, axis=-1, keepdims=True)
    scale = lax.rsqrt(jnp.mean(centre * centre, axis=-1, keepdims=True) + EPS)
    return (centre * scale, scale)


def norm_back(grad_in, normed, scale):
    centred = grad_in - jnp.mean(grad_in, axis=-1, keepdims=True)
    return scale * (centred - normed * jnp.mean(grad_in * normed, axis=-1, keepdims=True))


def rope_tables(positions):
    half_head = HEAD // 2
    frequency = 10000.0 ** (-(jnp.arange(half_head, dtype=jnp.float32) * 2.0) / HEAD)
    angles = positions.astype(jnp.float32)[:, None] * frequency[None, :]
    return (jnp.cos(angles), jnp.sin(angles))


def rotate(values, cos_part, sin_part, reverse):
    count = values.shape[0]
    heads = values.reshape(count, HEADS, HEAD)
    half_head = HEAD // 2
    leading = heads[..., :half_head]
    trailing = heads[..., half_head:]
    cosine = cos_part[:, None, :]
    sine_part = sin_part[:, None, :]
    if reverse:
        parts = [leading * cosine + trailing * sine_part, trailing * cosine - leading * sine_part]
    else:
        parts = [leading * cosine - trailing * sine_part, trailing * cosine + leading * sine_part]
    return jnp.concatenate(parts, axis=-1).reshape(count, D)


def split_heads(values):
    count = values.shape[0]
    return values.reshape(count, HEADS // together, together * HEAD).transpose(1, 0, 2)


def join_heads(values):
    groups, count, width = values.shape
    return values.transpose(1, 0, 2).reshape(count, groups * width)


def allowed_pairs(query_copy, query_block, query_doc, key_copy, key_block, key_doc):
    same_doc = query_doc[:, None] == key_doc[None, :]
    query_noisy = (query_copy == 0)[:, None]
    key_noisy = (key_copy == 0)[None, :]
    query_column = query_block[:, None]
    key_row = key_block[None, :]
    inner = query_noisy & key_noisy & (key_row == query_column)
    earlier = query_noisy & ~key_noisy & (key_row < query_column)
    causal = ~query_noisy & ~key_noisy & (key_row <= query_column)
    return same_doc & (inner | earlier | causal)


def masked_scores(query_group, key_group, allowed):
    query_heads = query_group.reshape(query_group.shape[0], together, HEAD)
    key_heads = key_group.reshape(key_group.shape[0], together, HEAD)
    raw = jnp.einsum(
        "qhd,khd->hqk", query_heads, key_heads, preferred_element_type=jnp.float32
    ) * HEAD ** (-0.5)
    return (jnp.where(allowed[None], raw, -1e30), query_heads, key_heads)


def group_forward(items, allowed):
    query_group, key_group, value_group = items
    count = query_group.shape[0]
    scores, query_heads, key_heads = masked_scores(query_group, key_group, allowed)
    value_heads = value_group.reshape(value_group.shape[0], together, HEAD)
    top = jnp.max(scores, axis=-1, keepdims=True)
    weights = jnp.exp(scores - top)
    total = jnp.sum(weights, axis=-1, keepdims=True)
    probs = (weights / total).astype(jnp.bfloat16)
    mixed = jnp.einsum("hqk,khd->qhd", probs, value_heads, preferred_element_type=jnp.float32)
    return (mixed.reshape(count, together * HEAD), (top + jnp.log(total))[..., 0])


def group_backward(items, allowed, tail):
    query_group, key_group, value_group, grad_group, log_total = items
    count = query_group.shape[0]
    key_count = key_group.shape[0]
    scores, query_heads, key_heads = masked_scores(query_group, key_group, allowed)
    value_heads = value_group.reshape(key_count, together, HEAD)
    grad_heads = grad_group.reshape(count, together, HEAD)
    probs = jnp.exp(scores - log_total[..., None])
    prob_grad = jnp.einsum(
        "qhd,khd->hqk", grad_heads, value_heads, preferred_element_type=jnp.float32
    )
    centre = jnp.sum(probs * prob_grad, axis=-1, keepdims=True)
    score_grad = (probs * (prob_grad - centre)).astype(jnp.bfloat16)
    query_grad = jnp.einsum(
        "hqk,khd->qhd", score_grad, key_heads, preferred_element_type=jnp.float32
    ) * HEAD ** (-0.5)
    tail_probs = probs.astype(jnp.bfloat16)
    value_grad = jnp.einsum(
        "hqk,qhd->khd", tail_probs, grad_heads, preferred_element_type=jnp.float32
    )
    key_grad = jnp.einsum(
        "hqk,qhd->khd", score_grad, query_heads, preferred_element_type=jnp.float32
    ) * HEAD ** (-0.5)
    return (
        query_grad.reshape(count, together * HEAD),
        key_grad.reshape(tail, together * HEAD),
        value_grad.reshape(tail, together * HEAD),
        centre[..., 0],
    )


def reduce_grads(grads):
    shards = (
        lax.psum_scatter(grads[0], "fsdp", scatter_dimension=0, tiled=True),
        lax.psum_scatter(grads[1], "fsdp", scatter_dimension=0, tiled=True),
        lax.psum_scatter(grads[2], "fsdp", scatter_dimension=0, tiled=True),
        lax.psum_scatter(grads[3], "fsdp", scatter_dimension=0, tiled=True),
        lax.psum_scatter(grads[4], "fsdp", scatter_dimension=0, tiled=True),
        lax.psum_scatter(grads[5], "fsdp", scatter_dimension=0, tiled=True),
        lax.psum_scatter(grads[6], "fsdp", scatter_dimension=0, tiled=True),
        lax.psum_scatter(grads[7], "fsdp", scatter_dimension=0, tiled=True),
        lax.psum_scatter(grads[8], "fsdp", scatter_dimension=0, tiled=True),
    )
    return lax.psum(
        (
            shards[0],
            shards[1],
            shards[2],
            shards[3],
            shards[4],
            shards[5],
            shards[6],
            shards[7],
            shards[8],
        ),
        "ctx",
    )


def add_tuples(left_items, right_items):
    return tuple((left_item + right_item for left_item, right_item in zip(left_items, right_items)))


def general_body(
    clean_in,
    segments,
    noise,
    mask_embed,
    norm1_gain,
    qkv_weight,
    out_weight,
    norm2_gain,
    up_weight,
    up_bias,
    down_weight,
    down_bias,
    out_grad,
):
    qkv_full, out_full, gain_low, embed_low = (
        lax.all_gather(qkv_weight, "fsdp", axis=0, tiled=True),
        lax.all_gather(out_weight, "fsdp", axis=0, tiled=True),
        lax.all_gather(norm1_gain, "fsdp", axis=0, tiled=True),
        lax.all_gather(mask_embed, "fsdp", axis=0, tiled=True),
    )
    up_full, up_low, down_full, down_low, gain_two_low = (
        lax.all_gather(up_weight, "fsdp", axis=0, tiled=True),
        lax.all_gather(up_bias, "fsdp", axis=0, tiled=True),
        lax.all_gather(down_weight, "fsdp", axis=0, tiled=True),
        lax.all_gather(down_bias, "fsdp", axis=0, tiled=True),
        lax.all_gather(norm2_gain, "fsdp", axis=0, tiled=True),
    )
    gain_one = gain_low.astype(jnp.float32)
    gain_two = gain_two_low.astype(jnp.float32)
    embed_row = embed_low.astype(jnp.float32)
    up_shift = up_low.astype(jnp.float32)
    down_shift = down_low.astype(jnp.float32)
    micro_count = clean_in.shape[0]
    piece = clean_in.shape[2]
    local_rows = 2 * piece
    ctx_count = lax.axis_size("ctx")
    ctx_rank = lax.axis_index("ctx")
    span = jnp.arange(piece, dtype=jnp.int32)
    local_pos = jnp.concatenate(
        [ctx_rank * piece + span, (2 * ctx_count - 1 - ctx_rank) * piece + span]
    )
    ranks = jnp.arange(ctx_count, dtype=jnp.int32)[:, None]
    far_pos = jnp.concatenate(
        [ranks * piece + span[None, :], (2 * ctx_count - 1 - ranks) * piece + span[None, :]], axis=1
    ).reshape(-1)
    seq_len = ctx_count * local_rows
    cos_part, sin_part = rope_tables(jnp.concatenate([local_pos, local_pos]))
    query_copy = jnp.concatenate(
        [jnp.zeros((local_rows,), jnp.int32), jnp.ones((local_rows,), jnp.int32)]
    )
    key_copy = jnp.concatenate(
        [jnp.ones((seq_len,), jnp.int32), jnp.zeros((local_rows,), jnp.int32)]
    )
    query_block = jnp.concatenate([local_pos, local_pos]) // BLK
    key_block = jnp.concatenate([far_pos, local_pos]) // BLK
    full_shapes = ((D,), (D,), (D, 3 * D), (D, D), (D,), (D, FF), (FF,), (FF, D), (D,))
    totals = tuple((jnp.zeros(shape_item, jnp.float32) for shape_item in full_shapes))
    tail = seq_len + local_rows
    outputs = []
    input_grads = []
    for micro_step in range(micro_count):
        clean_rows = clean_in[micro_step].reshape(local_rows, D).astype(jnp.float32)
        noise_rows = noise[micro_step].reshape(-1)
        masked_rows = noise_rows[:, None] == 1
        doc_local = segments[micro_step].reshape(-1).astype(jnp.float32)
        noisy_rows = jnp.where(masked_rows, embed_row[None, :], clean_rows)
        stacked = jnp.concatenate([noisy_rows, clean_rows], axis=0)
        normed_one, scale_one = normalize(stacked)
        h_one = (normed_one * gain_one).astype(jnp.bfloat16)
        projected = jnp.dot(h_one, qkv_full, preferred_element_type=jnp.float32)
        queries = rotate(projected[:, :D], cos_part, sin_part, False).astype(jnp.bfloat16)
        keys = rotate(projected[:, D : 2 * D], cos_part, sin_part, False).astype(jnp.bfloat16)
        values = projected[:, 2 * D :].astype(jnp.bfloat16)
        far_keys, far_values, far_docs = (
            lax.all_gather(keys[local_rows:], "ctx", axis=0, tiled=True),
            lax.all_gather(values[local_rows:], "ctx", axis=0, tiled=True),
            lax.all_gather(doc_local.astype(jnp.bfloat16), "ctx", axis=0, tiled=True),
        )
        key_all = jnp.concatenate([far_keys, keys[:local_rows]], axis=0)
        value_all = jnp.concatenate([far_values, values[:local_rows]], axis=0)
        query_doc = jnp.concatenate([doc_local, doc_local])
        key_doc = jnp.concatenate([far_docs.astype(jnp.float32), doc_local])
        allowed = allowed_pairs(query_copy, query_block, query_doc, key_copy, key_block, key_doc)
        query_groups = split_heads(queries)
        key_groups = split_heads(key_all)
        value_groups = split_heads(value_all)
        mixed_groups, log_totals = lax.map(
            partial(group_forward, allowed=allowed), (query_groups, key_groups, value_groups)
        )
        mixed = join_heads(mixed_groups).astype(jnp.bfloat16)
        resid = stacked + jnp.dot(mixed, out_full, preferred_element_type=jnp.float32)
        normed_two, scale_two = normalize(resid)
        h_two = (normed_two * gain_two).astype(jnp.bfloat16)
        hidden = jnp.dot(h_two, up_full, preferred_element_type=jnp.float32) + up_shift
        active = jax.nn.gelu(hidden, approximate=True).astype(jnp.bfloat16)
        result = resid + jnp.dot(active, down_full, preferred_element_type=jnp.float32) + down_shift
        outputs.append(result.astype(jnp.bfloat16).reshape(2, 2, piece, D))
        cotangent = out_grad[micro_step].reshape(2 * local_rows, D).astype(jnp.float32)
        grad_out = cotangent.astype(jnp.bfloat16)
        down_grad = jnp.einsum("rf,rd->fd", active, grad_out, preferred_element_type=jnp.float32)
        down_shift_grad = jnp.sum(grad_out.astype(jnp.float32), axis=0)
        grad_active = jnp.einsum(
            "rd,fd->rf", grad_out, down_full, preferred_element_type=jnp.float32
        )
        unused, gelu_back = jax.vjp(partial(jax.nn.gelu, approximate=True), hidden)
        grad_hidden = gelu_back(grad_active)[0].astype(jnp.bfloat16)
        up_grad = jnp.einsum("rd,rf->df", h_two, grad_hidden, preferred_element_type=jnp.float32)
        up_shift_grad = jnp.sum(grad_hidden.astype(jnp.float32), axis=0)
        grad_h_two = jnp.einsum(
            "rf,df->rd", grad_hidden, up_full, preferred_element_type=jnp.float32
        )
        gain_two_grad = jnp.sum(grad_h_two * normed_two, axis=0)
        grad_resid = cotangent + norm_back(grad_h_two * gain_two, normed_two, scale_two)
        grad_attn = grad_resid.astype(jnp.bfloat16)
        out_grad_full = jnp.einsum(
            "rd,re->de", mixed, grad_attn, preferred_element_type=jnp.float32
        )
        grad_mixed = jnp.einsum(
            "re,de->rd", grad_attn, out_full, preferred_element_type=jnp.float32
        ).astype(jnp.bfloat16)
        query_grads, key_grads, value_grads, centres = lax.map(
            partial(group_backward, allowed=allowed, tail=tail),
            (query_groups, key_groups, value_groups, split_heads(grad_mixed), log_totals),
        )
        query_grad = join_heads(query_grads)
        key_grad_all = join_heads(key_grads)
        value_grad_all = join_heads(value_grads)
        key_mine, value_mine = (
            lax.psum_scatter(key_grad_all[:seq_len], "ctx", scatter_dimension=0, tiled=True),
            lax.psum_scatter(value_grad_all[:seq_len], "ctx", scatter_dimension=0, tiled=True),
        )
        key_grad = jnp.concatenate([key_grad_all[seq_len:], key_mine], axis=0)
        value_grad = jnp.concatenate([value_grad_all[seq_len:], value_mine], axis=0)
        grad_proj = jnp.concatenate(
            [
                rotate(query_grad, cos_part, sin_part, True),
                rotate(key_grad, cos_part, sin_part, True),
                value_grad,
            ],
            axis=1,
        ).astype(jnp.bfloat16)
        qkv_grad = jnp.einsum("rd,re->de", h_one, grad_proj, preferred_element_type=jnp.float32)
        grad_h_one = jnp.einsum(
            "re,de->rd", grad_proj, qkv_full, preferred_element_type=jnp.float32
        )
        gain_one_grad = jnp.sum(grad_h_one * normed_one, axis=0)
        grad_rows = grad_resid + norm_back(grad_h_one * gain_one, normed_one, scale_one)
        grad_noisy = grad_rows[:local_rows]
        input_grads.append(
            (grad_rows[local_rows:] + jnp.where(masked_rows, 0.0, grad_noisy)).reshape(2, piece, D)
        )
        embed_grad = jnp.sum(jnp.where(masked_rows, grad_noisy, 0.0), axis=0)
        step_grads = (
            embed_grad,
            gain_one_grad,
            qkv_grad,
            out_grad_full,
            gain_two_grad,
            up_grad,
            up_shift_grad,
            down_grad,
            down_shift_grad,
        )
        totals = add_tuples(totals, step_grads)
    reduced = reduce_grads(totals)
    block_out = jnp.stack(outputs)
    input_grad = jnp.stack(input_grads)
    return (
        block_out,
        input_grad,
        reduced[0],
        reduced[1],
        reduced[2],
        reduced[3],
        reduced[4],
        reduced[5],
        reduced[6],
        reduced[7],
        reduced[8],
    )


PAIR=2*HEAD; PAIRS=D//PAIR
NEG=-1e30
VMEM_LIMIT=60<<20
F32=jnp.float32; BF=jnp.bfloat16

def dot_nn(a,b): return lax.dot_general(a,b,(((1,),(0,)),((),())),preferred_element_type=F32)
def dot_nt(a,b): return lax.dot_general(a,b,(((1,),(1,)),((),())),preferred_element_type=F32)
def dot_tn(a,b): return lax.dot_general(a,b,(((0,),(0,)),((),())),preferred_element_type=F32)

def tiles_of(half):
    return [(s,min(128,half-s)) for s in range(0,half,128)]

def norm_rows(rows):
    centre=rows-jnp.mean(rows,axis=-1,keepdims=True)
    scale=lax.rsqrt(jnp.mean(centre*centre,axis=-1,keepdims=True)+EPS)
    return centre*scale, scale

def swap_halves(z):
    lane=lax.broadcasted_iota(jnp.int32,z.shape,1)
    low=(lane & (HEAD-1)) < HEAD//2
    return jnp.where(low,pltpu.roll(z,PAIR-HEAD//2,1),pltpu.roll(z,HEAD//2,1))

def head_stack(z):
    lane=lax.broadcasted_iota(jnp.int32,z.shape,1)
    first=lane<HEAD
    zero=jnp.zeros_like(z)
    return jnp.concatenate([jnp.where(first,z,zero),jnp.where(first,zero,z)],axis=0)

def head_merge(z):
    n=z.shape[0]//2
    lane=lax.broadcasted_iota(jnp.int32,(n,z.shape[1]),1)
    return jnp.where(lane<HEAD,z[:n],z[n:])

def layer_rows(xc_ref,noise_ref,emb_ref):
    clean=xc_ref[...].astype(F32)
    noisy=jnp.where(noise_ref[...]==1,emb_ref[...].astype(F32),clean)
    return noisy,clean

def fwd_attn_kernel(half,xc,noise,segc,segr,small,wqkv,wout,trig,
                    q_o,k_o,v_o,mix_o,lse_o,x1_o,h_s,bias_s,self_s,mix_s):
    p=pl.program_id(0)
    tiles=tiles_of(half)
    @pl.when(p==0)
    def _():
        g=vector_row(small,1)
        clean=jnp.concatenate([xc[i] for i in range(9)],axis=0).astype(F32)
        noisy=jnp.where(noise[...]==1,vector_row(small,0),clean)
        for c,rows in enumerate((noisy,clean)):
            x1_o[c*half:(c+1)*half]=rows
            n,_=norm_rows(rows)
            h_s[c*half:(c+1)*half]=(n*g).astype(BF)
        for s,m in tiles:
            n=s+m
            qb=(lax.broadcasted_iota(jnp.int32,(m,n),0)+s)//BLK
            kb=lax.broadcasted_iota(jnp.int32,(m,n),1)//BLK
            same=segc[s:n]==segr[:,:n]
            bias_s[0,s:n,:n]=jnp.where(same&(kb<qb),0.0,NEG)
            bias_s[1,s:n,:n]=jnp.where(same&(kb<=qb),0.0,NEG)
            qb=lax.broadcasted_iota(jnp.int32,(m,m),0)//BLK
            kb=lax.broadcasted_iota(jnp.int32,(m,m),1)//BLK
            same=segc[s:n]==segr[:,s:n]
            self_s[s:n,:m]=jnp.where(same&(kb==qb),0.0,NEG)
    h=h_s[...]
    cs=jnp.concatenate([trig[:,:PAIR]]*2,axis=0)
    sn=jnp.concatenate([trig[:,PAIR:]]*2,axis=0)
    block=lambda i: wqkv[:,pl.ds(pl.multiple_of(i*D+p*PAIR,PAIR),PAIR)]
    zq=dot_nn(h,jnp.concatenate([block(0),block(1)],axis=1))
    z=zq[:,:PAIR]; q_o[...]=((z*cs+swap_halves(z)*sn).astype(BF)*BF(HEAD**-0.5)).astype(BF)
    z=zq[:,PAIR:]; k_o[...]=(z*cs+swap_halves(z)*sn).astype(BF)
    v_o[...]=dot_nn(h,block(2)).astype(BF)
    idx=0
    for s,m in tiles:
        n=s+m
        for c in (0,1):
            qs=head_stack(q_o[c*half+s:c*half+n])
            kc=k_o[half:half+n]; vc=v_o[half:half+n]
            sc=dot_nt(qs,kc).reshape(2,m,n)+bias_s[c,s:n,:n][None]
            top=jnp.max(sc,axis=-1,keepdims=True)
            if c==0:
                ss=dot_nt(qs,k_o[s:n]).reshape(2,m,m)+self_s[s:n,:m][None]
                top=jnp.maximum(top,jnp.max(ss,axis=-1,keepdims=True))
            w=jnp.exp(sc-top); tot=jnp.sum(w,axis=-1,keepdims=True)
            o=dot_nn(w.astype(BF).reshape(2*m,n),vc)
            if c==0:
                w2=jnp.exp(ss-top); tot=tot+jnp.sum(w2,axis=-1,keepdims=True)
                o=o+dot_nn(w2.astype(BF).reshape(2*m,m),v_o[s:n])
            tot=tot.reshape(2*m,1)
            o=o*(1.0/tot)
            mx=head_merge(o).astype(BF)
            mix_o[c*half+s:c*half+n]=mx
            mix_s[p,c*half+s:c*half+n]=mx
            lse=top.reshape(2*m,1)+jnp.log(tot)
            lse_o[0,idx:idx+1,:2*m]=jnp.broadcast_to(lse,(2*m,128)).T[0:1]
            idx+=1
    @pl.when(p==pl.num_programs(0)-1)
    def _():
        full=jnp.concatenate([mix_s[i] for i in range(PAIRS)],axis=1)
        x1_o[...]=x1_o[...]+dot_nn(full,wout[...])

def whole(shape): return pl.BlockSpec(shape,lambda *i:(0,)*len(shape))

def vector_row(small,i):
    return jnp.concatenate([small[f,i:i+1,:D//4] for f in range(4)],axis=1).astype(F32)

def fwd_attn_comm_kernel(half,*refs):
    clean,meta,gout,trig,qkv,out,up,down,small=refs[:9]
    q_o,k_o,v_o,mix_o,lse_o,x1_o,noise_o,segc_o,segr_o,vec_o,bias_o,qkv_o,out_o,up_o,down_o,cot_o,clean_o=refs[9:26]
    h_s,bias_s,self_s,mix_s,clean_s,meta_s,small_s,qkv_s,out_s,trig_s=refs[26:36]
    a_send,a_recv,m_send,m_recv,c_send,c_recv,w_send,w_recv,s_send,s_recv,local=refs[36:]
    p=pl.program_id(0)
    c,f=place_ids()
    piece=half//9
    weight=lambda i,shard,full,parts: GatherRows(shard,full,w_send.at[i],w_recv.at[i],local.at[i],parts)
    w_qkv,w_out,w_up,w_down=weight(0,qkv,qkv_s,3),weight(1,out,out_s,1),weight(2,up,up_o,3),GatherRows(down,down_o,w_send.at[3],w_recv.at[3],local.at[3],3,False)
    rows=ToUnit(lambda q,h:clean.at[q,h],lambda t:clean_s.at[t],a_send,a_recv,local.at[4])
    notes=ToUnit(lambda q,h:meta.at[2*q+h],lambda t:meta_s.at[t],m_send,m_recv,local.at[5])
    grads=[ToUnit(lambda q,h:gout.at[q,0,h],lambda t:cot_o.at[t],c_send,c_recv,local.at[6])]
    copies=[pltpu.make_async_copy(qkv_s,qkv_o,local.at[8]),pltpu.make_async_copy(out_s,out_o,local.at[9]),pltpu.make_async_copy(clean_s,clean_o,local.at[10])]
    others=[f+1-2*(f%2),(f+2)%4,3-f]
    @pl.when(p==0)
    def _():
        meet(True,(1,2,3))
        w_qkv.begin()
        notes.begin()
        rows.begin()
        sends=[remote(small,small_s.at[f],s_send.at[i],s_recv.at[i],{"fsdp":other}) for i,other in enumerate(others)]
        for d in sends: d.start()
        own=pltpu.make_async_copy(small,small_s.at[f],local.at[11])
        own.start()
        table=pltpu.make_async_copy(trig.at[c%2],trig_s,local.at[12])
        table.start()
        w_out.begin()
        w_up.begin()
        w_down.begin()
        for i in range(3): w_qkv.relay_far(i)
        @pl.when(c%2==1)
        def _():
            clean_s[7:9]=jnp.zeros((2,)+clean_s.shape[1:],BF)
            line=lax.broadcasted_iota(jnp.int32,(2,)+meta_s.shape[1:],1)
            meta_s[7:9]=jnp.where(line==0,-1,0)
            pad=pltpu.make_async_copy(clean_s.at[pl.ds(7,2)],cot_o.at[pl.ds(7,2)],local.at[13])
            pad.start()
            pad.wait()
        for i in range(3): w_qkv.relay_x(i)
        for r in grads: r.begin_straight()
        own.wait()
        table.wait()
        for i,other in enumerate(others):
            sends[i].wait_send()
            remote(small_s.at[other],small_s.at[other],s_send.at[i],s_recv.at[i],{"fsdp":other}).wait_recv()
        notes.finish()
        note=lambda i: jnp.concatenate([meta_s[i,0:1],meta_s[i,1:2]],axis=1).astype(F32)
        for i in range(9):
            t=jnp.broadcast_to(note(i),(128,128)).T
            segc_o[i*piece:(i+1)*piece]=t[:piece,0:1]
            noise_o[i*piece:(i+1)*piece]=t[piece:,0:1].astype(jnp.int32)
        for i in range(5):
            segr_o[:,i*128:(i+1)*128]=jnp.concatenate([meta_s[2*i,0:1],meta_s[min(2*i+1,8),0:1]],axis=1).astype(F32)
        for i in range(4): vec_o[i:i+1]=vector_row(small_s,(2,3,0,1)[i])
        for g in range(4): bias_o[:,g*768:(g+1)*768]=jnp.concatenate([small_s[g,4+i:5+i] for i in range(4)],axis=1).astype(F32)
        rows.finish()
        w_qkv.finish()
        copies[0].start()
        copies[2].start()
    fwd_attn_kernel(half,clean_s,noise_o,segc_o,segr_o,small_s,qkv_s,out_s,trig_s,q_o,k_o,v_o,mix_o,lse_o,x1_o,h_s,bias_s,self_s,mix_s)
    def at(i,*ops):
        @pl.when(p==i)
        def _():
            for op in ops: op()
    at(0,w_out.relay_far,*[partial(w_up.relay_far,i) for i in range(2)])
    at(1,w_out.relay_x,partial(w_up.relay_far,2),partial(w_up.relay_x,0),grads[0].begin_across)
    at(2,w_out.finish,copies[1].start,partial(w_up.relay_x,1),partial(w_down.relay_far,0))
    at(3,partial(w_up.relay_x,2),partial(w_down.relay_far,1))
    at(4,partial(w_down.relay_far,2))
    @pl.when(p==pl.num_programs(0)-1)
    def _():
        for w in (w_up,w_down): w.finish()
        for r in grads: r.finish()
        for d in copies: d.wait()

def whole(shape): return pl.BlockSpec(shape,lambda *i:(0,)*len(shape))
def once(shape): return pl.BlockSpec(shape,lambda *i:(0,)*len(shape),pipeline_mode=pl.Buffered(1))

def fwd_attn(clean,meta,gout,trig,qkv,out,up,down,small):
    piece=clean.shape[2]; half=9*piece; R=2*half
    nt=len(tiles_of(half))*2; ntp=-(-nt//8)*8
    rows=pl.BlockSpec((R,PAIR),lambda p:(0,p))
    sds=jax.ShapeDtypeStruct
    return pl.pallas_call(partial(fwd_attn_comm_kernel,half),grid=(PAIRS,),
        in_specs=[ANYSPACE]*4+[once(a.shape) for a in (qkv,out,up,down,small)],
        out_specs=[rows,rows,rows,rows,pl.BlockSpec((1,ntp,256),lambda p:(p,0,0)),whole((R,D)),whole((half,1)),whole((half,1)),whole((1,640)),whole((4,D)),whole((1,FF))]+[ANYSPACE]*6,
        out_shape=[sds((R,D),BF)]*4+[sds((PAIRS,ntp,256),F32),sds((R,D),F32),sds((half,1),jnp.int32),sds((half,1),F32),sds((1,640),F32),sds((4,D),F32),sds((1,FF),F32),
            sds((D,3*D),BF),sds((D,D),BF),sds((D,FF),BF),sds((FF,D),BF),sds((9,piece,D),BF),sds((9,piece,D),BF)],
        scratch_shapes=[pltpu.VMEM((R,D),BF),pltpu.VMEM((2,half,half),F32),pltpu.VMEM((half,128),F32),pltpu.VMEM((PAIRS,R,PAIR),BF),
            pltpu.VMEM((9,piece,D),BF),pltpu.VMEM((9,)+meta.shape[1:],jnp.int32),pltpu.VMEM((4,)+small.shape,BF),pltpu.VMEM((D,3*D),BF),pltpu.VMEM((D,D),BF),pltpu.VMEM((half,2*PAIR),F32),
            DMA((8,)),DMA((9,)),DMA((8,)),DMA((9,)),DMA((8,)),DMA((9,)),DMA((4,13)),DMA((4,13)),DMA((3,)),DMA((3,)),DMA((14,))],
        compiler_params=pltpu.CompilerParams(vmem_limit_bytes=VMEM_LIMIT,dimension_semantics=("arbitrary",),collective_id=1,has_side_effects=True),
        cost_estimate=pl.CostEstimate(flops=2*R*D*(3*D+D)+24*R*half*D//2*2,bytes_accessed=16<<20,transcendentals=R*half*HEADS),
        name="fwd_attn")(clean,meta,gout,trig,qkv,out,up,down,small)

GC=(2.0/3.141592653589793)**0.5
def cols(refs): return jnp.concatenate([r[...] for r in refs],axis=1)
def rowcat(refs): return jnp.concatenate([r[...] for r in refs],axis=0)
STEPS=FF//512
def up_specs(): return [pl.BlockSpec((D,128),(lambda s:(lambda j:(0,s*STEPS+j)))(s)) for s in range(4)]
def down_specs(): return [pl.BlockSpec((128,D),(lambda s:(lambda j:(s*STEPS+j,0)))(s)) for s in range(4)]
def bias_specs(): return [pl.BlockSpec((1,128),(lambda s:(lambda j:(0,s*STEPS+j)))(s)) for s in range(4)]

FFN_TABLE={2: [(0, None, 0)], 4: [(1, None, 0), (0, 0, 1)], 6: [(2, None, 0), (1, 0, 1)], 8: [(3, None, 0), (0, 1, None), (2, 0, 1)], 9: [(3, 0, None)], 10: [(4, None, 0), (1, 1, None)], 12: [(5, None, 0)]}
FFN_END=[(4, 0), (2, 1), (5, 0)]
ATTN_TABLE={0: [(3, None, 1), (4, None, 1), (5, None, 1), (0, None, 2), (1, None, 2), (2, None, 2)], 1: [(6, None, 0)], 2: [(0, 2, 3), (6, 0, 1)], 3: [(0, 3, 4), (1, 2, 3), (3, 1, 2)], 4: [(7, None, 0), (0, 4, 5), (2, 2, 3)], 5: [(0, 5, 6), (1, 3, 4), (3, 2, 3), (4, 1, 2), (7, 0, 1), (2, 3, 4)], 6: [(0, 6, 7)], 7: [(1, 4, 5), (3, 3, 4), (4, 2, 3), (2, 4, 5), (5, 1, 2)], 8: [(8, None, 0), (0, 7, None), (1, 5, 6), (6, 1, 2)], 9: [(1, 6, 7), (2, 5, 6), (3, 4, 5), (4, 3, 4), (5, 2, 3), (7, 1, 2), (6, 2, 3), (8, 0, 1)], 10: [(2, 6, 7)], 11: [(1, 7, None), (3, 5, 6), (4, 4, 5), (5, 3, 4), (6, 3, 4), (7, 2, 3), (8, 1, 2)], 12: [(9, None, 0)]}
TAIL_ORDER=[("sums", None, 0), (2, 7, None), (3, 6, 7), (4, 5, 6), (5, 4, 5), (6, 4, 5), (7, 3, 4), (8, 2, 3), (9, 0, 1), ("rows", None, 1), ("rows", None, 2), ("sums", 0, 1), (4, 6, 7), ("sums", 1, 2), (3, 7, None), (5, 5, 6), (6, 5, 6), (8, 3, 4), (9, 1, 2), ("rows", None, 3), (7, 4, 5), ("sums", 2, 3), (4, 7, None), ("sums", 3, 4), (5, 6, 7), (9, 2, 3), ("rows", None, 4), (6, 6, 7), (8, 4, 5), ("sums", 4, None), (9, 3, 4), ("rows", None, 5), (5, 7, None), (7, 5, 6), (6, 7, None), (8, 5, 6), (9, 4, 5), ("rows", None, 6), (7, 6, 7), (8, 6, 7), (9, 5, 6), ("rows", None, 7), (7, 7, None), (9, 6, 7), (8, 7, None), (9, 7, None)]

def after(state,table,end):
    state=dict(state)
    for ops in table.values():
        for chunk,take,start in ops:
            if take is not None: state[chunk]=take
    state.update(end)
    return state
FFN_STATE=after({},FFN_TABLE,FFN_END)
def in_state(state,ids,low,high): return [i for i in ids if low<=state[i]<=high]
def started(chunk,table):
    return [start for ops in table.values() for i,take,start in ops if i==chunk and start is not None]

def run_table(table,chunks,position,pid,steps,per_step):
    for i in range(steps):
        ops=table.get(per_step*i+position+1,[])
        if ops:
            @pl.when(pid==i)
            def _(): do_ops(ops,chunks)

def do_ops(ops,chunks):
    for i,take,start in ops:
        if take is not None: chunks[i].take(take)
        if start is not None: chunks[i].start(start)

PHASE=2*STEPS

def ffn_kernel(x1,vec,*refs):
    wup,bup,wdn,rest=refs[:4],refs[4:8],refs[8:12],refs[12:]
    gain,bdn=vec.at[0:1],vec.at[1:2]
    gy0,gout,dbup_o,dbdn_o,dgain_o,gx1_o,block_o,pair_o,total_o,final_o=rest[:10]
    h_s,hT_s,acc,gy_s,out_s,act_s,gu_s,grad_s,pair_s,far_s,total_s,send,recv,g_send,g_recv,b_send,b_recv,local=rest[10:]
    g=pl.program_id(0)
    R=h_s.shape[0]; ch=R//3; piece=R//18
    chunks=[Reduce(TILE,send.at[i],recv.at[i],grad=grad_s.at[i%2],pair=pair_s.at[i],far=far_s.at[i],total=total_s.at[i]) for i in range(STEPS)]
    arrive=ToUnit(lambda q,h:gout.at[q,1,h],lambda t:gy_s.at[9+t],g_send,g_recv,local.at[0])
    leave=[FromUnit(lambda t,i=i:out_s.at[9*i+t],lambda q,h,i=i:block_o.at[q,i,h],b_send.at[i],b_recv.at[i],local.at[1+i]) for i in range(2)]
    first=pltpu.make_async_copy(gy0,gy_s.at[pl.ds(0,9)],local.at[3])
    rows=lambda ref,i: ref[6*i:6*i+6].reshape(ch,D)
    wu=lambda: cols(wup)
    wd=lambda: rowcat(wdn)
    bias=cols(bup).astype(F32)
    @pl.when(g==0)
    def _():
        meet(True,(1,2))
        arrive.begin()
        first.start()
        @pl.when(lax.rem(place_ids()[0],2)==1)
        def _():
            gy_s[16:18]=jnp.zeros((2,)+gy_s.shape[1:],BF)
        n,_=norm_rows(x1[...])
        h=(n*gain[...].astype(F32)).astype(BF)
        h_s[...]=h
        hT_s[...]=h.T
        acc[...]=x1[...]+bdn[...].astype(F32)
    for copy in range(2):
        @pl.when((g>=copy*STEPS)&(g<(copy+1)*STEPS))
        def _():
            for i in range(2):
                r=slice((2*copy+i)*R//4,(2*copy+i+1)*R//4)
                u=dot_nn(h_s[r],wu())+bias
                act=(0.5*u*(1.0+jnp.tanh(GC*(u+0.044715*u*u*u)))).astype(BF)
                acc[r]+=dot_nn(act,wd())
        @pl.when(g==(copy+1)*STEPS-1)
        def _():
            out_s[9*copy:9*copy+9]=acc[copy*R//2:(copy+1)*R//2].astype(BF).reshape(9,piece,D)
            leave[copy].begin()
    @pl.when(g==PHASE-1)
    def _():
        arrive.finish()
        first.wait()
        acc[...]=jnp.zeros_like(acc)
        dbdn_o[...]=jnp.sum(gy_s[...].astype(F32).reshape(R,D),axis=0,keepdims=True)
    @pl.when(g>=PHASE)
    def _():
        j=g-PHASE
        for i in range(2,STEPS):
            @pl.when(j==i)
            def _(): chunks[i-2].sent(0)
        slot=lax.rem(j,2)
        for i in range(3):
            r=slice(i*ch,(i+1)*ch)
            u=dot_nn(h_s[r],wu())+bias
            ga=dot_nt(rows(gy_s,i),wd())
            u2=u*u
            t=jnp.tanh(GC*(u+0.044715*u*u2))
            a=0.5*(1.0+t)
            gu=((a+0.5*u*(1.0-t*t)*(GC*(1.0+3*0.044715*u2)))*ga).astype(BF)
            act_s[r]=(u*a).astype(BF)
            gu_s[r]=gu
            acc[r]+=dot_nt(gu,wu())
        run_table(FFN_TABLE,chunks,0,j,STEPS,2)
        def put(s,row,value):
            for k in range(0,value.shape[0],64):
                grad_s[slot,s%2,s//2,(row+k)//TILE,(row+k)%TILE:(row+k)%TILE+64]=value[k:k+64]
        r=dot_tn(act_s[...],gy_s[...].reshape(R,D)).astype(BF)
        for s in range(4):
            for t in range(6): put(s,768+t*128,r[s*128:(s+1)*128,t*128:(t+1)*128])
        r=dot_nn(hT_s[...],gu_s[...]).astype(BF)
        for s in range(4):
            for t in range(4): put(s,t*192,r[s*192:(s+1)*192,t*128:(t+1)*128])
        dbup_o[...]=jnp.sum(gu_s[...].astype(F32),axis=0,keepdims=True)
        run_table(FFN_TABLE,chunks,1,j,STEPS,2)
    @pl.when(g==pl.num_programs(0)-1)
    def _():
        n,scale=norm_rows(x1[...])
        g2=acc[...]
        dgain_o[...]=jnp.sum(g2*n,axis=0,keepdims=True)
        e=g2*gain[...].astype(F32)
        acc[...]=gy_s[...].astype(F32).reshape(R,D)+scale*(e-jnp.mean(e,axis=-1,keepdims=True)-n*jnp.mean(e*n,axis=-1,keepdims=True))
        outs=[pltpu.make_async_copy(acc,gx1_o,local.at[5])]
        outs[0].start()
        for i,stage in FFN_END: chunks[i].take(stage)
        for low,high,source,target in ((0,0,pair_s,pair_o),(1,3,total_s,total_o)):
            for place,i in enumerate(in_state(FFN_STATE,range(STEPS),low,high)):
                outs.append(pltpu.make_async_copy(source.at[i],target.at[place],local.at[5+len(outs)]))
                outs[-1].start()
        for i in range(STEPS):
            stages=started(i,FFN_TABLE)
            chunks[i].sent(*[x for x in stages if x>0 or i>=STEPS-2])
        for r in leave: r.finish()
        for d in outs: d.wait()

def ffn(x1,vec,wup,bup,wdn,gy0,gout):
    R=x1.shape[0]; half=R//2; piece=half//9
    count=lambda low,high: max(1,len(in_state(FFN_STATE,range(STEPS),low,high)))
    tile=lambda j: lax.rem(j,STEPS)
    ups=[pl.BlockSpec((D,128),(lambda s:(lambda j:(0,s*STEPS+tile(j))))(s)) for s in range(4)]
    downs=[pl.BlockSpec((128,D),(lambda s:(lambda j:(s*STEPS+tile(j),0)))(s)) for s in range(4)]
    biases=[pl.BlockSpec((1,128),(lambda s:(lambda j:(0,s*STEPS+tile(j))))(s)) for s in range(4)]
    return pl.pallas_call(ffn_kernel,grid=(PHASE+STEPS,),
        in_specs=[once((R,D)),once((4,D))]+ups+biases+downs+[ANYSPACE]*2,
        out_specs=[pl.BlockSpec((1,512),lambda j:(0,jnp.maximum(j-PHASE,0))),whole((1,D)),whole((1,D))]+[ANYSPACE]*5,
        out_shape=[jax.ShapeDtypeStruct((1,FF),F32),jax.ShapeDtypeStruct((1,D),F32),jax.ShapeDtypeStruct((1,D),F32),jax.ShapeDtypeStruct((R,D),F32),jax.ShapeDtypeStruct((4,2,2,piece,D),BF),
            jax.ShapeDtypeStruct((count(0,0),2,2,TILE,128),BF),jax.ShapeDtypeStruct((count(1,3),2,TILE,128),BF),jax.ShapeDtypeStruct((1,2,TILE,128),BF)],
        scratch_shapes=[pltpu.VMEM((R,D),BF),pltpu.VMEM((D,R),BF),pltpu.VMEM((R,D),F32),pltpu.VMEM((18,piece,D),BF),pltpu.VMEM((18,piece,D),BF),pltpu.VMEM((R,512),BF),pltpu.VMEM((R,512),BF),
            pltpu.VMEM((2,2,2,2,TILE,128),BF),pltpu.VMEM((STEPS,2,2,TILE,128),BF),pltpu.VMEM((STEPS,2,TILE,128),BF),pltpu.VMEM((STEPS,2,TILE,128),BF),
            DMA((STEPS,8)),DMA((STEPS,8)),DMA((8,)),DMA((9,)),DMA((2,8)),DMA((2,8)),DMA((STEPS+7,))],
        compiler_params=pltpu.CompilerParams(vmem_limit_bytes=VMEM_LIMIT,dimension_semantics=("arbitrary",),collective_id=2,has_side_effects=True),
        cost_estimate=pl.CostEstimate(flops=14*R*D*FF,bytes_accessed=40<<20,transcendentals=2*R*FF),
        name="ffn")(x1,vec,*[wup]*4,*[bup]*4,*[wdn]*4,gy0,gout)

def bwd_attn_kernel(half,xc,noise,segc,segr,vec,gx1,q,k,v,mix,lse,wq,wk,wv,wout,trig,mixed,gain_two,down_shift,up_shift,tile_pair,tile_total,tile_final,
                    tiles_o,wings_o,gin_o,sums_o,hT_s,gh,biasT_s,selfT_s,dq_s,dk_s,dv_s,ga,trig_s,
                    t_pair,t_far,t_total,t_over,t_final,w_grad,w_pair,w_far,w_total,w_over,w_final,gin_s,sum_s,in_s,t_send,t_recv,w_send,w_recv,v_send,v_recv,a_send,a_recv,local):
    p=pl.program_id(0)
    emb,gain=vec.at[2:3],vec.at[3:4]
    rank,_=place_ids()
    R=2*half
    tiles=tiles_of(half)
    pairs=in_state(FFN_STATE,range(STEPS),0,0)
    fars=in_state(FFN_STATE,range(STEPS),0,0)
    slot=lambda ids,i: ids.index(i) if i in ids else 0
    chunks=[Reduce(TILE,t_send.at[i],t_recv.at[i],pair=t_pair.at[slot(pairs,i)],far=t_far.at[slot(fars,i)],total=t_total.at[i],over=t_over.at[i],final=t_final.at[i]) for i in range(STEPS)]
    chunks+=[Reduce(WING,w_send.at[i],w_recv.at[i],grad=w_grad.at[i],pair=w_pair.at[i],far=w_far.at[i],total=w_total.at[i],over=w_over.at[i],final=w_final.at[i]) for i in range(4)]
    def tick(position):
        run_table(ATTN_TABLE,chunks,position,p,PAIRS,2)
    @pl.when(p==0)
    def _():
        loads=[pltpu.make_async_copy(trig.at[rank%2],trig_s,local.at[2])]
        loads[0].start()
        for low,high,source,target in ((0,0,tile_pair,t_pair),(1,3,tile_total,t_total),(4,7,tile_final,t_final)):
            for place,i in enumerate(in_state(FFN_STATE,range(STEPS),low,high)):
                loads.append(pltpu.make_async_copy(source.at[place],target.at[place if low==0 else i],local.at[2+len(loads)]))
                loads[-1].start()
        ga[...]=gx1[...].astype(BF)
        for d in loads: d.wait()
        meet(True,(1,2))
        do_ops(ATTN_TABLE.get(0,[]),chunks)
        g=gain[...].astype(F32)
        for c,rows in enumerate(layer_rows(xc,noise,emb)):
            n,_=norm_rows(rows)
            hT_s[:,c*half:(c+1)*half]=(n*g).astype(BF).T
        gh[...]=jnp.zeros_like(gh)
        for s,m in tiles:
            n=s+m
            qb=(lax.broadcasted_iota(jnp.int32,(n,m),1)+s)//BLK
            kb=lax.broadcasted_iota(jnp.int32,(n,m),0)//BLK
            same=segc[:n]==segr[:,s:n]
            biasT_s[0,:n,s:n]=jnp.where(same&(kb<qb),0.0,NEG)
            biasT_s[1,:n,s:n]=jnp.where(same&(kb<=qb),0.0,NEG)
            qb=lax.broadcasted_iota(jnp.int32,(m,m),1)//BLK
            kb=lax.broadcasted_iota(jnp.int32,(m,m),0)//BLK
            same=segc[s:n]==segr[:,s:n]
            selfT_s[s:n,:m]=jnp.where(same&(kb==qb),0.0,NEG)
    gm=dot_nt(ga[...],wout[...]).astype(BF)
    @pl.when(p==0)
    def _():
        r=dot_tn(mixed[...],ga[...]).astype(BF)
        for a in range(4):
            for t in range(6): w_grad[0,a%2,a//2,t//3,t%3*192:(t%3+1)*192]=r[a*192:(a+1)*192,t*128:(t+1)*128]
    gd=gm.astype(F32)*mix[...].astype(F32)
    dk_s[...]=jnp.zeros_like(dk_s); dv_s[...]=jnp.zeros_like(dv_s)
    idx=0
    for s,m in tiles:
        n=s+m
        for c in (0,1):
            rs=slice(c*half+s,c*half+n)
            qs=head_stack(q[rs]); gs=head_stack(gm[rs])
            delta=jnp.sum(head_stack(gd[rs]).T,axis=0,keepdims=True)
            row=lse[0,idx:idx+1,:2*m]
            def part(krows,bias):
                kc=k[krows]; vc=v[krows]
                st=dot_nt(kc,qs)+jnp.concatenate([bias,bias],axis=1)
                pt=jnp.exp(st-row)
                dp=dot_nt(vc,gs)
                ds=(pt*(dp-delta)).astype(BF)
                dv_s[krows]+=dot_nn(pt.astype(BF),gs)
                dk_s[krows]+=dot_nn(ds,qs)
                return dot_tn(ds,kc)
            dq=part(slice(half,half+n),biasT_s[c,:n,s:n])
            if c==0: dq=dq+part(slice(s,n),selfT_s[s:n,:m])
            dq_s[rs]=head_merge(dq)*HEAD**-0.5
            idx+=1
        if s==256: tick(0)
    cs=jnp.concatenate([trig_s[:,:PAIR]]*2,axis=0)
    sn=jnp.concatenate([trig_s[:,PAIR:]]*2,axis=0)
    z=jnp.concatenate([(g[...]*cs-swap_halves(g[...])*sn).astype(BF) for g in (dq_s,dk_s)]+[dv_s[...].astype(BF)],axis=1)
    r=dot_nn(hT_s[...],z).astype(BF)
    group=1+p//2
    for a in range(4):
        for t in range(3):
            w_grad[group,a%2,a//2,lax.rem(p,2),t*192:(t+1)*192]=r[a*192:(a+1)*192,t*128:(t+1)*128]
    gh[...]+=dot_nt(z,cols((wq,wk,wv)))
    tick(1)
    @pl.when(p==pl.num_programs(0)-1)
    def _():
        g=gain[...].astype(F32)
        outs=[]; dg=0.0
        for c,rows in enumerate(layer_rows(xc,noise,emb)):
            n,scale=norm_rows(rows)
            g1=gh[c*half:(c+1)*half]
            dg=dg+jnp.sum(g1*n,axis=0,keepdims=True)
            e=g1*g
            outs.append(gx1[c*half:(c+1)*half]+scale*(e-jnp.mean(e,axis=-1,keepdims=True)-n*jnp.mean(e*n,axis=-1,keepdims=True)))
        masked=noise[...]==1
        gin=(outs[1]+jnp.where(masked,0.0,outs[0])).astype(BF)
        gin_s[...]=gin.reshape(gin_s.shape)
        demb=jnp.sum(jnp.where(masked,outs[0],0.0),axis=0,keepdims=True)
        row=0
        for part in (demb,dg,gain_two,down_shift):
            for n in range(D//128):
                sum_s[0,row:row+1]=part[:,n*128:(n+1)*128]
                row+=1
        for a in range(4):
            for n in range(STEPS):
                sum_s[0,row:row+1]=up_shift[:,n*512+a*128:n*512+(a+1)*128]
                row+=1
        units=FromUnit(lambda t:gin_s.at[t],lambda q,h:gin_o.at[q,h],a_send,a_recv,local.at[0])
        some=chunks[STEPS]
        vectors=[remote(sum_s.at[n],in_s.at[n],v_send.at[n],v_recv.at[n],where) for n,where in enumerate((some.sib,some.far_id,some.xn,some.z1n,some.z2n))]
        for item,take,start in TAIL_ORDER:
            if item=="rows":
                if start==1: units.begin_rest()
                units.begin_one(start)
            elif item=="sums":
                if take is not None:
                    vectors[take].wait_recv()
                    sum_s[take+1]=sum_s[take]+in_s[take]
                if start is not None: vectors[start].start()
            else: do_ops([(item,take,start)],chunks)
        stores=[pltpu.make_async_copy(t_final,tiles_o,local.at[1]),pltpu.make_async_copy(w_final,wings_o,local.at[2])]
        for d in stores: d.start()
        sums_o[...]=sum_s[5]
        for d in vectors: d.wait_send()
        for n,chunk in enumerate(chunks):
            chunk.sent(*(started(n,ATTN_TABLE)+[start for item,take,start in TAIL_ORDER if item==n and start is not None]))
        units.finish()
        for d in stores: d.wait()

def bwd_attn(xc,noise,segc,segr,vec,gx1,q,k,v,mix,lse,wqkv,wout,trig,vectors,tile_pair,tile_total,tile_final):
    half=xc.shape[0]; R=2*half; piece=half//9
    ntp=lse.shape[1]
    ws=[pl.BlockSpec((D,PAIR),(lambda off:(lambda p:(0,off+p)))(o*PAIRS)) for o in range(3)]
    rows=pl.BlockSpec((R,PAIR),lambda p:(0,p))
    pairs=max(1,len(in_state(FFN_STATE,range(STEPS),0,0)))
    return pl.pallas_call(partial(bwd_attn_kernel,half),grid=(PAIRS,),
        in_specs=[once((half,D)),once((half,1)),once((half,1)),once((1,640)),once((4,D)),once((R,D)),rows,rows,rows,rows,
                  pl.BlockSpec((1,ntp,256),lambda p:(p,0,0)),*ws,pl.BlockSpec((PAIR,D),lambda p:(p,0)),ANYSPACE,once((R,D))]+[once(a.shape) for a in vectors]+[ANYSPACE]*3,
        out_specs=[ANYSPACE]*3+[whole((48,128))],
        out_shape=[jax.ShapeDtypeStruct((STEPS,2,TILE,128),BF),jax.ShapeDtypeStruct((4,2,WING,128),BF),jax.ShapeDtypeStruct((4,2,piece,D),BF),jax.ShapeDtypeStruct((48,128),F32)],
        scratch_shapes=[pltpu.VMEM((D,R),BF),pltpu.VMEM((R,D),F32),pltpu.VMEM((2,half,-(-half//128)*128),F32),pltpu.VMEM((half,128),F32)]+[pltpu.VMEM((R,PAIR),F32)]*3+[pltpu.VMEM((R,D),BF),pltpu.VMEM((half,2*PAIR),F32)]
            +[pltpu.VMEM((pairs,2,2,TILE,128),BF),pltpu.VMEM((pairs,2,TILE,128),BF),pltpu.VMEM((STEPS,2,TILE,128),BF),pltpu.VMEM((STEPS,2*TILE,128),BF),pltpu.VMEM((STEPS,2,TILE,128),BF),
              pltpu.VMEM((4,2,2,2,WING,128),BF),pltpu.VMEM((4,2,2,WING,128),BF),pltpu.VMEM((4,2,WING,128),BF),pltpu.VMEM((4,2,WING,128),BF),pltpu.VMEM((4,2*WING,128),BF),pltpu.VMEM((4,2,WING,128),BF),pltpu.VMEM((9,piece,D),BF),pltpu.VMEM((6,48,128),F32),pltpu.VMEM((5,48,128),F32),
              DMA((STEPS,8)),DMA((STEPS,8)),DMA((4,8)),DMA((4,8)),DMA((5,)),DMA((5,)),DMA((8,)),DMA((8,)),DMA((16,))],
        compiler_params=pltpu.CompilerParams(vmem_limit_bytes=VMEM_LIMIT,dimension_semantics=("arbitrary",),collective_id=3,has_side_effects=True),
        cost_estimate=pl.CostEstimate(flops=4*R*D*(3*D+D)+60*R*half*D//2*2,bytes_accessed=30<<20,transcendentals=R*half*HEADS),
        name="bwd_attn")(xc,noise,segc,segr,vec,gx1,q,k,v,mix,lse,wqkv,wqkv,wqkv,wout,trig,mix,*vectors,tile_pair,tile_total,tile_final)

def assemble(ffn,wings,gin,block):
    piece=gin.shape[2]
    sds=jax.ShapeDtypeStruct
    quarter=lambda i: (jnp.minimum(i,3),0,0)
    up,out,qkv,down,grad,rows=pl.pallas_call(assemble_kernel,grid=(STEPS,),
        in_specs=[pl.BlockSpec((1,2,TILE,128),lambda i:(i,0,0,0)),pl.BlockSpec((None,None,WING,128),lambda i:(1+i//2,lax.rem(i,2),0,0)),
            pl.BlockSpec((None,None,192,128),lambda i:(0,i//3,lax.rem(i,3),0)),pl.BlockSpec((2,piece,D),quarter),pl.BlockSpec((4,piece,D),quarter)],
        out_specs=[ANYSPACE]*3+[pl.BlockSpec((128,D),lambda i:(i,0)),pl.BlockSpec((2,piece,D),quarter),pl.BlockSpec((4,piece,D),quarter)],
        out_shape=[sds((192,FF),F32),sds((192,D),F32),sds((192,3*D),F32),sds((768,D),F32),sds((8,piece,D),F32),sds((16,piece,D),BF)],
        scratch_shapes=[pltpu.VMEM((2,8,192,128),F32),DMA((2,8))],
        compiler_params=pltpu.CompilerParams(vmem_limit_bytes=VMEM_LIMIT,dimension_semantics=("arbitrary",)),
        name="assemble")(ffn,wings,wings,gin.reshape(8,piece,D),block.reshape(16,piece,D))
    return up,down,out,qkv,grad,rows


DMA = pltpu.SemaphoreType.DMA
MESH = pl.DeviceIdType.MESH
INVMEM = pl.BlockSpec(memory_space=pltpu.VMEM)
ANYSPACE = pl.BlockSpec(memory_space=pl.ANY)


def place_ids():
    return lax.axis_index("ctx"), lax.axis_index("fsdp")


def meet(all_ranks, fsdp_partners):
    c, f = place_ids()
    sem = pltpu.get_barrier_semaphore()
    count = 0
    ranks = [(c + s) % 8 for s in range(1, 8)] if all_ranks else [c + 1 - 2 * (c % 2)]
    for rank in ranks:
        pl.semaphore_signal(sem, inc=1, device_id={"ctx": rank}, device_id_type=MESH)
        count += 1
    for s in fsdp_partners:
        other = (f + 2) % 4 if s == 2 else f + 1 - 2 * (f % 2) if s == 1 else 3 - f
        pl.semaphore_signal(sem, inc=1, device_id={"fsdp": other}, device_id_type=MESH)
        count += 1
    pl.semaphore_wait(sem, count)


def remote(src, dst, send, recv, where):
    return pltpu.make_async_remote_copy(src_ref=src, dst_ref=dst, send_sem=send, recv_sem=recv, device_id=where,
                                        device_id_type=MESH)


class ToUnit:
    def __init__(self, source, target, send, recv, local):
        self.source, self.target, self.send, self.recv, self.local = source, target, send, recv, local
        self.c, _ = place_ids()

    def message(self, s):
        c = self.c
        t = (c + s) % 8
        odd, last = t % 2, c // 7
        slot = (1 - odd) * c + odd * ((1 - last) * (6 - c) + last * 8)
        return remote(self.source(t // 2, odd), self.target(slot), self.send.at[s], self.recv.at[slot],
                      {"ctx": t - odd * last})

    def begin(self):
        for s in (1, 7, 3, 5, 2, 6, 4):
            self.message(s).start()

        @pl.when(self.c == 7)
        def _():
            self.message(0).start()

        @pl.when(self.c != 7)
        def _():
            self.own_safe().start()

    def begin_straight(self):
        for s in (2, 4, 6):
            self.message(s).start()

        @pl.when(self.c != 7)
        def _():
            self.own_safe().start()

    def begin_across(self):
        for s in (1, 3, 5, 7):
            self.message(s).start()

        @pl.when(self.c == 7)
        def _():
            self.message(0).start()

    def own_safe(self):
        c = self.c
        part = c % 2
        slot = (1 - part) * c + part * (6 - c + c // 7)
        return pltpu.make_async_copy(self.source(c // 2, part), self.target(slot), self.local)

    def finish(self):
        c = self.c
        part = c % 2

        @pl.when(c == 7)
        def _():
            self.message(0).wait_send()

        @pl.when(c != 7)
        def _():
            self.own_safe().wait()

        for s in range(1, 8):
            self.message(s).wait_send()
        own = (1 - part) * c + part * (6 - c)
        for slot in range(9):
            take = slot != own
            if slot > 6:
                take = take & (part == 0)

            @pl.when(take)
            def _():
                remote(self.target(slot), self.target(slot), self.send.at[0], self.recv.at[slot], {"ctx": c}).wait_recv()


class FromUnit:
    def __init__(self, source, target, send, recv, local):
        self.source, self.target, self.send, self.recv, self.local = source, target, send, recv, local
        self.c, _ = place_ids()

    def message(self, s):
        c = self.c
        part = c % 2
        rank = (c + s) % 8
        slot = (1 - part) * rank + part * (6 - rank + rank // 7)
        return remote(self.source(slot), self.target(c // 2, part), self.send.at[s], self.recv.at[c], {"ctx": rank})

    def extra(self):
        c = self.c
        seq = c // 2
        return remote(self.source(8), self.target(seq, 1), self.send.at[0], self.recv.at[2 * seq + 1], {"ctx": 7})

    def own(self):
        c = self.c
        part = c % 2
        slot = (1 - part) * c + part * (6 - c + c // 7)
        return pltpu.make_async_copy(self.source(slot), self.target(c // 2, part), self.local)

    def each(self, remote_op, own_op):
        c = self.c
        part = c % 2
        @pl.when(part == 0)
        def _():
            remote_op(self.extra())

        for s in (1, 7, 3, 5, 2, 6, 4):
            rank = (c + s) % 8

            @pl.when((part == 0) | (rank != 7))
            def _():
                remote_op(self.message(s))

        @pl.when(c != 7)
        def _():
            own_op(self.own())

    def begin_one(self, s):
        c = self.c

        @pl.when((c % 2 == 0) | ((c + s) % 8 != 7))
        def _():
            self.message(s).start()

    def begin_rest(self):
        c = self.c

        @pl.when(c % 2 == 0)
        def _():
            self.extra().start()

        @pl.when(c != 7)
        def _():
            self.own().start()

    def begin(self):
        self.each(lambda m: m.start(), lambda m: m.start())

    def finish(self):
        self.each(lambda m: m.wait_send(), lambda m: m.wait())
        c = self.c
        for block in range(8):
            @pl.when((c == 7) | (c != block))
            def _():
                ref = self.target(block // 2, block % 2)
                remote(ref, ref, self.send.at[0], self.recv.at[block], {"ctx": c}).wait_recv()


class GatherRows:
    def __init__(self, shard, full, send, recv, local, parts=1, share=True):
        c, f = place_ids()
        n = shard.shape[0]
        n2 = n // 2 if share else n
        m = n2 // parts
        h = c % 2 if share else 0
        sib, far, xn = f + 1 - 2 * (f % 2), (f + 2) % 4, c + 1 - 2 * (c % 2)
        diag = (sib + 2) % 4
        rows = lambda start, size: full.at[pl.ds(pl.multiple_of(start, 16), size)]
        same = lambda ref, i, where: remote(ref, ref, send.at[i], recv.at[i], where)
        mine = rows(f * n, n)
        self.copy = pltpu.make_async_copy(shard, mine, local)
        self.to_core = remote(shard, mine, send.at[0], recv.at[0], {"fsdp": sib})
        self.from_core = same(rows(sib * n, n), 0, {"fsdp": sib})
        self.to_far, self.from_far, self.to_x, self.from_x = [], [], [], []
        self.near_core, self.away_core, self.from_near, self.from_away = [], [], [], []
        for i in range(parts):
            a, b = h * n2 + i * m, (1 - h) * n2 + i * m
            near, away = rows(far * n + a, m), rows(far * n + b, m)
            k = 1 + 4 * i
            self.to_far.append(remote(shard.at[pl.ds(pl.multiple_of(a, 16), m)], rows(f * n + a, m), send.at[k], recv.at[k],
                                      {"fsdp": far}))
            self.from_far.append(same(near, k, {"fsdp": far}))
            self.near_core.append(same(near, k + 2, {"fsdp": sib}))
            self.from_near.append(same(rows(diag * n + a, m), k + 2, {"fsdp": sib}))
            if share:
                self.to_x.append(same(near, k + 1, {"ctx": xn}))
                self.from_x.append(same(away, k + 1, {"ctx": xn}))
                self.away_core.append(same(away, k + 3, {"fsdp": sib}))
                self.from_away.append(same(rows(diag * n + b, m), k + 3, {"fsdp": sib}))

    def begin(self):
        for copy in self.to_far:
            copy.start()
        self.to_core.start()
        self.copy.start()

    def relay_far(self, i=0):
        self.from_far[i].wait_recv()
        if self.to_x:
            self.to_x[i].start()
        self.near_core[i].start()

    def relay_x(self, i=0):
        self.from_x[i].wait_recv()
        self.away_core[i].start()

    def finish(self):
        self.copy.wait()
        for copy in [self.to_core] + self.to_far + self.to_x + self.near_core + self.away_core:
            copy.wait_send()
        for copy in [self.from_core] + self.from_near + self.from_away:
            copy.wait_recv()


class Reduce:
    def __init__(self, rows, send, recv, across=False, grad=None, pair=None, far=None, total=None, over=None, final=None):
        c, f = place_ids()
        self.send, self.recv, self.across = send, recv, across
        self.grad, self.pair, self.far, self.total, self.over, self.final = grad, pair, far, total, over, final
        self.core, self.y, self.x = f % 2, f // 2, c % 2
        z1, z2 = (c // 2) % 2, c // 4
        self.sib, self.far_id = {"fsdp": f + 1 - 2 * self.core}, {"fsdp": (f + 2) % 4}
        self.xn, self.z1n, self.z2n = {"ctx": c + 1 - 2 * self.x}, {"ctx": c + 2 - 4 * z1}, {"ctx": c + 4 - 8 * z2}
        half, quarter = rows // 2, rows // 4
        self.rows = rows
        self.levels = [(z1 * half, (1 - z1) * half, half, rows, self.z1n)]
        base = z1 * half
        self.levels.append((base + z2 * quarter, base + (1 - z2) * quarter, quarter, rows + half, self.z2n))

    def at(self, ref, start, size):
        return ref.at[self.x, pl.ds(pl.multiple_of(start, 16), size)]

    def copy(self, stage):
        x, y = self.x, self.y
        if stage == 0:
            source, target, where = self.grad.at[1 - self.core], self.pair, self.sib
        elif stage == 1 and self.across:
            source, target, where = self.pair.at[:, 1 - x], self.far, self.xn
        elif stage == 1:
            source, target, where = self.pair.at[1 - y], self.far, self.far_id
        elif stage == 2 and self.across:
            source, target, where = self.pair.at[1 - y, x], self.over.at[pl.ds(0, self.rows)], self.far_id
        elif stage == 2:
            source, target, where = self.total.at[1 - x], self.over.at[pl.ds(0, self.rows)], self.xn
        elif stage < 5:
            keep, give, size, offset, where = self.levels[stage - 3]
            source, target = self.at(self.total, give, size), self.over.at[pl.ds(offset, size)]
        elif stage < 7:
            keep, give, size, offset, where = self.levels[6 - stage]
            source = target = self.at(self.final, keep, size)
        else:
            source, target, where = self.final.at[x], self.final.at[x], self.xn
        return remote(source, target, self.send.at[stage], self.recv.at[stage], where)

    def start(self, stage):
        self.copy(stage).start()

    def take(self, stage):
        x, y = self.x, self.y
        if stage < 5:
            self.copy(stage).wait_recv()
        if stage == 0:
            self.pair[...] = self.pair[...] + self.grad[self.core]
        elif stage == 1 and self.across:
            for i in range(2):
                self.pair[i, x] = self.pair[i, x] + self.far[i]
        elif stage == 1:
            self.total[...] = self.far[...] + self.pair[y]
        elif stage == 2 and self.across:
            self.total[x] = self.pair[y, x] + self.over[pl.ds(0, self.rows)]
        elif stage == 2:
            self.total[x] = self.total[x] + self.over[pl.ds(0, self.rows)]
        elif stage < 5:
            keep, give, size, offset, where = self.levels[stage - 3]
            into = self.at(self.final if stage == 4 else self.total, keep, size)
            into[...] = self.at(self.total, keep, size)[...] + self.over[pl.ds(offset, size)]
        elif stage < 7:
            keep, give, size, offset, where = self.levels[6 - stage]
            ref = self.at(self.final, give, size)
            remote(ref, ref, self.send.at[stage], self.recv.at[stage], where).wait_recv()
        else:
            ref = self.final.at[1 - x]
            remote(ref, ref, self.send.at[7], self.recv.at[7], self.xn).wait_recv()

    def sent(self, *stages):
        for stage in stages:
            self.copy(stage).wait_send()


TILE = 768
WING = 576


def assemble_kernel(ffn, pair, out, gin, block, up_o, out_o, qkv_o, down_o, gin_o, block_o, stage, sem):
    i = pl.program_id(0)
    slot = lax.rem(i, 2)

    def copies(step, place):
        column = lambda k: pl.ds(pl.multiple_of(k * 128, 128), 128)
        targets = [up_o.at[:, column(s * STEPS + step)] for s in range(4)] + [out_o.at[:, column(step)]]
        targets += [qkv_o.at[:, column(w * PAIRS + step)] for w in range(3)]
        return [pltpu.make_async_copy(stage.at[place, k], target, sem.at[place, k]) for k, target in enumerate(targets)]

    @pl.when(i >= 2)
    def _():
        for copy in copies(i - 2, slot):
            copy.wait()

    tile = lambda r: ffn[0, r // TILE, r % TILE:r % TILE + 64].astype(F32)
    for r in range(0, 192, 64):
        for s in range(4):
            stage[slot, s, r:r + 64] = tile(s * 192 + r)
        stage[slot, 4, r:r + 64] = out[r:r + 64].astype(F32)
        for w in range(3):
            stage[slot, 5 + w, r:r + 64] = pair[w * 192 + r:w * 192 + r + 64].astype(F32)
    for copy in copies(i, slot):
        copy.start()
    for t in range(6):
        for r in range(0, 128, 64):
            down_o[r:r + 64, t * 128:(t + 1) * 128] = tile(768 + t * 128 + r)
    gin_o[...] = gin[...].astype(F32)
    block_o[...] = block[...]

    @pl.when(i == STEPS - 1)
    def _():
        for copy in copies(i - 1, 1 - slot) + copies(i, slot):
            copy.wait()


def rope_constant(half):
    position = np.arange(2 * half, dtype=np.float32)
    frequency = np.float32(10000.0) ** (-(np.arange(HEAD // 2, dtype=np.float32) * np.float32(2.0)) / np.float32(HEAD))
    angles = (position[:, None] * frequency[None, :]).astype(np.float64)
    cosine, sine = np.cos(angles), np.sin(angles)
    table = np.concatenate([np.tile(cosine, (1, 4)), np.tile(np.concatenate([-sine, sine], axis=1), (1, 2))], axis=1)
    return jnp.asarray(table.reshape(2, half, 4 * HEAD).astype(np.float32))


def even_body(clean_in, segments, noise, mask_embed, norm1_gain, qkv_weight, out_weight, norm2_gain, up_weight, up_bias,
              down_weight, down_bias, out_grad):
    place = lax.axis_index("fsdp")
    piece = clean_in.shape[2]
    half = 9 * piece
    width = mask_embed.shape[0]
    line = lax.broadcasted_iota(jnp.int32, (8, 8, piece), 1)
    meta = jnp.where(line == 0, segments.reshape(8, 1, piece), noise.reshape(8, 1, piece))
    row = lax.broadcasted_iota(jnp.int32, (16, width), 0)
    small = jnp.zeros((16, width), BF)
    for i, vector in enumerate((mask_embed, norm1_gain, norm2_gain, down_bias)):
        small = jnp.where(row == i, vector[None], small)
    for i in range(4):
        small = jnp.where(row == 4 + i, up_bias[i * width:(i + 1) * width][None], small)
    q, k, v, mixed, lse, resid, mask, seg_col, seg_row, vectors, up_shift, qkv_full, out_full, up_full, down_full, cotangent, clean = fwd_attn(
        clean_in, meta, out_grad, rope_constant(half), qkv_weight, out_weight, up_weight, down_weight, small)
    clean = clean.reshape(half, D)
    up_shift_grad, down_shift_grad, gain_two_grad, grad_resid, block_out, tile_pair, tile_total, tile_final = ffn(
        resid, vectors, up_full, up_shift, down_full, cotangent, out_grad)
    tiles, wings, input_grad, sums = bwd_attn(
        clean, mask, seg_col, seg_row, vectors, grad_resid, q, k, v, mixed, lse, qkv_full, out_full, rope_constant(half),
        (gain_two_grad, down_shift_grad, up_shift_grad), tile_pair, tile_total, tile_final)
    up_sum, down_sum, out_sum, qkv_sum, input_grad, block_out = assemble(tiles, wings, input_grad, block_out)
    input_grad = input_grad.reshape(clean_in.shape)
    block_out = block_out.reshape(out_grad.shape)
    sums = sums.reshape(-1)
    own = [lax.dynamic_slice_in_dim(sums, i * D + place * width, width) for i in range(4)]
    own_up = lax.dynamic_slice_in_dim(sums, 4 * D + place * (FF // 4), FF // 4)
    return (block_out, input_grad, own[0], own[1], qkv_sum, out_sum, own[2], up_sum, own_up, down_sum, own[3])


def choose_body(axes, *arrays):
    even = axes["ctx"] == 8 and axes["fsdp"] == 4 and arrays[0].shape[0] == 4
    return (even_body if even else general_body)(*arrays)


def solution(mesh):
    placed = (
        P("fsdp", None, "ctx", None),
        P("fsdp", None, "ctx"),
        P("fsdp", None, "ctx"),
        P("fsdp"),
        P("fsdp"),
        P("fsdp", None),
        P("fsdp", None),
        P("fsdp"),
        P("fsdp", None),
        P("fsdp"),
        P("fsdp", None),
        P("fsdp"),
        P("fsdp", None, None, "ctx", None),
    )
    return jax.shard_map(
        partial(choose_body, dict(mesh.shape)),
        mesh=mesh,
        in_specs=placed,
        out_specs=(
            P("fsdp", None, None, "ctx", None),
            P("fsdp", None, "ctx", None),
            P("fsdp"),
            P("fsdp"),
            P("fsdp", None),
            P("fsdp", None),
            P("fsdp"),
            P("fsdp", None),
            P("fsdp"),
            P("fsdp", None),
            P("fsdp"),
        ),
        check_vma=False,
    )
```

```python
from functools import partial

import jax
import jax.numpy as jnp
import numpy as np
from jax import lax
from jax.experimental import pallas as pl
from jax.experimental.pallas import tpu as pltpu
from jax.sharding import PartitionSpec as P

D = 768
HEADS = 12
HEAD = 64
FF = 3072
BLK = 16


EPS = 1e-05
together = 4


def normalize(values):
    centre = values - jnp.mean(values, axis=-1, keepdims=True)
    scale = lax.rsqrt(jnp.mean(centre * centre, axis=-1, keepdims=True) + EPS)
    return (centre * scale, scale)


def norm_back(grad_in, normed, scale):
    centred = grad_in - jnp.mean(grad_in, axis=-1, keepdims=True)
    return scale * (centred - normed * jnp.mean(grad_in * normed, axis=-1, keepdims=True))


def rope_tables(positions):
    half_head = HEAD // 2
    frequency = 10000.0 ** (-(jnp.arange(half_head, dtype=jnp.float32) * 2.0) / HEAD)
    angles = positions.astype(jnp.float32)[:, None] * frequency[None, :]
    return (jnp.cos(angles), jnp.sin(angles))


def rotate(values, cos_part, sin_part, reverse):
    count = values.shape[0]
    heads = values.reshape(count, HEADS, HEAD)
    half_head = HEAD // 2
    leading = heads[..., :half_head]
    trailing = heads[..., half_head:]
    cosine = cos_part[:, None, :]
    sine_part = sin_part[:, None, :]
    if reverse:
        parts = [leading * cosine + trailing * sine_part, trailing * cosine - leading * sine_part]
    else:
        parts = [leading * cosine - trailing * sine_part, trailing * cosine + leading * sine_part]
    return jnp.concatenate(parts, axis=-1).reshape(count, D)


def split_heads(values):
    count = values.shape[0]
    return values.reshape(count, HEADS // together, together * HEAD).transpose(1, 0, 2)


def join_heads(values):
    groups, count, width = values.shape
    return values.transpose(1, 0, 2).reshape(count, groups * width)


def allowed_pairs(query_copy, query_block, query_doc, key_copy, key_block, key_doc):
    same_doc = query_doc[:, None] == key_doc[None, :]
    query_noisy = (query_copy == 0)[:, None]
    key_noisy = (key_copy == 0)[None, :]
    query_column = query_block[:, None]
    key_row = key_block[None, :]
    inner = query_noisy & key_noisy & (key_row == query_column)
    earlier = query_noisy & ~key_noisy & (key_row < query_column)
    causal = ~query_noisy & ~key_noisy & (key_row <= query_column)
    return same_doc & (inner | earlier | causal)


def masked_scores(query_group, key_group, allowed):
    query_heads = query_group.reshape(query_group.shape[0], together, HEAD)
    key_heads = key_group.reshape(key_group.shape[0], together, HEAD)
    raw = jnp.einsum(
        "qhd,khd->hqk", query_heads, key_heads, preferred_element_type=jnp.float32
    ) * HEAD ** (-0.5)
    return (jnp.where(allowed[None], raw, -1e30), query_heads, key_heads)


def group_forward(items, allowed):
    query_group, key_group, value_group = items
    count = query_group.shape[0]
    scores, query_heads, key_heads = masked_scores(query_group, key_group, allowed)
    value_heads = value_group.reshape(value_group.shape[0], together, HEAD)
    top = jnp.max(scores, axis=-1, keepdims=True)
    weights = jnp.exp(scores - top)
    total = jnp.sum(weights, axis=-1, keepdims=True)
    probs = (weights / total).astype(jnp.bfloat16)
    mixed = jnp.einsum("hqk,khd->qhd", probs, value_heads, preferred_element_type=jnp.float32)
    return (mixed.reshape(count, together * HEAD), (top + jnp.log(total))[..., 0])


def group_backward(items, allowed, tail):
    query_group, key_group, value_group, grad_group, log_total = items
    count = query_group.shape[0]
    key_count = key_group.shape[0]
    scores, query_heads, key_heads = masked_scores(query_group, key_group, allowed)
    value_heads = value_group.reshape(key_count, together, HEAD)
    grad_heads = grad_group.reshape(count, together, HEAD)
    probs = jnp.exp(scores - log_total[..., None])
    prob_grad = jnp.einsum(
        "qhd,khd->hqk", grad_heads, value_heads, preferred_element_type=jnp.float32
    )
    centre = jnp.sum(probs * prob_grad, axis=-1, keepdims=True)
    score_grad = (probs * (prob_grad - centre)).astype(jnp.bfloat16)
    query_grad = jnp.einsum(
        "hqk,khd->qhd", score_grad, key_heads, preferred_element_type=jnp.float32
    ) * HEAD ** (-0.5)
    tail_probs = probs.astype(jnp.bfloat16)
    value_grad = jnp.einsum(
        "hqk,qhd->khd", tail_probs, grad_heads, preferred_element_type=jnp.float32
    )
    key_grad = jnp.einsum(
        "hqk,qhd->khd", score_grad, query_heads, preferred_element_type=jnp.float32
    ) * HEAD ** (-0.5)
    return (
        query_grad.reshape(count, together * HEAD),
        key_grad.reshape(tail, together * HEAD),
        value_grad.reshape(tail, together * HEAD),
        centre[..., 0],
    )


def reduce_grads(grads):
    shards = (
        lax.psum_scatter(grads[0], "fsdp", scatter_dimension=0, tiled=True),
        lax.psum_scatter(grads[1], "fsdp", scatter_dimension=0, tiled=True),
        lax.psum_scatter(grads[2], "fsdp", scatter_dimension=0, tiled=True),
        lax.psum_scatter(grads[3], "fsdp", scatter_dimension=0, tiled=True),
        lax.psum_scatter(grads[4], "fsdp", scatter_dimension=0, tiled=True),
        lax.psum_scatter(grads[5], "fsdp", scatter_dimension=0, tiled=True),
        lax.psum_scatter(grads[6], "fsdp", scatter_dimension=0, tiled=True),
        lax.psum_scatter(grads[7], "fsdp", scatter_dimension=0, tiled=True),
        lax.psum_scatter(grads[8], "fsdp", scatter_dimension=0, tiled=True),
    )
    return lax.psum(
        (
            shards[0],
            shards[1],
            shards[2],
            shards[3],
            shards[4],
            shards[5],
            shards[6],
            shards[7],
            shards[8],
        ),
        "ctx",
    )


def add_tuples(left_items, right_items):
    return tuple((left_item + right_item for left_item, right_item in zip(left_items, right_items)))


def general_body(
    clean_in,
    segments,
    noise,
    mask_embed,
    norm1_gain,
    qkv_weight,
    out_weight,
    norm2_gain,
    up_weight,
    up_bias,
    down_weight,
    down_bias,
    out_grad,
):
    qkv_full, out_full, gain_low, embed_low = (
        lax.all_gather(qkv_weight, "fsdp", axis=0, tiled=True),
        lax.all_gather(out_weight, "fsdp", axis=0, tiled=True),
        lax.all_gather(norm1_gain, "fsdp", axis=0, tiled=True),
        lax.all_gather(mask_embed, "fsdp", axis=0, tiled=True),
    )
    up_full, up_low, down_full, down_low, gain_two_low = (
        lax.all_gather(up_weight, "fsdp", axis=0, tiled=True),
        lax.all_gather(up_bias, "fsdp", axis=0, tiled=True),
        lax.all_gather(down_weight, "fsdp", axis=0, tiled=True),
        lax.all_gather(down_bias, "fsdp", axis=0, tiled=True),
        lax.all_gather(norm2_gain, "fsdp", axis=0, tiled=True),
    )
    gain_one = gain_low.astype(jnp.float32)
    gain_two = gain_two_low.astype(jnp.float32)
    embed_row = embed_low.astype(jnp.float32)
    up_shift = up_low.astype(jnp.float32)
    down_shift = down_low.astype(jnp.float32)
    micro_count = clean_in.shape[0]
    piece = clean_in.shape[2]
    local_rows = 2 * piece
    ctx_count = lax.axis_size("ctx")
    ctx_rank = lax.axis_index("ctx")
    span = jnp.arange(piece, dtype=jnp.int32)
    local_pos = jnp.concatenate(
        [ctx_rank * piece + span, (2 * ctx_count - 1 - ctx_rank) * piece + span]
    )
    ranks = jnp.arange(ctx_count, dtype=jnp.int32)[:, None]
    far_pos = jnp.concatenate(
        [ranks * piece + span[None, :], (2 * ctx_count - 1 - ranks) * piece + span[None, :]], axis=1
    ).reshape(-1)
    seq_len = ctx_count * local_rows
    cos_part, sin_part = rope_tables(jnp.concatenate([local_pos, local_pos]))
    query_copy = jnp.concatenate(
        [jnp.zeros((local_rows,), jnp.int32), jnp.ones((local_rows,), jnp.int32)]
    )
    key_copy = jnp.concatenate(
        [jnp.ones((seq_len,), jnp.int32), jnp.zeros((local_rows,), jnp.int32)]
    )
    query_block = jnp.concatenate([local_pos, local_pos]) // BLK
    key_block = jnp.concatenate([far_pos, local_pos]) // BLK
    full_shapes = ((D,), (D,), (D, 3 * D), (D, D), (D,), (D, FF), (FF,), (FF, D), (D,))
    totals = tuple((jnp.zeros(shape_item, jnp.float32) for shape_item in full_shapes))
    tail = seq_len + local_rows
    outputs = []
    input_grads = []
    for micro_step in range(micro_count):
        clean_rows = clean_in[micro_step].reshape(local_rows, D).astype(jnp.float32)
        noise_rows = noise[micro_step].reshape(-1)
        masked_rows = noise_rows[:, None] == 1
        doc_local = segments[micro_step].reshape(-1).astype(jnp.float32)
        noisy_rows = jnp.where(masked_rows, embed_row[None, :], clean_rows)
        stacked = jnp.concatenate([noisy_rows, clean_rows], axis=0)
        normed_one, scale_one = normalize(stacked)
        h_one = (normed_one * gain_one).astype(jnp.bfloat16)
        projected = jnp.dot(h_one, qkv_full, preferred_element_type=jnp.float32)
        queries = rotate(projected[:, :D], cos_part, sin_part, False).astype(jnp.bfloat16)
        keys = rotate(projected[:, D : 2 * D], cos_part, sin_part, False).astype(jnp.bfloat16)
        values = projected[:, 2 * D :].astype(jnp.bfloat16)
        far_keys, far_values, far_docs = (
            lax.all_gather(keys[local_rows:], "ctx", axis=0, tiled=True),
            lax.all_gather(values[local_rows:], "ctx", axis=0, tiled=True),
            lax.all_gather(doc_local.astype(jnp.bfloat16), "ctx", axis=0, tiled=True),
        )
        key_all = jnp.concatenate([far_keys, keys[:local_rows]], axis=0)
        value_all = jnp.concatenate([far_values, values[:local_rows]], axis=0)
        query_doc = jnp.concatenate([doc_local, doc_local])
        key_doc = jnp.concatenate([far_docs.astype(jnp.float32), doc_local])
        allowed = allowed_pairs(query_copy, query_block, query_doc, key_copy, key_block, key_doc)
        query_groups = split_heads(queries)
        key_groups = split_heads(key_all)
        value_groups = split_heads(value_all)
        mixed_groups, log_totals = lax.map(
            partial(group_forward, allowed=allowed), (query_groups, key_groups, value_groups)
        )
        mixed = join_heads(mixed_groups).astype(jnp.bfloat16)
        resid = stacked + jnp.dot(mixed, out_full, preferred_element_type=jnp.float32)
        normed_two, scale_two = normalize(resid)
        h_two = (normed_two * gain_two).astype(jnp.bfloat16)
        hidden = jnp.dot(h_two, up_full, preferred_element_type=jnp.float32) + up_shift
        active = jax.nn.gelu(hidden, approximate=True).astype(jnp.bfloat16)
        result = resid + jnp.dot(active, down_full, preferred_element_type=jnp.float32) + down_shift
        outputs.append(result.astype(jnp.bfloat16).reshape(2, 2, piece, D))
        cotangent = out_grad[micro_step].reshape(2 * local_rows, D).astype(jnp.float32)
        grad_out = cotangent.astype(jnp.bfloat16)
        down_grad = jnp.einsum("rf,rd->fd", active, grad_out, preferred_element_type=jnp.float32)
        down_shift_grad = jnp.sum(grad_out.astype(jnp.float32), axis=0)
        grad_active = jnp.einsum(
            "rd,fd->rf", grad_out, down_full, preferred_element_type=jnp.float32
        )
        unused, gelu_back = jax.vjp(partial(jax.nn.gelu, approximate=True), hidden)
        grad_hidden = gelu_back(grad_active)[0].astype(jnp.bfloat16)
        up_grad = jnp.einsum("rd,rf->df", h_two, grad_hidden, preferred_element_type=jnp.float32)
        up_shift_grad = jnp.sum(grad_hidden.astype(jnp.float32), axis=0)
        grad_h_two = jnp.einsum(
            "rf,df->rd", grad_hidden, up_full, preferred_element_type=jnp.float32
        )
        gain_two_grad = jnp.sum(grad_h_two * normed_two, axis=0)
        grad_resid = cotangent + norm_back(grad_h_two * gain_two, normed_two, scale_two)
        grad_attn = grad_resid.astype(jnp.bfloat16)
        out_grad_full = jnp.einsum(
            "rd,re->de", mixed, grad_attn, preferred_element_type=jnp.float32
        )
        grad_mixed = jnp.einsum(
            "re,de->rd", grad_attn, out_full, preferred_element_type=jnp.float32
        ).astype(jnp.bfloat16)
        query_grads, key_grads, value_grads, centres = lax.map(
            partial(group_backward, allowed=allowed, tail=tail),
            (query_groups, key_groups, value_groups, split_heads(grad_mixed), log_totals),
        )
        query_grad = join_heads(query_grads)
        key_grad_all = join_heads(key_grads)
        value_grad_all = join_heads(value_grads)
        key_mine, value_mine = (
            lax.psum_scatter(key_grad_all[:seq_len], "ctx", scatter_dimension=0, tiled=True),
            lax.psum_scatter(value_grad_all[:seq_len], "ctx", scatter_dimension=0, tiled=True),
        )
        key_grad = jnp.concatenate([key_grad_all[seq_len:], key_mine], axis=0)
        value_grad = jnp.concatenate([value_grad_all[seq_len:], value_mine], axis=0)
        grad_proj = jnp.concatenate(
            [
                rotate(query_grad, cos_part, sin_part, True),
                rotate(key_grad, cos_part, sin_part, True),
                value_grad,
            ],
            axis=1,
        ).astype(jnp.bfloat16)
        qkv_grad = jnp.einsum("rd,re->de", h_one, grad_proj, preferred_element_type=jnp.float32)
        grad_h_one = jnp.einsum(
            "re,de->rd", grad_proj, qkv_full, preferred_element_type=jnp.float32
        )
        gain_one_grad = jnp.sum(grad_h_one * normed_one, axis=0)
        grad_rows = grad_resid + norm_back(grad_h_one * gain_one, normed_one, scale_one)
        grad_noisy = grad_rows[:local_rows]
        input_grads.append(
            (grad_rows[local_rows:] + jnp.where(masked_rows, 0.0, grad_noisy)).reshape(2, piece, D)
        )
        embed_grad = jnp.sum(jnp.where(masked_rows, grad_noisy, 0.0), axis=0)
        step_grads = (
            embed_grad,
            gain_one_grad,
            qkv_grad,
            out_grad_full,
            gain_two_grad,
            up_grad,
            up_shift_grad,
            down_grad,
            down_shift_grad,
        )
        totals = add_tuples(totals, step_grads)
    reduced = reduce_grads(totals)
    block_out = jnp.stack(outputs)
    input_grad = jnp.stack(input_grads)
    return (
        block_out,
        input_grad,
        reduced[0],
        reduced[1],
        reduced[2],
        reduced[3],
        reduced[4],
        reduced[5],
        reduced[6],
        reduced[7],
        reduced[8],
    )


PAIR=2*HEAD; PAIRS=D//PAIR
NEG=-1e30
VMEM_LIMIT=60<<20
F32=jnp.float32; BF=jnp.bfloat16

def dot_nn(a,b): return lax.dot_general(a,b,(((1,),(0,)),((),())),preferred_element_type=F32)
def dot_nt(a,b): return lax.dot_general(a,b,(((1,),(1,)),((),())),preferred_element_type=F32)
def dot_tn(a,b): return lax.dot_general(a,b,(((0,),(0,)),((),())),preferred_element_type=F32)

def tiles_of(half):
    return [(s,min(128,half-s)) for s in range(0,half,128)]

def norm_rows(rows):
    centre=rows-jnp.mean(rows,axis=-1,keepdims=True)
    scale=lax.rsqrt(jnp.mean(centre*centre,axis=-1,keepdims=True)+EPS)
    return centre*scale, scale

def swap_halves(z):
    lane=lax.broadcasted_iota(jnp.int32,z.shape,1)
    low=(lane & (HEAD-1)) < HEAD//2
    return jnp.where(low,pltpu.roll(z,PAIR-HEAD//2,1),pltpu.roll(z,HEAD//2,1))

def head_stack(z):
    lane=lax.broadcasted_iota(jnp.int32,z.shape,1)
    first=lane<HEAD
    zero=jnp.zeros_like(z)
    return jnp.concatenate([jnp.where(first,z,zero),jnp.where(first,zero,z)],axis=0)

def head_merge(z):
    n=z.shape[0]//2
    lane=lax.broadcasted_iota(jnp.int32,(n,z.shape[1]),1)
    return jnp.where(lane<HEAD,z[:n],z[n:])

def layer_rows(xc_ref,noise_ref,emb_ref):
    clean=xc_ref[...].astype(F32)
    noisy=jnp.where(noise_ref[...]==1,emb_ref[...].astype(F32),clean)
    return noisy,clean

def fwd_attn_kernel(half,xc,noise,segc,segr,small,wqkv,wout,trig,
                    q_o,k_o,v_o,mix_o,lse_o,x1_o,h_s,bias_s,self_s,mix_s):
    p=pl.program_id(0)
    tiles=tiles_of(half)
    @pl.when(p==0)
    def _():
        g=vector_row(small,1)
        clean=jnp.concatenate([xc[i] for i in range(9)],axis=0).astype(F32)
        noisy=jnp.where(noise[...]==1,vector_row(small,0),clean)
        for c,rows in enumerate((noisy,clean)):
            x1_o[c*half:(c+1)*half]=rows
            n,_=norm_rows(rows)
            h_s[c*half:(c+1)*half]=(n*g).astype(BF)
        for s,m in tiles:
            n=s+m
            qb=(lax.broadcasted_iota(jnp.int32,(m,n),0)+s)//BLK
            kb=lax.broadcasted_iota(jnp.int32,(m,n),1)//BLK
            same=segc[s:n]==segr[:,:n]
            bias_s[0,s:n,:n]=jnp.where(same&(kb<qb),0.0,NEG)
            bias_s[1,s:n,:n]=jnp.where(same&(kb<=qb),0.0,NEG)
            qb=lax.broadcasted_iota(jnp.int32,(m,m),0)//BLK
            kb=lax.broadcasted_iota(jnp.int32,(m,m),1)//BLK
            same=segc[s:n]==segr[:,s:n]
            self_s[s:n,:m]=jnp.where(same&(kb==qb),0.0,NEG)
    h=h_s[...]
    cs=jnp.concatenate([trig[:,:PAIR]]*2,axis=0)
    sn=jnp.concatenate([trig[:,PAIR:]]*2,axis=0)
    block=lambda i: wqkv[:,pl.ds(pl.multiple_of(i*D+p*PAIR,PAIR),PAIR)]
    zq=dot_nn(h,jnp.concatenate([block(0),block(1)],axis=1))
    z=zq[:,:PAIR]; q_o[...]=((z*cs+swap_halves(z)*sn).astype(BF)*BF(HEAD**-0.5)).astype(BF)
    z=zq[:,PAIR:]; k_o[...]=(z*cs+swap_halves(z)*sn).astype(BF)
    v_o[...]=dot_nn(h,block(2)).astype(BF)
    idx=0
    for s,m in tiles:
        n=s+m
        for c in (0,1):
            qs=head_stack(q_o[c*half+s:c*half+n])
            kc=k_o[half:half+n]; vc=v_o[half:half+n]
            sc=dot_nt(qs,kc).reshape(2,m,n)+bias_s[c,s:n,:n][None]
            top=jnp.max(sc,axis=-1,keepdims=True)
            if c==0:
                ss=dot_nt(qs,k_o[s:n]).reshape(2,m,m)+self_s[s:n,:m][None]
                top=jnp.maximum(top,jnp.max(ss,axis=-1,keepdims=True))
            w=jnp.exp(sc-top); tot=jnp.sum(w,axis=-1,keepdims=True)
            o=dot_nn(w.astype(BF).reshape(2*m,n),vc)
            if c==0:
                w2=jnp.exp(ss-top); tot=tot+jnp.sum(w2,axis=-1,keepdims=True)
                o=o+dot_nn(w2.astype(BF).reshape(2*m,m),v_o[s:n])
            tot=tot.reshape(2*m,1)
            o=o*(1.0/tot)
            mx=head_merge(o).astype(BF)
            mix_o[c*half+s:c*half+n]=mx
            mix_s[p,c*half+s:c*half+n]=mx
            lse=top.reshape(2*m,1)+jnp.log(tot)
            lse_o[0,idx:idx+1,:2*m]=jnp.broadcast_to(lse,(2*m,128)).T[0:1]
            idx+=1
    @pl.when(p==pl.num_programs(0)-1)
    def _():
        full=jnp.concatenate([mix_s[i] for i in range(PAIRS)],axis=1)
        x1_o[...]=x1_o[...]+dot_nn(full,wout[...])

def whole(shape): return pl.BlockSpec(shape,lambda *i:(0,)*len(shape))

def vector_row(small,i):
    return jnp.concatenate([small[f,i:i+1,:D//4] for f in range(4)],axis=1).astype(F32)

def fwd_attn_comm_kernel(half,*refs):
    clean,meta,gout,trig,qkv,out,up,down,small=refs[:9]
    q_o,k_o,v_o,mix_o,lse_o,x1_o,noise_o,segc_o,segr_o,vec_o,bias_o,qkv_o,out_o,up_o,down_o,cot_o,clean_o=refs[9:26]
    h_s,bias_s,self_s,mix_s,clean_s,meta_s,small_s,qkv_s,out_s,trig_s=refs[26:36]
    a_send,a_recv,m_send,m_recv,c_send,c_recv,w_send,w_recv,s_send,s_recv,local=refs[36:]
    p=pl.program_id(0)
    c,f=place_ids()
    piece=half//9
    weight=lambda i,shard,full,parts: GatherRows(shard,full,w_send.at[i],w_recv.at[i],local.at[i],parts)
    w_qkv,w_out,w_up,w_down=weight(0,qkv,qkv_s,3),weight(1,out,out_s,1),weight(2,up,up_o,3),GatherRows(down,down_o,w_send.at[3],w_recv.at[3],local.at[3],3,False)
    rows=ToUnit(lambda q,h:clean.at[q,h],lambda t:clean_s.at[t],a_send,a_recv,local.at[4])
    notes=ToUnit(lambda q,h:meta.at[2*q+h],lambda t:meta_s.at[t],m_send,m_recv,local.at[5])
    grads=[ToUnit(lambda q,h:gout.at[q,0,h],lambda t:cot_o.at[t],c_send,c_recv,local.at[6])]
    copies=[pltpu.make_async_copy(qkv_s,qkv_o,local.at[8]),pltpu.make_async_copy(out_s,out_o,local.at[9]),pltpu.make_async_copy(clean_s,clean_o,local.at[10])]
    others=[f+1-2*(f%2),(f+2)%4,3-f]
    @pl.when(p==0)
    def _():
        meet(True,(1,2,3))
        w_qkv.begin()
        notes.begin()
        rows.begin()
        sends=[remote(small,small_s.at[f],s_send.at[i],s_recv.at[i],{"fsdp":other}) for i,other in enumerate(others)]
        for d in sends: d.start()
        own=pltpu.make_async_copy(small,small_s.at[f],local.at[11])
        own.start()
        table=pltpu.make_async_copy(trig.at[c%2],trig_s,local.at[12])
        table.start()
        w_out.begin()
        w_up.begin()
        w_down.begin()
        for i in range(3): w_qkv.relay_far(i)
        @pl.when(c%2==1)
        def _():
            clean_s[7:9]=jnp.zeros((2,)+clean_s.shape[1:],BF)
            line=lax.broadcasted_iota(jnp.int32,(2,)+meta_s.shape[1:],1)
            meta_s[7:9]=jnp.where(line==0,-1,0)
            pad=pltpu.make_async_copy(clean_s.at[pl.ds(7,2)],cot_o.at[pl.ds(7,2)],local.at[13])
            pad.start()
            pad.wait()
        for i in range(3): w_qkv.relay_x(i)
        for r in grads: r.begin_straight()
        own.wait()
        table.wait()
        for i,other in enumerate(others):
            sends[i].wait_send()
            remote(small_s.at[other],small_s.at[other],s_send.at[i],s_recv.at[i],{"fsdp":other}).wait_recv()
        notes.finish()
        note=lambda i: jnp.concatenate([meta_s[i,0:1],meta_s[i,1:2]],axis=1).astype(F32)
        for i in range(9):
            t=jnp.broadcast_to(note(i),(128,128)).T
            segc_o[i*piece:(i+1)*piece]=t[:piece,0:1]
            noise_o[i*piece:(i+1)*piece]=t[piece:,0:1].astype(jnp.int32)
        for i in range(5):
            segr_o[:,i*128:(i+1)*128]=jnp.concatenate([meta_s[2*i,0:1],meta_s[min(2*i+1,8),0:1]],axis=1).astype(F32)
        for i in range(4): vec_o[i:i+1]=vector_row(small_s,(2,3,0,1)[i])
        for g in range(4): bias_o[:,g*768:(g+1)*768]=jnp.concatenate([small_s[g,4+i:5+i] for i in range(4)],axis=1).astype(F32)
        rows.finish()
        w_qkv.finish()
        copies[0].start()
        copies[2].start()
    fwd_attn_kernel(half,clean_s,noise_o,segc_o,segr_o,small_s,qkv_s,out_s,trig_s,q_o,k_o,v_o,mix_o,lse_o,x1_o,h_s,bias_s,self_s,mix_s)
    def at(i,*ops):
        @pl.when(p==i)
        def _():
            for op in ops: op()
    at(0,w_out.relay_far,*[partial(w_up.relay_far,i) for i in range(2)])
    at(1,w_out.relay_x,partial(w_up.relay_far,2),partial(w_up.relay_x,0))
    at(2,w_out.finish,copies[1].start,partial(w_up.relay_x,1),partial(w_down.relay_far,0),grads[0].begin_across)
    at(3,partial(w_up.relay_x,2),partial(w_down.relay_far,1))
    at(4,partial(w_down.relay_far,2))
    @pl.when(p==pl.num_programs(0)-1)
    def _():
        for w in (w_up,w_down): w.finish()
        for r in grads: r.finish()
        for d in copies: d.wait()

def whole(shape): return pl.BlockSpec(shape,lambda *i:(0,)*len(shape))
def once(shape): return pl.BlockSpec(shape,lambda *i:(0,)*len(shape),pipeline_mode=pl.Buffered(1))

def fwd_attn(clean,meta,gout,trig,qkv,out,up,down,small):
    piece=clean.shape[2]; half=9*piece; R=2*half
    nt=len(tiles_of(half))*2; ntp=-(-nt//8)*8
    rows=pl.BlockSpec((R,PAIR),lambda p:(0,p))
    sds=jax.ShapeDtypeStruct
    return pl.pallas_call(partial(fwd_attn_comm_kernel,half),grid=(PAIRS,),
        in_specs=[ANYSPACE]*4+[once(a.shape) for a in (qkv,out,up,down,small)],
        out_specs=[rows,rows,rows,rows,pl.BlockSpec((1,ntp,256),lambda p:(p,0,0)),whole((R,D)),whole((half,1)),whole((half,1)),whole((1,640)),whole((4,D)),whole((1,FF))]+[ANYSPACE]*6,
        out_shape=[sds((R,D),BF)]*4+[sds((PAIRS,ntp,256),F32),sds((R,D),F32),sds((half,1),jnp.int32),sds((half,1),F32),sds((1,640),F32),sds((4,D),F32),sds((1,FF),F32),
            sds((D,3*D),BF),sds((D,D),BF),sds((D,FF),BF),sds((FF,D),BF),sds((9,piece,D),BF),sds((9,piece,D),BF)],
        scratch_shapes=[pltpu.VMEM((R,D),BF),pltpu.VMEM((2,half,half),F32),pltpu.VMEM((half,128),F32),pltpu.VMEM((PAIRS,R,PAIR),BF),
            pltpu.VMEM((9,piece,D),BF),pltpu.VMEM((9,)+meta.shape[1:],jnp.int32),pltpu.VMEM((4,)+small.shape,BF),pltpu.VMEM((D,3*D),BF),pltpu.VMEM((D,D),BF),pltpu.VMEM((half,2*PAIR),F32),
            DMA((8,)),DMA((9,)),DMA((8,)),DMA((9,)),DMA((8,)),DMA((9,)),DMA((4,13)),DMA((4,13)),DMA((3,)),DMA((3,)),DMA((14,))],
        compiler_params=pltpu.CompilerParams(vmem_limit_bytes=VMEM_LIMIT,dimension_semantics=("arbitrary",),collective_id=1,has_side_effects=True),
        cost_estimate=pl.CostEstimate(flops=2*R*D*(3*D+D)+24*R*half*D//2*2,bytes_accessed=16<<20,transcendentals=R*half*HEADS),
        name="fwd_attn")(clean,meta,gout,trig,qkv,out,up,down,small)

GC=(2.0/3.141592653589793)**0.5
def cols(refs): return jnp.concatenate([r[...] for r in refs],axis=1)
def rowcat(refs): return jnp.concatenate([r[...] for r in refs],axis=0)
STEPS=FF//512
def up_specs(): return [pl.BlockSpec((D,128),(lambda s:(lambda j:(0,s*STEPS+j)))(s)) for s in range(4)]
def down_specs(): return [pl.BlockSpec((128,D),(lambda s:(lambda j:(s*STEPS+j,0)))(s)) for s in range(4)]
def bias_specs(): return [pl.BlockSpec((1,128),(lambda s:(lambda j:(0,s*STEPS+j)))(s)) for s in range(4)]

FFN_TABLE={2: [(0, None, 0)], 4: [(1, None, 0), (0, 0, 1)], 6: [(2, None, 0), (1, 0, 1)], 8: [(3, None, 0), (0, 1, None), (2, 0, 1)], 9: [(3, 0, None)], 10: [(4, None, 0), (1, 1, None)], 12: [(5, None, 0)]}
FFN_END=[(4, 0), (2, 1), (5, 0)]
ATTN_TABLE={0: [(3, None, 1), (4, None, 1), (5, None, 1), (0, None, 2), (1, None, 2), (2, None, 2)], 1: [(6, None, 0)], 2: [(0, 2, 3), (6, 0, 1)], 3: [(0, 3, 4), (1, 2, 3), (3, 1, 2)], 4: [(7, None, 0), (0, 4, 5), (2, 2, 3)], 5: [(0, 5, 6), (1, 3, 4), (3, 2, 3), (4, 1, 2), (7, 0, 1), (2, 3, 4)], 6: [(0, 6, 7)], 7: [(1, 4, 5), (3, 3, 4), (4, 2, 3), (2, 4, 5), (5, 1, 2)], 8: [(8, None, 0), (0, 7, None), (1, 5, 6), (6, 1, 2)], 9: [(1, 6, 7), (2, 5, 6), (3, 4, 5), (4, 3, 4), (5, 2, 3), (7, 1, 2), (6, 2, 3), (8, 0, 1)], 10: [(2, 6, 7)], 11: [(1, 7, None), (3, 5, 6), (4, 4, 5), (5, 3, 4), (6, 3, 4), (7, 2, 3), (8, 1, 2)], 12: [(9, None, 0)]}
TAIL_ORDER=[("sums", None, 0), (2, 7, None), (3, 6, 7), (4, 5, 6), (5, 4, 5), (6, 4, 5), (7, 3, 4), (8, 2, 3), (9, 0, 1), ("rows", None, 1), ("rows", None, 2), ("sums", 0, 1), (4, 6, 7), ("sums", 1, 2), (3, 7, None), (5, 5, 6), (6, 5, 6), (8, 3, 4), (9, 1, 2), ("rows", None, 3), (7, 4, 5), ("sums", 2, 3), (4, 7, None), ("sums", 3, 4), (5, 6, 7), (9, 2, 3), ("rows", None, 4), (6, 6, 7), (8, 4, 5), ("sums", 4, None), (9, 3, 4), ("rows", None, 5), (5, 7, None), (7, 5, 6), (6, 7, None), (8, 5, 6), (9, 4, 5), ("rows", None, 6), (7, 6, 7), (8, 6, 7), (9, 5, 6), ("rows", None, 7), (7, 7, None), (9, 6, 7), (8, 7, None), (9, 7, None)]

def after(state,table,end):
    state=dict(state)
    for ops in table.values():
        for chunk,take,start in ops:
            if take is not None: state[chunk]=take
    state.update(end)
    return state
FFN_STATE=after({},FFN_TABLE,FFN_END)
def in_state(state,ids,low,high): return [i for i in ids if low<=state[i]<=high]
def started(chunk,table):
    return [start for ops in table.values() for i,take,start in ops if i==chunk and start is not None]

def run_table(table,chunks,position,pid,steps,per_step):
    for i in range(steps):
        ops=table.get(per_step*i+position+1,[])
        if ops:
            @pl.when(pid==i)
            def _(): do_ops(ops,chunks)

def do_ops(ops,chunks):
    for i,take,start in ops:
        if take is not None: chunks[i].take(take)
        if start is not None: chunks[i].start(start)

PHASE=2*STEPS

def ffn_kernel(x1,vec,*refs):
    wup,bup,wdn,rest=refs[:4],refs[4:8],refs[8:12],refs[12:]
    gain,bdn=vec.at[0:1],vec.at[1:2]
    gy0,gout,dbup_o,dbdn_o,dgain_o,gx1_o,block_o,pair_o,total_o,final_o=rest[:10]
    h_s,hT_s,acc,gy_s,out_s,act_s,gu_s,grad_s,pair_s,far_s,total_s,send,recv,g_send,g_recv,b_send,b_recv,local=rest[10:]
    g=pl.program_id(0)
    R=h_s.shape[0]; ch=R//3; piece=R//18
    chunks=[Reduce(TILE,send.at[i],recv.at[i],grad=grad_s.at[i%2],pair=pair_s.at[i],far=far_s.at[i],total=total_s.at[i]) for i in range(STEPS)]
    arrive=ToUnit(lambda q,h:gout.at[q,1,h],lambda t:gy_s.at[9+t],g_send,g_recv,local.at[0])
    leave=[FromUnit(lambda t,i=i:out_s.at[9*i+t],lambda q,h,i=i:block_o.at[q,i,h],b_send.at[i],b_recv.at[i],local.at[1+i]) for i in range(2)]
    first=pltpu.make_async_copy(gy0,gy_s.at[pl.ds(0,9)],local.at[3])
    rows=lambda ref,i: ref[6*i:6*i+6].reshape(ch,D)
    wu=lambda: cols(wup)
    wd=lambda: rowcat(wdn)
    bias=cols(bup).astype(F32)
    @pl.when(g==0)
    def _():
        meet(True,(1,2))
        arrive.begin()
        first.start()
        @pl.when(lax.rem(place_ids()[0],2)==1)
        def _():
            gy_s[16:18]=jnp.zeros((2,)+gy_s.shape[1:],BF)
        n,_=norm_rows(x1[...])
        h=(n*gain[...].astype(F32)).astype(BF)
        h_s[...]=h
        hT_s[...]=h.T
        acc[...]=x1[...]+bdn[...].astype(F32)
    for copy in range(2):
        @pl.when((g>=copy*STEPS)&(g<(copy+1)*STEPS))
        def _():
            for i in range(2):
                r=slice((2*copy+i)*R//4,(2*copy+i+1)*R//4)
                u=dot_nn(h_s[r],wu())+bias
                act=(0.5*u*(1.0+jnp.tanh(GC*(u+0.044715*u*u*u)))).astype(BF)
                acc[r]+=dot_nn(act,wd())
        @pl.when(g==(copy+1)*STEPS-1)
        def _():
            out_s[9*copy:9*copy+9]=acc[copy*R//2:(copy+1)*R//2].astype(BF).reshape(9,piece,D)
            leave[copy].begin()
    @pl.when(g==PHASE-1)
    def _():
        arrive.finish()
        first.wait()
        acc[...]=jnp.zeros_like(acc)
        dbdn_o[...]=jnp.sum(gy_s[...].astype(F32).reshape(R,D),axis=0,keepdims=True)
    @pl.when(g>=PHASE)
    def _():
        j=g-PHASE
        for i in range(2,STEPS):
            @pl.when(j==i)
            def _(): chunks[i-2].sent(0)
        slot=lax.rem(j,2)
        for i in range(3):
            r=slice(i*ch,(i+1)*ch)
            u=dot_nn(h_s[r],wu())+bias
            ga=dot_nt(rows(gy_s,i),wd())
            u2=u*u
            t=jnp.tanh(GC*(u+0.044715*u*u2))
            a=0.5*(1.0+t)
            gu=((a+0.5*u*(1.0-t*t)*(GC*(1.0+3*0.044715*u2)))*ga).astype(BF)
            act_s[r]=(u*a).astype(BF)
            gu_s[r]=gu
            acc[r]+=dot_nt(gu,wu())
        run_table(FFN_TABLE,chunks,0,j,STEPS,2)
        def put(s,row,value):
            for k in range(0,value.shape[0],64):
                grad_s[slot,s%2,s//2,(row+k)//TILE,(row+k)%TILE:(row+k)%TILE+64]=value[k:k+64]
        r=dot_tn(act_s[...],gy_s[...].reshape(R,D)).astype(BF)
        for s in range(4):
            for t in range(6): put(s,768+t*128,r[s*128:(s+1)*128,t*128:(t+1)*128])
        r=dot_nn(hT_s[...],gu_s[...]).astype(BF)
        for s in range(4):
            for t in range(4): put(s,t*192,r[s*192:(s+1)*192,t*128:(t+1)*128])
        dbup_o[...]=jnp.sum(gu_s[...].astype(F32),axis=0,keepdims=True)
        run_table(FFN_TABLE,chunks,1,j,STEPS,2)
    @pl.when(g==pl.num_programs(0)-1)
    def _():
        n,scale=norm_rows(x1[...])
        g2=acc[...]
        dgain_o[...]=jnp.sum(g2*n,axis=0,keepdims=True)
        e=g2*gain[...].astype(F32)
        acc[...]=gy_s[...].astype(F32).reshape(R,D)+scale*(e-jnp.mean(e,axis=-1,keepdims=True)-n*jnp.mean(e*n,axis=-1,keepdims=True))
        outs=[pltpu.make_async_copy(acc,gx1_o,local.at[5])]
        outs[0].start()
        for i,stage in FFN_END: chunks[i].take(stage)
        for low,high,source,target in ((0,0,pair_s,pair_o),(1,3,total_s,total_o)):
            for place,i in enumerate(in_state(FFN_STATE,range(STEPS),low,high)):
                outs.append(pltpu.make_async_copy(source.at[i],target.at[place],local.at[5+len(outs)]))
                outs[-1].start()
        for i in range(STEPS):
            stages=started(i,FFN_TABLE)
            chunks[i].sent(*[x for x in stages if x>0 or i>=STEPS-2])
        for r in leave: r.finish()
        for d in outs: d.wait()

def ffn(x1,vec,wup,bup,wdn,gy0,gout):
    R=x1.shape[0]; half=R//2; piece=half//9
    count=lambda low,high: max(1,len(in_state(FFN_STATE,range(STEPS),low,high)))
    tile=lambda j: lax.rem(j,STEPS)
    ups=[pl.BlockSpec((D,128),(lambda s:(lambda j:(0,s*STEPS+tile(j))))(s)) for s in range(4)]
    downs=[pl.BlockSpec((128,D),(lambda s:(lambda j:(s*STEPS+tile(j),0)))(s)) for s in range(4)]
    biases=[pl.BlockSpec((1,128),(lambda s:(lambda j:(0,s*STEPS+tile(j))))(s)) for s in range(4)]
    return pl.pallas_call(ffn_kernel,grid=(PHASE+STEPS,),
        in_specs=[once((R,D)),once((4,D))]+ups+biases+downs+[ANYSPACE]*2,
        out_specs=[pl.BlockSpec((1,512),lambda j:(0,jnp.maximum(j-PHASE,0))),whole((1,D)),whole((1,D))]+[ANYSPACE]*5,
        out_shape=[jax.ShapeDtypeStruct((1,FF),F32),jax.ShapeDtypeStruct((1,D),F32),jax.ShapeDtypeStruct((1,D),F32),jax.ShapeDtypeStruct((R,D),F32),jax.ShapeDtypeStruct((4,2,2,piece,D),BF),
            jax.ShapeDtypeStruct((count(0,0),2,2,TILE,128),BF),jax.ShapeDtypeStruct((count(1,3),2,TILE,128),BF),jax.ShapeDtypeStruct((1,2,TILE,128),BF)],
        scratch_shapes=[pltpu.VMEM((R,D),BF),pltpu.VMEM((D,R),BF),pltpu.VMEM((R,D),F32),pltpu.VMEM((18,piece,D),BF),pltpu.VMEM((18,piece,D),BF),pltpu.VMEM((R,512),BF),pltpu.VMEM((R,512),BF),
            pltpu.VMEM((2,2,2,2,TILE,128),BF),pltpu.VMEM((STEPS,2,2,TILE,128),BF),pltpu.VMEM((STEPS,2,TILE,128),BF),pltpu.VMEM((STEPS,2,TILE,128),BF),
            DMA((STEPS,8)),DMA((STEPS,8)),DMA((8,)),DMA((9,)),DMA((2,8)),DMA((2,8)),DMA((STEPS+7,))],
        compiler_params=pltpu.CompilerParams(vmem_limit_bytes=VMEM_LIMIT,dimension_semantics=("arbitrary",),collective_id=2,has_side_effects=True),
        cost_estimate=pl.CostEstimate(flops=14*R*D*FF,bytes_accessed=40<<20,transcendentals=2*R*FF),
        name="ffn")(x1,vec,*[wup]*4,*[bup]*4,*[wdn]*4,gy0,gout)

def bwd_attn_kernel(half,xc,noise,segc,segr,vec,gx1,q,k,v,mix,lse,wq,wk,wv,wout,trig,mixed,gain_two,down_shift,up_shift,tile_pair,tile_total,tile_final,
                    tiles_o,wings_o,gin_o,sums_o,hT_s,gh,biasT_s,selfT_s,dq_s,dk_s,dv_s,ga,trig_s,
                    t_pair,t_far,t_total,t_over,t_final,w_grad,w_pair,w_far,w_total,w_over,w_final,gin_s,sum_s,in_s,t_send,t_recv,w_send,w_recv,v_send,v_recv,a_send,a_recv,local):
    p=pl.program_id(0)
    emb,gain=vec.at[2:3],vec.at[3:4]
    rank,_=place_ids()
    R=2*half
    tiles=tiles_of(half)
    pairs=in_state(FFN_STATE,range(STEPS),0,0)
    fars=in_state(FFN_STATE,range(STEPS),0,0)
    slot=lambda ids,i: ids.index(i) if i in ids else 0
    chunks=[Reduce(TILE,t_send.at[i],t_recv.at[i],pair=t_pair.at[slot(pairs,i)],far=t_far.at[slot(fars,i)],total=t_total.at[i],over=t_over.at[i],final=t_final.at[i]) for i in range(STEPS)]
    chunks+=[Reduce(WING,w_send.at[i],w_recv.at[i],grad=w_grad.at[i],pair=w_pair.at[i],far=w_far.at[i],total=w_total.at[i],over=w_over.at[i],final=w_final.at[i]) for i in range(4)]
    def tick(position):
        run_table(ATTN_TABLE,chunks,position,p,PAIRS,2)
    @pl.when(p==0)
    def _():
        loads=[pltpu.make_async_copy(trig.at[rank%2],trig_s,local.at[2])]
        loads[0].start()
        for low,high,source,target in ((0,0,tile_pair,t_pair),(1,3,tile_total,t_total),(4,7,tile_final,t_final)):
            for place,i in enumerate(in_state(FFN_STATE,range(STEPS),low,high)):
                loads.append(pltpu.make_async_copy(source.at[place],target.at[place if low==0 else i],local.at[2+len(loads)]))
                loads[-1].start()
        ga[...]=gx1[...].astype(BF)
        for d in loads: d.wait()
        meet(True,(1,2))
        do_ops(ATTN_TABLE.get(0,[]),chunks)
        g=gain[...].astype(F32)
        for c,rows in enumerate(layer_rows(xc,noise,emb)):
            n,_=norm_rows(rows)
            hT_s[:,c*half:(c+1)*half]=(n*g).astype(BF).T
        gh[...]=jnp.zeros_like(gh)
        for s,m in tiles:
            n=s+m
            qb=(lax.broadcasted_iota(jnp.int32,(n,m),1)+s)//BLK
            kb=lax.broadcasted_iota(jnp.int32,(n,m),0)//BLK
            same=segc[:n]==segr[:,s:n]
            biasT_s[0,:n,s:n]=jnp.where(same&(kb<qb),0.0,NEG)
            biasT_s[1,:n,s:n]=jnp.where(same&(kb<=qb),0.0,NEG)
            qb=lax.broadcasted_iota(jnp.int32,(m,m),1)//BLK
            kb=lax.broadcasted_iota(jnp.int32,(m,m),0)//BLK
            same=segc[s:n]==segr[:,s:n]
            selfT_s[s:n,:m]=jnp.where(same&(kb==qb),0.0,NEG)
    gm=dot_nt(ga[...],wout[...]).astype(BF)
    @pl.when(p==0)
    def _():
        r=dot_tn(mixed[...],ga[...]).astype(BF)
        for a in range(4):
            for t in range(6): w_grad[0,a%2,a//2,t//3,t%3*192:(t%3+1)*192]=r[a*192:(a+1)*192,t*128:(t+1)*128]
    gd=gm.astype(F32)*mix[...].astype(F32)
    dk_s[...]=jnp.zeros_like(dk_s); dv_s[...]=jnp.zeros_like(dv_s)
    idx=0
    for s,m in tiles:
        n=s+m
        for c in (0,1):
            rs=slice(c*half+s,c*half+n)
            qs=head_stack(q[rs]); gs=head_stack(gm[rs])
            delta=jnp.sum(head_stack(gd[rs]).T,axis=0,keepdims=True)
            row=lse[0,idx:idx+1,:2*m]
            def part(krows,bias):
                kc=k[krows]; vc=v[krows]
                st=dot_nt(kc,qs)+jnp.concatenate([bias,bias],axis=1)
                pt=jnp.exp(st-row)
                dp=dot_nt(vc,gs)
                ds=(pt*(dp-delta)).astype(BF)
                dv_s[krows]+=dot_nn(pt.astype(BF),gs)
                dk_s[krows]+=dot_nn(ds,qs)
                return dot_tn(ds,kc)
            dq=part(slice(half,half+n),biasT_s[c,:n,s:n])
            if c==0: dq=dq+part(slice(s,n),selfT_s[s:n,:m])
            dq_s[rs]=head_merge(dq)*HEAD**-0.5
            idx+=1
        if s==256: tick(0)
    cs=jnp.concatenate([trig_s[:,:PAIR]]*2,axis=0)
    sn=jnp.concatenate([trig_s[:,PAIR:]]*2,axis=0)
    z=jnp.concatenate([(g[...]*cs-swap_halves(g[...])*sn).astype(BF) for g in (dq_s,dk_s)]+[dv_s[...].astype(BF)],axis=1)
    r=dot_nn(hT_s[...],z).astype(BF)
    group=1+p//2
    for a in range(4):
        for t in range(3):
            w_grad[group,a%2,a//2,lax.rem(p,2),t*192:(t+1)*192]=r[a*192:(a+1)*192,t*128:(t+1)*128]
    gh[...]+=dot_nt(z,cols((wq,wk,wv)))
    tick(1)
    @pl.when(p==pl.num_programs(0)-1)
    def _():
        g=gain[...].astype(F32)
        outs=[]; dg=0.0
        for c,rows in enumerate(layer_rows(xc,noise,emb)):
            n,scale=norm_rows(rows)
            g1=gh[c*half:(c+1)*half]
            dg=dg+jnp.sum(g1*n,axis=0,keepdims=True)
            e=g1*g
            outs.append(gx1[c*half:(c+1)*half]+scale*(e-jnp.mean(e,axis=-1,keepdims=True)-n*jnp.mean(e*n,axis=-1,keepdims=True)))
        masked=noise[...]==1
        gin=(outs[1]+jnp.where(masked,0.0,outs[0])).astype(BF)
        gin_s[...]=gin.reshape(gin_s.shape)
        demb=jnp.sum(jnp.where(masked,outs[0],0.0),axis=0,keepdims=True)
        row=0
        for part in (demb,dg,gain_two,down_shift):
            for n in range(D//128):
                sum_s[0,row:row+1]=part[:,n*128:(n+1)*128]
                row+=1
        for a in range(4):
            for n in range(STEPS):
                sum_s[0,row:row+1]=up_shift[:,n*512+a*128:n*512+(a+1)*128]
                row+=1
        units=FromUnit(lambda t:gin_s.at[t],lambda q,h:gin_o.at[q,h],a_send,a_recv,local.at[0])
        some=chunks[STEPS]
        vectors=[remote(sum_s.at[n],in_s.at[n],v_send.at[n],v_recv.at[n],where) for n,where in enumerate((some.sib,some.far_id,some.xn,some.z1n,some.z2n))]
        for item,take,start in TAIL_ORDER:
            if item=="rows":
                if start==1: units.begin_rest()
                units.begin_one(start)
            elif item=="sums":
                if take is not None:
                    vectors[take].wait_recv()
                    sum_s[take+1]=sum_s[take]+in_s[take]
                if start is not None: vectors[start].start()
            else: do_ops([(item,take,start)],chunks)
        stores=[pltpu.make_async_copy(t_final,tiles_o,local.at[1]),pltpu.make_async_copy(w_final,wings_o,local.at[2])]
        for d in stores: d.start()
        sums_o[...]=sum_s[5]
        for d in vectors: d.wait_send()
        for n,chunk in enumerate(chunks):
            chunk.sent(*(started(n,ATTN_TABLE)+[start for item,take,start in TAIL_ORDER if item==n and start is not None]))
        units.finish()
        for d in stores: d.wait()

def bwd_attn(xc,noise,segc,segr,vec,gx1,q,k,v,mix,lse,wqkv,wout,trig,vectors,tile_pair,tile_total,tile_final):
    half=xc.shape[0]; R=2*half; piece=half//9
    ntp=lse.shape[1]
    ws=[pl.BlockSpec((D,PAIR),(lambda off:(lambda p:(0,off+p)))(o*PAIRS)) for o in range(3)]
    rows=pl.BlockSpec((R,PAIR),lambda p:(0,p))
    pairs=max(1,len(in_state(FFN_STATE,range(STEPS),0,0)))
    return pl.pallas_call(partial(bwd_attn_kernel,half),grid=(PAIRS,),
        in_specs=[once((half,D)),once((half,1)),once((half,1)),once((1,640)),once((4,D)),once((R,D)),rows,rows,rows,rows,
                  pl.BlockSpec((1,ntp,256),lambda p:(p,0,0)),*ws,pl.BlockSpec((PAIR,D),lambda p:(p,0)),ANYSPACE,once((R,D))]+[once(a.shape) for a in vectors]+[ANYSPACE]*3,
        out_specs=[ANYSPACE]*3+[whole((48,128))],
        out_shape=[jax.ShapeDtypeStruct((STEPS,2,TILE,128),BF),jax.ShapeDtypeStruct((4,2,WING,128),BF),jax.ShapeDtypeStruct((4,2,piece,D),BF),jax.ShapeDtypeStruct((48,128),F32)],
        scratch_shapes=[pltpu.VMEM((D,R),BF),pltpu.VMEM((R,D),F32),pltpu.VMEM((2,half,-(-half//128)*128),F32),pltpu.VMEM((half,128),F32)]+[pltpu.VMEM((R,PAIR),F32)]*3+[pltpu.VMEM((R,D),BF),pltpu.VMEM((half,2*PAIR),F32)]
            +[pltpu.VMEM((pairs,2,2,TILE,128),BF),pltpu.VMEM((pairs,2,TILE,128),BF),pltpu.VMEM((STEPS,2,TILE,128),BF),pltpu.VMEM((STEPS,2*TILE,128),BF),pltpu.VMEM((STEPS,2,TILE,128),BF),
              pltpu.VMEM((4,2,2,2,WING,128),BF),pltpu.VMEM((4,2,2,WING,128),BF),pltpu.VMEM((4,2,WING,128),BF),pltpu.VMEM((4,2,WING,128),BF),pltpu.VMEM((4,2*WING,128),BF),pltpu.VMEM((4,2,WING,128),BF),pltpu.VMEM((9,piece,D),BF),pltpu.VMEM((6,48,128),F32),pltpu.VMEM((5,48,128),F32),
              DMA((STEPS,8)),DMA((STEPS,8)),DMA((4,8)),DMA((4,8)),DMA((5,)),DMA((5,)),DMA((8,)),DMA((8,)),DMA((16,))],
        compiler_params=pltpu.CompilerParams(vmem_limit_bytes=VMEM_LIMIT,dimension_semantics=("arbitrary",),collective_id=3,has_side_effects=True),
        cost_estimate=pl.CostEstimate(flops=4*R*D*(3*D+D)+60*R*half*D//2*2,bytes_accessed=30<<20,transcendentals=R*half*HEADS),
        name="bwd_attn")(xc,noise,segc,segr,vec,gx1,q,k,v,mix,lse,wqkv,wqkv,wqkv,wout,trig,mix,*vectors,tile_pair,tile_total,tile_final)

def assemble(ffn,wings,gin,block):
    piece=gin.shape[2]
    sds=jax.ShapeDtypeStruct
    quarter=lambda i: (jnp.minimum(i,3),0,0)
    up,out,qkv,down,grad,rows=pl.pallas_call(assemble_kernel,grid=(STEPS,),
        in_specs=[pl.BlockSpec((1,2,TILE,128),lambda i:(i,0,0,0)),pl.BlockSpec((None,None,WING,128),lambda i:(1+i//2,lax.rem(i,2),0,0)),
            pl.BlockSpec((None,None,192,128),lambda i:(0,i//3,lax.rem(i,3),0)),pl.BlockSpec((2,piece,D),quarter),pl.BlockSpec((4,piece,D),quarter)],
        out_specs=[ANYSPACE]*3+[pl.BlockSpec((128,D),lambda i:(i,0)),pl.BlockSpec((2,piece,D),quarter),pl.BlockSpec((4,piece,D),quarter)],
        out_shape=[sds((192,FF),F32),sds((192,D),F32),sds((192,3*D),F32),sds((768,D),F32),sds((8,piece,D),F32),sds((16,piece,D),BF)],
        scratch_shapes=[pltpu.VMEM((2,8,192,128),F32),DMA((2,8))],
        compiler_params=pltpu.CompilerParams(vmem_limit_bytes=VMEM_LIMIT,dimension_semantics=("arbitrary",)),
        name="assemble")(ffn,wings,wings,gin.reshape(8,piece,D),block.reshape(16,piece,D))
    return up,down,out,qkv,grad,rows


DMA = pltpu.SemaphoreType.DMA
MESH = pl.DeviceIdType.MESH
INVMEM = pl.BlockSpec(memory_space=pltpu.VMEM)
ANYSPACE = pl.BlockSpec(memory_space=pl.ANY)


def place_ids():
    return lax.axis_index("ctx"), lax.axis_index("fsdp")


def meet(all_ranks, fsdp_partners):
    c, f = place_ids()
    sem = pltpu.get_barrier_semaphore()
    count = 0
    ranks = [(c + s) % 8 for s in range(1, 8)] if all_ranks else [c + 1 - 2 * (c % 2)]
    for rank in ranks:
        pl.semaphore_signal(sem, inc=1, device_id={"ctx": rank}, device_id_type=MESH)
        count += 1
    for s in fsdp_partners:
        other = (f + 2) % 4 if s == 2 else f + 1 - 2 * (f % 2) if s == 1 else 3 - f
        pl.semaphore_signal(sem, inc=1, device_id={"fsdp": other}, device_id_type=MESH)
        count += 1
    pl.semaphore_wait(sem, count)


def remote(src, dst, send, recv, where):
    return pltpu.make_async_remote_copy(src_ref=src, dst_ref=dst, send_sem=send, recv_sem=recv, device_id=where,
                                        device_id_type=MESH)


class ToUnit:
    def __init__(self, source, target, send, recv, local):
        self.source, self.target, self.send, self.recv, self.local = source, target, send, recv, local
        self.c, _ = place_ids()

    def message(self, s):
        c = self.c
        t = (c + s) % 8
        odd, last = t % 2, c // 7
        slot = (1 - odd) * c + odd * ((1 - last) * (6 - c) + last * 8)
        return remote(self.source(t // 2, odd), self.target(slot), self.send.at[s], self.recv.at[slot],
                      {"ctx": t - odd * last})

    def begin(self):
        for s in (1, 7, 3, 5, 2, 6, 4):
            self.message(s).start()

        @pl.when(self.c == 7)
        def _():
            self.message(0).start()

        @pl.when(self.c != 7)
        def _():
            self.own_safe().start()

    def begin_straight(self):
        for s in (2, 4, 6):
            self.message(s).start()

        @pl.when(self.c != 7)
        def _():
            self.own_safe().start()

    def begin_across(self):
        for s in (1, 3, 5, 7):
            self.message(s).start()

        @pl.when(self.c == 7)
        def _():
            self.message(0).start()

    def own_safe(self):
        c = self.c
        part = c % 2
        slot = (1 - part) * c + part * (6 - c + c // 7)
        return pltpu.make_async_copy(self.source(c // 2, part), self.target(slot), self.local)

    def finish(self):
        c = self.c
        part = c % 2

        @pl.when(c == 7)
        def _():
            self.message(0).wait_send()

        @pl.when(c != 7)
        def _():
            self.own_safe().wait()

        for s in range(1, 8):
            self.message(s).wait_send()
        own = (1 - part) * c + part * (6 - c)
        for slot in range(9):
            take = slot != own
            if slot > 6:
                take = take & (part == 0)

            @pl.when(take)
            def _():
                remote(self.target(slot), self.target(slot), self.send.at[0], self.recv.at[slot], {"ctx": c}).wait_recv()


class FromUnit:
    def __init__(self, source, target, send, recv, local):
        self.source, self.target, self.send, self.recv, self.local = source, target, send, recv, local
        self.c, _ = place_ids()

    def message(self, s):
        c = self.c
        part = c % 2
        rank = (c + s) % 8
        slot = (1 - part) * rank + part * (6 - rank + rank // 7)
        return remote(self.source(slot), self.target(c // 2, part), self.send.at[s], self.recv.at[c], {"ctx": rank})

    def extra(self):
        c = self.c
        seq = c // 2
        return remote(self.source(8), self.target(seq, 1), self.send.at[0], self.recv.at[2 * seq + 1], {"ctx": 7})

    def own(self):
        c = self.c
        part = c % 2
        slot = (1 - part) * c + part * (6 - c + c // 7)
        return pltpu.make_async_copy(self.source(slot), self.target(c // 2, part), self.local)

    def each(self, remote_op, own_op):
        c = self.c
        part = c % 2
        @pl.when(part == 0)
        def _():
            remote_op(self.extra())

        for s in (1, 7, 3, 5, 2, 6, 4):
            rank = (c + s) % 8

            @pl.when((part == 0) | (rank != 7))
            def _():
                remote_op(self.message(s))

        @pl.when(c != 7)
        def _():
            own_op(self.own())

    def begin_one(self, s):
        c = self.c

        @pl.when((c % 2 == 0) | ((c + s) % 8 != 7))
        def _():
            self.message(s).start()

    def begin_rest(self):
        c = self.c

        @pl.when(c % 2 == 0)
        def _():
            self.extra().start()

        @pl.when(c != 7)
        def _():
            self.own().start()

    def begin(self):
        self.each(lambda m: m.start(), lambda m: m.start())

    def finish(self):
        self.each(lambda m: m.wait_send(), lambda m: m.wait())
        c = self.c
        for block in range(8):
            @pl.when((c == 7) | (c != block))
            def _():
                ref = self.target(block // 2, block % 2)
                remote(ref, ref, self.send.at[0], self.recv.at[block], {"ctx": c}).wait_recv()


class GatherRows:
    def __init__(self, shard, full, send, recv, local, parts=1, share=True):
        c, f = place_ids()
        n = shard.shape[0]
        n2 = n // 2 if share else n
        m = n2 // parts
        h = c % 2 if share else 0
        sib, far, xn = f + 1 - 2 * (f % 2), (f + 2) % 4, c + 1 - 2 * (c % 2)
        diag = (sib + 2) % 4
        rows = lambda start, size: full.at[pl.ds(pl.multiple_of(start, 16), size)]
        same = lambda ref, i, where: remote(ref, ref, send.at[i], recv.at[i], where)
        mine = rows(f * n, n)
        self.copy = pltpu.make_async_copy(shard, mine, local)
        self.to_core = remote(shard, mine, send.at[0], recv.at[0], {"fsdp": sib})
        self.from_core = same(rows(sib * n, n), 0, {"fsdp": sib})
        self.to_far, self.from_far, self.to_x, self.from_x = [], [], [], []
        self.near_core, self.away_core, self.from_near, self.from_away = [], [], [], []
        for i in range(parts):
            a, b = h * n2 + i * m, (1 - h) * n2 + i * m
            near, away = rows(far * n + a, m), rows(far * n + b, m)
            k = 1 + 4 * i
            self.to_far.append(remote(shard.at[pl.ds(pl.multiple_of(a, 16), m)], rows(f * n + a, m), send.at[k], recv.at[k],
                                      {"fsdp": far}))
            self.from_far.append(same(near, k, {"fsdp": far}))
            self.near_core.append(same(near, k + 2, {"fsdp": sib}))
            self.from_near.append(same(rows(diag * n + a, m), k + 2, {"fsdp": sib}))
            if share:
                self.to_x.append(same(near, k + 1, {"ctx": xn}))
                self.from_x.append(same(away, k + 1, {"ctx": xn}))
                self.away_core.append(same(away, k + 3, {"fsdp": sib}))
                self.from_away.append(same(rows(diag * n + b, m), k + 3, {"fsdp": sib}))

    def begin(self):
        for copy in self.to_far:
            copy.start()
        self.to_core.start()
        self.copy.start()

    def relay_far(self, i=0):
        self.from_far[i].wait_recv()
        if self.to_x:
            self.to_x[i].start()
        self.near_core[i].start()

    def relay_x(self, i=0):
        self.from_x[i].wait_recv()
        self.away_core[i].start()

    def finish(self):
        self.copy.wait()
        for copy in [self.to_core] + self.to_far + self.to_x + self.near_core + self.away_core:
            copy.wait_send()
        for copy in [self.from_core] + self.from_near + self.from_away:
            copy.wait_recv()


class Reduce:
    def __init__(self, rows, send, recv, across=False, grad=None, pair=None, far=None, total=None, over=None, final=None):
        c, f = place_ids()
        self.send, self.recv, self.across = send, recv, across
        self.grad, self.pair, self.far, self.total, self.over, self.final = grad, pair, far, total, over, final
        self.core, self.y, self.x = f % 2, f // 2, c % 2
        z1, z2 = (c // 2) % 2, c // 4
        self.sib, self.far_id = {"fsdp": f + 1 - 2 * self.core}, {"fsdp": (f + 2) % 4}
        self.xn, self.z1n, self.z2n = {"ctx": c + 1 - 2 * self.x}, {"ctx": c + 2 - 4 * z1}, {"ctx": c + 4 - 8 * z2}
        half, quarter = rows // 2, rows // 4
        self.rows = rows
        self.levels = [(z1 * half, (1 - z1) * half, half, rows, self.z1n)]
        base = z1 * half
        self.levels.append((base + z2 * quarter, base + (1 - z2) * quarter, quarter, rows + half, self.z2n))

    def at(self, ref, start, size):
        return ref.at[self.x, pl.ds(pl.multiple_of(start, 16), size)]

    def copy(self, stage):
        x, y = self.x, self.y
        if stage == 0:
            source, target, where = self.grad.at[1 - self.core], self.pair, self.sib
        elif stage == 1 and self.across:
            source, target, where = self.pair.at[:, 1 - x], self.far, self.xn
        elif stage == 1:
            source, target, where = self.pair.at[1 - y], self.far, self.far_id
        elif stage == 2 and self.across:
            source, target, where = self.pair.at[1 - y, x], self.over.at[pl.ds(0, self.rows)], self.far_id
        elif stage == 2:
            source, target, where = self.total.at[1 - x], self.over.at[pl.ds(0, self.rows)], self.xn
        elif stage < 5:
            keep, give, size, offset, where = self.levels[stage - 3]
            source, target = self.at(self.total, give, size), self.over.at[pl.ds(offset, size)]
        elif stage < 7:
            keep, give, size, offset, where = self.levels[6 - stage]
            source = target = self.at(self.final, keep, size)
        else:
            source, target, where = self.final.at[x], self.final.at[x], self.xn
        return remote(source, target, self.send.at[stage], self.recv.at[stage], where)

    def start(self, stage):
        self.copy(stage).start()

    def take(self, stage):
        x, y = self.x, self.y
        if stage < 5:
            self.copy(stage).wait_recv()
        if stage == 0:
            self.pair[...] = self.pair[...] + self.grad[self.core]
        elif stage == 1 and self.across:
            for i in range(2):
                self.pair[i, x] = self.pair[i, x] + self.far[i]
        elif stage == 1:
            self.total[...] = self.far[...] + self.pair[y]
        elif stage == 2 and self.across:
            self.total[x] = self.pair[y, x] + self.over[pl.ds(0, self.rows)]
        elif stage == 2:
            self.total[x] = self.total[x] + self.over[pl.ds(0, self.rows)]
        elif stage < 5:
            keep, give, size, offset, where = self.levels[stage - 3]
            into = self.at(self.final if stage == 4 else self.total, keep, size)
            into[...] = self.at(self.total, keep, size)[...] + self.over[pl.ds(offset, size)]
        elif stage < 7:
            keep, give, size, offset, where = self.levels[6 - stage]
            ref = self.at(self.final, give, size)
            remote(ref, ref, self.send.at[stage], self.recv.at[stage], where).wait_recv()
        else:
            ref = self.final.at[1 - x]
            remote(ref, ref, self.send.at[7], self.recv.at[7], self.xn).wait_recv()

    def sent(self, *stages):
        for stage in stages:
            self.copy(stage).wait_send()


TILE = 768
WING = 576


def assemble_kernel(ffn, pair, out, gin, block, up_o, out_o, qkv_o, down_o, gin_o, block_o, stage, sem):
    i = pl.program_id(0)
    slot = lax.rem(i, 2)

    def copies(step, place):
        column = lambda k: pl.ds(pl.multiple_of(k * 128, 128), 128)
        targets = [up_o.at[:, column(s * STEPS + step)] for s in range(4)] + [out_o.at[:, column(step)]]
        targets += [qkv_o.at[:, column(w * PAIRS + step)] for w in range(3)]
        return [pltpu.make_async_copy(stage.at[place, k], target, sem.at[place, k]) for k, target in enumerate(targets)]

    @pl.when(i >= 2)
    def _():
        for copy in copies(i - 2, slot):
            copy.wait()

    tile = lambda r: ffn[0, r // TILE, r % TILE:r % TILE + 64].astype(F32)
    for r in range(0, 192, 64):
        for s in range(4):
            stage[slot, s, r:r + 64] = tile(s * 192 + r)
        stage[slot, 4, r:r + 64] = out[r:r + 64].astype(F32)
        for w in range(3):
            stage[slot, 5 + w, r:r + 64] = pair[w * 192 + r:w * 192 + r + 64].astype(F32)
    for copy in copies(i, slot):
        copy.start()
    for t in range(6):
        for r in range(0, 128, 64):
            down_o[r:r + 64, t * 128:(t + 1) * 128] = tile(768 + t * 128 + r)
    gin_o[...] = gin[...].astype(F32)
    block_o[...] = block[...]

    @pl.when(i == STEPS - 1)
    def _():
        for copy in copies(i - 1, 1 - slot) + copies(i, slot):
            copy.wait()


def rope_constant(half):
    position = np.arange(2 * half, dtype=np.float32)
    frequency = np.float32(10000.0) ** (-(np.arange(HEAD // 2, dtype=np.float32) * np.float32(2.0)) / np.float32(HEAD))
    angles = (position[:, None] * frequency[None, :]).astype(np.float64)
    cosine, sine = np.cos(angles), np.sin(angles)
    table = np.concatenate([np.tile(cosine, (1, 4)), np.tile(np.concatenate([-sine, sine], axis=1), (1, 2))], axis=1)
    return jnp.asarray(table.reshape(2, half, 4 * HEAD).astype(np.float32))


def even_body(clean_in, segments, noise, mask_embed, norm1_gain, qkv_weight, out_weight, norm2_gain, up_weight, up_bias,
              down_weight, down_bias, out_grad):
    place = lax.axis_index("fsdp")
    piece = clean_in.shape[2]
    half = 9 * piece
    width = mask_embed.shape[0]
    line = lax.broadcasted_iota(jnp.int32, (8, 8, piece), 1)
    meta = jnp.where(line == 0, segments.reshape(8, 1, piece), noise.reshape(8, 1, piece))
    row = lax.broadcasted_iota(jnp.int32, (16, width), 0)
    small = jnp.zeros((16, width), BF)
    for i, vector in enumerate((mask_embed, norm1_gain, norm2_gain, down_bias)):
        small = jnp.where(row == i, vector[None], small)
    for i in range(4):
        small = jnp.where(row == 4 + i, up_bias[i * width:(i + 1) * width][None], small)
    q, k, v, mixed, lse, resid, mask, seg_col, seg_row, vectors, up_shift, qkv_full, out_full, up_full, down_full, cotangent, clean = fwd_attn(
        clean_in, meta, out_grad, rope_constant(half), qkv_weight, out_weight, up_weight, down_weight, small)
    clean = clean.reshape(half, D)
    up_shift_grad, down_shift_grad, gain_two_grad, grad_resid, block_out, tile_pair, tile_total, tile_final = ffn(
        resid, vectors, up_full, up_shift, down_full, cotangent, out_grad)
    tiles, wings, input_grad, sums = bwd_attn(
        clean, mask, seg_col, seg_row, vectors, grad_resid, q, k, v, mixed, lse, qkv_full, out_full, rope_constant(half),
        (gain_two_grad, down_shift_grad, up_shift_grad), tile_pair, tile_total, tile_final)
    up_sum, down_sum, out_sum, qkv_sum, input_grad, block_out = assemble(tiles, wings, input_grad, block_out)
    input_grad = input_grad.reshape(clean_in.shape)
    block_out = block_out.reshape(out_grad.shape)
    sums = sums.reshape(-1)
    own = [lax.dynamic_slice_in_dim(sums, i * D + place * width, width) for i in range(4)]
    own_up = lax.dynamic_slice_in_dim(sums, 4 * D + place * (FF // 4), FF // 4)
    return (block_out, input_grad, own[0], own[1], qkv_sum, out_sum, own[2], up_sum, own_up, down_sum, own[3])


def choose_body(axes, *arrays):
    even = axes["ctx"] == 8 and axes["fsdp"] == 4 and arrays[0].shape[0] == 4
    return (even_body if even else general_body)(*arrays)


def solution(mesh):
    placed = (
        P("fsdp", None, "ctx", None),
        P("fsdp", None, "ctx"),
        P("fsdp", None, "ctx"),
        P("fsdp"),
        P("fsdp"),
        P("fsdp", None),
        P("fsdp", None),
        P("fsdp"),
        P("fsdp", None),
        P("fsdp"),
        P("fsdp", None),
        P("fsdp"),
        P("fsdp", None, None, "ctx", None),
    )
    return jax.shard_map(
        partial(choose_body, dict(mesh.shape)),
        mesh=mesh,
        in_specs=placed,
        out_specs=(
            P("fsdp", None, None, "ctx", None),
            P("fsdp", None, "ctx", None),
            P("fsdp"),
            P("fsdp"),
            P("fsdp", None),
            P("fsdp", None),
            P("fsdp"),
            P("fsdp", None),
            P("fsdp"),
            P("fsdp", None),
            P("fsdp"),
        ),
        check_vma=False,
    )
```
